32 devices in a mesh: docs: 8 (over y, x, core), heads: 4 (over z).
Axes of the slice: x: 2, y: 2, z: 4, core: 2. Of those that a mesh axis runs over, the one named last changes fastest.
Arguments:
- layer_input: bfloat16 [16384, 768], P(('docs', 'heads')), may hold values from -6 to 6
- token_boxes: int32 [2, 16384], P(None, 'docs'), may hold values from 0 to 999, as said below
- lengths: int32 [32], P('docs'), may hold values from 32 to 512, as said below
- w_qkv: bfloat16 [768, 3, 768], P(None, None, 'heads'), may hold values from -0.21875 to 0.21875
- qv_bias: bfloat16 [2, 768], P(None, 'heads'), may hold values from -3 to 3
- rel_tables: bfloat16 [2, 12, 32], P(None, 'heads'), may hold values from -4 to 4
- w_out: bfloat16 [768, 768], replicated, may hold values from -0.875 to 0.875
- out_bias: float32 [768], replicated, may hold values from -1 to 1
- gain_one: float32 [768], replicated, may hold values from 0.5 to 1.5
- shift_one: float32 [768], replicated, may hold values from -1 to 1
- w_in: bfloat16 [768, 3072], replicated, may hold values from -0.21875 to 0.21875
- in_bias: float32 [3072], replicated, may hold values from -1 to 1
- w_back: bfloat16 [3072, 768], replicated, may hold values from -0.109375 to 0.109375
- back_bias: float32 [768], replicated, may hold values from -1 to 1
- gain_two: float32 [768], replicated, may hold values from 0.5 to 1.5
- shift_two: float32 [768], replicated, may hold values from -1 to 1
- cotangent: bfloat16 [16384, 768], P(('docs', 'heads')), may hold values from -6 to 6
Outputs:
- layer_output: bfloat16 [16384, 768], P(('docs', 'heads'))
- grad_input: bfloat16 [16384, 768], P(('docs', 'heads'))
- grad_qkv: float32 [768, 3, 768], P(None, None, 'heads')
- grad_qv_bias: float32 [2, 768], P(None, 'heads')
- grad_tables: float32 [2, 12, 32], P(None, 'heads')
- grad_out: float32 [768, 768], P('docs')
- grad_out_bias: float32 [768], P('docs')
- grad_gain_one: float32 [768], P('docs')
- grad_shift_one: float32 [768], P('docs')
- grad_in: float32 [768, 3072], P('docs')
- grad_in_bias: float32 [3072], P('docs')
- grad_back: float32 [3072, 768], P('docs')
- grad_back_bias: float32 [768], P('docs')
- grad_gain_two: float32 [768], P('docs')
- grad_shift_two: float32 [768], P('docs')
The draws below stay inside these ranges and needn't reach their ends.
Inputs may be any that keep to these rules, and one draw needn't show every extreme that they name: `lengths`: filled tokens of each window; slots after them are padding. Some window is full in every draw. `token_boxes`: box coordinates of each token, row 0 left and row 1 top, on a page of 1000 by 1000.
All inputs are finite; a program needn't handle non-finite values.
Results may differ from the reference program's by a relative error of at most 0.017.
The reference program's roundings to bfloat16 on the way count: a program that leaves them out, or rounds other values in their place, can miss the bound.
Values may be sent and summed in bfloat16 or wider, within the bound.
No kernel may reach another device: no remote copies, remote signals or barrier semaphores. Data moves between devices by JAX's collectives and lax.ppermute only.
A program may use at most 192 MiB of HBM per device.

```python
import math
import jax
import jax.numpy as jnp
from jax import lax

D = 768
HEADS = 12
HEAD_DIM = 64
FF = 3072
NBUCKET = 32
L = 512
WIN_GROUP = 4
WINDOWS = 32
TOKENS = 16384
N_DOCS = 8


def draw_lengths(key, part):
    floor_len = L // 16
    spare_room = L - floor_len
    first_key, second_key, third_key = jax.random.split(key, 3)
    left_side = jax.random.randint(first_key, (WINDOWS,), 0, spare_room + 1)
    right_side = jax.random.randint(second_key, (WINDOWS,), 0, spare_room + 1)
    drawn_len = floor_len + left_side * right_side // spare_room
    chosen = jax.random.randint(third_key, (), 0, WINDOWS)
    return jnp.where(jnp.arange(WINDOWS) == chosen, L, drawn_len).astype(jnp.int32)


def draw_token_boxes(key, part):
    across_key, down_key = jax.random.split(key)
    positions = jnp.arange(TOKENS, dtype=jnp.int32) % L
    left_edge = positions % 12 * 83 + jax.random.randint(across_key, (TOKENS,), 0, 87)
    top_edge = jnp.minimum(positions // 12 * 24 + jax.random.randint(down_key, (TOKENS,), 0, 8), 999)
    return jnp.stack([left_edge, top_edge]).astype(jnp.int32)


def with_spikes(array, rng, source, target, shards_of, factor):
    owner, partner = [(jnp.arange(array.shape[axis_at]) // (array.shape[axis_at] // shards_of)).reshape([-1 if axis == axis_at else 1 for axis in range(array.ndim)]) for axis_at in (source, target)]
    chosen = jax.random.permutation(rng, shards_of)[partner]
    strong = (owner == chosen) | (owner == (partner + shards_of // 2) % shards_of)
    return jnp.where(strong, factor * array, array)


def block_levels(key, extent, cuts, low, high):
    factor_of, own = 1.0, jax.random.fold_in(key, 6)
    for position, blocks in cuts:
        draws = jnp.exp(jax.random.uniform(jax.random.fold_in(own, position), (blocks,), jnp.float32, low / len(cuts), high / len(cuts)))
        factor_of = factor_of * jnp.repeat(draws, extent[position] // blocks).reshape([-1 if axis == position else 1 for axis in range(len(extent))])
    return factor_of


def scatter_about(rng, shape, scale, bound, cuts=(), kind=jnp.bfloat16):
    gain = block_levels(rng, shape, cuts, -0.22, 0.18) if cuts else 1.0
    values = jax.random.normal(rng, shape, jnp.float32) * scale * gain
    return jnp.minimum(jnp.maximum(values, -bound), bound).astype(kind)


def gaussian_with(own_key, dims, deviation, reach, pieces, heavy, kind=jnp.bfloat16):
    drawn = deviation * jax.random.normal(own_key, dims, jnp.float32)
    if pieces:
        drawn = drawn * block_levels(own_key, dims, pieces, -0.22, 0.18)
    return jnp.clip(with_spikes(drawn, jax.random.fold_in(own_key, 3), *heavy), -reach, reach).astype(kind)


def setup_inputs(seed: int = 0) -> dict:
    arg_keys = jax.random.split(jax.random.key(seed), 18)
    layer_input = scatter_about(arg_keys[0], (TOKENS, D), 1.0, 6.0, ((0, 32),))
    token_boxes = draw_token_boxes(jax.random.fold_in(arg_keys[17], 71), 0)
    lengths = draw_lengths(jax.random.fold_in(arg_keys[17], 71), 0)
    w_qkv = scatter_about(arg_keys[3], (D, 3, D), D ** -0.5, 0.21875, ((2, 4),))
    qv_bias = scatter_about(arg_keys[4], (2, D), 0.5, 3.0, ((1, 4),))
    rel_tables = scatter_about(arg_keys[5], (2, HEADS, NBUCKET), 1.0, 4.0, ((1, 4),))
    w_out = scatter_about(arg_keys[6], (D, D), (D // 16) ** -0.5, 0.875)
    out_bias = scatter_about(arg_keys[7], (D,), 0.2, 1.0, (), jnp.float32)
    gain_one = jnp.clip(1.0 + 0.1 * jax.random.normal(arg_keys[8], (D,), jnp.float32), 0.5, 1.5)
    shift_one = scatter_about(arg_keys[9], (D,), 0.2, 1.0, (), jnp.float32)
    w_in = scatter_about(arg_keys[10], (D, FF), D ** -0.5, 0.21875)
    in_bias = scatter_about(arg_keys[11], (FF,), 0.2, 1.0, (), jnp.float32)
    w_back = scatter_about(arg_keys[12], (FF, D), FF ** -0.5, 0.109375)
    back_bias = scatter_about(arg_keys[13], (D,), 0.2, 1.0, (), jnp.float32)
    gain_two = jnp.clip(1.0 + 0.1 * jax.random.normal(arg_keys[14], (D,), jnp.float32), 0.5, 1.5)
    shift_two = scatter_about(arg_keys[15], (D,), 0.2, 1.0, (), jnp.float32)
    cotangent = gaussian_with(arg_keys[16], (TOKENS, D), 1.0, 6.0, ((0, 32),), (0, 1, 32, 2.75))
    return {"layer_input": layer_input, "token_boxes": token_boxes, "lengths": lengths, "w_qkv": w_qkv, "qv_bias": qv_bias, "rel_tables": rel_tables, "w_out": w_out, "out_bias": out_bias, "gain_one": gain_one, "shift_one": shift_one, "w_in": w_in, "in_bias": in_bias, "w_back": w_back, "back_bias": back_bias, "gain_two": gain_two, "shift_two": shift_two, "cotangent": cotangent}


@jax.custom_vjp
def low(v):
    return lax.optimization_barrier(v.astype(jnp.bfloat16)).astype(jnp.float32)

@jax.custom_vjp
def low_back(v):
    return v

def low_keep(v):
    return (low(v), None)

def low_pass(kept, grad):
    return (grad,)

def back_keep(v):
    return (v, None)

def back_low(kept, grad):
    return (low(grad),)
low.defvjp(low_keep, low_pass)
low_back.defvjp(back_keep, back_low)
EPS = 1e-05
NEG = -1000000000.0
THRESHOLDS = (1, 2, 3, 4, 6, 8, 12, 16, 24, 32, 48, 64, 96, 128, 192)

def bucket_pair(box_win):
    positions = jnp.arange(box_win.shape[1], dtype=jnp.int32)
    offset = positions[None, :] - positions[:, None]
    distance = jnp.abs(offset)
    level_count = jnp.zeros(offset.shape, jnp.int32)
    for threshold in THRESHOLDS:
        level_count = level_count + (distance >= threshold).astype(jnp.int32)
    first_bucket = level_count + 16 * (offset > 0).astype(jnp.int32)
    across = box_win[0][None, :] - box_win[0][:, None]
    upward = box_win[1][None, :] - box_win[1][:, None]
    horizontal = jnp.zeros(offset.shape, jnp.int32)
    for threshold in (-128, -32, -8, 0):
        horizontal = horizontal + (across >= threshold).astype(jnp.int32)
    for threshold in (8, 32, 128):
        horizontal = horizontal + (across > threshold).astype(jnp.int32)
    vertical = (upward >= -24).astype(jnp.int32) + (upward >= 0).astype(jnp.int32) + (upward > 24).astype(jnp.int32)
    return (first_bucket, 8 * vertical + horizontal)

def hi_dot(left, right):
    return jnp.dot(left, right, precision=lax.Precision.HIGHEST, preferred_element_type=jnp.float32)

def norm_rows(values, gain_row, shift_row):
    centred = values - lax.optimization_barrier(jnp.mean(values, axis=-1, keepdims=True))
    spread = lax.rsqrt(lax.optimization_barrier(jnp.mean(centred * centred, axis=-1, keepdims=True)) + EPS)
    return centred * spread * gain_row + shift_row

def window_attention(query_win, key_win, value_win, length_win, box_win, tables):
    first_bucket, second_bucket = bucket_pair(box_win)
    scale = 1.0 / math.sqrt(HEAD_DIM)
    scores = scale * jnp.einsum('ihd,jhd->hij', query_win, key_win, precision=lax.Precision.HIGHEST)
    scores = scores + tables[0][:, first_bucket] + tables[1][:, second_bucket]
    valid = jnp.arange(scores.shape[-1], dtype=jnp.int32) < length_win
    scores = low_back(jnp.where(valid[None, None, :], scores, NEG))
    attn_probs = jax.nn.softmax(scores, axis=-1)
    return jnp.einsum('hij,jhd->ihd', low(attn_probs), value_win, precision=lax.Precision.HIGHEST)

def layer_block(row_block, box_block, len_block, w_qkv, qv_bias, rel_tables, w_out, out_bias, gain_one, shift_one, w_in, in_bias, w_back, back_bias, gain_two, shift_two):
    width = row_block.shape[1]
    count_win = row_block.shape[0] // L
    head_count = rel_tables.shape[1]
    zero_keys = jnp.zeros((width,), row_block.dtype)
    bias_row = jnp.concatenate([qv_bias[0], zero_keys, qv_bias[1]])
    qkv_rows = low_back(low(hi_dot(row_block, w_qkv.reshape(width, 3 * width)) + bias_row))
    split = qkv_rows.reshape(count_win, L, 3, head_count, width // head_count)
    box_win = box_block.reshape(2, count_win, L).transpose(1, 0, 2)
    checked = jax.checkpoint(window_attention)
    context = lax.map(lambda window_items: checked(*window_items, rel_tables), (split[:, :, 0], split[:, :, 1], split[:, :, 2], len_block, box_win))
    context = low_back(low(context.reshape(count_win * L, width)))
    attended = low_back(hi_dot(context, w_out) + out_bias)
    normed_one = norm_rows(row_block + attended, gain_one, shift_one)
    pre_act = low_back(hi_dot(low(normed_one), w_in) + in_bias)
    acted = low(jax.nn.gelu(pre_act, approximate=False))
    branch = low_back(hi_dot(acted, w_back) + back_bias)
    return norm_rows(normed_one + branch, gain_two, shift_two)

def reference(layer_input, token_boxes, lengths, w_qkv, qv_bias, rel_tables, w_out, out_bias, gain_one, shift_one, w_in, in_bias, w_back, back_bias, gain_two, shift_two, cotangent):
    params = tuple((value.astype(jnp.float32) for value in (w_qkv, qv_bias, rel_tables, w_out, out_bias, gain_one, shift_one, w_in, in_bias, w_back, back_bias, gain_two, shift_two)))
    group_rows = WIN_GROUP * L
    rows_all = layer_input.astype(jnp.float32).reshape(N_DOCS, group_rows, D)
    cot_all = cotangent.astype(jnp.float32).reshape(N_DOCS, group_rows, D)
    box_all = token_boxes.reshape(2, N_DOCS, group_rows).transpose(1, 0, 2)
    len_all = lengths.reshape(N_DOCS, WIN_GROUP)

    def group_step(totals, group_items):
        row_block, cot_rows, box_block, len_block = group_items

        def forward(rows_in, *weights):
            return layer_block(rows_in, box_block, len_block, *weights)
        result, pullback = jax.vjp(forward, row_block, *params)
        grads_all = pullback(cot_rows)
        totals = tuple((total + extra for total, extra in zip(totals, grads_all[1:])))
        return (totals, (result.astype(jnp.bfloat16), grads_all[0].astype(jnp.bfloat16)))
    zeros_init = tuple((jnp.zeros_like(value) for value in params))
    totals, (outputs_all, inputs_all) = lax.scan(group_step, zeros_init, (rows_all, cot_all, box_all, len_all))
    return (outputs_all.reshape(TOKENS, D), inputs_all.reshape(TOKENS, D), totals[0], totals[1], totals[2], totals[3], totals[4], totals[5], totals[6], totals[7], totals[8], totals[9], totals[10], totals[11], totals[12])
```

```python
import math

import jax
import jax.numpy as jnp
from jax import lax
from jax.experimental import pallas as pl
from jax.experimental.pallas import tpu as pltpu
from jax.sharding import PartitionSpec as P

HEAD_DIM = 64
L = 512
EPS = 1e-05
NEG = -1000000000.0
THRESHOLDS = (1, 2, 3, 4, 6, 8, 12, 16, 24, 32, 48, 64, 96, 128, 192)
ROOT_HALF = 1.0 / math.sqrt(2.0)
DENSITY_SCALE = 1.0 / math.sqrt(2.0 * math.pi)
SCALE = 0.125
BR = 64
RT = 64
BF = jnp.bfloat16
F32 = jnp.float32
I32 = jnp.int32
NT = (((1,), (1,)), ((), ()))


def first_bucket_of(offset):
    distance = jnp.abs(offset)
    count = jnp.where(offset > 0, 16, 0).astype(I32)
    for threshold in THRESHOLDS:
        count = count + jnp.where(distance >= threshold, 1, 0).astype(I32)
    return count


def second_bucket_of(across, upward):
    horizontal = jnp.zeros(across.shape, I32)
    for threshold in (-128, -32, -8, 0):
        horizontal = horizontal + jnp.where(across >= threshold, 1, 0)
    for threshold in (8, 32, 128):
        horizontal = horizontal + jnp.where(across > threshold, 1, 0)
    vertical = (
        jnp.where(upward >= -24, 8, 0)
        + jnp.where(upward >= 0, 8, 0)
        + jnp.where(upward > 24, 8, 0)
    )
    return vertical + horizontal


def bucket_kernel(len_ref, row_ref, col_ref, out_ref):
    filled = len_ref[0]
    for step in range(L // BR):
        rows = slice(step * BR, (step + 1) * BR)
        across = row_ref[0:1, :] - col_ref[rows, 0:1]
        upward = row_ref[1:2, :] - col_ref[rows, 1:2]
        column = lax.broadcasted_iota(I32, (BR, L), 1)
        out_ref[rows, :] = jnp.where(column < filled, second_bucket_of(across, upward), 32)


def second_buckets(lengths, box_rows, box_cols):
    return pl.pallas_call(
        bucket_kernel,
        in_specs=[pl.BlockSpec(memory_space=pltpu.SMEM)]
        + [pl.BlockSpec(memory_space=pltpu.VMEM)] * 2,
        out_specs=pl.BlockSpec(memory_space=pltpu.VMEM),
        out_shape=jax.ShapeDtypeStruct((L, L), I32),
        name="second_buckets",
    )(lengths, box_rows, box_cols)


def lookup(table_row, index):
    table = jnp.broadcast_to(table_row, (index.shape[0], 128))
    return jnp.concatenate(
        [
            jnp.take_along_axis(
                table, index[:, c : c + 128], axis=1, mode="promise_in_bounds"
            )
            for c in range(0, index.shape[1], 128)
        ],
        axis=1,
    )


def head_window(head, width):
    start = head * HEAD_DIM // 128 * 128
    return start, min(128, width - start), head * HEAD_DIM - start


def only_head(rows, low):
    if rows.shape[1] == HEAD_DIM:
        return rows
    lane = lax.broadcasted_iota(I32, rows.shape, 1)
    return jnp.where((lane >= low) & (lane < low + HEAD_DIM), rows, jnp.zeros_like(rows))


def forward_kernel(
    z_ref, x_ref, w_ref, bias_ref, first_ref, second_ref, bucket_ref,
    ctx_ref, probs_ref, qkv_ref, near_sc, bias_sc,
):
    heads = probs_ref.shape[1]
    width = heads * HEAD_DIM

    @pl.when(pl.program_id(0) == 0)
    def _():
        for d in range(-3, 4):
            offset = (
                128 * d
                + lax.broadcasted_iota(I32, (128, 128), 1)
                - lax.broadcasted_iota(I32, (128, 128), 0)
            )
            near_sc[d + 3] = first_bucket_of(offset)

    total = jnp.dot(x_ref[...], w_ref[0], preferred_element_type=F32) + bias_ref[0]
    qkv_ref[0] = total.astype(BF)
    for h in range(heads):
        c0, w, low = head_window(h, width)
        for d in range(7):
            bias_sc[d] = lookup(first_ref[0, h : h + 1, :], near_sc[d])
        key = qkv_ref[0, :, width + c0 : width + c0 + w]
        value = qkv_ref[0, :, 2 * width + c0 : 2 * width + c0 + w]
        query = only_head(qkv_ref[0, :, c0 : c0 + w] * jnp.asarray(SCALE, BF), low)
        for step in range(L // BR):
            rows = slice(step * BR, (step + 1) * BR)
            tile, inner = step * BR // 128, step * BR % 128
            scores = lax.dot_general(query[rows], key, NT, preferred_element_type=F32)
            near = jnp.concatenate(
                [bias_sc[t - tile + 3, inner : inner + BR, :] for t in range(L // 128)],
                axis=1,
            )
            scores = scores + near + lookup(second_ref[0, h : h + 1, :], bucket_ref[rows, :])
            raised = jnp.exp(scores - jnp.max(scores, axis=1, keepdims=True))
            normalizer = jnp.sum(raised, axis=1, keepdims=True)
            probs_ref[0, h, rows, :] = (raised * (1.0 / normalizer)).astype(BF)
        out = jnp.dot(probs_ref[0, h], value, preferred_element_type=F32)
        ctx_ref[0, :, h * HEAD_DIM : (h + 1) * HEAD_DIM] = out[:, low : low + HEAD_DIM].astype(BF)


def attend_forward(z, x, w, bias, first, second, bucket):
    groups, depth, columns = w.shape
    heads = columns // (3 * HEAD_DIM)
    return pl.pallas_call(
        forward_kernel,
        grid_spec=pltpu.PrefetchScalarGridSpec(
            num_scalar_prefetch=1,
            grid=(groups,),
            in_specs=[
                pl.BlockSpec((L, depth), lambda g, z: (0, 0)),
                pl.BlockSpec((1, depth, columns), lambda g, z: (g, 0, 0)),
                pl.BlockSpec((1, 1, columns), lambda g, z: (g, 0, 0)),
                pl.BlockSpec((1, 8, 128), lambda g, z: (g, 0, 0)),
                pl.BlockSpec((1, 8, 128), lambda g, z: (g, 0, 0)),
                pl.BlockSpec((L, L), lambda g, z: (0, 0)),
            ],
            out_specs=[
                pl.BlockSpec((1, L, columns // 3), lambda g, z: ((g + z[0]) % groups, 0, 0)),
                pl.BlockSpec((1, heads, L, L), lambda g, z: (g, 0, 0, 0)),
                pl.BlockSpec((1, L, columns), lambda g, z: (g, 0, 0)),
            ],
            scratch_shapes=[pltpu.VMEM((7, 128, 128), I32), pltpu.VMEM((7, 128, 128), F32)],
        ),
        out_shape=[
            jax.ShapeDtypeStruct((groups, L, columns // 3), BF),
            jax.ShapeDtypeStruct((groups, heads, L, L), BF),
            jax.ShapeDtypeStruct((groups, L, columns), BF),
        ],
        name="attend_forward",
        compiler_params=pltpu.CompilerParams(vmem_limit_bytes=48 << 20),
    )(z, x, w, bias, first, second, bucket)


def backward_kernel(
    z_ref, xt_ref, w_ref, qkv_ref, probs_ref, grad_ref,
    dw_ref, dx_ref, ds_ref, sums_ref, rows_sc, flip_sc, turn_sc,
):
    group = pl.program_id(0)
    heads = probs_ref.shape[1]
    width = heads * HEAD_DIM
    turn_sc[0:width, :] = jnp.transpose(qkv_ref[0, :, 0:width])
    turn_sc[width : 2 * width, :] = jnp.transpose(grad_ref[0])
    for h in range(heads):
        c0, w, low = head_window(h, width)
        own = slice(h * HEAD_DIM, (h + 1) * HEAD_DIM)
        own_v = slice(width + h * HEAD_DIM, width + (h + 1) * HEAD_DIM)
        key = qkv_ref[0, :, width + c0 : width + c0 + w]
        value = qkv_ref[0, :, 2 * width + c0 : 2 * width + c0 + w]
        grad = only_head(grad_ref[0, :, c0 : c0 + w], low)
        for step in range(L // BR):
            rows = slice(step * BR, (step + 1) * BR)
            grad_probs = lax.dot_general(grad[rows], value, NT, preferred_element_type=F32)
            probs = probs_ref[0, h, rows, :].astype(F32)
            terms = probs * grad_probs
            inner = jnp.sum(terms, axis=1, keepdims=True)
            ds_ref[0, h, rows, :] = (terms - probs * inner).astype(BF)
        dq = jnp.dot(ds_ref[0, h], key, preferred_element_type=F32)
        rows_sc[:, own] = (dq[:, low : low + HEAD_DIM] * SCALE).astype(BF)
        dk = jnp.dot(turn_sc[own, :], ds_ref[0, h], preferred_element_type=F32)
        flip_sc[own, :] = (dk * SCALE).astype(BF)
        dv = jnp.dot(turn_sc[own_v, :], probs_ref[0, h], preferred_element_type=F32)
        flip_sc[own_v, :] = dv.astype(BF)
    rows_sc[:, width:] = jnp.transpose(flip_sc[...])
    grads = rows_sc[...]
    dw_ref[0] = jnp.dot(xt_ref[...], grads, preferred_element_type=F32).astype(BF)
    dx = lax.dot_general(grads, w_ref[0], NT, preferred_element_type=F32)

    @pl.when(group == 0)
    def _():
        dx_ref[...] = dx

    @pl.when(group > 0)
    def _():
        dx_ref[...] += dx

    sums_ref[0] = jnp.sum(grads.astype(F32), axis=0, keepdims=True)


def attend_backward(z, xt, w, qkv, probs, grad_ctx):
    groups, depth, columns = w.shape
    heads = columns // (3 * HEAD_DIM)
    width = columns // 3
    return pl.pallas_call(
        backward_kernel,
        grid_spec=pltpu.PrefetchScalarGridSpec(
            num_scalar_prefetch=1,
            grid=(groups,),
            in_specs=[
                pl.BlockSpec((depth, L), lambda g, z: (0, 0)),
                pl.BlockSpec((1, depth, columns), lambda g, z: (g, 0, 0)),
                pl.BlockSpec((1, L, columns), lambda g, z: (g, 0, 0)),
                pl.BlockSpec((1, heads, L, L), lambda g, z: (g, 0, 0, 0)),
                pl.BlockSpec((1, L, width), lambda g, z: ((g + z[0]) % groups, 0, 0)),
            ],
            out_specs=[
                pl.BlockSpec((1, depth, columns), lambda g, z: ((g + z[0]) % groups, 0, 0)),
                pl.BlockSpec((L, depth), lambda g, z: (0, 0)),
                pl.BlockSpec((1, heads, L, L), lambda g, z: ((g + z[0]) % groups, 0, 0, 0)),
                pl.BlockSpec((1, 1, columns), lambda g, z: ((g + z[0]) % groups, 0, 0)),
            ],
            scratch_shapes=[
                pltpu.VMEM((L, columns), BF),
                pltpu.VMEM((2 * width, L), BF),
                pltpu.VMEM((2 * width, L), BF),
            ],
        ),
        out_shape=[
            jax.ShapeDtypeStruct((groups, depth, columns), BF),
            jax.ShapeDtypeStruct((L, depth), F32),
            jax.ShapeDtypeStruct((groups, heads, L, L), BF),
            jax.ShapeDtypeStruct((groups, 1, columns), F32),
        ],
        name="attend_backward",
        compiler_params=pltpu.CompilerParams(vmem_limit_bytes=56 << 20),
    )(z, xt, w, qkv, probs, grad_ctx)


def table_kernel(ds_ref, bucket_ref, out_ref, acc_sc, hot_sc):
    step = pl.program_id(0)
    groups, heads = ds_ref.shape[0], ds_ref.shape[1]
    total = groups * heads
    half = 32 * 8

    @pl.when(step == 0)
    def _():
        acc_sc[...] = jnp.zeros_like(acc_sc)

    for u in range(RT // 8):
        part = slice(u * 8, (u + 1) * 8)
        second = bucket_ref[part, :]
        offset = lax.broadcasted_iota(I32, (8, L), 1) - (
            lax.broadcasted_iota(I32, (8, L), 0) + step * RT + u * 8
        )
        first = first_bucket_of(offset)
        for t in range(0, 32, 2):
            for base, bucket in ((0, first), (half, second)):
                hot_sc[base + t * 8 : base + (t + 2) * 8, :] = jnp.concatenate(
                    [jnp.where(bucket == t, 1.0, 0.0), jnp.where(bucket == t + 1, 1.0, 0.0)],
                    axis=0,
                ).astype(BF)
        left = jnp.concatenate(
            [ds_ref[h // heads, h % heads, part, :] for h in range(total)], axis=0
        )
        acc_sc[...] += lax.dot_general(left, hot_sc[...], NT, preferred_element_type=F32)

    @pl.when(step == pl.num_programs(0) - 1)
    def _():
        shape = (total * 8, 2 * half)
        same = lax.broadcasted_iota(I32, shape, 0) % 8 == lax.broadcasted_iota(I32, shape, 1) % 8
        kept = jnp.where(same, acc_sc[...], 0.0)
        fold = (2 * half, 64)
        right = (
            lax.broadcasted_iota(I32, fold, 0) // 8 == lax.broadcasted_iota(I32, fold, 1)
        ).astype(F32)
        spread = (16, total * 8)
        left = (
            lax.broadcasted_iota(I32, spread, 1) // 8 == lax.broadcasted_iota(I32, spread, 0)
        ).astype(F32)
        exact = lax.Precision.HIGHEST
        folded = jnp.dot(kept, right, preferred_element_type=F32, precision=exact)
        out_ref[...] = jnp.dot(left, folded, preferred_element_type=F32, precision=exact)


def table_gradients(ds, bucket):
    groups, heads = ds.shape[0], ds.shape[1]
    return pl.pallas_call(
        table_kernel,
        grid=(L // RT,),
        in_specs=[
            pl.BlockSpec((groups, heads, RT, L), lambda r: (0, 0, r, 0)),
            pl.BlockSpec((RT, L), lambda r: (r, 0)),
        ],
        out_specs=pl.BlockSpec((16, 64), lambda r: (0, 0)),
        out_shape=jax.ShapeDtypeStruct((16, 64), F32),
        scratch_shapes=[
            pltpu.VMEM((groups * heads * 8, 512), F32),
            pltpu.VMEM((512, L), BF),
        ],
        name="table_gradients",
    )(ds, bucket)


def swap(array, bit):
    count = lax.axis_size("docs")
    return lax.ppermute(array, "docs", [(i, i ^ (1 << bit)) for i in range(count)])


def fetch(array, shift):
    count = lax.axis_size("heads")
    return lax.ppermute(array, "heads", [((i + shift) % count, i) for i in range(count)])


def half_step(current, bit, axis, docs):
    mine = (docs >> bit) & 1
    sent = lax.dynamic_index_in_dim(current, 1 - mine, axis, keepdims=False)
    kept = lax.dynamic_index_in_dim(current, mine, axis, keepdims=False)
    got = swap(sent, bit)
    return (kept.astype(F32) + got.astype(F32)).astype(BF)


def reduce_docs(blocks):
    count, rows, columns = blocks.shape
    bits = count.bit_length() - 1
    docs = lax.axis_index("docs")
    current = blocks.reshape((2,) * bits + (rows, columns))
    current = half_step(current, 0, bits - 1, docs)
    cut = rows // 2 // 8 * 8
    results = []
    for number, piece in enumerate((current[..., :cut, :], current[..., cut:, :])):
        left = list(range(bits - 1, 0, -1))
        order = list(range(1, bits)) if number == 0 else list(range(bits - 1, 0, -1))
        for bit in order:
            piece = half_step(piece, bit, left.index(bit), docs)
            left.remove(bit)
        results.append(piece)
    return jnp.concatenate(results, axis=0)


def spread_docs(block):
    count = lax.axis_size("docs")
    bits = count.bit_length() - 1
    docs = lax.axis_index("docs")
    current = block
    for done, bit in enumerate(range(bits - 1, -1, -1)):
        got = swap(current, bit)
        mine = ((docs >> bit) & 1) == 1
        current = jnp.stack(
            [jnp.where(mine, got, current), jnp.where(mine, current, got)], axis=done
        )
    return current.reshape((count,) + block.shape)


def sum_heads(parts):
    got = lax.all_to_all(parts, "heads", split_axis=0, concat_axis=0, tiled=True)
    return jnp.sum(got.astype(F32), axis=0).astype(BF)


def in_order(pieces, z):
    count = len(pieces)
    twice = jnp.stack(list(pieces) + list(pieces[:-1]))
    return lax.dynamic_slice_in_dim(twice, (count - z) % count, count, axis=0)


def spread_heads(block, z):
    count = lax.axis_size("heads")
    return in_order([block] + [fetch(block, s) for s in range(1, count)], z)


def norm_forward(values, gain_row, shift_row):
    centred = values - jnp.mean(values, axis=-1, keepdims=True)
    scale_rows = lax.rsqrt(jnp.mean(centred * centred, axis=-1, keepdims=True) + EPS)
    unit_rows = centred * scale_rows
    return (unit_rows * gain_row + shift_row, unit_rows, scale_rows)


def norm_back(upstream, unit_rows, scale_rows, gain_row):
    scaled = upstream * gain_row
    inner_term = (
        scaled
        - jnp.mean(scaled, axis=-1, keepdims=True)
        - unit_rows * jnp.mean(scaled * unit_rows, axis=-1, keepdims=True)
    )
    return (
        scale_rows * inner_term,
        jnp.sum(upstream * unit_rows, axis=0),
        jnp.sum(upstream, axis=0),
    )


def gelu_slope(values):
    cumulative = 0.5 * (1.0 + lax.erf(values * ROOT_HALF))
    density = jnp.exp(-0.5 * values * values) * DENSITY_SCALE
    return cumulative + values * density


def body(
    layer_input, token_boxes, lengths, w_qkv, qv_bias, rel_tables, w_out, out_bias,
    gain_one, shift_one, w_in, in_bias, w_back, back_bias, gain_two, shift_two, cotangent,
):
    width = layer_input.shape[1]
    groups = lax.axis_size("heads")
    count = lax.axis_size("docs")
    docs = lax.axis_index("docs")
    z = lax.axis_index("heads")
    own = w_qkv.shape[2]
    heads = rel_tables.shape[1]
    buckets = rel_tables.shape[2]
    columns = 3 * own

    box = lax.dynamic_slice_in_dim(token_boxes, z * L, L, axis=1)
    length = lax.dynamic_slice_in_dim(lengths, z, 1)
    bucket = second_buckets(length, box, box.T)

    matrix = w_qkv.reshape(width, columns)
    bias_row = jnp.concatenate([qv_bias[0], jnp.zeros((own,), BF), qv_bias[1]])
    table_row = jnp.pad(rel_tables.reshape(-1), (0, columns - rel_tables.size))
    extra = jnp.pad(jnp.stack([bias_row, table_row]), ((0, 14), (0, 0)))
    share = width // count
    piece = jnp.concatenate(
        [lax.dynamic_slice_in_dim(matrix, docs * share, share, axis=0), extra], axis=0
    )
    arrived = jnp.stack([fetch(piece, s) for s in range(1, groups)])
    extras = jnp.concatenate([extra[None], arrived[:, share:]], axis=0)
    others = spread_docs(arrived[:, :share].reshape((groups - 1) * share, columns))
    others = others.reshape(count, groups - 1, share, columns).transpose(1, 0, 2, 3)
    weights = jnp.concatenate(
        [matrix[None], others.reshape(groups - 1, width, columns)], axis=0
    )
    biases = extras[:, 0:1].astype(F32)
    tables = extras[:, 1, : 2 * heads * buckets].reshape(groups, 2, heads, buckets).astype(F32)
    first = jnp.pad(tables[:, 0], ((0, 0), (0, 8 - heads), (0, 128 - buckets)))
    second = jnp.pad(
        tables[:, 1],
        ((0, 0), (0, 8 - heads), (0, 128 - buckets)),
        constant_values=NEG,
    )
    z_one = z.reshape(1).astype(I32)
    context, probs, qkv = attend_forward(
        z_one, layer_input, weights, biases, first, second, bucket
    )

    w_out_heads = w_out.reshape(groups, own, width)
    projected = jnp.einsum("aic,acd->id", context, w_out_heads, preferred_element_type=F32)
    rows_in = layer_input.astype(F32)
    attended = projected + out_bias
    normed_one, unit_one, inv_one = norm_forward(rows_in + attended, gain_one, shift_one)
    normed_low = normed_one.astype(BF)
    pre_act = jnp.dot(normed_low, w_in, preferred_element_type=F32) + in_bias
    acted = jax.nn.gelu(pre_act, approximate=False).astype(BF)
    branch = jnp.dot(acted, w_back, preferred_element_type=F32) + back_bias
    final_rows, unit_two, inv_two = norm_forward(normed_one + branch, gain_two, shift_two)
    layer_output = final_rows.astype(BF)
    grad_mid, grad_gain_two, grad_shift_two = norm_back(
        cotangent.astype(F32), unit_two, inv_two, gain_two
    )
    grad_branch = grad_mid.astype(BF)
    grad_back_bias = jnp.sum(grad_branch, axis=0, dtype=F32)
    grad_back = jnp.einsum("rf,rd->fd", acted, grad_branch, preferred_element_type=F32)
    grad_acted = jnp.einsum("rd,fd->rf", grad_branch, w_back, preferred_element_type=F32)
    grad_pre = (grad_acted * gelu_slope(pre_act)).astype(BF)
    grad_in_bias = jnp.sum(grad_pre, axis=0, dtype=F32)
    grad_in = jnp.einsum("rd,rf->df", normed_low, grad_pre, preferred_element_type=F32)
    grad_hidden = grad_mid + jnp.einsum(
        "rf,df->rd", grad_pre, w_in, preferred_element_type=F32
    )
    grad_first, grad_gain_one, grad_shift_one = norm_back(grad_hidden, unit_one, inv_one, gain_one)
    grad_attended = grad_first.astype(BF)
    grad_out_bias = jnp.sum(grad_attended, axis=0, dtype=F32)
    grad_out = jnp.einsum(
        "aic,id->acd", context, grad_attended, preferred_element_type=F32
    ).reshape(width, width)
    grad_context = jnp.einsum(
        "id,acd->aic", grad_attended, w_out_heads, preferred_element_type=F32
    ).astype(BF)

    small = [
        grad_out_bias, grad_in_bias, grad_back_bias,
        grad_gain_one, grad_shift_one, grad_gain_two, grad_shift_two,
    ]
    small_rows = jnp.concatenate([item.reshape(count, -1) for item in small], axis=1)
    small_size = small_rows.shape[1]
    parts = w_in.shape[1] // width
    used = 2 * parts * share + share
    short = -(-small_size // width)
    rows = -(-(used + short) // (8 * groups)) * 8 * groups
    small_rows = jnp.pad(small_rows, ((0, 0), (0, (rows - used) * width - small_size)))
    dense = jnp.concatenate(
        [
            grad_back.astype(BF).reshape(count, parts * share, width),
            grad_in.astype(BF)
            .reshape(count, share, parts, width)
            .transpose(0, 2, 1, 3)
            .reshape(count, parts * share, width),
            grad_out.astype(BF).reshape(count, share, width),
            small_rows.astype(BF).reshape(count, rows - used, width),
        ],
        axis=1,
    )
    dense = reduce_docs(dense)
    dense = sum_heads(dense.reshape(groups, rows // groups, width))
    dense = spread_heads(dense, z).reshape(rows, width).astype(F32)
    out_back = dense[: parts * share]
    out_in = (
        dense[parts * share : 2 * parts * share]
        .reshape(parts, share, width)
        .transpose(1, 0, 2)
        .reshape(share, parts * width)
    )
    out_out = dense[2 * parts * share : used]
    flat = dense[used:].reshape(-1)
    smalls, cursor = [], 0
    for item in small:
        size = item.size // count
        smalls.append(flat[cursor : cursor + size])
        cursor += size

    dw, dx, ds, sums = attend_backward(
        z_one, layer_input.T, weights, qkv, probs, grad_context
    )
    tables_sum = table_gradients(ds, bucket)
    tables_sum = tables_sum[: groups * heads].reshape(groups, heads, 2, buckets)
    tables_sum = tables_sum.transpose(0, 2, 1, 3).reshape(groups, 1, 2 * heads * buckets)
    tables_sum = jnp.pad(tables_sum, ((0, 0), (0, 0), (0, columns - 2 * heads * buckets)))
    tail = jnp.concatenate([sums, tables_sum], axis=1).astype(BF)
    tail = jnp.pad(tail, ((0, 0), (0, 6), (0, 0)))
    blocks = dw.reshape(groups, count, share, columns).transpose(1, 0, 2, 3)
    first_only = jnp.pad(tail[None], ((0, count - 1), (0, 0), (0, 0), (0, 0)))
    blocks = jnp.concatenate([blocks, first_only], axis=2)
    mine = reduce_docs(blocks.reshape(count, groups * (share + 8), columns))
    mine = sum_heads(mine.reshape(groups, share + 8, columns))
    full = spread_docs(mine)
    grad_qkv = full[:, :share].reshape(width, 3, own).astype(F32)
    ends = full[0, share:].astype(F32)
    grad_qv_bias = jnp.stack([ends[0, :own], ends[0, 2 * own :]])
    grad_tables = ends[1, : 2 * heads * buckets].reshape(2, heads, buckets)
    grad_input = (grad_first + dx).astype(BF)
    return (
        layer_output,
        grad_input,
        grad_qkv,
        grad_qv_bias,
        grad_tables,
        out_out,
        smalls[0],
        smalls[3],
        smalls[4],
        out_in,
        smalls[1],
        out_back,
        smalls[2],
        smalls[5],
        smalls[6],
    )


def solution(mesh):
    rows = P(("docs", "heads"), None)
    return jax.shard_map(
        body,
        mesh=mesh,
        in_specs=(
            rows,
            P(None, "docs"),
            P("docs"),
            P(None, None, "heads"),
            P(None, "heads"),
            P(None, "heads", None),
            P(),
            P(),
            P(),
            P(),
            P(),
            P(),
            P(),
            P(),
            P(),
            P(),
            rows,
        ),
        out_specs=(
            rows,
            rows,
            P(None, None, "heads"),
            P(None, "heads"),
            P(None, "heads", None),
            P("docs", None),
            P("docs"),
            P("docs"),
            P("docs"),
            P("docs", None),
            P("docs"),
            P("docs", None),
            P("docs"),
            P("docs"),
            P("docs"),
        ),
        check_vma=False,
    )
```

```python
import functools
import math

import jax
import jax.numpy as jnp
from jax import lax
from jax.experimental import pallas as pl
from jax.experimental.pallas import tpu as pltpu
from jax.sharding import PartitionSpec as P

HEAD_DIM = 64
L = 512
EPS = 1e-05
NEG = -1000000000.0
THRESHOLDS = (1, 2, 3, 4, 6, 8, 12, 16, 24, 32, 48, 64, 96, 128, 192)
ROOT_HALF = 1.0 / math.sqrt(2.0)
DENSITY_SCALE = 1.0 / math.sqrt(2.0 * math.pi)
SCALE = 0.125
KC = 32
QB = 128
RT = 64
FC = 768
MB = 256
BF = jnp.bfloat16
F32 = jnp.float32
I32 = jnp.int32
NT = (((1,), (1,)), ((), ()))


def whole(*shape):
    return pl.BlockSpec(shape, lambda *_: (0,) * len(shape))


def limit(mebibytes):
    return pltpu.CompilerParams(vmem_limit_bytes=mebibytes << 20)


HINT = pl.CostEstimate(flops=1, bytes_accessed=1, transcendentals=0)


def shaped(dtype, *shape):
    return jax.ShapeDtypeStruct(shape, dtype)


def first_bucket_of(offset):
    distance = jnp.abs(offset)
    count = jnp.where(offset > 0, 16, 0).astype(I32)
    for threshold in THRESHOLDS:
        count = count + jnp.where(distance >= threshold, 1, 0).astype(I32)
    return count


def second_bucket_of(across, upward):
    horizontal = jnp.zeros(across.shape, I32)
    for threshold in (-128, -32, -8, 0):
        horizontal = horizontal + jnp.where(across >= threshold, 1, 0)
    for threshold in (8, 32, 128):
        horizontal = horizontal + jnp.where(across > threshold, 1, 0)
    vertical = (
        jnp.where(upward >= -24, 8, 0)
        + jnp.where(upward >= 0, 8, 0)
        + jnp.where(upward > 24, 8, 0)
    )
    return vertical + horizontal


PLACE = ("heads", "core", "x", "y")


def bucket_kernel(place_ref, len_ref, box_ref, out_ref):
    filled = len_ref[place_ref[0]]
    boxes = box_ref[...].astype(F32)
    turned = jnp.transpose(jnp.concatenate([boxes] * 4, axis=0)).astype(I32)
    size = 64
    for step in range(L // size):
        rows = slice(step * size, (step + 1) * size)
        across = turned[rows, 0:1] - box_ref[0:1, :]
        upward = turned[rows, 1:2] - box_ref[1:2, :]
        key = lax.broadcasted_iota(I32, (size, L), 0) + step * size
        out_ref[rows, :] = jnp.where(key < filled, second_bucket_of(across, upward), 32)


def second_buckets(place, lengths, boxes):
    return pl.pallas_call(
        bucket_kernel,
        grid_spec=pltpu.PrefetchScalarGridSpec(
            num_scalar_prefetch=2,
            grid=(1,),
            in_specs=[pl.BlockSpec((2, L), lambda i, place, lengths: (0, place[0]))],
            out_specs=whole(L, L),
        ),
        out_shape=shaped(I32, L, L),
        name="second_buckets",
        compiler_params=limit(12),
        cost_estimate=HINT,
    )(place, lengths, boxes)


def lookup(table_row, index):
    table = jnp.broadcast_to(table_row, (index.shape[0], 128))
    return jnp.concatenate(
        [
            jnp.take_along_axis(
                table, index[:, c : c + 128], axis=1, mode="promise_in_bounds"
            )
            for c in range(0, index.shape[1], 128)
        ],
        axis=1,
    )


def head_window(head, width):
    start = head * HEAD_DIM // 128 * 128
    return start, min(128, width - start), head * HEAD_DIM - start


def eights(rows):
    return rows.reshape(rows.shape[0] // 8, 8, rows.shape[1])


def column(row):
    return jnp.transpose(jnp.broadcast_to(row, (8, row.shape[1])))[:, 0:1]


def forward_kernel(gathered, place_ref, x_ref, *refs):
    sources = refs[: 4 if gathered else 1]
    extra_ref, bucket_ref = refs[len(sources) : len(sources) + 2]
    rest = refs[len(sources) + 2 :]
    if gathered:
        w_ref, rest = rest[0], rest[1:]
    else:
        w_ref = sources[0]
    ctx_ref, turned_ref, raised_ref, qkv_ref, inverse_ref = rest[:5]
    index_sc, near_sc, score_sc, query_sc, key_sc = rest[5:10]
    heads = raised_ref.shape[1]
    width = heads * HEAD_DIM

    @pl.when(pl.program_id(0) == 0)
    def _():
        for d in range(-2, 3):
            offset = (
                128 * d
                + lax.broadcasted_iota(I32, (128, 128), 0)
                - lax.broadcasted_iota(I32, (128, 128), 1)
            )
            index_sc[d + 2] = first_bucket_of(offset)
        query_sc[...] = jnp.zeros_like(query_sc)

    if gathered:
        whole_sc = rest[10]
        core, here_x, here_y = place_ref[1], place_ref[2], place_ref[3]
        cut = sources[0].shape[3]
        size = cut + sources[1].shape[3]
        for far_y in range(2):
            for far_x in range(2):
                chip = (here_y ^ far_y) * 2 + (here_x ^ far_x)
                for side, pair in ((core, sources[:2]), (1 - core, sources[2:])):
                    at = (chip * 2 + side) * size
                    first = pl.multiple_of(at, 8)
                    whole_sc[pl.ds(first, cut), :] = pair[0][far_y, far_x, 0].astype(F32)
                    second = pl.multiple_of(at + cut, 8)
                    whole_sc[pl.ds(second, size - cut), :] = pair[1][far_x, far_y, 0].astype(F32)
        w_ref[0] = whole_sc[...].astype(BF)

    extra = extra_ref[0, 0:1, :].astype(F32)
    query_bias, value_bias = extra[:, 0:width], extra[:, width : 2 * width]
    first_tables = extra[:, 2 * width : 2 * width + 128]
    second_tables = extra[:, 2 * width + 128 : 2 * width + 256]
    query = lax.dot_general(w_ref[0, 0:width, :], x_ref[...], NT, preferred_element_type=F32)
    qkv_ref[0, 0:width, :] = (query + column(query_bias)).astype(BF)
    key = lax.dot_general(
        w_ref[0, width : 2 * width, :], x_ref[...], NT, preferred_element_type=F32
    )
    qkv_ref[0, width : 2 * width, :] = key.astype(BF)
    value = lax.dot_general(
        w_ref[0, 2 * width : 3 * width, :], x_ref[...], NT, preferred_element_type=F32
    )
    qkv_ref[0, 2 * width : 3 * width, :] = (value + column(value_bias)).astype(BF)
    key_sc[...] = lax.dot_general(
        x_ref[...], w_ref[0, width : 2 * width, :], NT, preferred_element_type=F32
    ).astype(BF)
    inverse_ref[0] = jnp.zeros_like(inverse_ref[0])
    lane = lax.broadcasted_iota(I32, (1, 128), 1)
    for h in range(heads):
        c0, w, low = head_window(h, width)
        own = slice(h * HEAD_DIM, (h + 1) * HEAD_DIM)
        query_sc[h, low : low + HEAD_DIM, :] = qkv_ref[0, own, :] * jnp.asarray(SCALE, BF)
        row = first_tables if h == 0 else jnp.roll(first_tables, -32 * h, axis=1)
        other = second_tables if h == 0 else jnp.roll(second_tables, -32 * h, axis=1)
        other = jnp.where(lane < 32, other, NEG)
        for d in range(5):
            near_sc[h, d] = lookup(row, index_sc[d])
        far = {
            -3: jnp.broadcast_to(row[:, 15:16], (KC, 128)),
            3: jnp.broadcast_to(row[:, 31:32], (KC, 128)),
        }
        key = key_sc[:, c0 : c0 + w]
        for block in range(L // QB):
            cols = slice(block * QB, (block + 1) * QB)
            score_sc[h] = jnp.dot(key, query_sc[h, 0:w, cols], preferred_element_type=F32)
            peak = None
            for step in range(L // KC):
                rows = slice(step * KC, (step + 1) * KC)
                d, inner = step * KC // 128 - block, step * KC % 128
                near = far[d] if abs(d) == 3 else near_sc[h, d + 2, inner : inner + KC, :]
                scores = score_sc[h, rows, :] + near
                scores = scores + lookup(other, bucket_ref[rows, cols])
                score_sc[h, rows, :] = scores
                part = jnp.max(eights(scores), axis=0)
                peak = part if peak is None else jnp.maximum(peak, part)
            peak = jnp.max(peak, axis=0, keepdims=True)
            sums = None
            for step in range(L // KC):
                rows = slice(step * KC, (step + 1) * KC)
                raised = jnp.exp(score_sc[h, rows, :] - peak)
                raised_ref[0, h, rows, cols] = raised.astype(BF)
                part = jnp.sum(eights(raised), axis=0)
                sums = part if sums is None else sums + part
            inverse_ref[0, h : h + 1, cols] = 1.0 / jnp.sum(sums, axis=0, keepdims=True)
        at = 2 * width + h * HEAD_DIM
        out = jnp.dot(
            qkv_ref[0, at : at + HEAD_DIM, :], raised_ref[0, h], preferred_element_type=F32
        )
        turned_ref[0, own, :] = (out * inverse_ref[0, h : h + 1, :]).astype(BF)
    ctx_ref[0] = jnp.transpose(turned_ref[0])


def each(*shape):
    return pl.BlockSpec((1,) + shape, lambda g, *_: (g,) + (0,) * len(shape))


def attend_forward(place, x, sources, extra, bucket):
    gathered = len(sources) == 4
    groups, depth = extra.shape[0], x.shape[1]
    if gathered:
        columns = 8 * (sources[0].shape[3] + sources[1].shape[3])
        inputs = [
            pl.BlockSpec(
                (2, 2, 1) + source.shape[3:], lambda g, place: (0, 0, g, 0, 0)
            )
            for source in sources
        ]
    else:
        columns = sources[0].shape[1]
        inputs = [each(columns, depth)]
    heads = columns // (3 * HEAD_DIM)
    width = columns // 3
    out_specs = [
        each(L, width), each(width, L), each(heads, L, L), each(columns, L), each(8, L)
    ]
    out_shape = [
        shaped(BF, groups, L, width),
        shaped(BF, groups, width, L),
        shaped(BF, groups, heads, L, L),
        shaped(BF, groups, columns, L),
        shaped(F32, groups, 8, L),
    ]
    scratch = [
        pltpu.VMEM((5, 128, 128), I32),
        pltpu.VMEM((heads, 5, 128, 128), F32),
        pltpu.VMEM((heads, L, QB), F32),
        pltpu.VMEM((heads, 128, L), BF),
        pltpu.VMEM((L, width), BF),
    ]
    if gathered:
        out_specs = [each(columns, depth)] + out_specs
        out_shape = [shaped(BF, groups, columns, depth)] + out_shape
        scratch = scratch + [pltpu.VMEM((columns, depth), F32)]
    return pl.pallas_call(
        functools.partial(forward_kernel, gathered),
        grid_spec=pltpu.PrefetchScalarGridSpec(
            num_scalar_prefetch=1,
            grid=(groups,),
            in_specs=[whole(L, depth)] + inputs + [each(8, depth), whole(L, L)],
            out_specs=out_specs,
            scratch_shapes=scratch,
        ),
        out_shape=out_shape,
        name="attend_forward",
        compiler_params=limit(36),
        cost_estimate=HINT,
    )(place, x, *sources, extra, bucket)


def backward_kernel(
    halved, place_ref, x_ref, w_ref, qkv_ref, raised_ref, inverse_ref, grad_ref, start_ref, *refs
):
    outs = refs[: 5 if halved else 4]
    dx_ref, ds_ref, sums_ref = outs[:3]
    pad_sc, term_sc, rows_sc, turn_sc, value_sc = refs[len(outs) : len(outs) + 5]
    group = pl.program_id(0)
    heads = raised_ref.shape[1]
    width = heads * HEAD_DIM

    @pl.when(group == 0)
    def _():
        pad_sc[...] = jnp.zeros_like(pad_sc)
        dx_ref[...] = start_ref[...]

    value_sc[...] = jnp.transpose(qkv_ref[0, 2 * width : 3 * width, :])
    for h in range(heads):
        c0, w, low = head_window(h, width)
        own = slice(h * HEAD_DIM, (h + 1) * HEAD_DIM)
        pad_sc[h, low : low + HEAD_DIM, :] = grad_ref[0, own, :]
        value = value_sc[:, c0 : c0 + w]
        for block in range(L // QB):
            cols = slice(block * QB, (block + 1) * QB)
            term_sc[h] = jnp.dot(value, pad_sc[h, 0:w, cols], preferred_element_type=F32)
            sums = None
            for step in range(L // KC):
                rows = slice(step * KC, (step + 1) * KC)
                terms = term_sc[h, rows, :] * raised_ref[0, h, rows, cols].astype(F32)
                term_sc[h, rows, :] = terms
                part = jnp.sum(eights(terms), axis=0)
                sums = part if sums is None else sums + part
            inner = jnp.sum(sums, axis=0, keepdims=True) * inverse_ref[0, h : h + 1, cols]
            for step in range(L // KC):
                rows = slice(step * KC, (step + 1) * KC)
                raised = raised_ref[0, h, rows, cols].astype(F32)
                ds_ref[0, h, rows, cols] = (term_sc[h, rows, :] - raised * inner).astype(BF)
        scale = jnp.asarray(SCALE, BF)
        at = width + h * HEAD_DIM
        turn_sc[own, :] = jnp.dot(
            qkv_ref[0, at : at + HEAD_DIM, :] * scale, ds_ref[0, h], preferred_element_type=F32
        ).astype(BF)
        dk = lax.dot_general(
            ds_ref[0, h], qkv_ref[0, c0 : c0 + w, :] * scale, NT, preferred_element_type=F32
        )
        rows_sc[:, at : at + HEAD_DIM] = dk[:, low : low + HEAD_DIM].astype(BF)
        dv = lax.dot_general(
            raised_ref[0, h], grad_ref[0, c0 : c0 + w, :], NT, preferred_element_type=F32
        )
        at = 2 * width + h * HEAD_DIM
        rows_sc[:, at : at + HEAD_DIM] = dv[:, low : low + HEAD_DIM].astype(BF)
    rows_sc[:, 0:width] = jnp.transpose(turn_sc[0:width, :])
    turn_sc[width:, :] = jnp.transpose(rows_sc[:, width:])
    weights = jnp.dot(turn_sc[...], x_ref[...], preferred_element_type=F32)
    if halved:
        sent_ref, kept_ref = outs[3:]
        all_sc = refs[len(outs) + 5]
        all_sc[...] = weights
        core = place_ref[1]
        chips, size = kept_ref.shape[1], kept_ref.shape[2]
        for chip in range(chips):
            for side, ref in ((1 - core, sent_ref), (core, kept_ref)):
                at = pl.multiple_of((chip * 2 + side) * size, 8)
                ref[0, chip] = all_sc[pl.ds(at, size), :].astype(BF)
    else:
        outs[3][0] = weights.astype(BF)
    dx_ref[...] += jnp.dot(rows_sc[...], w_ref[0], preferred_element_type=F32)
    sums_ref[0] = jnp.sum(rows_sc[...].astype(F32), axis=0, keepdims=True)


def attend_backward(place, halves, x, w, qkv, raised, inverse, grad, start):
    groups, columns, depth = w.shape
    heads = columns // (3 * HEAD_DIM)
    width = columns // 3
    out_specs = [whole(L, depth), each(heads, L, L), each(1, columns)]
    out_shape = [
        shaped(F32, L, depth),
        shaped(BF, groups, heads, L, L),
        shaped(F32, groups, 1, columns),
    ]
    scratch = [
        pltpu.VMEM((heads, 128, L), BF),
        pltpu.VMEM((heads, L, QB), F32),
        pltpu.VMEM((L, columns), BF),
        pltpu.VMEM((columns, L), BF),
        pltpu.VMEM((L, width), BF),
    ]
    if halves:
        size = columns // (2 * halves)
        out_specs += [each(halves, size, depth)] * 2
        out_shape += [shaped(BF, groups, halves, size, depth)] * 2
        scratch += [pltpu.VMEM((columns, depth), F32)]
    else:
        out_specs += [each(columns, depth)]
        out_shape += [shaped(BF, groups, columns, depth)]
    return pl.pallas_call(
        functools.partial(backward_kernel, bool(halves)),
        grid_spec=pltpu.PrefetchScalarGridSpec(
            num_scalar_prefetch=1,
            grid=(groups,),
            in_specs=[
                whole(L, depth),
                each(columns, depth),
                each(columns, L),
                each(heads, L, L),
                each(8, L),
                each(width, L),
                whole(L, depth),
            ],
            out_specs=out_specs,
            scratch_shapes=scratch,
        ),
        out_shape=out_shape,
        name="attend_backward",
        compiler_params=limit(40),
        cost_estimate=HINT,
    )(place, x, w, qkv, raised, inverse, grad, start)


def table_kernel(*refs):
    bucket_ref, out_ref, acc_sc, hot_sc = refs[-4:]
    step = pl.program_id(0)
    blocks = [
        (ref, g, h) for ref in refs[:-4] for g in range(ref.shape[0]) for h in range(ref.shape[1])
    ]
    heads = len(blocks)
    half = 32 * 8

    @pl.when(step == 0)
    def _():
        acc_sc[...] = jnp.zeros_like(acc_sc)

    for u in range(RT // 8):
        part = slice(u * 8, (u + 1) * 8)
        second = bucket_ref[part, :]
        offset = (
            lax.broadcasted_iota(I32, (8, L), 0)
            + (step * RT + u * 8)
            - lax.broadcasted_iota(I32, (8, L), 1)
        )
        first = first_bucket_of(offset)
        for t in range(0, 32, 2):
            for base, bucket in ((0, first), (half, second)):
                hot_sc[base + t * 8 : base + (t + 2) * 8, :] = jnp.concatenate(
                    [jnp.where(bucket == t, 1.0, 0.0), jnp.where(bucket == t + 1, 1.0, 0.0)],
                    axis=0,
                ).astype(BF)
        left = jnp.concatenate([ref[g, h, part, :] for ref, g, h in blocks], axis=0)
        acc_sc[...] += lax.dot_general(left, hot_sc[...], NT, preferred_element_type=F32)

    @pl.when(step == pl.num_programs(0) - 1)
    def _():
        shape = (heads * 8, 2 * half)
        same = lax.broadcasted_iota(I32, shape, 0) % 8 == lax.broadcasted_iota(I32, shape, 1) % 8
        kept = jnp.where(same, acc_sc[...], 0.0)
        fold = (2 * half, 64)
        right = (
            lax.broadcasted_iota(I32, fold, 0) // 8 == lax.broadcasted_iota(I32, fold, 1)
        ).astype(F32)
        spread = (16, heads * 8)
        left = (
            lax.broadcasted_iota(I32, spread, 1) // 8 == lax.broadcasted_iota(I32, spread, 0)
        ).astype(F32)
        exact = lax.Precision.HIGHEST
        folded = jnp.dot(kept, right, preferred_element_type=F32, precision=exact)
        out_ref[...] = jnp.dot(left, folded, preferred_element_type=F32, precision=exact)


def table_gradients(ds, bucket):
    heads = sum(item.shape[0] * item.shape[1] for item in ds)
    return pl.pallas_call(
        table_kernel,
        grid=(L // RT,),
        in_specs=[
            pl.BlockSpec(item.shape[:2] + (RT, L), lambda r: (0, 0, r, 0)) for item in ds
        ]
        + [pl.BlockSpec((RT, L), lambda r: (r, 0))],
        out_specs=whole(16, 64),
        out_shape=shaped(F32, 16, 64),
        scratch_shapes=[pltpu.VMEM((heads * 8, 512), F32), pltpu.VMEM((512, L), BF)],
        name="table_gradients",
        compiler_params=limit(16),
        cost_estimate=HINT,
    )(*ds, bucket)


def mean_of(rows):
    return jnp.mean(rows, axis=-1, keepdims=True)


def normalize(rows):
    centred = rows - mean_of(rows)
    inverse = lax.rsqrt(mean_of(centred * centred) + EPS)
    return centred * inverse, inverse


def normalize_back(scaled, unit, inverse):
    return inverse * (scaled - mean_of(scaled) - unit * mean_of(scaled * unit))


def gelu_parts(values):
    size = jnp.abs(values)
    t = 1.0 / (1.0 + (0.3275911 * ROOT_HALF) * size)
    bell = jnp.exp(values * values * -0.5)
    series = 1.061405429
    for term in (-1.453152027, 1.421413741, -0.284496736, 0.254829592):
        series = term + t * series
    tail = (0.5 * t) * series * bell
    below = jnp.where(values >= 0, 1.0 - tail, tail)
    return values * below, below + values * (bell * DENSITY_SCALE)


def column_sum(rows):
    return jnp.sum(rows, axis=0, keepdims=True)


def up_kernel(
    place_ref, x_ref, ctx_own_ref, ctx_ref, wo_ref, bo_ref, g1_ref, s1_ref, wi_ref, bi_ref, wb_ref,
    bb_ref, g2_ref, s2_ref, cot_ref,
    out_ref, mid_ref, branch_ref, turned_ref, slope_ref, unit_ref, inverse_ref, low_ref, sums_ref,
    normed_sc, low_sc, acc_sc,
):
    step = pl.program_id(0)
    groups = wo_ref.shape[0]

    @pl.when(step == 0)
    def _():
        for r in range(L // MB):
            rows = slice(r * MB, (r + 1) * MB)
            total = x_ref[rows, :].astype(F32) + bo_ref[...]
            for s in range(groups):
                ctx = ctx_own_ref[0, rows, :] if s == 0 else ctx_ref[s - 1, rows, :]
                quarter = lax.rem(place_ref[0] + s, groups)
                total = total + jnp.dot(ctx, wo_ref[quarter], preferred_element_type=F32)
            unit, inverse = normalize(total)
            unit_ref[rows, :] = unit
            inverse_ref[rows, :] = jnp.broadcast_to(inverse, (MB, 128))
            normed = unit * g1_ref[...] + s1_ref[...]
            normed_sc[rows, :] = normed
            low_sc[rows, :] = normed.astype(BF)
        low_ref[...] = jnp.transpose(low_sc[...])
        acc_sc[...] = jnp.zeros_like(acc_sc)

    for r in range(L // MB):
        rows = slice(r * MB, (r + 1) * MB)
        pre = jnp.dot(low_sc[rows, :], wi_ref[...], preferred_element_type=F32) + bi_ref[...]
        acted, slope = gelu_parts(pre)
        acted = acted.astype(BF)
        slope_ref[rows, :] = slope.astype(BF)
        turned_ref[:, rows] = jnp.transpose(acted)
        acc_sc[rows, :] += jnp.dot(acted, wb_ref[...], preferred_element_type=F32)

    @pl.when(step == pl.num_programs(0) - 1)
    def _():
        gain_sum = shift_sum = bias_sum = None
        for r in range(L // MB):
            rows = slice(r * MB, (r + 1) * MB)
            unit, inverse = normalize(normed_sc[rows, :] + (acc_sc[rows, :] + bb_ref[...]))
            out_ref[rows, :] = (unit * g2_ref[...] + s2_ref[...]).astype(BF)
            upstream = cot_ref[rows, :].astype(F32)
            middle = normalize_back(upstream * g2_ref[...], unit, inverse)
            mid_ref[rows, :] = middle
            branch = middle.astype(BF)
            branch_ref[rows, :] = branch
            parts = (
                column_sum(upstream * unit),
                column_sum(upstream),
                column_sum(branch.astype(F32)),
            )
            gain_sum = parts[0] if r == 0 else gain_sum + parts[0]
            shift_sum = parts[1] if r == 0 else shift_sum + parts[1]
            bias_sum = parts[2] if r == 0 else bias_sum + parts[2]
        sums_ref[0:1, :] = gain_sum
        sums_ref[1:2, :] = shift_sum
        sums_ref[2:3, :] = bias_sum


def feed_up(place, x, ctx_own, ctx, w_out, bo, g1, s1, w_in, bi, w_back, bb, g2, s2, cot):
    width = x.shape[1]
    units = w_in.shape[1]
    groups, own = w_out.shape[0], w_out.shape[1]
    row = whole(1, width)
    return pl.pallas_call(
        up_kernel,
        grid_spec=pltpu.PrefetchScalarGridSpec(
            num_scalar_prefetch=1,
            grid=(units // FC,),
            in_specs=[
                whole(L, width),
                whole(1, L, own),
                whole(groups - 1, L, own),
                whole(groups, own, width),
                row,
                row,
                row,
                pl.BlockSpec((width, FC), lambda n, place: (0, n)),
                pl.BlockSpec((1, FC), lambda n, place: (0, n)),
                pl.BlockSpec((FC, width), lambda n, place: (n, 0)),
                row,
                row,
                row,
                whole(L, width),
            ],
            out_specs=[
                whole(L, width),
                whole(L, width),
                whole(L, width),
                pl.BlockSpec((FC, L), lambda n, place: (n, 0)),
                pl.BlockSpec((L, FC), lambda n, place: (0, n)),
                whole(L, width),
                whole(L, 128),
                whole(width, L),
                whole(8, width),
            ],
            scratch_shapes=[
                pltpu.VMEM((L, width), F32),
                pltpu.VMEM((L, width), BF),
                pltpu.VMEM((L, width), F32),
            ],
        ),
        out_shape=[
            shaped(BF, L, width),
            shaped(F32, L, width),
            shaped(BF, L, width),
            shaped(BF, units, L),
            shaped(BF, L, units),
            shaped(F32, L, width),
            shaped(F32, L, 128),
            shaped(BF, width, L),
            shaped(F32, 8, width),
        ],
        name="feed_up",
        compiler_params=limit(44),
        cost_estimate=HINT,
    )(place, x, ctx_own, ctx, w_out, bo, g1, s1, w_in, bi, w_back, bb, g2, s2, cot)


def down_kernel(
    halved, place_ref, branch_ref, slope_ref, wb_ref, wi_ref, low_ref, mid_ref, unit_ref,
    inverse_ref, g1_ref, wo_ref, turned_own_ref, turned_ref, norm_own_ref, norm_ref, *refs
):
    bias_ref, first_ref, grad_own_ref, grad_ref, sums_ref = refs[:5]
    weight_refs = refs[5 : 7 if halved else 6]
    acc_sc, pre_sc, weight_sc = refs[-3:]
    step = pl.program_id(0)
    last = pl.num_programs(0) - 1
    groups, own = wo_ref.shape[0], wo_ref.shape[1]

    def give():
        if not halved:
            weight_refs[0][...] = weight_sc[...]
            return
        core = place_ref[1]
        chips, size = weight_refs[0].shape[0], weight_refs[0].shape[1]
        for chip in range(chips):
            for side, ref in ((1 - core, weight_refs[0]), (core, weight_refs[1])):
                at = pl.multiple_of((chip * 2 + side) * size, size)
                ref[chip] = weight_sc[pl.ds(at, size), :]

    @pl.when(step == 0)
    def _():
        acc_sc[...] = mid_ref[...]

    @pl.when(step < last)
    def _():
        total = None
        for r in range(L // MB):
            rows = slice(r * MB, (r + 1) * MB)
            pre = lax.dot_general(
                branch_ref[rows, :], wb_ref[...], NT, preferred_element_type=F32
            ) * slope_ref[rows, :].astype(F32)
            pre = pre.astype(BF)
            pre_sc[rows, :] = pre
            part = column_sum(pre.astype(F32))
            total = part if r == 0 else total + part
            acc_sc[rows, :] += lax.dot_general(
                pre, wi_ref[...], NT, preferred_element_type=F32
            )
        bias_ref[0:1, :] = total
        weight_sc[...] = jnp.dot(
            low_ref[...], pre_sc[...], preferred_element_type=F32
        ).astype(BF)
        give()

    @pl.when(step == last)
    def _():
        gain_sum = shift_sum = bias_sum = None
        for r in range(L // MB):
            rows = slice(r * MB, (r + 1) * MB)
            hidden = acc_sc[rows, :]
            unit = unit_ref[rows, :]
            first = normalize_back(hidden * g1_ref[...], unit, inverse_ref[rows, 0:1])
            first_ref[rows, :] = first
            attended = first.astype(BF)
            pre_sc[rows, :] = attended
            parts = (
                column_sum(hidden * unit),
                column_sum(hidden),
                column_sum(attended.astype(F32)),
            )
            gain_sum = parts[0] if r == 0 else gain_sum + parts[0]
            shift_sum = parts[1] if r == 0 else shift_sum + parts[1]
            bias_sum = parts[2] if r == 0 else bias_sum + parts[2]
        sums_ref[0:1, :] = gain_sum
        sums_ref[1:2, :] = shift_sum
        sums_ref[2:3, :] = bias_sum
        for s in range(groups):
            quarter = lax.rem(place_ref[0] + s, groups)
            turned = turned_own_ref[0] if s == 0 else turned_ref[s - 1]
            norm = norm_own_ref[0] if s == 0 else norm_ref[s - 1]
            at = pl.multiple_of(quarter * own, own)
            weight_sc[pl.ds(at, own), :] = jnp.dot(
                turned, pre_sc[...], preferred_element_type=F32
            ).astype(BF)
            grads = lax.dot_general(
                wo_ref[quarter], pre_sc[...], NT, preferred_element_type=F32
            )
            for h in range(own // HEAD_DIM):
                rows = slice(h * HEAD_DIM, (h + 1) * HEAD_DIM)
                scaled = (grads[rows, :] * norm[h : h + 1, :]).astype(BF)
                if s == 0:
                    grad_own_ref[0, rows, :] = scaled
                else:
                    grad_ref[s - 1, rows, :] = scaled
        give()


def feed_down(place, halves, branch, slope, w_back, w_in, low, mid, unit, inverse, g1, w_out,
              turned_own, turned, norm_own, norm):
    width = branch.shape[1]
    units = w_in.shape[1]
    groups, own = w_out.shape[0], w_out.shape[1]
    steps = units // FC
    inside = lambda n: jnp.minimum(n, steps - 1)
    out_specs = [
        pl.BlockSpec((8, FC), lambda n, place: (0, inside(n))),
        whole(L, width),
        whole(1, own, L),
        whole(groups - 1, own, L),
        whole(8, width),
    ]
    out_shape = [
        shaped(F32, 8, units),
        shaped(F32, L, width),
        shaped(BF, 1, own, L),
        shaped(BF, groups - 1, own, L),
        shaped(F32, 8, width),
    ]
    if halves:
        size = width // (2 * halves)
        out_specs += [pl.BlockSpec((halves, size, FC), lambda n, place: (0, 0, n))] * 2
        out_shape += [shaped(BF, halves, size, units + width)] * 2
    else:
        out_specs += [pl.BlockSpec((width, FC), lambda n, place: (0, n))]
        out_shape += [shaped(BF, width, units + width)]
    return pl.pallas_call(
        functools.partial(down_kernel, bool(halves)),
        grid_spec=pltpu.PrefetchScalarGridSpec(
            num_scalar_prefetch=1,
            grid=(steps + 1,),
            in_specs=[
                whole(L, width),
                pl.BlockSpec((L, FC), lambda n, place: (0, inside(n))),
                pl.BlockSpec((FC, width), lambda n, place: (inside(n), 0)),
                pl.BlockSpec((width, FC), lambda n, place: (0, inside(n))),
                whole(width, L),
                whole(L, width),
                whole(L, width),
                whole(L, 128),
                whole(1, width),
                whole(groups, own, width),
                whole(1, own, L),
                whole(groups - 1, own, L),
                whole(1, 8, L),
                whole(groups - 1, 8, L),
            ],
            out_specs=out_specs,
            scratch_shapes=[
                pltpu.VMEM((L, width), F32),
                pltpu.VMEM((L, FC), BF),
                pltpu.VMEM((width, FC), BF),
            ],
        ),
        out_shape=out_shape,
        name="feed_down",
        compiler_params=limit(44),
        cost_estimate=HINT,
    )(place, branch, slope, w_back, w_in, low, mid, unit, inverse, g1, w_out,
      turned_own, turned, norm_own, norm)


def product_kernel(place_ref, left_ref, right_ref, out_ref):
    out_ref[...] = jnp.dot(
        left_ref[...], right_ref[...], preferred_element_type=F32
    ).astype(BF)


def product(place, left, right, sizes):
    rows, depth = left.shape
    columns = right.shape[1]
    count, size, halved = sizes
    take = (lambda n, place: (2 * n + 1 - place[1], 0)) if halved else (lambda n, place: (n, 0))
    return pl.pallas_call(
        product_kernel,
        grid_spec=pltpu.PrefetchScalarGridSpec(
            num_scalar_prefetch=1,
            grid=(count,),
            in_specs=[pl.BlockSpec((size, depth), take), whole(depth, columns)],
            out_specs=pl.BlockSpec((size, columns), lambda n, place: (n, 0)),
        ),
        out_shape=shaped(BF, count * size, columns),
        name="back_weights",
        compiler_params=limit(24),
        cost_estimate=HINT,
    )(place, left, right)


def kept_kernel(place_ref, left_ref, right_ref, got_ref, a_sent, a_kept, b_sent, b_kept):
    chip = pl.program_id(0)
    chip_y, chip_x = chip // 2, lax.rem(chip, 2)
    here_x, here_y = place_ref[2], place_ref[3]
    value = jnp.dot(left_ref[...], right_ref[...], preferred_element_type=F32)
    value = (value + got_ref[0].astype(F32)).astype(BF)
    cut = a_sent.shape[1]

    @pl.when(chip_x == here_x)
    def _():
        a_kept[chip_y] = value[:cut, :]

    @pl.when(chip_x != here_x)
    def _():
        a_sent[chip_y] = value[:cut, :]

    @pl.when(chip_y == here_y)
    def _():
        b_kept[chip_x] = value[cut:, :]

    @pl.when(chip_y != here_y)
    def _():
        b_sent[chip_x] = value[cut:, :]


def product_kept(place, left, right, got):
    chips, size, columns = got.shape
    depth = left.shape[1]
    part = whole(2, size // 2, columns)
    return pl.pallas_call(
        kept_kernel,
        grid_spec=pltpu.PrefetchScalarGridSpec(
            num_scalar_prefetch=1,
            grid=(chips,),
            in_specs=[
                pl.BlockSpec((size, depth), lambda n, place: (2 * n + place[1], 0)),
                whole(depth, columns),
                pl.BlockSpec((1, size, columns), lambda n, place: (n, 0, 0)),
            ],
            out_specs=[part] * 4,
        ),
        out_shape=[shaped(BF, 2, size // 2, columns)] * 4,
        name="kept_weights",
        compiler_params=limit(24),
        cost_estimate=HINT,
    )(place, left, right, got)


def total_of(*items):
    total = items[0].astype(F32)
    for item in items[1:]:
        total = total + item.astype(F32)
    return total.astype(BF)


def chips_kernel(count, layout, place_ref, *refs):
    inputs, outs = refs[:count], refs[count:]
    here_x, here_y = place_ref[2], place_ref[3]
    for order, (way, sources) in enumerate(layout):
        sent, kept = outs[2 * order], outs[2 * order + 1]
        start = 0
        for number, low, high in sources:
            kept_ref, got_ref = inputs[2 * number], inputs[2 * number + 1]
            for g in range(kept_ref.shape[0]):
                rows = slice(start, start + high - low)
                start += high - low
                for other in range(2):
                    for out, far in ((sent, 1), (kept, 0)):
                        if way == "x":
                            chip = other * 2 + (here_x ^ far)
                        else:
                            chip = (here_y ^ far) * 2 + other
                        out[other, rows, :] = total_of(
                            kept_ref[g, chip, low:high, :], got_ref[g, chip, low:high, :]
                        )


def sum_chips(place, pairs, parts, block):
    specs, out_specs, out_shape = [], [], []
    columns = pairs[0][0].shape[-1]
    for kept, _ in pairs:
        shape = kept.shape[:3] + (block,)
        specs += [pl.BlockSpec(shape, lambda n, place: (0, 0, 0, n))] * 2
    for _, sources in parts:
        height = sum(pairs[n][0].shape[0] * (high - low) for n, low, high in sources)
        out_specs += [pl.BlockSpec((2, height, block), lambda n, place: (0, 0, n))] * 2
        out_shape += [shaped(BF, 2, height, columns)] * 2
    return pl.pallas_call(
        functools.partial(chips_kernel, 2 * len(pairs), parts),
        grid_spec=pltpu.PrefetchScalarGridSpec(
            num_scalar_prefetch=1, grid=(columns // block,), in_specs=specs, out_specs=out_specs
        ),
        out_shape=out_shape,
        name="sum_chips",
        compiler_params=limit(24),
        cost_estimate=HINT,
    )(place, *[item for pair in pairs for item in pair])


def pairs_kernel(place_ref, a_kept, a_got, b_kept, b_got, a_sent, a_own, b_sent, b_own):
    here_x, here_y = place_ref[2], place_ref[3]
    for here, kept, got, sent, own in (
        (here_y, a_kept, a_got, a_sent, a_own),
        (here_x, b_kept, b_got, b_sent, b_own),
    ):
        sent[...] = total_of(kept[1 - here], got[1 - here])
        own[...] = total_of(kept[here], got[here])


def sum_pairs(place, a_kept, a_got, b_kept, b_got, block):
    columns = a_kept.shape[-1]
    spec = lambda item: pl.BlockSpec((2, item.shape[1], block), lambda n, place: (0, 0, n))
    flat = lambda item: pl.BlockSpec((item.shape[1], block), lambda n, place: (0, n))
    return pl.pallas_call(
        pairs_kernel,
        grid_spec=pltpu.PrefetchScalarGridSpec(
            num_scalar_prefetch=1,
            grid=(columns // block,),
            in_specs=[spec(a_kept), spec(a_got), spec(b_kept), spec(b_got)],
            out_specs=[flat(a_kept)] * 2 + [flat(b_kept)] * 2,
        ),
        out_shape=[shaped(BF, a_kept.shape[1], columns)] * 2
        + [shaped(BF, b_kept.shape[1], columns)] * 2,
        name="sum_pairs",
        compiler_params=limit(24),
        cost_estimate=HINT,
    )(place, a_kept, a_got, b_kept, b_got)


def cut_kernel(turned, place_ref, a_kept, a_got, b_kept, b_got, *refs):
    outs, sum_sc = refs[:-1], refs[-1]
    cut = a_kept.shape[0]
    sum_sc[0:cut, :] = a_kept[...].astype(F32) + a_got[...].astype(F32)
    sum_sc[cut:, :] = b_kept[...].astype(F32) + b_got[...].astype(F32)
    size = outs[0].shape[0]
    for s, out in enumerate(outs):
        if turned:
            out[...] = sum_sc[s * size : (s + 1) * size, :].astype(BF)
        else:
            at = pl.multiple_of(lax.rem(place_ref[0] + s, len(outs)) * size, 8)
            out[...] = sum_sc[pl.ds(at, size), :].astype(BF)


def cut_quarters(place, a_kept, a_got, b_kept, b_got, block, turned):
    columns = a_kept.shape[-1]
    height = a_kept.shape[0] + b_kept.shape[0]
    groups = lax.axis_size("heads")
    spec = lambda item: pl.BlockSpec((item.shape[0], block), lambda n, place: (0, n))
    return pl.pallas_call(
        functools.partial(cut_kernel, turned),
        grid_spec=pltpu.PrefetchScalarGridSpec(
            num_scalar_prefetch=1,
            grid=(columns // block,),
            in_specs=[spec(a_kept), spec(a_got), spec(b_kept), spec(b_got)],
            out_specs=[pl.BlockSpec((height // groups, block), lambda n, place: (0, n))] * groups,
            scratch_shapes=[pltpu.VMEM((height, block), F32)],
        ),
        out_shape=[shaped(BF, height // groups, columns)] * groups,
        name="cut_quarters",
        compiler_params=limit(24),
        cost_estimate=HINT,
    )(place, a_kept, a_got, b_kept, b_got)


def join_kernel(count, place_ref, *refs):
    pieces, outs = refs[:count], refs[count:]
    size = pieces[0].shape[0]
    start = 0
    for out in outs:
        for s, piece in enumerate(pieces):
            at = pl.multiple_of(lax.rem(place_ref[0] + s, len(pieces)) * size, 8)
            out[pl.ds(at, size), :] = piece[:, start : start + out.shape[1]].astype(F32)
        start += out.shape[1]


def join_quarters(place, pieces, widths):
    vmem = pl.BlockSpec(memory_space=pltpu.VMEM)
    rows = len(pieces) * pieces[0].shape[0]
    return pl.pallas_call(
        functools.partial(join_kernel, len(pieces)),
        in_specs=[pl.BlockSpec(memory_space=pltpu.SMEM)] + [vmem] * len(pieces),
        out_specs=[vmem] * len(widths),
        out_shape=[shaped(F32, rows, width) for width in widths],
        name="join_quarters",
        compiler_params=limit(16),
        cost_estimate=HINT,
    )(place, *pieces)


def chips_join_kernel(place_ref, mine_a, mine_b, got_a, got_b, out_ref):
    core, here_x, here_y = place_ref[1], place_ref[2], place_ref[3]
    cut = mine_a.shape[2]
    size = cut + mine_b.shape[2]
    for far_y in range(2):
        for far_x in range(2):
            chip = (here_y ^ far_y) * 2 + (here_x ^ far_x)
            for side, a_ref, b_ref in ((core, mine_a, mine_b), (1 - core, got_a, got_b)):
                at = (chip * 2 + side) * size
                first = pl.multiple_of(at, 8)
                out_ref[pl.ds(first, cut), :] = a_ref[far_y, far_x].astype(F32)
                second = pl.multiple_of(at + cut, 8)
                out_ref[pl.ds(second, size - cut), :] = b_ref[far_x, far_y].astype(F32)


def join_chips(place, mine_a, mine_b, got_a, got_b):
    vmem = pl.BlockSpec(memory_space=pltpu.VMEM)
    rows = 8 * (mine_a.shape[2] + mine_b.shape[2])
    return pl.pallas_call(
        chips_join_kernel,
        in_specs=[pl.BlockSpec(memory_space=pltpu.SMEM)] + [vmem] * 4,
        out_specs=vmem,
        out_shape=shaped(F32, rows, mine_a.shape[-1]),
        name="join_chips",
        compiler_params=limit(16),
        cost_estimate=HINT,
    )(place, mine_a, mine_b, got_a, got_b)


def tie(values, *others):
    return lax.optimization_barrier((values, others))[0]


def swap(array, bit):
    count = lax.axis_size("docs")
    return lax.ppermute(array, "docs", [(i, i ^ (1 << bit)) for i in range(count)])


def fetch(array, shift):
    count = lax.axis_size("heads")
    return lax.ppermute(array, "heads", [((i + shift) % count, i) for i in range(count)])


def exchange_heads(parts):
    count = lax.axis_size("heads")
    return [
        lax.ppermute(parts[s], "heads", [(i, (i + s) % count) for i in range(count)])
        for s in range(1, count)
    ]


def spread_heads(block):
    return [block] + [fetch(block, s) for s in range(1, lax.axis_size("heads"))]


def in_order(pieces, z):
    count = len(pieces)
    twice = jnp.stack(list(pieces) + list(pieces[:-1]))
    return lax.dynamic_slice_in_dim(twice, (count - z) % count, count, axis=0)


def sum_everywhere(rows):
    for bit in range(lax.axis_size("docs").bit_length() - 1):
        rows = rows + swap(rows, bit)
    count = lax.axis_size("heads")
    for bit in range(count.bit_length() - 1):
        rows = rows + lax.ppermute(rows, "heads", [(i, i ^ (1 << bit)) for i in range(count)])
    return rows


def spread_plane(first, second):
    got = [swap(first, 1), swap(second, 2)]
    first, second = jnp.stack([first, got[0]]), jnp.stack([second, got[1]])
    got = [swap(first, 2), swap(second, 1)]
    return jnp.stack([first, got[0]]), jnp.stack([second, got[1]])


def reduce_docs(blocks):
    bits = blocks.shape[0].bit_length() - 1
    docs = lax.axis_index("docs")
    current = blocks.reshape((2,) * bits + blocks.shape[1:])
    for bit in range(bits):
        mine = (docs >> bit) & 1
        axis = bits - 1 - bit
        sent = lax.dynamic_index_in_dim(current, 1 - mine, axis, keepdims=False)
        kept = lax.dynamic_index_in_dim(current, mine, axis, keepdims=False)
        current = total_of(kept, swap(sent, bit))
    return current


def spread_docs(block):
    count = lax.axis_size("docs")
    docs = lax.axis_index("docs")
    current = block
    for done, bit in enumerate(range(count.bit_length() - 2, -1, -1)):
        got = swap(current, bit)
        mine = ((docs >> bit) & 1) == 1
        current = jnp.stack(
            [jnp.where(mine, got, current), jnp.where(mine, current, got)], axis=done
        )
    return current.reshape((count,) + block.shape)


def body(
    layer_input, token_boxes, lengths, w_qkv, qv_bias, rel_tables, w_out, out_bias,
    gain_one, shift_one, w_in, in_bias, w_back, back_bias, gain_two, shift_two, cotangent,
):
    width = layer_input.shape[1]
    units = w_in.shape[1]
    groups = lax.axis_size("heads")
    count = lax.axis_size("docs")
    docs = lax.axis_index("docs")
    z = lax.axis_index("heads")
    own = w_qkv.shape[2]
    heads = rel_tables.shape[1]
    buckets = rel_tables.shape[2]
    columns = 3 * own
    share = width // count
    small = columns // count
    chips = 4 if count == 8 and share % 16 == 0 and small % 8 == 0 else 0
    place = jnp.stack([z, docs & 1, (docs >> 1) & 1, (docs >> 2) & 1]).astype(I32)

    matrix = w_qkv.transpose(1, 2, 0).reshape(columns, width)
    room = jnp.zeros((128 - heads * buckets,), BF)
    line = jnp.concatenate(
        [qv_bias[0], qv_bias[1], rel_tables[0].reshape(-1), room, rel_tables[1].reshape(-1), room]
    )
    extra = jnp.pad(line[None], ((0, 7), (0, width - line.shape[0])))
    piece = jnp.concatenate(
        [lax.dynamic_slice_in_dim(matrix, docs * small, small, axis=0), extra], axis=0
    )
    got = [fetch(piece, s) for s in range(1, groups)]
    bucket = second_buckets(place, lengths, token_boxes)

    ctx_own, turned_own, raised_own, qkv_own, norm_own = attend_forward(
        place, layer_input, (matrix[None],), extra[None], bucket
    )
    arrived = jnp.stack(tie(got, ctx_own))
    if chips:
        cut = (small // 2 + 7) // 8 * 8
        first, second = spread_plane(arrived[:, :cut], arrived[:, cut:small])
        weights, ctx, turned, raised, qkv, norm = attend_forward(
            place, layer_input, (first, second, swap(first, 0), swap(second, 0)),
            arrived[:, small:], bucket,
        )
    else:
        weights = spread_docs(arrived[:, :small]).transpose(1, 0, 2, 3)
        weights = weights.reshape(groups - 1, columns, width)
        ctx, turned, raised, qkv, norm = attend_forward(
            place, layer_input, (weights,), arrived[:, small:], bucket
        )

    w_out_heads = w_out.reshape(groups, own, width)
    flat = lambda vector: vector.reshape(1, -1)
    layer_output, grad_mid, grad_branch, acted, slope, unit, inverse, low, up_sums = feed_up(
        place, layer_input, ctx_own, ctx, w_out_heads, flat(out_bias), flat(gain_one),
        flat(shift_one), w_in, flat(in_bias), w_back, flat(back_bias), flat(gain_two),
        flat(shift_two), cotangent,
    )
    down = lambda branch: feed_down(
        place, chips, branch, slope, w_back, w_in, low, grad_mid, unit, inverse, flat(gain_one),
        w_out_heads, turned_own, turned, norm_own, norm,
    )
    attend_back = lambda s, t, grad, start: attend_backward(
        place, chips, layer_input, weights[s:t], qkv[s:t], raised[s:t], norm[s:t], grad, start
    )

    def short_sums(score_grads, sums, bucket):
        tables = table_gradients(score_grads, bucket)[: groups * heads]
        tables = tables.reshape(groups, heads, 2, buckets).transpose(0, 2, 1, 3)
        sums = jnp.concatenate(sums, axis=0)[:, 0]
        quarters = jnp.concatenate(
            [sums[:, :own], sums[:, 2 * own :], tables.reshape(groups, 2 * heads * buckets)],
            axis=1,
        )
        quarters = jnp.pad(quarters, ((0, 0), (0, width - quarters.shape[1])))
        quarters = in_order([quarters[s] for s in range(groups)], z)
        rows = jnp.concatenate(
            [down_sums[:3], up_sums[:3], in_sums[0].reshape(units // width, width), quarters],
            axis=0,
        )
        return tables, jnp.pad(rows, ((0, -rows.shape[0] % 8), (0, 0)))

    if chips:
        half = share // 2
        back_size = units // count
        sent = product(place, acted, grad_branch, (chips, back_size, True))
        got = swap(sent.reshape(chips, back_size, width), 0)
        back = product_kept(place, acted, grad_branch, got)
        back_got = [swap(back[0], 1), swap(back[2], 2)]

        in_sums, grad_first, grad_own, grad_rest, down_sums, dense_sent, dense_kept = down(
            tie(grad_branch, back[0], back[2])
        )
        back_got = tie(back_got, grad_first)
        back = sum_pairs(place, back[1], back_got[0], back[3], back_got[1], width // 2)
        back_got = [swap(back[0], 2), swap(back[2], 1)]
        dense_sent = tie(dense_sent, back[0])
        dense_got = swap(dense_sent, 0)

        dx, ds_own, sums_own, own_sent, own_kept = attend_backward(
            place, chips, layer_input, matrix[None], qkv_own, raised_own, norm_own,
            tie(grad_own, dense_sent, back[0], back[2]), grad_first,
        )
        dense_got = tie(dense_got, dx)
        dense = sum_chips(
            place,
            [(dense_kept[None], dense_got[None])],
            (("x", ((0, 0, half),)), ("y", ((0, half, share),))),
            FC,
        )
        dense_got = [swap(dense[0], 1), swap(dense[2], 2)]
        own_sent = tie(own_sent, dense[0])
        own_got = swap(own_sent, 0)
        dx, ds_one, sums_one, one_sent, one_kept = attend_back(
            0, 1, tie(grad_rest[0:1], dense[0], dense[2], own_sent), dx
        )
        back_got = tie(back_got, dx)
        back = cut_quarters(place, back[1], back_got[0], back[3], back_got[1], width // 2, False)
        back_got = exchange_heads(back)
        one_sent = tie(one_sent, back[0])
        one_got = swap(one_sent, 0)
        dx, ds_two, sums_two, two_sent, two_kept = attend_back(
            1, groups - 1, tie(grad_rest[1:], back, one_sent), dx
        )
        dense_got, own_got, one_got, back_got = tie((dense_got, own_got, one_got, back_got), dx)
        dense = sum_pairs(place, dense[1], dense_got[0], dense[3], dense_got[1], FC)
        last_a = sum_chips(
            place, [(own_kept, own_got), (one_kept, one_got)],
            (("x", ((0, 0, small), (1, 0, small))),), width // 2,
        )
        last_a, dense = list(last_a), list(dense)
        two_sent, last_a[0], dense[0], dense[2] = tie(
            (two_sent, last_a[0], dense[0], dense[2]), last_a[1], dense[1]
        )
        two_got = swap(two_sent, 0)
        last_a_got = swap(last_a[0], 1)
        dense_got = [swap(dense[0], 2), swap(dense[2], 1)]
        back_own = tie(total_of(back[0], *back_got), last_a[0], dense[0])
        back = spread_heads(back_own)
        tables, total = short_sums(
            (ds_own, ds_one, ds_two), (sums_own, sums_one, sums_two),
            tie(bucket, back_own, two_sent, last_a[0], dense[0], dense[2]),
        )
        two_got, dense_got = tie((two_got, dense_got), tables)
        last_b = sum_chips(place, [(two_kept, two_got)], (("y", ((0, 0, small),)),), width // 2)
        last_b_got = swap(last_b[0], 2)
        dense = cut_quarters(place, dense[1], dense_got[0], dense[3], dense_got[1], FC, False)
        dense_got = exchange_heads(dense)
        total = sum_everywhere(tie(total, dense[0], last_b[0]))
        last = sum_pairs(place, last_a[1], last_a_got, last_b[1], last_b_got, width // 2)
        last_got = [swap(last[0], 2), swap(last[2], 1)]
        dense = spread_heads(total_of(dense[0], *dense_got))
        last = cut_quarters(place, last[1], last_got[0], last[3], last_got[1], width // 2, True)
        last_got = exchange_heads(last)
        quarter = total_of(last[0], *last_got)
        first, second = spread_plane(quarter[:cut], quarter[cut:])
        full = join_chips(place, first, second, swap(first, 0), swap(second, 0))
        (out_back,) = join_quarters(place, back, (width,))
        out_in, out_out = join_quarters(place, dense, (units, width))
    else:
        back_grads = product(place, acted, grad_branch, (units // FC, FC, False))
        in_sums, grad_first, grad_own, grad_rest, down_sums, dense_grads = down(grad_branch)
        dx, ds_own, sums_own, dw_own = attend_backward(
            place, chips, layer_input, matrix[None], qkv_own, raised_own, norm_own, grad_own,
            grad_first,
        )
        dx, ds_rest, sums_rest, dw_rest = attend_back(0, groups - 1, grad_rest, dx)
        total = sum_everywhere(short_sums((ds_own, ds_rest), (sums_own, sums_rest), bucket)[1])

        def dense_rows(grads):
            rows = reduce_docs(grads.reshape(count, -1, grads.shape[1]))
            parts = rows.reshape(-1, groups, width)
            parts = [
                lax.dynamic_index_in_dim(parts, (z + s) % groups, 1, keepdims=False)
                for s in range(groups)
            ]
            pieces = spread_heads(total_of(parts[0], *exchange_heads(parts)))
            return in_order(pieces, z).transpose(1, 0, 2).reshape(rows.shape).astype(F32)

        out_back = dense_rows(back_grads)
        rows = dense_rows(dense_grads)
        out_in, out_out = rows[:, :units], rows[:, units:]
        blocks = jnp.concatenate([dw_own, dw_rest]).reshape(groups, count, small, width)
        blocks = blocks.transpose(1, 0, 2, 3).reshape(count, groups * small, width)
        blocks = reduce_docs(blocks).reshape(groups, small, width)
        parts = [blocks[s] for s in range(groups)]
        full = spread_docs(total_of(parts[0], *exchange_heads(parts)))
        full = full.reshape(columns, width).astype(F32)

    mine = lambda vector: lax.dynamic_slice_in_dim(
        vector, docs * (vector.shape[0] // count), vector.shape[0] // count
    )
    deep = units // width
    ends = lax.dynamic_index_in_dim(total, 6 + deep + z, 0, keepdims=False)
    return (
        layer_output,
        dx.astype(BF),
        full.reshape(3, own, width).transpose(2, 0, 1),
        ends[: 2 * own].reshape(2, own),
        ends[2 * own : 2 * own + 2 * heads * buckets].reshape(2, heads, buckets),
        out_out,
        mine(total[2]),
        mine(total[0]),
        mine(total[1]),
        out_in,
        mine(total[6 : 6 + deep].reshape(-1)),
        out_back,
        mine(total[5]),
        mine(total[3]),
        mine(total[4]),
    )


def solution(mesh):
    rows = P(("docs", "heads"), None)
    return jax.shard_map(
        body,
        mesh=mesh,
        in_specs=(
            rows,
            P(None, "docs"),
            P("docs"),
            P(None, None, "heads"),
            P(None, "heads"),
            P(None, "heads", None),
            P(),
            P(),
            P(),
            P(),
            P(),
            P(),
            P(),
            P(),
            P(),
            P(),
            rows,
        ),
        out_specs=(
            rows,
            rows,
            P(None, None, "heads"),
            P(None, "heads"),
            P(None, "heads", None),
            P("docs", None),
            P("docs"),
            P("docs"),
            P("docs"),
            P("docs", None),
            P("docs"),
            P("docs", None),
            P("docs"),
            P("docs"),
            P("docs"),
        ),
        check_vma=False,
    )
```

```python
import functools
import math

import jax
import jax.numpy as jnp
from jax import lax
from jax.experimental import pallas as pl
from jax.experimental.pallas import tpu as pltpu
from jax.sharding import PartitionSpec as P

HEAD_DIM = 64
L = 512
EPS = 1e-05
NEG = -1000000000.0
THRESHOLDS = (1, 2, 3, 4, 6, 8, 12, 16, 24, 32, 48, 64, 96, 128, 192)
ROOT_HALF = 1.0 / math.sqrt(2.0)
DENSITY_SCALE = 1.0 / math.sqrt(2.0 * math.pi)
SCALE = 0.125
KC = 32
QB = 128
RT = 64
FC = 768
MB = 256
BF = jnp.bfloat16
F32 = jnp.float32
I32 = jnp.int32
NT = (((1,), (1,)), ((), ()))


def whole(*shape):
    return pl.BlockSpec(shape, lambda *_: (0,) * len(shape))


def limit(mebibytes):
    return pltpu.CompilerParams(vmem_limit_bytes=mebibytes << 20)


HINT = pl.CostEstimate(flops=1, bytes_accessed=1, transcendentals=0)


def shaped(dtype, *shape):
    return jax.ShapeDtypeStruct(shape, dtype)


def first_bucket_of(offset):
    distance = jnp.abs(offset)
    count = jnp.where(offset > 0, 16, 0).astype(I32)
    for threshold in THRESHOLDS:
        count = count + jnp.where(distance >= threshold, 1, 0).astype(I32)
    return count


def second_bucket_of(across, upward):
    horizontal = jnp.zeros(across.shape, I32)
    for threshold in (-128, -32, -8, 0):
        horizontal = horizontal + jnp.where(across >= threshold, 1, 0)
    for threshold in (8, 32, 128):
        horizontal = horizontal + jnp.where(across > threshold, 1, 0)
    vertical = (
        jnp.where(upward >= -24, 8, 0)
        + jnp.where(upward >= 0, 8, 0)
        + jnp.where(upward > 24, 8, 0)
    )
    return vertical + horizontal


PLACE = ("heads", "core", "x", "y")


def bucket_kernel(place_ref, len_ref, box_ref, out_ref):
    filled = len_ref[place_ref[0]]
    boxes = box_ref[...].astype(F32)
    turned = jnp.transpose(jnp.concatenate([boxes] * 4, axis=0)).astype(I32)
    size = 64
    for step in range(L // size):
        rows = slice(step * size, (step + 1) * size)
        across = turned[rows, 0:1] - box_ref[0:1, :]
        upward = turned[rows, 1:2] - box_ref[1:2, :]
        key = lax.broadcasted_iota(I32, (size, L), 0) + step * size
        out_ref[rows, :] = jnp.where(key < filled, second_bucket_of(across, upward), 32)


def second_buckets(place, lengths, boxes):
    return pl.pallas_call(
        bucket_kernel,
        grid_spec=pltpu.PrefetchScalarGridSpec(
            num_scalar_prefetch=2,
            grid=(1,),
            in_specs=[pl.BlockSpec((2, L), lambda i, place, lengths: (0, place[0]))],
            out_specs=whole(L, L),
        ),
        out_shape=shaped(I32, L, L),
        name="second_buckets",
        compiler_params=limit(12),
        cost_estimate=HINT,
    )(place, lengths, boxes)


def lookup(table_row, index):
    table = jnp.broadcast_to(table_row, (index.shape[0], 128))
    return jnp.concatenate(
        [
            jnp.take_along_axis(
                table, index[:, c : c + 128], axis=1, mode="promise_in_bounds"
            )
            for c in range(0, index.shape[1], 128)
        ],
        axis=1,
    )


def head_window(head, width):
    start = head * HEAD_DIM // 128 * 128
    return start, min(128, width - start), head * HEAD_DIM - start


def eights(rows):
    return rows.reshape(rows.shape[0] // 8, 8, rows.shape[1])


def column(row):
    return jnp.transpose(jnp.broadcast_to(row, (8, row.shape[1])))[:, 0:1]


def forward_kernel(gathered, place_ref, x_ref, *refs):
    sources = refs[: 4 if gathered else 1]
    extra_ref, bucket_ref = refs[len(sources) : len(sources) + 2]
    rest = refs[len(sources) + 2 :]
    if gathered:
        w_ref, rest = rest[0], rest[1:]
    else:
        w_ref = sources[0]
    ctx_ref, turned_ref, raised_ref, qkv_ref, inverse_ref = rest[:5]
    index_sc, near_sc, score_sc, query_sc, key_sc = rest[5:10]
    heads = raised_ref.shape[1]
    width = heads * HEAD_DIM

    @pl.when(pl.program_id(0) == 0)
    def _():
        for d in range(-2, 3):
            offset = (
                128 * d
                + lax.broadcasted_iota(I32, (128, 128), 0)
                - lax.broadcasted_iota(I32, (128, 128), 1)
            )
            index_sc[d + 2] = first_bucket_of(offset)
        query_sc[...] = jnp.zeros_like(query_sc)

    if gathered:
        whole_sc = rest[10]
        core, here_x, here_y = place_ref[1], place_ref[2], place_ref[3]
        cut = sources[0].shape[3]
        size = cut + sources[1].shape[3]
        for far_y in range(2):
            for far_x in range(2):
                chip = (here_y ^ far_y) * 2 + (here_x ^ far_x)
                for side, pair in ((core, sources[:2]), (1 - core, sources[2:])):
                    at = (chip * 2 + side) * size
                    first = pl.multiple_of(at, 8)
                    whole_sc[pl.ds(first, cut), :] = pair[0][far_y, far_x, 0].astype(F32)
                    second = pl.multiple_of(at + cut, 8)
                    whole_sc[pl.ds(second, size - cut), :] = pair[1][far_x, far_y, 0].astype(F32)
        w_ref[0] = whole_sc[...].astype(BF)

    extra = extra_ref[0, 0:1, :].astype(F32)
    query_bias, value_bias = extra[:, 0:width], extra[:, width : 2 * width]
    first_tables = extra[:, 2 * width : 2 * width + 128]
    second_tables = extra[:, 2 * width + 128 : 2 * width + 256]
    query = lax.dot_general(w_ref[0, 0:width, :], x_ref[...], NT, preferred_element_type=F32)
    qkv_ref[0, 0:width, :] = (query + column(query_bias)).astype(BF)
    key = lax.dot_general(
        w_ref[0, width : 2 * width, :], x_ref[...], NT, preferred_element_type=F32
    )
    qkv_ref[0, width : 2 * width, :] = key.astype(BF)
    value = lax.dot_general(
        w_ref[0, 2 * width : 3 * width, :], x_ref[...], NT, preferred_element_type=F32
    )
    qkv_ref[0, 2 * width : 3 * width, :] = (value + column(value_bias)).astype(BF)
    key_sc[...] = lax.dot_general(
        x_ref[...], w_ref[0, width : 2 * width, :], NT, preferred_element_type=F32
    ).astype(BF)
    inverse_ref[0] = jnp.zeros_like(inverse_ref[0])
    lane = lax.broadcasted_iota(I32, (1, 128), 1)
    for h in range(heads):
        c0, w, low = head_window(h, width)
        own = slice(h * HEAD_DIM, (h + 1) * HEAD_DIM)
        query_sc[h, low : low + HEAD_DIM, :] = qkv_ref[0, own, :] * jnp.asarray(SCALE, BF)
        row = first_tables if h == 0 else jnp.roll(first_tables, -32 * h, axis=1)
        other = second_tables if h == 0 else jnp.roll(second_tables, -32 * h, axis=1)
        other = jnp.where(lane < 32, other, NEG)
        for d in range(5):
            near_sc[h, d] = lookup(row, index_sc[d])
        far = {
            -3: jnp.broadcast_to(row[:, 15:16], (KC, 128)),
            3: jnp.broadcast_to(row[:, 31:32], (KC, 128)),
        }
        key = key_sc[:, c0 : c0 + w]
        for block in range(L // QB):
            cols = slice(block * QB, (block + 1) * QB)
            score_sc[h] = jnp.dot(key, query_sc[h, 0:w, cols], preferred_element_type=F32)
            peak = None
            for step in range(L // KC):
                rows = slice(step * KC, (step + 1) * KC)
                d, inner = step * KC // 128 - block, step * KC % 128
                near = far[d] if abs(d) == 3 else near_sc[h, d + 2, inner : inner + KC, :]
                scores = score_sc[h, rows, :] + near
                scores = scores + lookup(other, bucket_ref[rows, cols])
                score_sc[h, rows, :] = scores
                part = jnp.max(eights(scores), axis=0)
                peak = part if peak is None else jnp.maximum(peak, part)
            peak = jnp.max(peak, axis=0, keepdims=True)
            sums = None
            for step in range(L // KC):
                rows = slice(step * KC, (step + 1) * KC)
                raised = jnp.exp(score_sc[h, rows, :] - peak)
                raised_ref[0, h, rows, cols] = raised.astype(BF)
                part = jnp.sum(eights(raised), axis=0)
                sums = part if sums is None else sums + part
            inverse_ref[0, h : h + 1, cols] = 1.0 / jnp.sum(sums, axis=0, keepdims=True)
        at = 2 * width + h * HEAD_DIM
        out = jnp.dot(
            qkv_ref[0, at : at + HEAD_DIM, :], raised_ref[0, h], preferred_element_type=F32
        )
        turned_ref[0, own, :] = (out * inverse_ref[0, h : h + 1, :]).astype(BF)
    ctx_ref[0] = jnp.transpose(turned_ref[0])


def each(*shape):
    return pl.BlockSpec((1,) + shape, lambda g, *_: (g,) + (0,) * len(shape))


def attend_forward(place, x, sources, extra, bucket):
    gathered = len(sources) == 4
    groups, depth = extra.shape[0], x.shape[1]
    if gathered:
        columns = 8 * (sources[0].shape[3] + sources[1].shape[3])
        inputs = [
            pl.BlockSpec(
                (2, 2, 1) + source.shape[3:], lambda g, place: (0, 0, g, 0, 0)
            )
            for source in sources
        ]
    else:
        columns = sources[0].shape[1]
        inputs = [each(columns, depth)]
    heads = columns // (3 * HEAD_DIM)
    width = columns // 3
    out_specs = [
        each(L, width), each(width, L), each(heads, L, L), each(columns, L), each(8, L)
    ]
    out_shape = [
        shaped(BF, groups, L, width),
        shaped(BF, groups, width, L),
        shaped(BF, groups, heads, L, L),
        shaped(BF, groups, columns, L),
        shaped(F32, groups, 8, L),
    ]
    scratch = [
        pltpu.VMEM((5, 128, 128), I32),
        pltpu.VMEM((heads, 5, 128, 128), F32),
        pltpu.VMEM((heads, L, QB), F32),
        pltpu.VMEM((heads, 128, L), BF),
        pltpu.VMEM((L, width), BF),
    ]
    if gathered:
        out_specs = [each(columns, depth)] + out_specs
        out_shape = [shaped(BF, groups, columns, depth)] + out_shape
        scratch = scratch + [pltpu.VMEM((columns, depth), F32)]
    return pl.pallas_call(
        functools.partial(forward_kernel, gathered),
        grid_spec=pltpu.PrefetchScalarGridSpec(
            num_scalar_prefetch=1,
            grid=(groups,),
            in_specs=[whole(L, depth)] + inputs + [each(8, depth), whole(L, L)],
            out_specs=out_specs,
            scratch_shapes=scratch,
        ),
        out_shape=out_shape,
        name="attend_forward",
        compiler_params=limit(22),
        cost_estimate=HINT,
    )(place, x, *sources, extra, bucket)


def backward_kernel(
    halved, place_ref, x_ref, w_ref, qkv_ref, raised_ref, inverse_ref, grad_ref, start_ref, *refs
):
    outs = refs[: 5 if halved else 4]
    dx_ref, ds_ref, sums_ref = outs[:3]
    pad_sc, term_sc, rows_sc, turn_sc, value_sc = refs[len(outs) : len(outs) + 5]
    group = pl.program_id(0)
    heads = raised_ref.shape[1]
    width = heads * HEAD_DIM

    @pl.when(group == 0)
    def _():
        pad_sc[...] = jnp.zeros_like(pad_sc)
        dx_ref[...] = start_ref[...]

    value_sc[...] = jnp.transpose(qkv_ref[0, 2 * width : 3 * width, :])
    for h in range(heads):
        c0, w, low = head_window(h, width)
        own = slice(h * HEAD_DIM, (h + 1) * HEAD_DIM)
        pad_sc[h, low : low + HEAD_DIM, :] = grad_ref[0, own, :]
        value = value_sc[:, c0 : c0 + w]
        for block in range(L // QB):
            cols = slice(block * QB, (block + 1) * QB)
            term_sc[h] = jnp.dot(value, pad_sc[h, 0:w, cols], preferred_element_type=F32)
            sums = None
            for step in range(L // KC):
                rows = slice(step * KC, (step + 1) * KC)
                terms = term_sc[h, rows, :] * raised_ref[0, h, rows, cols].astype(F32)
                term_sc[h, rows, :] = terms
                part = jnp.sum(eights(terms), axis=0)
                sums = part if sums is None else sums + part
            inner = jnp.sum(sums, axis=0, keepdims=True) * inverse_ref[0, h : h + 1, cols]
            for step in range(L // KC):
                rows = slice(step * KC, (step + 1) * KC)
                raised = raised_ref[0, h, rows, cols].astype(F32)
                ds_ref[0, h, rows, cols] = (term_sc[h, rows, :] - raised * inner).astype(BF)
        scale = jnp.asarray(SCALE, BF)
        at = width + h * HEAD_DIM
        turn_sc[own, :] = jnp.dot(
            qkv_ref[0, at : at + HEAD_DIM, :] * scale, ds_ref[0, h], preferred_element_type=F32
        ).astype(BF)
        dk = lax.dot_general(
            ds_ref[0, h], qkv_ref[0, c0 : c0 + w, :] * scale, NT, preferred_element_type=F32
        )
        rows_sc[:, at : at + HEAD_DIM] = dk[:, low : low + HEAD_DIM].astype(BF)
        dv = lax.dot_general(
            raised_ref[0, h], grad_ref[0, c0 : c0 + w, :], NT, preferred_element_type=F32
        )
        at = 2 * width + h * HEAD_DIM
        rows_sc[:, at : at + HEAD_DIM] = dv[:, low : low + HEAD_DIM].astype(BF)
    rows_sc[:, 0:width] = jnp.transpose(turn_sc[0:width, :])
    turn_sc[width:, :] = jnp.transpose(rows_sc[:, width:])
    weights = jnp.dot(turn_sc[...], x_ref[...], preferred_element_type=F32)
    if halved:
        sent_ref, kept_ref = outs[3:]
        all_sc = refs[len(outs) + 5]
        all_sc[...] = weights
        core = place_ref[1]
        chips, size = kept_ref.shape[1], kept_ref.shape[2]
        for chip in range(chips):
            for side, ref in ((1 - core, sent_ref), (core, kept_ref)):
                at = pl.multiple_of((chip * 2 + side) * size, 8)
                ref[0, chip] = all_sc[pl.ds(at, size), :].astype(BF)
    else:
        outs[3][0] = weights.astype(BF)
    dx_ref[...] += jnp.dot(rows_sc[...], w_ref[0], preferred_element_type=F32)
    sums_ref[0] = jnp.sum(rows_sc[...].astype(F32), axis=0, keepdims=True)


def attend_backward(place, halves, x, w, qkv, raised, inverse, grad, start, span=None):
    columns, depth = w.shape[1:]
    skip, stop = span or (0, w.shape[0])
    groups = stop - skip
    some = lambda *shape: pl.BlockSpec(
        (1,) + shape, lambda g, *_: (g + skip,) + (0,) * len(shape)
    )
    heads = columns // (3 * HEAD_DIM)
    width = columns // 3
    out_specs = [whole(L, depth), each(heads, L, L), each(1, columns)]
    out_shape = [
        shaped(F32, L, depth),
        shaped(BF, groups, heads, L, L),
        shaped(F32, groups, 1, columns),
    ]
    scratch = [
        pltpu.VMEM((heads, 128, L), BF),
        pltpu.VMEM((heads, L, QB), F32),
        pltpu.VMEM((L, columns), BF),
        pltpu.VMEM((columns, L), BF),
        pltpu.VMEM((L, width), BF),
    ]
    if halves:
        size = columns // (2 * halves)
        out_specs += [each(halves, size, depth)] * 2
        out_shape += [shaped(BF, groups, halves, size, depth)] * 2
        scratch += [pltpu.VMEM((columns, depth), F32)]
    else:
        out_specs += [each(columns, depth)]
        out_shape += [shaped(BF, groups, columns, depth)]
    return pl.pallas_call(
        functools.partial(backward_kernel, bool(halves)),
        grid_spec=pltpu.PrefetchScalarGridSpec(
            num_scalar_prefetch=1,
            grid=(groups,),
            in_specs=[
                whole(L, depth),
                some(columns, depth),
                some(columns, L),
                some(heads, L, L),
                some(8, L),
                some(width, L),
                whole(L, depth),
            ],
            out_specs=out_specs,
            scratch_shapes=scratch,
        ),
        out_shape=out_shape,
        name="attend_backward",
        compiler_params=limit(26),
        cost_estimate=HINT,
    )(place, x, w, qkv, raised, inverse, grad, start)


def table_kernel(count, *refs):
    sums = refs[count : 2 * count]
    bucket_ref, down_ref, up_ref, in_ref, out_ref, acc_sc, hot_sc = refs[2 * count :]
    step = pl.program_id(0)
    blocks = [
        (ref, g, h) for ref in refs[:count] for g in range(ref.shape[0]) for h in range(ref.shape[1])
    ]
    heads = len(blocks)
    half = 32 * 8

    @pl.when(step == 0)
    def _():
        acc_sc[...] = jnp.zeros_like(acc_sc)

    for u in range(RT // 8):
        part = slice(u * 8, (u + 1) * 8)
        second = bucket_ref[part, :]
        offset = (
            lax.broadcasted_iota(I32, (8, L), 0)
            + (step * RT + u * 8)
            - lax.broadcasted_iota(I32, (8, L), 1)
        )
        first = first_bucket_of(offset)
        for t in range(0, 32, 2):
            for base, bucket in ((0, first), (half, second)):
                hot_sc[base + t * 8 : base + (t + 2) * 8, :] = jnp.concatenate(
                    [jnp.where(bucket == t, 1.0, 0.0), jnp.where(bucket == t + 1, 1.0, 0.0)],
                    axis=0,
                ).astype(BF)
        left = jnp.concatenate([ref[g, h, part, :] for ref, g, h in blocks], axis=0)
        acc_sc[...] += lax.dot_general(left, hot_sc[...], NT, preferred_element_type=F32)

    @pl.when(step == pl.num_programs(0) - 1)
    def _():
        shape = (heads * 8, 2 * half)
        same = lax.broadcasted_iota(I32, shape, 0) % 8 == lax.broadcasted_iota(I32, shape, 1) % 8
        kept = jnp.where(same, acc_sc[...], 0.0)
        fold = (2 * half, 64)
        right = (
            lax.broadcasted_iota(I32, fold, 0) // 8 == lax.broadcasted_iota(I32, fold, 1)
        ).astype(F32)
        spread = (16, heads * 8)
        left = (
            lax.broadcasted_iota(I32, spread, 1) // 8 == lax.broadcasted_iota(I32, spread, 0)
        ).astype(F32)
        exact = lax.Precision.HIGHEST
        folded = jnp.dot(kept, right, preferred_element_type=F32, precision=exact)
        tables = jnp.dot(left, folded, preferred_element_type=F32, precision=exact)
        per = blocks[0][0].shape[1]
        wide = 2 * per * 32
        lanes = None
        for h in range(per):
            shape = (8, 16)
            rows = (
                lax.broadcasted_iota(I32, shape, 1) == lax.broadcasted_iota(I32, shape, 0) * per + h
            ).astype(F32)
            shape = (64, wide)
            source, target = lax.broadcasted_iota(I32, shape, 0), lax.broadcasted_iota(I32, shape, 1)
            moved = jnp.where(source < 32, source + h * 32, source + (per - 1 + h) * 32)
            part = jnp.dot(rows, tables, preferred_element_type=F32, precision=exact)
            part = jnp.dot(
                part, (target == moved).astype(F32), preferred_element_type=F32, precision=exact
            )
            lanes = part if lanes is None else lanes + part
        out_ref[...] = jnp.zeros_like(out_ref)
        out_ref[0:3, :] = down_ref[0:3, :]
        out_ref[3:6, :] = up_ref[0:3, :]
        width = out_ref.shape[1]
        deep = in_ref.shape[1] // width
        for n in range(deep):
            out_ref[6 + n : 7 + n, :] = in_ref[0:1, n * width : (n + 1) * width]
        group = 0
        for ref in sums:
            own = ref.shape[2] // 3
            for g in range(ref.shape[0]):
                row = slice(6 + deep + group, 7 + deep + group)
                out_ref[row, 0:own] = ref[g, :, 0:own]
                out_ref[row, own : 2 * own] = ref[g, :, 2 * own :]
                out_ref[row, 2 * own : 2 * own + wide] = lanes[group : group + 1, :]
                group += 1


def table_gradients(ds, sums, bucket, down, up, inner):
    heads = sum(item.shape[0] * item.shape[1] for item in ds)
    width = down.shape[1]
    rows = -(-(6 + inner.shape[1] // width + heads // ds[0].shape[1]) // 8) * 8
    return pl.pallas_call(
        functools.partial(table_kernel, len(ds)),
        grid=(L // RT,),
        in_specs=[
            pl.BlockSpec(item.shape[:2] + (RT, L), lambda r: (0, 0, r, 0)) for item in ds
        ]
        + [whole(*item.shape) for item in sums]
        + [pl.BlockSpec((RT, L), lambda r: (r, 0))]
        + [whole(*item.shape) for item in (down, up, inner)],
        out_specs=whole(rows, width),
        out_shape=shaped(F32, rows, width),
        scratch_shapes=[pltpu.VMEM((heads * 8, 512), F32), pltpu.VMEM((512, L), BF)],
        name="table_gradients",
        compiler_params=limit(14),
        cost_estimate=HINT,
    )(*ds, *sums, bucket, down, up, inner)


def mean_of(rows):
    return jnp.mean(rows, axis=-1, keepdims=True)


def normalize(rows):
    centred = rows - mean_of(rows)
    inverse = lax.rsqrt(mean_of(centred * centred) + EPS)
    return centred * inverse, inverse


def normalize_back(scaled, unit, inverse):
    return inverse * (scaled - mean_of(scaled) - unit * mean_of(scaled * unit))


def gelu_parts(values):
    size = jnp.abs(values)
    t = 1.0 / (1.0 + (0.3275911 * ROOT_HALF) * size)
    bell = jnp.exp(values * values * -0.5)
    series = 1.061405429
    for term in (-1.453152027, 1.421413741, -0.284496736, 0.254829592):
        series = term + t * series
    tail = (0.5 * t) * series * bell
    below = jnp.where(values >= 0, 1.0 - tail, tail)
    return values * below, below + values * (bell * DENSITY_SCALE)


def column_sum(rows):
    return jnp.sum(rows, axis=0, keepdims=True)


def up_kernel(
    place_ref, x_ref, ctx_own_ref, ctx_ref, wo_ref, bo_ref, g1_ref, s1_ref, wi_ref, bi_ref, wb_ref,
    bb_ref, g2_ref, s2_ref, cot_ref,
    out_ref, mid_ref, branch_ref, turned_ref, slope_ref, unit_ref, inverse_ref, low_ref, sums_ref,
    normed_sc, low_sc, acc_sc,
):
    step = pl.program_id(0)
    groups = wo_ref.shape[0]

    @pl.when(step == 0)
    def _():
        for r in range(L // MB):
            rows = slice(r * MB, (r + 1) * MB)
            total = x_ref[rows, :].astype(F32) + bo_ref[...]
            for s in range(groups):
                ctx = ctx_own_ref[0, rows, :] if s == 0 else ctx_ref[s - 1, rows, :]
                quarter = place_ref[0] ^ s
                total = total + jnp.dot(ctx, wo_ref[quarter], preferred_element_type=F32)
            unit, inverse = normalize(total)
            unit_ref[rows, :] = unit
            inverse_ref[rows, :] = jnp.broadcast_to(inverse, (MB, 128))
            normed = unit * g1_ref[...] + s1_ref[...]
            normed_sc[rows, :] = normed
            low_sc[rows, :] = normed.astype(BF)
        low_ref[...] = jnp.transpose(low_sc[...])
        acc_sc[...] = jnp.zeros_like(acc_sc)

    for r in range(L // MB):
        rows = slice(r * MB, (r + 1) * MB)
        pre = jnp.dot(low_sc[rows, :], wi_ref[...], preferred_element_type=F32) + bi_ref[...]
        acted, slope = gelu_parts(pre)
        acted = acted.astype(BF)
        slope_ref[rows, :] = slope.astype(BF)
        turned_ref[:, rows] = jnp.transpose(acted)
        acc_sc[rows, :] += jnp.dot(acted, wb_ref[...], preferred_element_type=F32)

    @pl.when(step == pl.num_programs(0) - 1)
    def _():
        gain_sum = shift_sum = bias_sum = None
        for r in range(L // MB):
            rows = slice(r * MB, (r + 1) * MB)
            unit, inverse = normalize(normed_sc[rows, :] + (acc_sc[rows, :] + bb_ref[...]))
            out_ref[rows, :] = (unit * g2_ref[...] + s2_ref[...]).astype(BF)
            upstream = cot_ref[rows, :].astype(F32)
            middle = normalize_back(upstream * g2_ref[...], unit, inverse)
            mid_ref[rows, :] = middle
            branch = middle.astype(BF)
            branch_ref[rows, :] = branch
            parts = (
                column_sum(upstream * unit),
                column_sum(upstream),
                column_sum(branch.astype(F32)),
            )
            gain_sum = parts[0] if r == 0 else gain_sum + parts[0]
            shift_sum = parts[1] if r == 0 else shift_sum + parts[1]
            bias_sum = parts[2] if r == 0 else bias_sum + parts[2]
        sums_ref[0:1, :] = gain_sum
        sums_ref[1:2, :] = shift_sum
        sums_ref[2:3, :] = bias_sum


def feed_up(place, x, ctx_own, ctx, w_out, bo, g1, s1, w_in, bi, w_back, bb, g2, s2, cot):
    width = x.shape[1]
    units = w_in.shape[1]
    groups, own = w_out.shape[0], w_out.shape[1]
    row = whole(1, width)
    return pl.pallas_call(
        up_kernel,
        grid_spec=pltpu.PrefetchScalarGridSpec(
            num_scalar_prefetch=1,
            grid=(units // FC,),
            in_specs=[
                whole(L, width),
                whole(1, L, own),
                whole(groups - 1, L, own),
                whole(groups, own, width),
                row,
                row,
                row,
                pl.BlockSpec((width, FC), lambda n, place: (0, n)),
                pl.BlockSpec((1, FC), lambda n, place: (0, n)),
                pl.BlockSpec((FC, width), lambda n, place: (n, 0)),
                row,
                row,
                row,
                whole(L, width),
            ],
            out_specs=[
                whole(L, width),
                whole(L, width),
                whole(L, width),
                pl.BlockSpec((FC, L), lambda n, place: (n, 0)),
                pl.BlockSpec((L, FC), lambda n, place: (0, n)),
                whole(L, width),
                whole(L, 128),
                whole(width, L),
                whole(8, width),
            ],
            scratch_shapes=[
                pltpu.VMEM((L, width), F32),
                pltpu.VMEM((L, width), BF),
                pltpu.VMEM((L, width), F32),
            ],
        ),
        out_shape=[
            shaped(BF, L, width),
            shaped(F32, L, width),
            shaped(BF, L, width),
            shaped(BF, units, L),
            shaped(BF, L, units),
            shaped(F32, L, width),
            shaped(F32, L, 128),
            shaped(BF, width, L),
            shaped(F32, 8, width),
        ],
        name="feed_up",
        compiler_params=limit(32),
        cost_estimate=HINT,
    )(place, x, ctx_own, ctx, w_out, bo, g1, s1, w_in, bi, w_back, bb, g2, s2, cot)


def down_kernel(
    halved, place_ref, branch_ref, slope_ref, wb_ref, wi_ref, low_ref, mid_ref, unit_ref,
    inverse_ref, g1_ref, wo_ref, turned_own_ref, turned_ref, norm_own_ref, norm_ref, *refs
):
    bias_ref, first_ref, grad_own_ref, grad_ref, sums_ref = refs[:5]
    weight_refs = refs[5 : 7 if halved else 6]
    acc_sc, pre_sc, weight_sc = refs[-3:]
    step = pl.program_id(0)
    last = pl.num_programs(0) - 1
    groups, own = wo_ref.shape[0], wo_ref.shape[1]

    def give():
        if not halved:
            weight_refs[0][...] = weight_sc[...]
            return
        core = place_ref[1]
        chips, size = weight_refs[0].shape[0], weight_refs[0].shape[1]
        for chip in range(chips):
            for side, ref in ((1 - core, weight_refs[0]), (core, weight_refs[1])):
                at = pl.multiple_of((chip * 2 + side) * size, size)
                ref[chip] = weight_sc[pl.ds(at, size), :]

    @pl.when(step == 0)
    def _():
        acc_sc[...] = mid_ref[...]

    @pl.when(step < last)
    def _():
        total = None
        for r in range(L // MB):
            rows = slice(r * MB, (r + 1) * MB)
            pre = lax.dot_general(
                branch_ref[rows, :], wb_ref[...], NT, preferred_element_type=F32
            ) * slope_ref[rows, :].astype(F32)
            pre = pre.astype(BF)
            pre_sc[rows, :] = pre
            part = column_sum(pre.astype(F32))
            total = part if r == 0 else total + part
            acc_sc[rows, :] += lax.dot_general(
                pre, wi_ref[...], NT, preferred_element_type=F32
            )
        bias_ref[0:1, :] = total
        weight_sc[...] = jnp.dot(
            low_ref[...], pre_sc[...], preferred_element_type=F32
        ).astype(BF)
        give()

    @pl.when(step == last)
    def _():
        gain_sum = shift_sum = bias_sum = None
        for r in range(L // MB):
            rows = slice(r * MB, (r + 1) * MB)
            hidden = acc_sc[rows, :]
            unit = unit_ref[rows, :]
            first = normalize_back(hidden * g1_ref[...], unit, inverse_ref[rows, 0:1])
            first_ref[rows, :] = first
            attended = first.astype(BF)
            pre_sc[rows, :] = attended
            parts = (
                column_sum(hidden * unit),
                column_sum(hidden),
                column_sum(attended.astype(F32)),
            )
            gain_sum = parts[0] if r == 0 else gain_sum + parts[0]
            shift_sum = parts[1] if r == 0 else shift_sum + parts[1]
            bias_sum = parts[2] if r == 0 else bias_sum + parts[2]
        sums_ref[0:1, :] = gain_sum
        sums_ref[1:2, :] = shift_sum
        sums_ref[2:3, :] = bias_sum
        for s in range(groups):
            quarter = place_ref[0] ^ s
            turned = turned_own_ref[0] if s == 0 else turned_ref[s - 1]
            norm = norm_own_ref[0] if s == 0 else norm_ref[s - 1]
            at = pl.multiple_of(quarter * own, own)
            weight_sc[pl.ds(at, own), :] = jnp.dot(
                turned, pre_sc[...], preferred_element_type=F32
            ).astype(BF)
            grads = lax.dot_general(
                wo_ref[quarter], pre_sc[...], NT, preferred_element_type=F32
            )
            for h in range(own // HEAD_DIM):
                rows = slice(h * HEAD_DIM, (h + 1) * HEAD_DIM)
                scaled = (grads[rows, :] * norm[h : h + 1, :]).astype(BF)
                if s == 0:
                    grad_own_ref[0, rows, :] = scaled
                else:
                    grad_ref[s - 1, rows, :] = scaled
        give()


def feed_down(place, halves, branch, slope, w_back, w_in, low, mid, unit, inverse, g1, w_out,
              turned_own, turned, norm_own, norm):
    width = branch.shape[1]
    units = w_in.shape[1]
    groups, own = w_out.shape[0], w_out.shape[1]
    steps = units // FC
    inside = lambda n: jnp.minimum(n, steps - 1)
    out_specs = [
        pl.BlockSpec((8, FC), lambda n, place: (0, inside(n))),
        whole(L, width),
        whole(1, own, L),
        whole(groups - 1, own, L),
        whole(8, width),
    ]
    out_shape = [
        shaped(F32, 8, units),
        shaped(F32, L, width),
        shaped(BF, 1, own, L),
        shaped(BF, groups - 1, own, L),
        shaped(F32, 8, width),
    ]
    if halves:
        size = width // (2 * halves)
        out_specs += [pl.BlockSpec((halves, size, FC), lambda n, place: (0, 0, n))] * 2
        out_shape += [shaped(BF, halves, size, units + width)] * 2
    else:
        out_specs += [pl.BlockSpec((width, FC), lambda n, place: (0, n))]
        out_shape += [shaped(BF, width, units + width)]
    return pl.pallas_call(
        functools.partial(down_kernel, bool(halves)),
        grid_spec=pltpu.PrefetchScalarGridSpec(
            num_scalar_prefetch=1,
            grid=(steps + 1,),
            in_specs=[
                whole(L, width),
                pl.BlockSpec((L, FC), lambda n, place: (0, inside(n))),
                pl.BlockSpec((FC, width), lambda n, place: (inside(n), 0)),
                pl.BlockSpec((width, FC), lambda n, place: (0, inside(n))),
                whole(width, L),
                whole(L, width),
                whole(L, width),
                whole(L, 128),
                whole(1, width),
                whole(groups, own, width),
                whole(1, own, L),
                whole(groups - 1, own, L),
                whole(1, 8, L),
                whole(groups - 1, 8, L),
            ],
            out_specs=out_specs,
            scratch_shapes=[
                pltpu.VMEM((L, width), F32),
                pltpu.VMEM((L, FC), BF),
                pltpu.VMEM((width, FC), BF),
            ],
        ),
        out_shape=out_shape,
        name="feed_down",
        compiler_params=limit(34),
        cost_estimate=HINT,
    )(place, branch, slope, w_back, w_in, low, mid, unit, inverse, g1, w_out,
      turned_own, turned, norm_own, norm)


def product_kernel(place_ref, left_ref, right_ref, out_ref):
    out_ref[...] = jnp.dot(
        left_ref[...], right_ref[...], preferred_element_type=F32
    ).astype(BF)


def product(place, left, right, sizes):
    rows, depth = left.shape
    columns = right.shape[1]
    count, size, halved = sizes
    take = (lambda n, place: (2 * n + 1 - place[1], 0)) if halved else (lambda n, place: (n, 0))
    return pl.pallas_call(
        product_kernel,
        grid_spec=pltpu.PrefetchScalarGridSpec(
            num_scalar_prefetch=1,
            grid=(count,),
            in_specs=[pl.BlockSpec((size, depth), take), whole(depth, columns)],
            out_specs=pl.BlockSpec((size, columns), lambda n, place: (n, 0)),
        ),
        out_shape=shaped(BF, count * size, columns),
        name="back_weights",
        compiler_params=limit(10),
        cost_estimate=HINT,
    )(place, left, right)


def kept_kernel(place_ref, left_ref, right_ref, got_ref, a_sent, a_kept, b_sent, b_kept):
    chip = pl.program_id(0)
    chip_y, chip_x = chip // 2, lax.rem(chip, 2)
    here_x, here_y = place_ref[2], place_ref[3]
    value = jnp.dot(left_ref[...], right_ref[...], preferred_element_type=F32)
    value = (value + got_ref[0].astype(F32)).astype(BF)
    cut = a_sent.shape[1]

    @pl.when(chip_x == here_x)
    def _():
        a_kept[chip_y] = value[:cut, :]

    @pl.when(chip_x != here_x)
    def _():
        a_sent[chip_y] = value[:cut, :]

    @pl.when(chip_y == here_y)
    def _():
        b_kept[chip_x] = value[cut:, :]

    @pl.when(chip_y != here_y)
    def _():
        b_sent[chip_x] = value[cut:, :]


def product_kept(place, left, right, got):
    chips, size, columns = got.shape
    depth = left.shape[1]
    part = whole(2, size // 2, columns)
    return pl.pallas_call(
        kept_kernel,
        grid_spec=pltpu.PrefetchScalarGridSpec(
            num_scalar_prefetch=1,
            grid=(chips,),
            in_specs=[
                pl.BlockSpec((size, depth), lambda n, place: (2 * n + place[1], 0)),
                whole(depth, columns),
                pl.BlockSpec((1, size, columns), lambda n, place: (n, 0, 0)),
            ],
            out_specs=[part] * 4,
        ),
        out_shape=[shaped(BF, 2, size // 2, columns)] * 4,
        name="kept_weights",
        compiler_params=limit(14),
        cost_estimate=HINT,
    )(place, left, right, got)


def total_of(*items):
    total = items[0].astype(F32)
    for item in items[1:]:
        total = total + item.astype(F32)
    return total.astype(BF)


def chips_kernel(count, layout, place_ref, *refs):
    inputs, outs = refs[:count], refs[count:]
    here_x, here_y = place_ref[2], place_ref[3]
    for order, (way, sources) in enumerate(layout):
        sent, kept = outs[2 * order], outs[2 * order + 1]
        start = 0
        for number, low, high in sources:
            kept_ref, got_ref = inputs[2 * number], inputs[2 * number + 1]
            for g in range(kept_ref.shape[0]):
                rows = slice(start, start + high - low)
                start += high - low
                for other in range(2):
                    for out, far in ((sent, 1), (kept, 0)):
                        if way == "x":
                            chip = other * 2 + (here_x ^ far)
                        else:
                            chip = (here_y ^ far) * 2 + other
                        out[other, rows, :] = total_of(
                            kept_ref[g, chip, low:high, :], got_ref[g, chip, low:high, :]
                        )


def sum_chips(place, pairs, parts, block):
    specs, out_specs, out_shape = [], [], []
    columns = pairs[0][0].shape[-1]
    for kept, _ in pairs:
        shape = kept.shape[:3] + (block,)
        specs += [pl.BlockSpec(shape, lambda n, place: (0, 0, 0, n))] * 2
    for _, sources in parts:
        height = sum(pairs[n][0].shape[0] * (high - low) for n, low, high in sources)
        out_specs += [pl.BlockSpec((2, height, block), lambda n, place: (0, 0, n))] * 2
        out_shape += [shaped(BF, 2, height, columns)] * 2
    return pl.pallas_call(
        functools.partial(chips_kernel, 2 * len(pairs), parts),
        grid_spec=pltpu.PrefetchScalarGridSpec(
            num_scalar_prefetch=1, grid=(columns // block,), in_specs=specs, out_specs=out_specs
        ),
        out_shape=out_shape,
        name="sum_chips",
        compiler_params=limit(14),
        cost_estimate=HINT,
    )(place, *[item for pair in pairs for item in pair])


def pairs_kernel(place_ref, a_kept, a_got, b_kept, b_got, a_sent, a_own, b_sent, b_own):
    here_x, here_y = place_ref[2], place_ref[3]
    for here, kept, got, sent, own in (
        (here_y, a_kept, a_got, a_sent, a_own),
        (here_x, b_kept, b_got, b_sent, b_own),
    ):
        sent[...] = total_of(kept[1 - here], got[1 - here])
        own[...] = total_of(kept[here], got[here])


def sum_pairs(place, a_kept, a_got, b_kept, b_got, block):
    columns = a_kept.shape[-1]
    spec = lambda item: pl.BlockSpec((2, item.shape[1], block), lambda n, place: (0, 0, n))
    flat = lambda item: pl.BlockSpec((item.shape[1], block), lambda n, place: (0, n))
    return pl.pallas_call(
        pairs_kernel,
        grid_spec=pltpu.PrefetchScalarGridSpec(
            num_scalar_prefetch=1,
            grid=(columns // block,),
            in_specs=[spec(a_kept), spec(a_got), spec(b_kept), spec(b_got)],
            out_specs=[flat(a_kept)] * 2 + [flat(b_kept)] * 2,
        ),
        out_shape=[shaped(BF, a_kept.shape[1], columns)] * 2
        + [shaped(BF, b_kept.shape[1], columns)] * 2,
        name="sum_pairs",
        compiler_params=limit(12),
        cost_estimate=HINT,
    )(place, a_kept, a_got, b_kept, b_got)


def cut_kernel(place_ref, a_kept, a_got, b_kept, b_got, sent, kept, sum_sc):
    cut = a_kept.shape[0]
    sum_sc[0:cut, :] = a_kept[...].astype(F32) + a_got[...].astype(F32)
    sum_sc[cut:, :] = b_kept[...].astype(F32) + b_got[...].astype(F32)
    size = kept.shape[1]
    for s, out in ((0, kept.at[0]), (1, sent.at[0]), (2, kept.at[1]), (3, sent.at[1])):
        at = pl.multiple_of((place_ref[0] ^ s) * size, 8)
        out[...] = sum_sc[pl.ds(at, size), :].astype(BF)


def cut_quarters(place, a_kept, a_got, b_kept, b_got, block):
    columns = a_kept.shape[-1]
    height = a_kept.shape[0] + b_kept.shape[0]
    spec = lambda item: pl.BlockSpec((item.shape[0], block), lambda n, place: (0, n))
    return pl.pallas_call(
        cut_kernel,
        grid_spec=pltpu.PrefetchScalarGridSpec(
            num_scalar_prefetch=1,
            grid=(columns // block,),
            in_specs=[spec(a_kept), spec(a_got), spec(b_kept), spec(b_got)],
            out_specs=[pl.BlockSpec((2, height // 4, block), lambda n, place: (0, 0, n))] * 2,
            scratch_shapes=[pltpu.VMEM((height, block), F32)],
        ),
        out_shape=[shaped(BF, 2, height // 4, columns)] * 2,
        name="cut_quarters",
        compiler_params=limit(12),
        cost_estimate=HINT,
    )(place, a_kept, a_got, b_kept, b_got)


def last_kernel(a_kept, a_got, b_kept, b_got, short_ref, *outs):
    size = outs[0].shape[0] - 16
    many = short_ref.shape[0] // 8 * 8
    first = 10
    for s, out in enumerate(outs):
        if s < 3:
            rows = slice(s * size, (s + 1) * size)
            out[0:size, :] = total_of(a_kept[rows, :], a_got[rows, :])
        else:
            out[0:size, :] = total_of(b_kept[...], b_got[...])
        row = lax.broadcasted_iota(I32, (many, short_ref.shape[1]), 0)
        short = jnp.where(row < first, short_ref[...], 0.0)
        short = short + jnp.where(row == first, short_ref[first + s : first + s + 1, :], 0.0)
        out[size : size + many, :] = short.astype(BF)


def cut_last(a_kept, a_got, b_kept, b_got, short):
    vmem = pl.BlockSpec(memory_space=pltpu.VMEM)
    size, columns = b_kept.shape
    return pl.pallas_call(
        last_kernel,
        in_specs=[vmem] * 5,
        out_specs=[vmem] * 4,
        out_shape=[shaped(BF, size + 16, columns)] * 4,
        name="cut_last",
        compiler_params=limit(8),
        cost_estimate=HINT,
    )(a_kept, a_got, b_kept, b_got, short)


def join_kernel(place_ref, own, one, two, *outs):
    size = own.shape[0]
    start = 0
    for out in outs:
        lanes = slice(start, start + out.shape[1])
        for s, piece in ((0, own[:, lanes]), (2, one[:, lanes]), (1, two[0, :, lanes]), (3, two[1, :, lanes])):
            at = pl.multiple_of((place_ref[0] ^ s) * size, 8)
            out[pl.ds(at, size), :] = piece.astype(F32)
        start += out.shape[1]


def join_quarters(place, own, one, two, widths):
    vmem = pl.BlockSpec(memory_space=pltpu.VMEM)
    return pl.pallas_call(
        join_kernel,
        in_specs=[pl.BlockSpec(memory_space=pltpu.SMEM)] + [vmem] * 3,
        out_specs=[vmem] * len(widths),
        out_shape=[shaped(F32, 4 * own.shape[0], width) for width in widths],
        name="join_quarters",
        compiler_params=limit(8),
        cost_estimate=HINT,
    )(place, own, one, two)


def chips_join_kernel(place_ref, mine_a, mine_b, got_a, got_b, out_ref):
    core, here_x, here_y = place_ref[1], place_ref[2], place_ref[3]
    cut = mine_a.shape[2]
    size = cut + mine_b.shape[2]
    for far_y in range(2):
        for far_x in range(2):
            chip = (here_y ^ far_y) * 2 + (here_x ^ far_x)
            for side, a_ref, b_ref in ((core, mine_a, mine_b), (1 - core, got_a, got_b)):
                at = (chip * 2 + side) * size
                first = pl.multiple_of(at, 8)
                out_ref[pl.ds(first, cut), :] = a_ref[far_y, far_x].astype(F32)
                second = pl.multiple_of(at + cut, 8)
                out_ref[pl.ds(second, size - cut), :] = b_ref[far_x, far_y].astype(F32)


def join_chips(place, mine_a, mine_b, got_a, got_b):
    vmem = pl.BlockSpec(memory_space=pltpu.VMEM)
    rows = 8 * (mine_a.shape[2] + mine_b.shape[2])
    return pl.pallas_call(
        chips_join_kernel,
        in_specs=[pl.BlockSpec(memory_space=pltpu.SMEM)] + [vmem] * 4,
        out_specs=vmem,
        out_shape=shaped(F32, rows, mine_a.shape[-1]),
        name="join_chips",
        compiler_params=limit(8),
        cost_estimate=HINT,
    )(place, mine_a, mine_b, got_a, got_b)


def tie(values, *others):
    return lax.optimization_barrier((values, others))[0]


def swap(array, bit):
    count = lax.axis_size("docs")
    return lax.ppermute(array, "docs", [(i, i ^ (1 << bit)) for i in range(count)])


def away(array, distance):
    count = lax.axis_size("heads")
    return lax.ppermute(array, "heads", [(i, i ^ distance) for i in range(count)])


def in_order(pieces, z):
    stacked = jnp.stack(pieces)
    picks = [lax.dynamic_index_in_dim(stacked, z ^ s, 0) for s in range(len(pieces))]
    return jnp.concatenate(picks, axis=0)


def tree(items):
    while len(items) > 1:
        items = [items[n] + items[n + 1] for n in range(0, len(items), 2)]
    return items[0]


def sum_everywhere(rows):
    for bit in range(lax.axis_size("docs").bit_length() - 1):
        rows = rows + swap(rows, bit)
    return tree([rows] + [away(rows, s) for s in range(1, lax.axis_size("heads"))])


def spread_plane(first, second):
    got = [swap(first, 1), swap(second, 2)]
    first, second = jnp.stack([first, got[0]]), jnp.stack([second, got[1]])
    got = [swap(first, 2), swap(second, 1)]
    return jnp.stack([first, got[0]]), jnp.stack([second, got[1]])


def reduce_docs(blocks):
    bits = blocks.shape[0].bit_length() - 1
    docs = lax.axis_index("docs")
    current = blocks.reshape((2,) * bits + blocks.shape[1:])
    for bit in range(bits):
        mine = (docs >> bit) & 1
        axis = bits - 1 - bit
        sent = lax.dynamic_index_in_dim(current, 1 - mine, axis, keepdims=False)
        kept = lax.dynamic_index_in_dim(current, mine, axis, keepdims=False)
        current = total_of(kept, swap(sent, bit))
    return current


def spread_docs(block):
    count = lax.axis_size("docs")
    docs = lax.axis_index("docs")
    current = block
    for done, bit in enumerate(range(count.bit_length() - 2, -1, -1)):
        got = swap(current, bit)
        mine = ((docs >> bit) & 1) == 1
        current = jnp.stack(
            [jnp.where(mine, got, current), jnp.where(mine, current, got)], axis=done
        )
    return current.reshape((count,) + block.shape)


def body(
    layer_input, token_boxes, lengths, w_qkv, qv_bias, rel_tables, w_out, out_bias,
    gain_one, shift_one, w_in, in_bias, w_back, back_bias, gain_two, shift_two, cotangent,
):
    width = layer_input.shape[1]
    units = w_in.shape[1]
    groups = lax.axis_size("heads")
    count = lax.axis_size("docs")
    docs = lax.axis_index("docs")
    z = lax.axis_index("heads")
    own = w_qkv.shape[2]
    heads = rel_tables.shape[1]
    buckets = rel_tables.shape[2]
    columns = 3 * own
    share = width // count
    small = columns // count
    chips = 4 if count == 8 and share % 16 == 0 and small % 8 == 0 else 0
    place = jnp.stack([z, docs & 1, (docs >> 1) & 1, (docs >> 2) & 1]).astype(I32)

    matrix = w_qkv.transpose(1, 2, 0).reshape(columns, width)
    room = jnp.zeros((128 - heads * buckets,), BF)
    line = jnp.concatenate(
        [qv_bias[0], qv_bias[1], rel_tables[0].reshape(-1), room, rel_tables[1].reshape(-1), room]
    )
    extra = jnp.pad(line[None], ((0, 7), (0, width - line.shape[0])))
    piece = jnp.concatenate(
        [lax.dynamic_slice_in_dim(matrix, docs * small, small, axis=0), extra], axis=0
    )
    got = [away(piece, s) for s in range(1, groups)]
    bucket = second_buckets(place, lengths, token_boxes)

    ctx_own, turned_own, raised_own, qkv_own, norm_own = attend_forward(
        place, layer_input, (matrix[None],), extra[None], bucket
    )
    arrived = jnp.stack(tie(got, ctx_own))
    if chips:
        cut = (small // 2 + 7) // 8 * 8
        first, second = spread_plane(arrived[:, :cut], arrived[:, cut:small])
        weights, ctx, turned, raised, qkv, norm = attend_forward(
            place, layer_input, (first, second, swap(first, 0), swap(second, 0)),
            arrived[:, small:], bucket,
        )
    else:
        weights = spread_docs(arrived[:, :small]).transpose(1, 0, 2, 3)
        weights = weights.reshape(groups - 1, columns, width)
        ctx, turned, raised, qkv, norm = attend_forward(
            place, layer_input, (weights,), arrived[:, small:], bucket
        )

    w_out_heads = w_out.reshape(groups, own, width)
    flat = lambda vector: vector.reshape(1, -1)
    layer_output, grad_mid, grad_branch, acted, slope, unit, inverse, low, up_sums = feed_up(
        place, layer_input, ctx_own, ctx, w_out_heads, flat(out_bias), flat(gain_one),
        flat(shift_one), w_in, flat(in_bias), w_back, flat(back_bias), flat(gain_two),
        flat(shift_two), cotangent,
    )
    down = lambda branch: feed_down(
        place, chips, branch, slope, w_back, w_in, low, grad_mid, unit, inverse, flat(gain_one),
        w_out_heads, turned_own, turned, norm_own, norm,
    )
    own_back = lambda grad, start: attend_backward(
        place, chips, layer_input, matrix[None], qkv_own, raised_own, norm_own, grad, start
    )
    rest_back = lambda span, grad, start: attend_backward(
        place, chips, layer_input, weights, qkv, raised, norm, grad, start, span
    )

    if chips:
        half = share // 2
        back_size = units // count
        sent = product(place, acted, grad_branch, (chips, back_size, True))
        got = swap(sent.reshape(chips, back_size, width), 0)
        back = product_kept(place, acted, grad_branch, got)
        back_got = [swap(back[0], 1), swap(back[2], 2)]

        in_sums, grad_first, grad_own, grad_rest, down_sums, dense_sent, dense_kept = down(
            tie(grad_branch, back[0], back[2])
        )
        back_got = tie(back_got, grad_first)
        back = sum_pairs(place, back[1], back_got[0], back[3], back_got[1], width // 2)
        back_got = [swap(back[0], 2), swap(back[2], 1)]
        dense_sent = tie(dense_sent, back[0])
        dense_got = swap(dense_sent, 0)

        dx, ds_own, sums_own, own_sent, own_kept = own_back(
            tie(grad_own, dense_sent, back[0], back[2]), grad_first
        )
        dense_got = tie(dense_got, dx)
        dense = sum_chips(
            place,
            [(dense_kept[None], dense_got[None])],
            (("x", ((0, 0, half),)), ("y", ((0, half, share),))),
            (units + width) // 3,
        )
        dense_got = [swap(dense[0], 1), swap(dense[2], 2)]
        own_sent = tie(own_sent, dense[0])
        own_got = swap(own_sent, 0)

        dx, ds_one, sums_one, one_sent, one_kept = rest_back(
            (0, 1), tie(grad_rest, dense[0], dense[2], own_sent), dx
        )
        back_got, own_got = tie((back_got, own_got), dx)
        back_sent, back = cut_quarters(
            place, back[1], back_got[0], back[3], back_got[1], width // 2
        )
        back_got = away(back_sent, 1)
        one_sent = tie(one_sent, back)
        one_got = swap(one_sent, 0)

        dx, ds_two, sums_two, two_sent, two_kept = rest_back(
            (1, 2), tie(grad_rest, back_sent, one_sent), dx
        )
        one_got, two_sent = tie((one_got, two_sent), dx)
        two_got = swap(two_sent, 0)

        dx, ds_three, sums_three, three_sent, three_kept = rest_back(
            (2, 3), tie(grad_rest, two_sent), dx
        )
        dense_got, back_got, two_got = tie((dense_got, back_got, two_got), dx)
        last_a = list(
            sum_chips(
                place,
                [(own_kept, own_got), (one_kept, one_got), (two_kept, two_got)],
                (("x", ((0, 0, small), (1, 0, small), (2, 0, small))),), width // 2,
            )
        )
        dense = list(
            sum_pairs(
                place, dense[1], dense_got[0], dense[3], dense_got[1], (units + width) // 2
            )
        )
        back = total_of(back, back_got)
        last_a[0], dense[0], dense[2], back, three_sent = tie(
            (last_a[0], dense[0], dense[2], back, three_sent), last_a[1], dense[1]
        )
        three_got = swap(three_sent, 0)
        last_a_got = swap(last_a[0], 1)
        dense_got = [swap(dense[0], 2), swap(dense[2], 1)]
        back_got = away(back[1], 2)
        last_b = sum_chips(
            place, [(three_kept, tie(three_got, last_a[0]))], (("y", ((0, 0, small),)),), width // 2
        )
        last_b_got = swap(last_b[0], 2)

        short = table_gradients(
            (ds_own, ds_one, ds_two, ds_three), (sums_own, sums_one, sums_two, sums_three),
            tie(bucket, last_b[0], last_a[0], back, dense[0], dense[2]), down_sums, up_sums, in_sums,
        )
        last_a_got, last_b_got, dense_got, back_got = tie(
            (last_a_got, last_b_got, dense_got, back_got), short
        )
        last = list(sum_pairs(place, last_a[1], last_a_got, last_b[1], last_b_got, width // 2))
        last_got = [swap(last[0], 2), swap(last[2], 1)]
        dense_got, back_got = tie((dense_got, back_got), last[0])
        dense_sent, dense = cut_quarters(
            place, dense[1], dense_got[0], dense[3], dense_got[1], (units + width) // 2
        )
        dense_got = away(dense_sent, 1)
        back = total_of(back[0], back_got)
        back_one = away(back, 2)
        last_got = tie(last_got, dense_sent, back)
        last = cut_last(last[1], last_got[0], last[3], last_got[1], short)
        last_got = [away(last[s], s) for s in range(1, groups)]
        dense_got, back_one = tie((dense_got, back_one), last[0])
        dense = total_of(dense, dense_got)
        dense_got = away(dense[1], 2)
        back_two = away(jnp.stack([back, back_one]), 1)
        last_got = tie(last_got, dense, back_one)
        quarter = total_of(last[0][:small], *[item[:small] for item in last_got])
        ends = tree([item[small:].astype(F32) for item in [last[0]] + last_got]).astype(BF)
        first, second = quarter[:cut], quarter[cut:]
        got = [swap(first, 1), swap(second, 2), swap(ends, 1)]
        back_two, dense_got = tie((back_two, dense_got), first, second)
        (out_back,) = join_quarters(place, back, back_one, back_two, (width,))
        dense = total_of(dense[0], dense_got)
        dense_one = away(dense, 2)
        got = tie(got, out_back, dense)
        first, second = jnp.stack([first, got[0]]), jnp.stack([second, got[1]])
        ends = total_of(ends, got[2])
        got = [swap(first, 2), swap(second, 1), swap(ends, 2)]
        dense_one = tie(dense_one, first, second)
        dense_two = away(jnp.stack([dense, dense_one]), 1)
        got = tie(got, dense_one)
        first, second = jnp.stack([first, got[0]]), jnp.stack([second, got[1]])
        ends = total_of(ends, got[2])
        got = [swap(first, 0), swap(second, 0), swap(ends, 0)]
        dense_two = tie(dense_two, first, second)
        out_in, out_out = join_quarters(place, dense, dense_one, dense_two, (units, width))
        got = tie(got, out_in)
        full = join_chips(place, first, second, got[0], got[1])
        total = ends.astype(F32) + got[2].astype(F32)
        ends = total[6 + units // width]
    else:
        back_grads = product(place, acted, grad_branch, (units // FC, FC, False))
        in_sums, grad_first, grad_own, grad_rest, down_sums, dense_grads = down(grad_branch)
        dx, ds_own, sums_own, dw_own = own_back(grad_own, grad_first)
        dx, ds_rest, sums_rest, dw_rest = rest_back(None, grad_rest, dx)
        short = table_gradients(
            (ds_own, ds_rest), (sums_own, sums_rest), bucket, down_sums, up_sums, in_sums
        )
        begin = 6 + units // width
        quarters = in_order([short[begin + s] for s in range(groups)], z)
        total = sum_everywhere(jnp.concatenate([short[:begin], quarters], axis=0))
        ends = lax.dynamic_index_in_dim(total, begin + z, 0, keepdims=False)

        def sum_heads(parts):
            return total_of(parts[0], *[away(parts[s], s) for s in range(1, groups)])

        def dense_rows(grads):
            rows = reduce_docs(grads.reshape(count, -1, grads.shape[1]))
            parts = rows.reshape(-1, groups, width)
            parts = [
                lax.dynamic_index_in_dim(parts, z ^ s, 1, keepdims=False) for s in range(groups)
            ]
            mine = sum_heads(parts)
            pieces = [mine] + [away(mine, s) for s in range(1, groups)]
            return in_order(pieces, z).transpose(1, 0, 2).reshape(rows.shape).astype(F32)

        out_back = dense_rows(back_grads)
        rows = dense_rows(dense_grads)
        out_in, out_out = rows[:, :units], rows[:, units:]
        blocks = jnp.concatenate([dw_own, dw_rest]).reshape(groups, count, small, width)
        blocks = blocks.transpose(1, 0, 2, 3).reshape(count, groups * small, width)
        blocks = reduce_docs(blocks).reshape(groups, small, width)
        full = spread_docs(sum_heads([blocks[s] for s in range(groups)]))
        full = full.reshape(columns, width).astype(F32)

    mine = lambda vector: lax.dynamic_slice_in_dim(
        vector, docs * (vector.shape[0] // count), vector.shape[0] // count
    )
    deep = units // width
    return (
        layer_output,
        dx.astype(BF),
        full.reshape(3, own, width).transpose(2, 0, 1),
        ends[: 2 * own].reshape(2, own),
        ends[2 * own : 2 * own + 2 * heads * buckets].reshape(2, heads, buckets),
        out_out,
        mine(total[2]),
        mine(total[0]),
        mine(total[1]),
        out_in,
        mine(total[6 : 6 + deep].reshape(-1)),
        out_back,
        mine(total[5]),
        mine(total[3]),
        mine(total[4]),
    )


def solution(mesh):
    rows = P(("docs", "heads"), None)
    return jax.shard_map(
        body,
        mesh=mesh,
        in_specs=(
            rows,
            P(None, "docs"),
            P("docs"),
            P(None, None, "heads"),
            P(None, "heads"),
            P(None, "heads", None),
            P(),
            P(),
            P(),
            P(),
            P(),
            P(),
            P(),
            P(),
            P(),
            P(),
            rows,
        ),
        out_specs=(
            rows,
            rows,
            P(None, None, "heads"),
            P(None, "heads"),
            P(None, "heads", None),
            P("docs", None),
            P("docs"),
            P("docs"),
            P("docs"),
            P("docs", None),
            P("docs"),
            P("docs", None),
            P("docs"),
            P("docs"),
            P("docs"),
        ),
        check_vma=False,
    )
```

```python
import functools
import math

import jax
import jax.numpy as jnp
from jax import lax
from jax.experimental import pallas as pl
from jax.experimental.pallas import tpu as pltpu
from jax.sharding import PartitionSpec as P

HEAD_DIM = 64
L = 512
EPS = 1e-05
NEG = -1000000000.0
THRESHOLDS = (1, 2, 3, 4, 6, 8, 12, 16, 24, 32, 48, 64, 96, 128, 192)
ROOT_HALF = 1.0 / math.sqrt(2.0)
DENSITY_SCALE = 1.0 / math.sqrt(2.0 * math.pi)
SCALE = 0.125
KC = 32
QB = 128
RT = 32
FC = 768
MB = 256
BF = jnp.bfloat16
F32 = jnp.float32
I32 = jnp.int32
NT = (((1,), (1,)), ((), ()))


def whole(*shape):
    return pl.BlockSpec(shape, lambda *_: (0,) * len(shape))


def limit(mebibytes):
    return pltpu.CompilerParams(vmem_limit_bytes=mebibytes << 20)


HINT = pl.CostEstimate(flops=1, bytes_accessed=1, transcendentals=0)


def shaped(dtype, *shape):
    return jax.ShapeDtypeStruct(shape, dtype)


def first_bucket_of(offset):
    distance = jnp.abs(offset)
    count = jnp.where(offset > 0, 16, 0).astype(I32)
    for threshold in THRESHOLDS:
        count = count + jnp.where(distance >= threshold, 1, 0).astype(I32)
    return count


def second_bucket_of(across, upward):
    horizontal = jnp.zeros(across.shape, I32)
    for threshold in (-128, -32, -8, 0):
        horizontal = horizontal + jnp.where(across >= threshold, 1, 0)
    for threshold in (8, 32, 128):
        horizontal = horizontal + jnp.where(across > threshold, 1, 0)
    vertical = (
        jnp.where(upward >= -24, 8, 0)
        + jnp.where(upward >= 0, 8, 0)
        + jnp.where(upward > 24, 8, 0)
    )
    return vertical + horizontal


PLACE = ("heads", "core", "x", "y")


def bucket_kernel(place_ref, len_ref, box_ref, out_ref, near_ref, turned_sc):
    filled = len_ref[place_ref[0]]
    boxes = box_ref[...].astype(F32)
    turned_sc[...] = jnp.transpose(jnp.concatenate([boxes] * 4, axis=0)).astype(I32)
    size = 64

    @pl.loop(0, L // size)
    def _(step):
        start = pl.multiple_of(step * size, size)
        rows = pl.ds(start, size)
        across = turned_sc[rows, 0:1] - box_ref[0:1, :]
        upward = turned_sc[rows, 1:2] - box_ref[1:2, :]
        key = lax.broadcasted_iota(I32, (size, L), 0) + start
        out_ref[rows, :] = jnp.where(key < filled, second_bucket_of(across, upward), 32)

    @pl.loop(0, near_ref.shape[0])
    def _(tile):
        offset = (
            128 * (tile - 2)
            + lax.broadcasted_iota(I32, (128, 128), 0)
            - lax.broadcasted_iota(I32, (128, 128), 1)
        )
        near_ref[tile] = first_bucket_of(offset)


def buckets_of(place, lengths, boxes):
    return pl.pallas_call(
        bucket_kernel,
        grid_spec=pltpu.PrefetchScalarGridSpec(
            num_scalar_prefetch=2,
            grid=(1,),
            in_specs=[pl.BlockSpec((2, L), lambda i, place, lengths: (0, place[0]))],
            out_specs=[whole(L, L), whole(5, 128, 128)],
            scratch_shapes=[pltpu.VMEM((L, 8), I32)],
        ),
        out_shape=[shaped(I32, L, L), shaped(I32, 5, 128, 128)],
        name="buckets",
        compiler_params=limit(6),
        cost_estimate=HINT,
    )(place, lengths, boxes)


def lookup(table_row, index):
    table = jnp.broadcast_to(table_row, (index.shape[0], 128))
    return jnp.concatenate(
        [
            jnp.take_along_axis(
                table, index[:, c : c + 128], axis=1, mode="promise_in_bounds"
            )
            for c in range(0, index.shape[1], 128)
        ],
        axis=1,
    )


def head_window(head, width):
    start = head * HEAD_DIM // 128 * 128
    return start, min(128, width - start), head * HEAD_DIM - start


def eights(rows):
    return rows.reshape(rows.shape[0] // 8, 8, rows.shape[1])


def column(row):
    return jnp.transpose(jnp.broadcast_to(row, (8, row.shape[1])))[:, 0:1]


def forward_kernel(gathered, place_ref, x_ref, *refs):
    sources = refs[: 4 if gathered else 1]
    extra_ref, bucket_ref, index_ref = refs[len(sources) : len(sources) + 3]
    rest = refs[len(sources) + 3 :]
    if gathered:
        w_ref, rest = rest[0], rest[1:]
    else:
        w_ref = sources[0]
    ctx_ref, turned_ref, raised_ref, qkv_ref, inverse_ref = rest[:5]
    near_sc, score_sc, query_sc, key_sc = rest[5:9]
    heads = raised_ref.shape[1]
    width = heads * HEAD_DIM

    @pl.when(pl.program_id(0) == 0)
    def _():
        query_sc[...] = jnp.zeros_like(query_sc)

    if gathered:
        whole_sc = rest[9]
        core, here_x, here_y = place_ref[1], place_ref[2], place_ref[3]
        cut = sources[0].shape[3]
        size = cut + sources[1].shape[3]
        for far_y in range(2):
            for far_x in range(2):
                chip = (here_y ^ far_y) * 2 + (here_x ^ far_x)
                for side, pair in ((core, sources[:2]), (1 - core, sources[2:])):
                    at = (chip * 2 + side) * size
                    first = pl.multiple_of(at, 8)
                    whole_sc[pl.ds(first, cut), :] = pair[0][far_y, far_x, 0].astype(F32)
                    second = pl.multiple_of(at + cut, 8)
                    whole_sc[pl.ds(second, size - cut), :] = pair[1][far_x, far_y, 0].astype(F32)
        w_ref[0] = whole_sc[...].astype(BF)

    extra = extra_ref[0, 0:1, :].astype(F32)
    query_bias, value_bias = extra[:, 0:width], extra[:, width : 2 * width]
    first_tables = extra[:, 2 * width : 2 * width + 128]
    second_tables = extra[:, 2 * width + 128 : 2 * width + 256]
    query = lax.dot_general(w_ref[0, 0:width, :], x_ref[...], NT, preferred_element_type=F32)
    qkv_ref[0, 0:width, :] = (query + column(query_bias)).astype(BF)
    key = lax.dot_general(
        w_ref[0, width : 2 * width, :], x_ref[...], NT, preferred_element_type=F32
    )
    qkv_ref[0, width : 2 * width, :] = key.astype(BF)
    value = lax.dot_general(
        w_ref[0, 2 * width : 3 * width, :], x_ref[...], NT, preferred_element_type=F32
    )
    qkv_ref[0, 2 * width : 3 * width, :] = (value + column(value_bias)).astype(BF)
    key_sc[...] = lax.dot_general(
        x_ref[...], w_ref[0, width : 2 * width, :], NT, preferred_element_type=F32
    ).astype(BF)
    inverse_ref[0] = jnp.zeros_like(inverse_ref[0])
    lane = lax.broadcasted_iota(I32, (1, 128), 1)
    for h in range(heads):
        c0, w, low = head_window(h, width)
        own = slice(h * HEAD_DIM, (h + 1) * HEAD_DIM)
        query_sc[h, low : low + HEAD_DIM, :] = qkv_ref[0, own, :] * jnp.asarray(SCALE, BF)
        row = first_tables if h == 0 else jnp.roll(first_tables, -32 * h, axis=1)
        other = second_tables if h == 0 else jnp.roll(second_tables, -32 * h, axis=1)
        other = jnp.where(lane < 32, other, NEG)
        for d in range(5):
            near_sc[h, d] = lookup(row, index_ref[d])
        far = {
            -3: jnp.broadcast_to(row[:, 15:16], (KC, 128)),
            3: jnp.broadcast_to(row[:, 31:32], (KC, 128)),
        }
        key = key_sc[:, c0 : c0 + w]
        for block in range(L // QB):
            cols = slice(block * QB, (block + 1) * QB)
            score_sc[h] = jnp.dot(key, query_sc[h, 0:w, cols], preferred_element_type=F32)
            peak = None
            for step in range(L // KC):
                rows = slice(step * KC, (step + 1) * KC)
                d, inner = step * KC // 128 - block, step * KC % 128
                near = far[d] if abs(d) == 3 else near_sc[h, d + 2, inner : inner + KC, :]
                scores = score_sc[h, rows, :] + near
                scores = scores + lookup(other, bucket_ref[rows, cols])
                score_sc[h, rows, :] = scores
                part = jnp.max(eights(scores), axis=0)
                peak = part if peak is None else jnp.maximum(peak, part)
            peak = jnp.max(peak, axis=0, keepdims=True)
            sums = None
            for step in range(L // KC):
                rows = slice(step * KC, (step + 1) * KC)
                raised = jnp.exp(score_sc[h, rows, :] - peak)
                raised_ref[0, h, rows, cols] = raised.astype(BF)
                part = jnp.sum(eights(raised), axis=0)
                sums = part if sums is None else sums + part
            inverse_ref[0, h : h + 1, cols] = 1.0 / jnp.sum(sums, axis=0, keepdims=True)
        at = 2 * width + h * HEAD_DIM
        out = jnp.dot(
            qkv_ref[0, at : at + HEAD_DIM, :], raised_ref[0, h], preferred_element_type=F32
        )
        turned_ref[0, own, :] = (out * inverse_ref[0, h : h + 1, :]).astype(BF)
    ctx_ref[0] = jnp.transpose(turned_ref[0])


def each(*shape):
    return pl.BlockSpec((1,) + shape, lambda g, *_: (g,) + (0,) * len(shape))


def attend_forward(place, x, sources, extra, bucket, near):
    gathered = len(sources) == 4
    groups, depth = extra.shape[0], x.shape[1]
    if gathered:
        columns = 8 * (sources[0].shape[3] + sources[1].shape[3])
        inputs = [
            pl.BlockSpec(
                (2, 2, 1) + source.shape[3:], lambda g, place: (0, 0, g, 0, 0)
            )
            for source in sources
        ]
    else:
        columns = sources[0].shape[1]
        inputs = [each(columns, depth)]
    heads = columns // (3 * HEAD_DIM)
    width = columns // 3
    out_specs = [
        each(L, width), each(width, L), each(heads, L, L), each(columns, L), each(8, L)
    ]
    out_shape = [
        shaped(BF, groups, L, width),
        shaped(BF, groups, width, L),
        shaped(BF, groups, heads, L, L),
        shaped(BF, groups, columns, L),
        shaped(F32, groups, 8, L),
    ]
    scratch = [
        pltpu.VMEM((heads, 5, 128, 128), F32),
        pltpu.VMEM((heads, L, QB), F32),
        pltpu.VMEM((heads, 128, L), BF),
        pltpu.VMEM((L, width), BF),
    ]
    if gathered:
        out_specs = [each(columns, depth)] + out_specs
        out_shape = [shaped(BF, groups, columns, depth)] + out_shape
        scratch = scratch + [pltpu.VMEM((columns, depth), F32)]
    return pl.pallas_call(
        functools.partial(forward_kernel, gathered),
        grid_spec=pltpu.PrefetchScalarGridSpec(
            num_scalar_prefetch=1,
            grid=(groups,),
            in_specs=[whole(L, depth)] + inputs + [each(8, depth), whole(L, L), whole(5, 128, 128)],
            out_specs=out_specs,
            scratch_shapes=scratch,
        ),
        out_shape=out_shape,
        name="attend_forward",
        compiler_params=limit(22),
        cost_estimate=HINT,
    )(place, x, *sources, extra, bucket, near)


def backward_kernel(
    halved, place_ref, x_ref, w_ref, qkv_ref, raised_ref, inverse_ref, grad_ref, start_ref, *refs
):
    outs = refs[: 5 if halved else 4]
    dx_ref, ds_ref, sums_ref = outs[:3]
    pad_sc, term_sc, rows_sc, turn_sc, value_sc = refs[len(outs) : len(outs) + 5]
    group = pl.program_id(0)
    heads = raised_ref.shape[1]
    width = heads * HEAD_DIM

    @pl.when(group == 0)
    def _():
        pad_sc[...] = jnp.zeros_like(pad_sc)
        dx_ref[...] = start_ref[...]

    value_sc[...] = jnp.transpose(qkv_ref[0, 2 * width : 3 * width, :])
    for h in range(heads):
        c0, w, low = head_window(h, width)
        own = slice(h * HEAD_DIM, (h + 1) * HEAD_DIM)
        pad_sc[h, low : low + HEAD_DIM, :] = grad_ref[0, own, :]
        value = value_sc[:, c0 : c0 + w]
        for block in range(L // QB):
            cols = slice(block * QB, (block + 1) * QB)
            term_sc[h] = jnp.dot(value, pad_sc[h, 0:w, cols], preferred_element_type=F32)
            sums = None
            for step in range(L // KC):
                rows = slice(step * KC, (step + 1) * KC)
                terms = term_sc[h, rows, :] * raised_ref[0, h, rows, cols].astype(F32)
                term_sc[h, rows, :] = terms
                part = jnp.sum(eights(terms), axis=0)
                sums = part if sums is None else sums + part
            inner = jnp.sum(sums, axis=0, keepdims=True) * inverse_ref[0, h : h + 1, cols]
            for step in range(L // KC):
                rows = slice(step * KC, (step + 1) * KC)
                raised = raised_ref[0, h, rows, cols].astype(F32)
                ds_ref[0, h, rows, cols] = (term_sc[h, rows, :] - raised * inner).astype(BF)
        scale = jnp.asarray(SCALE, BF)
        at = width + h * HEAD_DIM
        turn_sc[own, :] = jnp.dot(
            qkv_ref[0, at : at + HEAD_DIM, :] * scale, ds_ref[0, h], preferred_element_type=F32
        ).astype(BF)
        dk = lax.dot_general(
            ds_ref[0, h], qkv_ref[0, c0 : c0 + w, :] * scale, NT, preferred_element_type=F32
        )
        rows_sc[:, at : at + HEAD_DIM] = dk[:, low : low + HEAD_DIM].astype(BF)
        dv = lax.dot_general(
            raised_ref[0, h], grad_ref[0, c0 : c0 + w, :], NT, preferred_element_type=F32
        )
        at = 2 * width + h * HEAD_DIM
        rows_sc[:, at : at + HEAD_DIM] = dv[:, low : low + HEAD_DIM].astype(BF)
    rows_sc[:, 0:width] = jnp.transpose(turn_sc[0:width, :])
    turn_sc[width:, :] = jnp.transpose(rows_sc[:, width:])
    weights = jnp.dot(turn_sc[...], x_ref[...], preferred_element_type=F32)
    if halved:
        sent_ref, kept_ref = outs[3:]
        all_sc = refs[len(outs) + 5]
        all_sc[...] = weights
        core = place_ref[1]
        chips, size = kept_ref.shape[1], kept_ref.shape[2]
        for chip in range(chips):
            for side, ref in ((1 - core, sent_ref), (core, kept_ref)):
                at = pl.multiple_of((chip * 2 + side) * size, 8)
                ref[0, chip] = all_sc[pl.ds(at, size), :].astype(BF)
    else:
        outs[3][0] = weights.astype(BF)
    dx_ref[...] += jnp.dot(rows_sc[...], w_ref[0], preferred_element_type=F32)
    sums_ref[0] = jnp.sum(rows_sc[...].astype(F32), axis=0, keepdims=True)


def attend_backward(place, halves, x, w, qkv, raised, inverse, grad, start, span=None):
    columns, depth = w.shape[1:]
    skip, stop = span or (0, w.shape[0])
    groups = stop - skip
    some = lambda *shape: pl.BlockSpec(
        (1,) + shape, lambda g, *_: (g + skip,) + (0,) * len(shape)
    )
    heads = columns // (3 * HEAD_DIM)
    width = columns // 3
    out_specs = [whole(L, depth), each(heads, L, L), each(1, columns)]
    out_shape = [
        shaped(F32, L, depth),
        shaped(BF, groups, heads, L, L),
        shaped(F32, groups, 1, columns),
    ]
    scratch = [
        pltpu.VMEM((heads, 128, L), BF),
        pltpu.VMEM((heads, L, QB), F32),
        pltpu.VMEM((L, columns), BF),
        pltpu.VMEM((columns, L), BF),
        pltpu.VMEM((L, width), BF),
    ]
    if halves:
        size = columns // (2 * halves)
        out_specs += [each(halves, size, depth)] * 2
        out_shape += [shaped(BF, groups, halves, size, depth)] * 2
        scratch += [pltpu.VMEM((columns, depth), F32)]
    else:
        out_specs += [each(columns, depth)]
        out_shape += [shaped(BF, groups, columns, depth)]
    return pl.pallas_call(
        functools.partial(backward_kernel, bool(halves)),
        grid_spec=pltpu.PrefetchScalarGridSpec(
            num_scalar_prefetch=1,
            grid=(groups,),
            in_specs=[
                whole(L, depth),
                some(columns, depth),
                some(columns, L),
                some(heads, L, L),
                some(8, L),
                some(width, L),
                whole(L, depth),
            ],
            out_specs=out_specs,
            scratch_shapes=scratch,
        ),
        out_shape=out_shape,
        name="attend_backward",
        compiler_params=limit(26),
        cost_estimate=HINT,
    )(place, x, w, qkv, raised, inverse, grad, start)


def table_kernel(skip, *refs):
    bucket_ref, start_ref, acc_ref, hot_sc = refs[-4:]
    step = pl.program_id(0)
    blocks = [
        (ref, g, h) for ref in refs[:-4] for g in range(ref.shape[0]) for h in range(ref.shape[1])
    ]
    half = 32 * 8

    @pl.when(step == 0)
    def _():
        acc_ref[...] = start_ref[...]

    for u in range(RT // 8):
        part = slice(u * 8, (u + 1) * 8)
        second = bucket_ref[part, :]
        offset = (
            lax.broadcasted_iota(I32, (8, L), 0)
            + ((step + skip) * RT + u * 8)
            - lax.broadcasted_iota(I32, (8, L), 1)
        )
        first = first_bucket_of(offset)
        for t in range(0, 32, 2):
            for base, bucket in ((0, first), (half, second)):
                hot_sc[base + t * 8 : base + (t + 2) * 8, :] = jnp.concatenate(
                    [jnp.where(bucket == t, 1.0, 0.0), jnp.where(bucket == t + 1, 1.0, 0.0)],
                    axis=0,
                ).astype(BF)
        left = jnp.concatenate([ref[g, h, part, :] for ref, g, h in blocks], axis=0)
        acc_ref[...] += lax.dot_general(left, hot_sc[...], NT, preferred_element_type=F32)


def table_products(ds, bucket, start, part):
    heads = sum(item.shape[0] * item.shape[1] for item in ds)
    steps = L // RT // 2
    skip = part * steps
    return pl.pallas_call(
        functools.partial(table_kernel, skip),
        grid=(steps,),
        in_specs=[
            pl.BlockSpec(item.shape[:2] + (RT, L), lambda r: (0, 0, r + skip, 0)) for item in ds
        ]
        + [pl.BlockSpec((RT, L), lambda r: (r + skip, 0)), whole(heads * 8, 512)],
        out_specs=whole(heads * 8, 512),
        out_shape=shaped(F32, heads * 8, 512),
        scratch_shapes=[pltpu.VMEM((512, L), BF)],
        name="table_products",
        compiler_params=limit(14),
        cost_estimate=HINT,
    )(*ds, bucket, start)


def short_kernel(per, count, *refs):
    acc_ref, sums = refs[0], refs[1 : 1 + count]
    down_ref, up_ref, in_ref, out_ref = refs[1 + count :]
    heads = acc_ref.shape[0] // 8
    half = 32 * 8
    shape = (heads * 8, 2 * half)
    same = lax.broadcasted_iota(I32, shape, 0) % 8 == lax.broadcasted_iota(I32, shape, 1) % 8
    kept = jnp.where(same, acc_ref[...], 0.0)
    fold = (2 * half, 64)
    right = (
        lax.broadcasted_iota(I32, fold, 0) // 8 == lax.broadcasted_iota(I32, fold, 1)
    ).astype(F32)
    spread = (16, heads * 8)
    left = (
        lax.broadcasted_iota(I32, spread, 1) // 8 == lax.broadcasted_iota(I32, spread, 0)
    ).astype(F32)
    exact = lax.Precision.HIGHEST
    folded = jnp.dot(kept, right, preferred_element_type=F32, precision=exact)
    tables = jnp.dot(left, folded, preferred_element_type=F32, precision=exact)
    wide = 2 * per * 32
    lanes = None
    for h in range(per):
        shape = (8, 16)
        rows = (
            lax.broadcasted_iota(I32, shape, 1) == lax.broadcasted_iota(I32, shape, 0) * per + h
        ).astype(F32)
        shape = (64, wide)
        source, target = lax.broadcasted_iota(I32, shape, 0), lax.broadcasted_iota(I32, shape, 1)
        moved = jnp.where(source < 32, source + h * 32, source + (per - 1 + h) * 32)
        part = jnp.dot(rows, tables, preferred_element_type=F32, precision=exact)
        part = jnp.dot(
            part, (target == moved).astype(F32), preferred_element_type=F32, precision=exact
        )
        lanes = part if lanes is None else lanes + part
    out_ref[...] = jnp.zeros_like(out_ref)
    out_ref[0:3, :] = down_ref[0:3, :]
    out_ref[3:6, :] = up_ref[0:3, :]
    width = out_ref.shape[1]
    deep = in_ref.shape[1] // width
    for n in range(deep):
        out_ref[6 + n : 7 + n, :] = in_ref[0:1, n * width : (n + 1) * width]
    group = 0
    for ref in sums:
        own = ref.shape[2] // 3
        for g in range(ref.shape[0]):
            row = slice(6 + deep + group, 7 + deep + group)
            out_ref[row, 0:own] = ref[g, :, 0:own]
            out_ref[row, own : 2 * own] = ref[g, :, 2 * own :]
            out_ref[row, 2 * own : 2 * own + wide] = lanes[group : group + 1, :]
            group += 1


def short_rows(acc, sums, down, up, inner, per):
    width = down.shape[1]
    rows = -(-(6 + inner.shape[1] // width + acc.shape[0] // 8 // per) // 8) * 8
    vmem = pl.BlockSpec(memory_space=pltpu.VMEM)
    return pl.pallas_call(
        functools.partial(short_kernel, per, len(sums)),
        in_specs=[vmem] * (4 + len(sums)),
        out_specs=vmem,
        out_shape=shaped(F32, rows, width),
        name="short_rows",
        compiler_params=limit(6),
        cost_estimate=HINT,
    )(acc, *sums, down, up, inner)


def mean_of(rows):
    return jnp.mean(rows, axis=-1, keepdims=True)


def normalize(rows):
    centred = rows - mean_of(rows)
    inverse = lax.rsqrt(mean_of(centred * centred) + EPS)
    return centred * inverse, inverse


def normalize_back(scaled, unit, inverse):
    return inverse * (scaled - mean_of(scaled) - unit * mean_of(scaled * unit))


def gelu_parts(values):
    size = jnp.abs(values)
    t = 1.0 / (1.0 + (0.3275911 * ROOT_HALF) * size)
    bell = jnp.exp(values * values * -0.5)
    series = 1.061405429
    for term in (-1.453152027, 1.421413741, -0.284496736, 0.254829592):
        series = term + t * series
    tail = (0.5 * t) * series * bell
    below = jnp.where(values >= 0, 1.0 - tail, tail)
    return values * below, below + values * (bell * DENSITY_SCALE)


def column_sum(rows):
    return jnp.sum(rows, axis=0, keepdims=True)


def up_kernel(
    place_ref, x_ref, ctx_own_ref, ctx_ref, wo_ref, bo_ref, g1_ref, s1_ref, wi_ref, bi_ref, wb_ref,
    bb_ref, g2_ref, s2_ref, cot_ref,
    out_ref, mid_ref, branch_ref, turned_ref, slope_ref, unit_ref, inverse_ref, low_ref, sums_ref,
    normed_sc, low_sc, acc_sc,
):
    step = pl.program_id(0)
    groups = wo_ref.shape[0]

    @pl.when(step == 0)
    def _():
        @pl.loop(0, L // MB)
        def _(r):
            rows = pl.ds(pl.multiple_of(r * MB, MB), MB)
            total = x_ref[rows, :].astype(F32) + bo_ref[...]
            for s in range(groups):
                ctx = ctx_own_ref[0, rows, :] if s == 0 else ctx_ref[s - 1, rows, :]
                quarter = place_ref[0] ^ s
                total = total + jnp.dot(ctx, wo_ref[quarter], preferred_element_type=F32)
            unit, inverse = normalize(total)
            unit_ref[rows, :] = unit
            inverse_ref[rows, :] = jnp.broadcast_to(inverse, (MB, 128))
            normed = unit * g1_ref[...] + s1_ref[...]
            normed_sc[rows, :] = normed
            low_sc[rows, :] = normed.astype(BF)

        low_ref[...] = jnp.transpose(low_sc[...])
        acc_sc[...] = jnp.zeros_like(acc_sc)

    @pl.loop(0, L // MB)
    def _(r):
        rows = pl.ds(pl.multiple_of(r * MB, MB), MB)
        pre = jnp.dot(low_sc[rows, :], wi_ref[...], preferred_element_type=F32) + bi_ref[...]
        acted, slope = gelu_parts(pre)
        acted = acted.astype(BF)
        slope_ref[rows, :] = slope.astype(BF)
        turned_ref[:, rows] = jnp.transpose(acted)
        acc_sc[rows, :] += jnp.dot(acted, wb_ref[...], preferred_element_type=F32)

    @pl.when(step == pl.num_programs(0) - 1)
    def _():
        sums_ref[...] = jnp.zeros_like(sums_ref)

        @pl.loop(0, L // MB)
        def _(r):
            rows = pl.ds(pl.multiple_of(r * MB, MB), MB)
            unit, inverse = normalize(normed_sc[rows, :] + (acc_sc[rows, :] + bb_ref[...]))
            out_ref[rows, :] = (unit * g2_ref[...] + s2_ref[...]).astype(BF)
            upstream = cot_ref[rows, :].astype(F32)
            middle = normalize_back(upstream * g2_ref[...], unit, inverse)
            mid_ref[rows, :] = middle
            branch = middle.astype(BF)
            branch_ref[rows, :] = branch
            sums_ref[0:1, :] += column_sum(upstream * unit)
            sums_ref[1:2, :] += column_sum(upstream)
            sums_ref[2:3, :] += column_sum(branch.astype(F32))


def feed_up(place, x, ctx_own, ctx, w_out, bo, g1, s1, w_in, bi, w_back, bb, g2, s2, cot):
    width = x.shape[1]
    units = w_in.shape[1]
    groups, own = w_out.shape[0], w_out.shape[1]
    row = whole(1, width)
    return pl.pallas_call(
        up_kernel,
        grid_spec=pltpu.PrefetchScalarGridSpec(
            num_scalar_prefetch=1,
            grid=(units // FC,),
            in_specs=[
                whole(L, width),
                whole(1, L, own),
                whole(groups - 1, L, own),
                whole(groups, own, width),
                row,
                row,
                row,
                pl.BlockSpec((width, FC), lambda n, place: (0, n)),
                pl.BlockSpec((1, FC), lambda n, place: (0, n)),
                pl.BlockSpec((FC, width), lambda n, place: (n, 0)),
                row,
                row,
                row,
                whole(L, width),
            ],
            out_specs=[
                whole(L, width),
                whole(L, width),
                whole(L, width),
                pl.BlockSpec((FC, L), lambda n, place: (n, 0)),
                pl.BlockSpec((L, FC), lambda n, place: (0, n)),
                whole(L, width),
                whole(L, 128),
                whole(width, L),
                whole(8, width),
            ],
            scratch_shapes=[
                pltpu.VMEM((L, width), F32),
                pltpu.VMEM((L, width), BF),
                pltpu.VMEM((L, width), F32),
            ],
        ),
        out_shape=[
            shaped(BF, L, width),
            shaped(F32, L, width),
            shaped(BF, L, width),
            shaped(BF, units, L),
            shaped(BF, L, units),
            shaped(F32, L, width),
            shaped(F32, L, 128),
            shaped(BF, width, L),
            shaped(F32, 8, width),
        ],
        name="feed_up",
        compiler_params=limit(32),
        cost_estimate=HINT,
    )(place, x, ctx_own, ctx, w_out, bo, g1, s1, w_in, bi, w_back, bb, g2, s2, cot)


def down_kernel(
    halved, place_ref, branch_ref, slope_ref, wb_ref, wi_ref, low_ref, mid_ref, unit_ref,
    inverse_ref, g1_ref, wo_ref, turned_own_ref, turned_ref, norm_own_ref, norm_ref, *refs
):
    bias_ref, first_ref, grad_own_ref, grad_ref, sums_ref = refs[:5]
    weight_refs = refs[5 : 7 if halved else 6]
    acc_sc, pre_sc, weight_sc = refs[-3:]
    step = pl.program_id(0)
    last = pl.num_programs(0) - 1
    groups, own = wo_ref.shape[0], wo_ref.shape[1]

    def give():
        if not halved:
            weight_refs[0][...] = weight_sc[...]
            return
        core = place_ref[1]
        chips, size = weight_refs[0].shape[0], weight_refs[0].shape[1]
        for chip in range(chips):
            for side, ref in ((1 - core, weight_refs[0]), (core, weight_refs[1])):
                at = pl.multiple_of((chip * 2 + side) * size, size)
                ref[chip] = weight_sc[pl.ds(at, size), :]

    @pl.when(step == 0)
    def _():
        acc_sc[...] = mid_ref[...]

    @pl.when(step < last)
    def _():
        total = None
        for r in range(L // MB):
            rows = slice(r * MB, (r + 1) * MB)
            pre = lax.dot_general(
                branch_ref[rows, :], wb_ref[...], NT, preferred_element_type=F32
            ) * slope_ref[rows, :].astype(F32)
            pre = pre.astype(BF)
            pre_sc[rows, :] = pre
            part = column_sum(pre.astype(F32))
            total = part if r == 0 else total + part
            acc_sc[rows, :] += lax.dot_general(
                pre, wi_ref[...], NT, preferred_element_type=F32
            )
        bias_ref[0:1, :] = total
        weight_sc[...] = jnp.dot(
            low_ref[...], pre_sc[...], preferred_element_type=F32
        ).astype(BF)
        give()

    @pl.when(step == last)
    def _():
        sums_ref[...] = jnp.zeros_like(sums_ref)

        @pl.loop(0, L // MB)
        def _(r):
            rows = pl.ds(pl.multiple_of(r * MB, MB), MB)
            hidden = acc_sc[rows, :]
            unit = unit_ref[rows, :]
            first = normalize_back(hidden * g1_ref[...], unit, inverse_ref[rows, 0:1])
            first_ref[rows, :] = first
            attended = first.astype(BF)
            pre_sc[rows, :] = attended
            sums_ref[0:1, :] += column_sum(hidden * unit)
            sums_ref[1:2, :] += column_sum(hidden)
            sums_ref[2:3, :] += column_sum(attended.astype(F32))

        def quarter_of(s, turned, norm, out):
            quarter = place_ref[0] ^ s
            at = pl.multiple_of(quarter * own, own)
            weight_sc[pl.ds(at, own), :] = jnp.dot(
                turned, pre_sc[...], preferred_element_type=F32
            ).astype(BF)
            grads = lax.dot_general(
                wo_ref[quarter], pre_sc[...], NT, preferred_element_type=F32
            )
            for h in range(own // HEAD_DIM):
                rows = slice(h * HEAD_DIM, (h + 1) * HEAD_DIM)
                out[rows, :] = (grads[rows, :] * norm[h : h + 1, :]).astype(BF)

        quarter_of(0, turned_own_ref[0], norm_own_ref[0], grad_own_ref.at[0])

        @pl.loop(1, groups)
        def _(s):
            quarter_of(s, turned_ref[s - 1], norm_ref[s - 1], grad_ref.at[s - 1])

        give()


def feed_down(place, halves, branch, slope, w_back, w_in, low, mid, unit, inverse, g1, w_out,
              turned_own, turned, norm_own, norm):
    width = branch.shape[1]
    units = w_in.shape[1]
    groups, own = w_out.shape[0], w_out.shape[1]
    steps = units // FC
    inside = lambda n: jnp.minimum(n, steps - 1)
    out_specs = [
        pl.BlockSpec((8, FC), lambda n, place: (0, inside(n))),
        whole(L, width),
        whole(1, own, L),
        whole(groups - 1, own, L),
        whole(8, width),
    ]
    out_shape = [
        shaped(F32, 8, units),
        shaped(F32, L, width),
        shaped(BF, 1, own, L),
        shaped(BF, groups - 1, own, L),
        shaped(F32, 8, width),
    ]
    if halves:
        size = width // (2 * halves)
        out_specs += [pl.BlockSpec((halves, size, FC), lambda n, place: (0, 0, n))] * 2
        out_shape += [shaped(BF, halves, size, units + width)] * 2
    else:
        out_specs += [pl.BlockSpec((width, FC), lambda n, place: (0, n))]
        out_shape += [shaped(BF, width, units + width)]
    return pl.pallas_call(
        functools.partial(down_kernel, bool(halves)),
        grid_spec=pltpu.PrefetchScalarGridSpec(
            num_scalar_prefetch=1,
            grid=(steps + 1,),
            in_specs=[
                whole(L, width),
                pl.BlockSpec((L, FC), lambda n, place: (0, inside(n))),
                pl.BlockSpec((FC, width), lambda n, place: (inside(n), 0)),
                pl.BlockSpec((width, FC), lambda n, place: (0, inside(n))),
                whole(width, L),
                whole(L, width),
                whole(L, width),
                whole(L, 128),
                whole(1, width),
                whole(groups, own, width),
                whole(1, own, L),
                whole(groups - 1, own, L),
                whole(1, 8, L),
                whole(groups - 1, 8, L),
            ],
            out_specs=out_specs,
            scratch_shapes=[
                pltpu.VMEM((L, width), F32),
                pltpu.VMEM((L, FC), BF),
                pltpu.VMEM((width, FC), BF),
            ],
        ),
        out_shape=out_shape,
        name="feed_down",
        compiler_params=limit(34),
        cost_estimate=HINT,
    )(place, branch, slope, w_back, w_in, low, mid, unit, inverse, g1, w_out,
      turned_own, turned, norm_own, norm)


def product_kernel(place_ref, left_ref, right_ref, out_ref):
    out_ref[...] = jnp.dot(
        left_ref[...], right_ref[...], preferred_element_type=F32
    ).astype(BF)


def product(place, left, right, sizes):
    rows, depth = left.shape
    columns = right.shape[1]
    count, size, halved = sizes
    take = (lambda n, place: (2 * n + 1 - place[1], 0)) if halved else (lambda n, place: (n, 0))
    return pl.pallas_call(
        product_kernel,
        grid_spec=pltpu.PrefetchScalarGridSpec(
            num_scalar_prefetch=1,
            grid=(count,),
            in_specs=[pl.BlockSpec((size, depth), take), whole(depth, columns)],
            out_specs=pl.BlockSpec((size, columns), lambda n, place: (n, 0)),
        ),
        out_shape=shaped(BF, count * size, columns),
        name="back_weights",
        compiler_params=limit(10),
        cost_estimate=HINT,
    )(place, left, right)


def kept_kernel(place_ref, left_ref, right_ref, got_ref, a_sent, a_kept, b_sent, b_kept):
    chip = pl.program_id(0)
    chip_y, chip_x = chip // 2, lax.rem(chip, 2)
    here_x, here_y = place_ref[2], place_ref[3]
    value = jnp.dot(left_ref[...], right_ref[...], preferred_element_type=F32)
    value = (value + got_ref[0].astype(F32)).astype(BF)
    cut = a_sent.shape[1]

    @pl.when(chip_x == here_x)
    def _():
        a_kept[chip_y] = value[:cut, :]

    @pl.when(chip_x != here_x)
    def _():
        a_sent[chip_y] = value[:cut, :]

    @pl.when(chip_y == here_y)
    def _():
        b_kept[chip_x] = value[cut:, :]

    @pl.when(chip_y != here_y)
    def _():
        b_sent[chip_x] = value[cut:, :]


def product_kept(place, left, right, got):
    chips, size, columns = got.shape
    depth = left.shape[1]
    part = whole(2, size // 2, columns)
    return pl.pallas_call(
        kept_kernel,
        grid_spec=pltpu.PrefetchScalarGridSpec(
            num_scalar_prefetch=1,
            grid=(chips,),
            in_specs=[
                pl.BlockSpec((size, depth), lambda n, place: (2 * n + place[1], 0)),
                whole(depth, columns),
                pl.BlockSpec((1, size, columns), lambda n, place: (n, 0, 0)),
            ],
            out_specs=[part] * 4,
        ),
        out_shape=[shaped(BF, 2, size // 2, columns)] * 4,
        name="kept_weights",
        compiler_params=limit(14),
        cost_estimate=HINT,
    )(place, left, right, got)


def total_of(*items):
    total = items[0].astype(F32)
    for item in items[1:]:
        total = total + item.astype(F32)
    return total.astype(BF)


def chips_kernel(count, layout, place_ref, *refs):
    inputs, outs = refs[:count], refs[count:]
    here_x, here_y = place_ref[2], place_ref[3]
    for order, (way, sources) in enumerate(layout):
        sent, kept = outs[2 * order], outs[2 * order + 1]
        start = 0
        for number, low, high in sources:
            kept_ref, got_ref = inputs[2 * number], inputs[2 * number + 1]
            for g in range(kept_ref.shape[0]):
                rows = slice(start, start + high - low)
                start += high - low
                for other in range(2):
                    for out, far in ((sent, 1), (kept, 0)):
                        if way == "x":
                            chip = other * 2 + (here_x ^ far)
                        else:
                            chip = (here_y ^ far) * 2 + other
                        out[other, rows, :] = total_of(
                            kept_ref[g, chip, low:high, :], got_ref[g, chip, low:high, :]
                        )


def sum_chips(place, pairs, parts, block):
    specs, out_specs, out_shape = [], [], []
    columns = pairs[0][0].shape[-1]
    for kept, _ in pairs:
        shape = kept.shape[:3] + (block,)
        specs += [pl.BlockSpec(shape, lambda n, place: (0, 0, 0, n))] * 2
    for _, sources in parts:
        height = sum(pairs[n][0].shape[0] * (high - low) for n, low, high in sources)
        out_specs += [pl.BlockSpec((2, height, block), lambda n, place: (0, 0, n))] * 2
        out_shape += [shaped(BF, 2, height, columns)] * 2
    return pl.pallas_call(
        functools.partial(chips_kernel, 2 * len(pairs), parts),
        grid_spec=pltpu.PrefetchScalarGridSpec(
            num_scalar_prefetch=1, grid=(columns // block,), in_specs=specs, out_specs=out_specs
        ),
        out_shape=out_shape,
        name="sum_chips",
        compiler_params=limit(14),
        cost_estimate=HINT,
    )(place, *[item for pair in pairs for item in pair])


def pairs_kernel(place_ref, a_kept, a_got, b_kept, b_got, a_sent, a_own, b_sent, b_own):
    here_x, here_y = place_ref[2], place_ref[3]
    for here, kept, got, sent, own in (
        (here_y, a_kept, a_got, a_sent, a_own),
        (here_x, b_kept, b_got, b_sent, b_own),
    ):
        sent[...] = total_of(kept[1 - here], got[1 - here])
        own[...] = total_of(kept[here], got[here])


def sum_pairs(place, a_kept, a_got, b_kept, b_got, block):
    columns = a_kept.shape[-1]
    spec = lambda item: pl.BlockSpec((2, item.shape[1], block), lambda n, place: (0, 0, n))
    flat = lambda item: pl.BlockSpec((item.shape[1], block), lambda n, place: (0, n))
    return pl.pallas_call(
        pairs_kernel,
        grid_spec=pltpu.PrefetchScalarGridSpec(
            num_scalar_prefetch=1,
            grid=(columns // block,),
            in_specs=[spec(a_kept), spec(a_got), spec(b_kept), spec(b_got)],
            out_specs=[flat(a_kept)] * 2 + [flat(b_kept)] * 2,
        ),
        out_shape=[shaped(BF, a_kept.shape[1], columns)] * 2
        + [shaped(BF, b_kept.shape[1], columns)] * 2,
        name="sum_pairs",
        compiler_params=limit(12),
        cost_estimate=HINT,
    )(place, a_kept, a_got, b_kept, b_got)


def cut_kernel(place_ref, a_kept, a_got, b_kept, b_got, sent, kept, sum_sc):
    cut = a_kept.shape[0]
    sum_sc[0:cut, :] = a_kept[...].astype(F32) + a_got[...].astype(F32)
    sum_sc[cut:, :] = b_kept[...].astype(F32) + b_got[...].astype(F32)
    size = kept.shape[1]
    for s, out in ((0, kept.at[0]), (1, sent.at[0]), (2, kept.at[1]), (3, sent.at[1])):
        at = pl.multiple_of((place_ref[0] ^ s) * size, 8)
        out[...] = sum_sc[pl.ds(at, size), :].astype(BF)


def cut_quarters(place, a_kept, a_got, b_kept, b_got, block):
    columns = a_kept.shape[-1]
    height = a_kept.shape[0] + b_kept.shape[0]
    spec = lambda item: pl.BlockSpec((item.shape[0], block), lambda n, place: (0, n))
    return pl.pallas_call(
        cut_kernel,
        grid_spec=pltpu.PrefetchScalarGridSpec(
            num_scalar_prefetch=1,
            grid=(columns // block,),
            in_specs=[spec(a_kept), spec(a_got), spec(b_kept), spec(b_got)],
            out_specs=[pl.BlockSpec((2, height // 4, block), lambda n, place: (0, 0, n))] * 2,
            scratch_shapes=[pltpu.VMEM((height, block), F32)],
        ),
        out_shape=[shaped(BF, 2, height // 4, columns)] * 2,
        name="cut_quarters",
        compiler_params=limit(12),
        cost_estimate=HINT,
    )(place, a_kept, a_got, b_kept, b_got)


def last_kernel(a_kept, a_got, b_kept, b_got, short_ref, *outs):
    size = outs[0].shape[0] - 16
    many = short_ref.shape[0] // 8 * 8
    first = 10
    for s, out in enumerate(outs):
        rows = slice(s % 2 * size, (s % 2 + 1) * size)
        kept, got = (a_kept, a_got) if s < 2 else (b_kept, b_got)
        out[0:size, :] = total_of(kept[rows, :], got[rows, :])
        row = lax.broadcasted_iota(I32, (many, short_ref.shape[1]), 0)
        short = jnp.where(row < first, short_ref[...], 0.0)
        short = short + jnp.where(row == first, short_ref[first + s : first + s + 1, :], 0.0)
        out[size : size + many, :] = short.astype(BF)


def cut_last(a_kept, a_got, b_kept, b_got, short):
    vmem = pl.BlockSpec(memory_space=pltpu.VMEM)
    size, columns = b_kept.shape[0] // 2, b_kept.shape[1]
    return pl.pallas_call(
        last_kernel,
        in_specs=[vmem] * 5,
        out_specs=[vmem] * 4,
        out_shape=[shaped(BF, size + 16, columns)] * 4,
        name="cut_last",
        compiler_params=limit(8),
        cost_estimate=HINT,
    )(a_kept, a_got, b_kept, b_got, short)


def join_kernel(place_ref, own, one, two, *outs):
    size = own.shape[0]
    start = 0
    for out in outs:
        lanes = slice(start, start + out.shape[1])
        for s, piece in ((0, own[:, lanes]), (2, one[:, lanes]), (1, two[0, :, lanes]), (3, two[1, :, lanes])):
            at = pl.multiple_of((place_ref[0] ^ s) * size, 8)
            out[pl.ds(at, size), :] = piece.astype(F32)
        start += out.shape[1]


def join_quarters(place, own, one, two, widths):
    vmem = pl.BlockSpec(memory_space=pltpu.VMEM)
    return pl.pallas_call(
        join_kernel,
        in_specs=[pl.BlockSpec(memory_space=pltpu.SMEM)] + [vmem] * 3,
        out_specs=[vmem] * len(widths),
        out_shape=[shaped(F32, 4 * own.shape[0], width) for width in widths],
        name="join_quarters",
        compiler_params=limit(8),
        cost_estimate=HINT,
    )(place, own, one, two)


def chips_join_kernel(place_ref, mine_a, mine_b, got_a, got_b, ends_ref, got_ends, out_ref, *outs):
    core, here_x, here_y = place_ref[1], place_ref[2], place_ref[3]
    cut = mine_a.shape[2]
    size = cut + mine_b.shape[2]
    for far_y in range(2):
        for far_x in range(2):
            chip = (here_y ^ far_y) * 2 + (here_x ^ far_x)
            for side, a_ref, b_ref in ((core, mine_a, mine_b), (1 - core, got_a, got_b)):
                at = (chip * 2 + side) * size
                first = pl.multiple_of(at, 8)
                out_ref[pl.ds(first, cut), :] = a_ref[far_y, far_x].astype(F32)
                second = pl.multiple_of(at + cut, 8)
                out_ref[pl.ds(second, size - cut), :] = b_ref[far_x, far_y].astype(F32)
    total = ends_ref[...].astype(F32) + got_ends[...].astype(F32)
    bias_ref, tables_ref, inner_ref = outs[:3]
    vectors = outs[3:]
    here = (here_y * 2 + here_x) * 2 + core
    width = total.shape[1]
    share = vectors[0].shape[1]
    part = inner_ref.shape[1]
    deep = part * 8 // width
    slices = jnp.zeros((len(vectors), share), F32)
    inner = jnp.zeros((1, part), F32)
    for d in range(8):
        mine = here == d
        slices = slices + jnp.where(
            mine, total[0 : len(vectors), d * share : (d + 1) * share], 0.0
        )
        row, lane = 6 + d * part // width, d * part % width
        inner = inner + jnp.where(mine, total[row : row + 1, lane : lane + part], 0.0)
    inner_ref[...] = inner
    for n, ref in enumerate(vectors):
        ref[...] = slices[n : n + 1, :]
    short = total[6 + deep : 7 + deep, :]
    own = bias_ref.shape[1]
    bias_ref[0:1, :] = short[:, 0:own]
    bias_ref[1:2, :] = short[:, own : 2 * own]
    per, _, buckets = tables_ref.shape
    for n in range(2):
        for h in range(per):
            lane = 2 * own + (n * per + h) * buckets
            tables_ref[h, n : n + 1, :] = short[:, lane : lane + buckets]


def join_chips(place, mine_a, mine_b, got_a, got_b, ends, got_ends, units, own, heads, buckets):
    vmem = pl.BlockSpec(memory_space=pltpu.VMEM)
    rows = 8 * (mine_a.shape[2] + mine_b.shape[2])
    width = mine_a.shape[-1]
    out_shape = [
        shaped(F32, rows, width),
        shaped(F32, 2, own),
        shaped(F32, heads, 2, buckets),
        shaped(F32, 1, units // 8),
    ] + [shaped(F32, 1, width // 8)] * 6
    return pl.pallas_call(
        chips_join_kernel,
        in_specs=[pl.BlockSpec(memory_space=pltpu.SMEM)] + [vmem] * 6,
        out_specs=[vmem] * len(out_shape),
        out_shape=out_shape,
        name="join_chips",
        compiler_params=limit(8),
        cost_estimate=HINT,
    )(place, mine_a, mine_b, got_a, got_b, ends, got_ends)


def tie(values, *others):
    return lax.optimization_barrier((values, others))[0]


def swap(array, bit):
    count = lax.axis_size("docs")
    return lax.ppermute(array, "docs", [(i, i ^ (1 << bit)) for i in range(count)])


def away(array, distance):
    count = lax.axis_size("heads")
    return lax.ppermute(array, "heads", [(i, i ^ distance) for i in range(count)])


def in_order(pieces, z):
    stacked = jnp.stack(pieces)
    picks = [lax.dynamic_index_in_dim(stacked, z ^ s, 0) for s in range(len(pieces))]
    return jnp.concatenate(picks, axis=0)


def tree(items):
    while len(items) > 1:
        items = [items[n] + items[n + 1] for n in range(0, len(items), 2)]
    return items[0]


def sum_everywhere(rows):
    for bit in range(lax.axis_size("docs").bit_length() - 1):
        rows = rows + swap(rows, bit)
    return tree([rows] + [away(rows, s) for s in range(1, lax.axis_size("heads"))])


def spread_plane(first, second):
    got = [swap(first, 1), swap(second, 2)]
    first, second = jnp.stack([first, got[0]]), jnp.stack([second, got[1]])
    got = [swap(first, 2), swap(second, 1)]
    return jnp.stack([first, got[0]]), jnp.stack([second, got[1]])


def reduce_docs(blocks):
    bits = blocks.shape[0].bit_length() - 1
    docs = lax.axis_index("docs")
    current = blocks.reshape((2,) * bits + blocks.shape[1:])
    for bit in range(bits):
        mine = (docs >> bit) & 1
        axis = bits - 1 - bit
        sent = lax.dynamic_index_in_dim(current, 1 - mine, axis, keepdims=False)
        kept = lax.dynamic_index_in_dim(current, mine, axis, keepdims=False)
        current = total_of(kept, swap(sent, bit))
    return current


def spread_docs(block):
    count = lax.axis_size("docs")
    docs = lax.axis_index("docs")
    current = block
    for done, bit in enumerate(range(count.bit_length() - 2, -1, -1)):
        got = swap(current, bit)
        mine = ((docs >> bit) & 1) == 1
        current = jnp.stack(
            [jnp.where(mine, got, current), jnp.where(mine, current, got)], axis=done
        )
    return current.reshape((count,) + block.shape)


def body(
    layer_input, token_boxes, lengths, w_qkv, qv_bias, rel_tables, w_out, out_bias,
    gain_one, shift_one, w_in, in_bias, w_back, back_bias, gain_two, shift_two, cotangent,
):
    width = layer_input.shape[1]
    units = w_in.shape[1]
    groups = lax.axis_size("heads")
    count = lax.axis_size("docs")
    docs = lax.axis_index("docs")
    z = lax.axis_index("heads")
    own = w_qkv.shape[2]
    heads = rel_tables.shape[1]
    buckets = rel_tables.shape[2]
    columns = 3 * own
    share = width // count
    small = columns // count
    chips = 4 if count == 8 and share % 16 == 0 and small % 8 == 0 else 0
    place = jnp.stack([z, docs & 1, (docs >> 1) & 1, (docs >> 2) & 1]).astype(I32)

    matrix = w_qkv.transpose(1, 2, 0).reshape(columns, width)
    room = jnp.zeros((128 - heads * buckets,), BF)
    line = jnp.concatenate(
        [qv_bias[0], qv_bias[1], rel_tables[0].reshape(-1), room, rel_tables[1].reshape(-1), room]
    )
    extra = jnp.pad(line[None], ((0, 7), (0, width - line.shape[0])))
    piece = jnp.concatenate(
        [lax.dynamic_slice_in_dim(matrix, docs * small, small, axis=0), extra], axis=0
    )
    got = [away(piece, s) for s in range(1, groups)]
    bucket, near = buckets_of(place, lengths, token_boxes)

    ctx_own, turned_own, raised_own, qkv_own, norm_own = attend_forward(
        place, layer_input, (matrix[None],), extra[None], bucket, near
    )
    arrived = jnp.stack(tie(got, ctx_own))
    if chips:
        cut = (small // 2 + 7) // 8 * 8
        first, second = spread_plane(arrived[:, :cut], arrived[:, cut:small])
        weights, ctx, turned, raised, qkv, norm = attend_forward(
            place, layer_input, (first, second, swap(first, 0), swap(second, 0)),
            arrived[:, small:], bucket, near,
        )
    else:
        weights = spread_docs(arrived[:, :small]).transpose(1, 0, 2, 3)
        weights = weights.reshape(groups - 1, columns, width)
        ctx, turned, raised, qkv, norm = attend_forward(
            place, layer_input, (weights,), arrived[:, small:], bucket, near
        )

    w_out_heads = w_out.reshape(groups, own, width)
    flat = lambda vector: vector.reshape(1, -1)
    layer_output, grad_mid, grad_branch, acted, slope, unit, inverse, low, up_sums = feed_up(
        place, layer_input, ctx_own, ctx, w_out_heads, flat(out_bias), flat(gain_one),
        flat(shift_one), w_in, flat(in_bias), w_back, flat(back_bias), flat(gain_two),
        flat(shift_two), cotangent,
    )
    down = lambda branch: feed_down(
        place, chips, branch, slope, w_back, w_in, low, grad_mid, unit, inverse, flat(gain_one),
        w_out_heads, turned_own, turned, norm_own, norm,
    )
    own_back = lambda grad, start: attend_backward(
        place, chips, layer_input, matrix[None], qkv_own, raised_own, norm_own, grad, start
    )
    rest_back = lambda span, grad, start: attend_backward(
        place, chips, layer_input, weights, qkv, raised, norm, grad, start, span
    )

    if chips:
        half = share // 2
        back_size = units // count
        sent = product(place, acted, grad_branch, (chips, back_size, True))
        got = swap(sent.reshape(chips, back_size, width), 0)
        back = product_kept(place, acted, grad_branch, got)
        back_got = [swap(back[0], 1), swap(back[2], 2)]

        in_sums, grad_first, grad_own, grad_rest, down_sums, dense_sent, dense_kept = down(
            tie(grad_branch, back[0], back[2])
        )
        back_got = tie(back_got, grad_first)
        back = sum_pairs(place, back[1], back_got[0], back[3], back_got[1], width // 2)
        back_got = [swap(back[0], 2), swap(back[2], 1)]
        dense_sent = tie(dense_sent, back[0])
        dense_got = swap(dense_sent, 0)

        dx, ds_own, sums_own, own_sent, own_kept = own_back(
            tie(grad_own, dense_sent, back[0], back[2]), grad_first
        )
        dense_got, back_got = tie((dense_got, back_got), dx)
        dense = sum_chips(
            place,
            [(dense_kept[None], dense_got[None])],
            (("x", ((0, 0, half),)), ("y", ((0, half, share),))),
            (units + width) // 3,
        )
        back_sent, back = cut_quarters(
            place, back[1], back_got[0], back[3], back_got[1], width // 2
        )
        dense = list(dense)
        dense[0], dense[2], own_sent = tie((dense[0], dense[2], own_sent), back_sent)
        dense_got = [swap(dense[0], 1), swap(dense[2], 2)]
        back_got = away(back_sent, 1)
        own_got = swap(own_sent, 0)

        dx, ds_one, sums_one, one_sent, one_kept = rest_back(
            (0, 1), tie(grad_rest, dense[0], dense[2], own_sent, back_sent), dx
        )
        own_got, back_got = tie((own_got, back_got), dx)
        back = total_of(back, back_got)
        one_sent = tie(one_sent, back)
        one_got = swap(one_sent, 0)
        back_got = away(back[1], 2)

        dx, ds_two, sums_two, two_sent, two_kept = rest_back(
            (1, 3), tie(grad_rest, one_sent, back), dx
        )
        dense_got, back_got, one_got = tie((dense_got, back_got, one_got), dx)
        dense = list(
            sum_pairs(
                place, dense[1], dense_got[0], dense[3], dense_got[1], (units + width) // 2
            )
        )
        back = total_of(back[0], back_got)
        two_sent, dense[0], dense[2], back = tie((two_sent, dense[0], dense[2], back), dense[1])
        two_got = swap(two_sent, 0)
        dense_got = [swap(dense[0], 2), swap(dense[2], 1)]
        back_one = away(back, 2)
        scores = (ds_own, ds_one, ds_two)
        acc = table_products(
            scores, tie(bucket, back, two_sent, dense[0], dense[2]),
            jnp.zeros((groups * heads * 8, 512), F32), 0,
        )

        two_got, dense_got, back_one = tie((two_got, dense_got, back_one), acc)
        dense_sent, dense = cut_quarters(
            place, dense[1], dense_got[0], dense[3], dense_got[1], (units + width) // 2
        )
        own_got, one_got, two_got = tie((own_got, one_got, two_got), dense_sent)
        last_a = sum_chips(
            place, [(own_kept, own_got), (one_kept, one_got)],
            (("x", ((0, 0, small), (1, 0, small))),), width // 2,
        )
        last_b = sum_chips(place, [(two_kept, two_got)], (("y", ((0, 0, small),)),), width // 2)
        back_two = jnp.stack([back, back_one])
        last_a, last_b, dense_sent, back_two = tie((last_a, last_b, dense_sent, back_two))
        last_a_got = swap(last_a[0], 1)
        last_b_got = swap(last_b[0], 2)
        dense_got = away(dense_sent, 1)
        back_two = away(back_two, 1)
        acc = table_products(
            scores, tie(bucket, last_b[0], last_a[0], dense_sent), acc, 1
        )
        short = short_rows(acc, (sums_own, sums_one, sums_two), down_sums, up_sums, in_sums, heads)

        last_a_got, last_b_got, dense_got = tie((last_a_got, last_b_got, dense_got), acc)
        last = list(sum_pairs(place, last_a[1], last_a_got, last_b[1], last_b_got, width // 2))
        dense = total_of(dense, dense_got)
        last[0], last[2], dense = tie((last[0], last[2], dense), last[1])
        last_got = [swap(last[0], 2), swap(last[2], 1)]
        dense_got = away(dense[1], 2)
        last_got, short = tie((last_got, short), dense)
        last = cut_last(last[1], last_got[0], last[3], last_got[1], short)
        last_got = [away(last[s], s) for s in range(1, groups)]
        dense_got, back_two = tie((dense_got, back_two), last[0])
        dense = total_of(dense[0], dense_got)
        dense_one = away(dense, 2)
        (out_back,) = join_quarters(place, back, back_one, back_two, (width,))
        last_got = tie(last_got, dense, out_back)
        quarter = total_of(last[0][:small], *[item[:small] for item in last_got])
        ends = tree([item[small:].astype(F32) for item in [last[0]] + last_got]).astype(BF)
        first, second = quarter[:cut], quarter[cut:]
        got = [swap(first, 1), swap(second, 2), swap(ends, 1)]
        dense_one = tie(dense_one, first, second)
        dense_two = away(jnp.stack([dense, dense_one]), 1)
        got = tie(got, dense_one)
        first, second = jnp.stack([first, got[0]]), jnp.stack([second, got[1]])
        ends = total_of(ends, got[2])
        got = [swap(first, 2), swap(second, 1), swap(ends, 2)]
        dense_two = tie(dense_two, first, second)
        first, second = jnp.stack([first, got[0]]), jnp.stack([second, got[1]])
        ends = total_of(ends, got[2])
        got = [swap(first, 0), swap(second, 0), swap(ends, 0)]
        out_in, out_out = join_quarters(place, dense, dense_one, dense_two, (units, width))
        got = tie(got, out_in)
        full, grad_bias, grad_tables, grad_inner, *vectors = join_chips(
            place, first, second, got[0], got[1], ends, got[2], units, own, heads, buckets
        )
        grad_tables = grad_tables.transpose(1, 0, 2)
        vectors = [vector.reshape(share) for vector in vectors]
        grad_inner = grad_inner.reshape(units // count)
    else:
        back_grads = product(place, acted, grad_branch, (units // FC, FC, False))
        in_sums, grad_first, grad_own, grad_rest, down_sums, dense_grads = down(grad_branch)
        dx, ds_own, sums_own, dw_own = own_back(grad_own, grad_first)
        dx, ds_rest, sums_rest, dw_rest = rest_back(None, grad_rest, dx)
        acc = jnp.zeros((groups * heads * 8, 512), F32)
        for part in range(2):
            acc = table_products((ds_own, ds_rest), bucket, acc, part)
        short = short_rows(acc, (sums_own, sums_rest), down_sums, up_sums, in_sums, heads)
        begin = 6 + units // width
        quarters = in_order([short[begin + s] for s in range(groups)], z)
        total = sum_everywhere(jnp.concatenate([short[:begin], quarters], axis=0))
        ends = lax.dynamic_index_in_dim(total, begin + z, 0, keepdims=False)

        def sum_heads(parts):
            return total_of(parts[0], *[away(parts[s], s) for s in range(1, groups)])

        def dense_rows(grads):
            rows = reduce_docs(grads.reshape(count, -1, grads.shape[1]))
            parts = rows.reshape(-1, groups, width)
            parts = [
                lax.dynamic_index_in_dim(parts, z ^ s, 1, keepdims=False) for s in range(groups)
            ]
            mine = sum_heads(parts)
            pieces = [mine] + [away(mine, s) for s in range(1, groups)]
            return in_order(pieces, z).transpose(1, 0, 2).reshape(rows.shape).astype(F32)

        out_back = dense_rows(back_grads)
        rows = dense_rows(dense_grads)
        out_in, out_out = rows[:, :units], rows[:, units:]
        blocks = jnp.concatenate([dw_own, dw_rest]).reshape(groups, count, small, width)
        blocks = blocks.transpose(1, 0, 2, 3).reshape(count, groups * small, width)
        blocks = reduce_docs(blocks).reshape(groups, small, width)
        full = spread_docs(sum_heads([blocks[s] for s in range(groups)]))
        full = full.reshape(columns, width).astype(F32)

        mine = lambda vector: lax.dynamic_slice_in_dim(
            vector, docs * (vector.shape[0] // count), vector.shape[0] // count
        )
        grad_bias = ends[: 2 * own].reshape(2, own)
        grad_tables = ends[2 * own : 2 * own + 2 * heads * buckets].reshape(2, heads, buckets)
        vectors = [mine(total[n]) for n in range(6)]
        grad_inner = mine(total[6:begin].reshape(-1))
    return (
        layer_output,
        dx.astype(BF),
        full.reshape(3, own, width).transpose(2, 0, 1),
        grad_bias,
        grad_tables,
        out_out,
        vectors[2],
        vectors[0],
        vectors[1],
        out_in,
        grad_inner,
        out_back,
        vectors[5],
        vectors[3],
        vectors[4],
    )


def solution(mesh):
    rows = P(("docs", "heads"), None)
    return jax.shard_map(
        body,
        mesh=mesh,
        in_specs=(
            rows,
            P(None, "docs"),
            P("docs"),
            P(None, None, "heads"),
            P(None, "heads"),
            P(None, "heads", None),
            P(),
            P(),
            P(),
            P(),
            P(),
            P(),
            P(),
            P(),
            P(),
            P(),
            rows,
        ),
        out_specs=(
            rows,
            rows,
            P(None, None, "heads"),
            P(None, "heads"),
            P(None, "heads", None),
            P("docs", None),
            P("docs"),
            P("docs"),
            P("docs"),
            P("docs", None),
            P("docs"),
            P("docs", None),
            P("docs"),
            P("docs"),
            P("docs"),
        ),
        check_vma=False,
    )
```

```python
import functools
import math

import jax
import jax.numpy as jnp
from jax import lax
from jax.experimental import pallas as pl
from jax.experimental.pallas import tpu as pltpu
from jax.sharding import PartitionSpec as P

HEAD_DIM = 64
L = 512
EPS = 1e-05
NEG = -1000000000.0
THRESHOLDS = (1, 2, 3, 4, 6, 8, 12, 16, 24, 32, 48, 64, 96, 128, 192)
ROOT_HALF = 1.0 / math.sqrt(2.0)
DENSITY_SCALE = 1.0 / math.sqrt(2.0 * math.pi)
SCALE = 0.125
KC = 32
QB = 128
RT = 32
FC = 768
MB = 256
BF = jnp.bfloat16
F32 = jnp.float32
I32 = jnp.int32
NT = (((1,), (1,)), ((), ()))


def whole(*shape):
    return pl.BlockSpec(shape, lambda *_: (0,) * len(shape))


def limit(mebibytes):
    return pltpu.CompilerParams(vmem_limit_bytes=mebibytes << 20)


HINT = pl.CostEstimate(flops=1, bytes_accessed=1, transcendentals=0)


def shaped(dtype, *shape):
    return jax.ShapeDtypeStruct(shape, dtype)


def first_bucket_of(offset):
    distance = jnp.abs(offset)
    count = jnp.where(offset > 0, 16, 0).astype(I32)
    for threshold in THRESHOLDS:
        count = count + jnp.where(distance >= threshold, 1, 0).astype(I32)
    return count


def second_bucket_of(across, upward):
    horizontal = jnp.zeros(across.shape, I32)
    for threshold in (-128, -32, -8, 0):
        horizontal = horizontal + jnp.where(across >= threshold, 1, 0)
    for threshold in (8, 32, 128):
        horizontal = horizontal + jnp.where(across > threshold, 1, 0)
    vertical = (
        jnp.where(upward >= -24, 8, 0)
        + jnp.where(upward >= 0, 8, 0)
        + jnp.where(upward > 24, 8, 0)
    )
    return vertical + horizontal


PLACE = ("heads", "core", "x", "y")


def bucket_kernel(place_ref, len_ref, box_ref, out_ref, near_ref, turned_sc):
    filled = len_ref[place_ref[0]]
    boxes = box_ref[...].astype(F32)
    turned_sc[...] = jnp.transpose(jnp.concatenate([boxes] * 4, axis=0)).astype(I32)
    size = 64

    @pl.loop(0, L // size)
    def _(step):
        start = pl.multiple_of(step * size, size)
        rows = pl.ds(start, size)
        across = turned_sc[rows, 0:1] - box_ref[0:1, :]
        upward = turned_sc[rows, 1:2] - box_ref[1:2, :]
        key = lax.broadcasted_iota(I32, (size, L), 0) + start
        out_ref[rows, :] = jnp.where(key < filled, second_bucket_of(across, upward), 32)

    @pl.loop(0, near_ref.shape[0])
    def _(tile):
        offset = (
            128 * (tile - 2)
            + lax.broadcasted_iota(I32, (128, 128), 0)
            - lax.broadcasted_iota(I32, (128, 128), 1)
        )
        near_ref[tile] = first_bucket_of(offset)


def buckets_of(place, lengths, boxes):
    return pl.pallas_call(
        bucket_kernel,
        grid_spec=pltpu.PrefetchScalarGridSpec(
            num_scalar_prefetch=2,
            grid=(1,),
            in_specs=[pl.BlockSpec((2, L), lambda i, place, lengths: (0, place[0]))],
            out_specs=[whole(L, L), whole(5, 128, 128)],
            scratch_shapes=[pltpu.VMEM((L, 8), I32)],
        ),
        out_shape=[shaped(I32, L, L), shaped(I32, 5, 128, 128)],
        name="buckets",
        compiler_params=limit(6),
        cost_estimate=HINT,
    )(place, lengths, boxes)


def lookup(table_row, index):
    table = jnp.broadcast_to(table_row, (index.shape[0], 128))
    return jnp.concatenate(
        [
            jnp.take_along_axis(
                table, index[:, c : c + 128], axis=1, mode="promise_in_bounds"
            )
            for c in range(0, index.shape[1], 128)
        ],
        axis=1,
    )


def head_window(head, width):
    start = head * HEAD_DIM // 128 * 128
    return start, min(128, width - start), head * HEAD_DIM - start


def eights(rows):
    return rows.reshape(rows.shape[0] // 8, 8, rows.shape[1])


def column(row):
    return jnp.transpose(jnp.broadcast_to(row, (8, row.shape[1])))[:, 0:1]


def forward_kernel(gathered, place_ref, x_ref, *refs):
    sources = refs[: 4 if gathered else 1]
    extra_ref, bucket_ref, index_ref = refs[len(sources) : len(sources) + 3]
    rest = refs[len(sources) + 3 :]
    if gathered:
        w_ref, rest = rest[0], rest[1:]
    else:
        w_ref = sources[0]
    ctx_ref, turned_ref, raised_ref, qkv_ref, inverse_ref = rest[:5]
    near_sc, score_sc, query_sc, key_sc = rest[5:9]
    heads = raised_ref.shape[1]
    width = heads * HEAD_DIM

    @pl.when(pl.program_id(0) == 0)
    def _():
        query_sc[...] = jnp.zeros_like(query_sc)

    if gathered:
        whole_sc = rest[9]
        core, here_x, here_y = place_ref[1], place_ref[2], place_ref[3]
        cut = sources[0].shape[3]
        size = cut + sources[1].shape[3]
        for far_y in range(2):
            for far_x in range(2):
                chip = (here_y ^ far_y) * 2 + (here_x ^ far_x)
                for side, pair in ((core, sources[:2]), (1 - core, sources[2:])):
                    at = (chip * 2 + side) * size
                    first = pl.multiple_of(at, 8)
                    whole_sc[pl.ds(first, cut), :] = pair[0][far_y, far_x, 0].astype(F32)
                    second = pl.multiple_of(at + cut, 8)
                    whole_sc[pl.ds(second, size - cut), :] = pair[1][far_x, far_y, 0].astype(F32)
        w_ref[0] = whole_sc[...].astype(BF)

    extra = extra_ref[0, 0:1, :].astype(F32)
    query_bias, value_bias = extra[:, 0:width], extra[:, width : 2 * width]
    first_tables = extra[:, 2 * width : 2 * width + 128]
    second_tables = extra[:, 2 * width + 128 : 2 * width + 256]
    query = lax.dot_general(w_ref[0, 0:width, :], x_ref[...], NT, preferred_element_type=F32)
    qkv_ref[0, 0:width, :] = (query + column(query_bias)).astype(BF)
    key = lax.dot_general(
        w_ref[0, width : 2 * width, :], x_ref[...], NT, preferred_element_type=F32
    )
    qkv_ref[0, width : 2 * width, :] = key.astype(BF)
    value = lax.dot_general(
        w_ref[0, 2 * width : 3 * width, :], x_ref[...], NT, preferred_element_type=F32
    )
    qkv_ref[0, 2 * width : 3 * width, :] = (value + column(value_bias)).astype(BF)
    key_sc[...] = lax.dot_general(
        x_ref[...], w_ref[0, width : 2 * width, :], NT, preferred_element_type=F32
    ).astype(BF)
    inverse_ref[0] = jnp.zeros_like(inverse_ref[0])
    lane = lax.broadcasted_iota(I32, (1, 128), 1)
    for h in range(heads):
        c0, w, low = head_window(h, width)
        own = slice(h * HEAD_DIM, (h + 1) * HEAD_DIM)
        query_sc[h, low : low + HEAD_DIM, :] = qkv_ref[0, own, :] * jnp.asarray(SCALE, BF)
        row = first_tables if h == 0 else jnp.roll(first_tables, -32 * h, axis=1)
        other = second_tables if h == 0 else jnp.roll(second_tables, -32 * h, axis=1)
        other = jnp.where(lane < 32, other, NEG)
        for d in range(5):
            near_sc[h, d] = lookup(row, index_ref[d])
        far = {
            -3: jnp.broadcast_to(row[:, 15:16], (KC, 128)),
            3: jnp.broadcast_to(row[:, 31:32], (KC, 128)),
        }
        key = key_sc[:, c0 : c0 + w]
        for block in range(L // QB):
            cols = slice(block * QB, (block + 1) * QB)
            score_sc[h] = jnp.dot(key, query_sc[h, 0:w, cols], preferred_element_type=F32)
            peak = None
            for step in range(L // KC):
                rows = slice(step * KC, (step + 1) * KC)
                d, inner = step * KC // 128 - block, step * KC % 128
                near = far[d] if abs(d) == 3 else near_sc[h, d + 2, inner : inner + KC, :]
                scores = score_sc[h, rows, :] + near
                scores = scores + lookup(other, bucket_ref[rows, cols])
                score_sc[h, rows, :] = scores
                part = jnp.max(eights(scores), axis=0)
                peak = part if peak is None else jnp.maximum(peak, part)
            peak = jnp.max(peak, axis=0, keepdims=True)
            sums = None
            for step in range(L // KC):
                rows = slice(step * KC, (step + 1) * KC)
                raised = jnp.exp(score_sc[h, rows, :] - peak)
                raised_ref[0, h, rows, cols] = raised.astype(BF)
                part = jnp.sum(eights(raised), axis=0)
                sums = part if sums is None else sums + part
            inverse_ref[0, h : h + 1, cols] = 1.0 / jnp.sum(sums, axis=0, keepdims=True)
        at = 2 * width + h * HEAD_DIM
        out = jnp.dot(
            qkv_ref[0, at : at + HEAD_DIM, :], raised_ref[0, h], preferred_element_type=F32
        )
        turned_ref[0, own, :] = (out * inverse_ref[0, h : h + 1, :]).astype(BF)
    ctx_ref[0] = jnp.transpose(turned_ref[0])


def each(*shape):
    return pl.BlockSpec((1,) + shape, lambda g, *_: (g,) + (0,) * len(shape))


def attend_forward(place, x, sources, extra, bucket, near):
    gathered = len(sources) == 4
    groups, depth = extra.shape[0], x.shape[1]
    if gathered:
        columns = 8 * (sources[0].shape[3] + sources[1].shape[3])
        inputs = [
            pl.BlockSpec(
                (2, 2, 1) + source.shape[3:], lambda g, place: (0, 0, g, 0, 0)
            )
            for source in sources
        ]
    else:
        columns = sources[0].shape[1]
        inputs = [each(columns, depth)]
    heads = columns // (3 * HEAD_DIM)
    width = columns // 3
    out_specs = [
        each(L, width), each(width, L), each(heads, L, L), each(columns, L), each(8, L)
    ]
    out_shape = [
        shaped(BF, groups, L, width),
        shaped(BF, groups, width, L),
        shaped(BF, groups, heads, L, L),
        shaped(BF, groups, columns, L),
        shaped(F32, groups, 8, L),
    ]
    scratch = [
        pltpu.VMEM((heads, 5, 128, 128), F32),
        pltpu.VMEM((heads, L, QB), F32),
        pltpu.VMEM((heads, 128, L), BF),
        pltpu.VMEM((L, width), BF),
    ]
    if gathered:
        out_specs = [each(columns, depth)] + out_specs
        out_shape = [shaped(BF, groups, columns, depth)] + out_shape
        scratch = scratch + [pltpu.VMEM((columns, depth), F32)]
    return pl.pallas_call(
        functools.partial(forward_kernel, gathered),
        grid_spec=pltpu.PrefetchScalarGridSpec(
            num_scalar_prefetch=1,
            grid=(groups,),
            in_specs=[whole(L, depth)] + inputs + [each(8, depth), whole(L, L), whole(5, 128, 128)],
            out_specs=out_specs,
            scratch_shapes=scratch,
        ),
        out_shape=out_shape,
        name="attend_forward",
        compiler_params=limit(22),
        cost_estimate=HINT,
    )(place, x, *sources, extra, bucket, near)


def backward_kernel(
    halved, place_ref, x_ref, w_ref, qkv_ref, raised_ref, inverse_ref, grad_ref, start_ref, *refs
):
    outs = refs[: 5 if halved else 4]
    dx_ref, ds_ref, sums_ref = outs[:3]
    pad_sc, term_sc, rows_sc, turn_sc, value_sc = refs[len(outs) : len(outs) + 5]
    group = pl.program_id(0)
    heads = raised_ref.shape[1]
    width = heads * HEAD_DIM

    @pl.when(group == 0)
    def _():
        pad_sc[...] = jnp.zeros_like(pad_sc)
        dx_ref[...] = start_ref[...]

    value_sc[...] = jnp.transpose(qkv_ref[0, 2 * width : 3 * width, :])
    for h in range(heads):
        c0, w, low = head_window(h, width)
        own = slice(h * HEAD_DIM, (h + 1) * HEAD_DIM)
        pad_sc[h, low : low + HEAD_DIM, :] = grad_ref[0, own, :]
        value = value_sc[:, c0 : c0 + w]
        for block in range(L // QB):
            cols = slice(block * QB, (block + 1) * QB)
            term_sc[h] = jnp.dot(value, pad_sc[h, 0:w, cols], preferred_element_type=F32)
            sums = None
            for step in range(L // KC):
                rows = slice(step * KC, (step + 1) * KC)
                terms = term_sc[h, rows, :] * raised_ref[0, h, rows, cols].astype(F32)
                term_sc[h, rows, :] = terms
                part = jnp.sum(eights(terms), axis=0)
                sums = part if sums is None else sums + part
            inner = jnp.sum(sums, axis=0, keepdims=True) * inverse_ref[0, h : h + 1, cols]
            for step in range(L // KC):
                rows = slice(step * KC, (step + 1) * KC)
                raised = raised_ref[0, h, rows, cols].astype(F32)
                ds_ref[0, h, rows, cols] = (term_sc[h, rows, :] - raised * inner).astype(BF)
        scale = jnp.asarray(SCALE, BF)
        at = width + h * HEAD_DIM
        turn_sc[own, :] = jnp.dot(
            qkv_ref[0, at : at + HEAD_DIM, :] * scale, ds_ref[0, h], preferred_element_type=F32
        ).astype(BF)
        dk = lax.dot_general(
            ds_ref[0, h], qkv_ref[0, c0 : c0 + w, :] * scale, NT, preferred_element_type=F32
        )
        rows_sc[:, at : at + HEAD_DIM] = dk[:, low : low + HEAD_DIM].astype(BF)
        dv = lax.dot_general(
            raised_ref[0, h], grad_ref[0, c0 : c0 + w, :], NT, preferred_element_type=F32
        )
        at = 2 * width + h * HEAD_DIM
        rows_sc[:, at : at + HEAD_DIM] = dv[:, low : low + HEAD_DIM].astype(BF)
    rows_sc[:, 0:width] = jnp.transpose(turn_sc[0:width, :])
    turn_sc[width:, :] = jnp.transpose(rows_sc[:, width:])
    weights = jnp.dot(turn_sc[...], x_ref[...], preferred_element_type=F32)
    if halved:
        sent_ref, kept_ref = outs[3:]
        all_sc = refs[len(outs) + 5]
        all_sc[...] = weights
        core = place_ref[1]
        chips, size = kept_ref.shape[1], kept_ref.shape[2]
        for chip in range(chips):
            for side, ref in ((1 - core, sent_ref), (core, kept_ref)):
                at = pl.multiple_of((chip * 2 + side) * size, 8)
                ref[0, chip] = all_sc[pl.ds(at, size), :].astype(BF)
    else:
        outs[3][0] = weights.astype(BF)
    dx_ref[...] += jnp.dot(rows_sc[...], w_ref[0], preferred_element_type=F32)
    sums_ref[0] = jnp.sum(rows_sc[...].astype(F32), axis=0, keepdims=True)


def attend_backward(place, halves, x, w, qkv, raised, inverse, grad, start, span=None):
    columns, depth = w.shape[1:]
    skip, stop = span or (0, w.shape[0])
    groups = stop - skip
    some = lambda *shape: pl.BlockSpec(
        (1,) + shape, lambda g, *_: (g + skip,) + (0,) * len(shape)
    )
    heads = columns // (3 * HEAD_DIM)
    width = columns // 3
    out_specs = [whole(L, depth), each(heads, L, L), each(1, columns)]
    out_shape = [
        shaped(F32, L, depth),
        shaped(BF, groups, heads, L, L),
        shaped(F32, groups, 1, columns),
    ]
    scratch = [
        pltpu.VMEM((heads, 128, L), BF),
        pltpu.VMEM((heads, L, QB), F32),
        pltpu.VMEM((L, columns), BF),
        pltpu.VMEM((columns, L), BF),
        pltpu.VMEM((L, width), BF),
    ]
    if halves:
        size = columns // (2 * halves)
        out_specs += [each(halves, size, depth)] * 2
        out_shape += [shaped(BF, groups, halves, size, depth)] * 2
        scratch += [pltpu.VMEM((columns, depth), F32)]
    else:
        out_specs += [each(columns, depth)]
        out_shape += [shaped(BF, groups, columns, depth)]
    return pl.pallas_call(
        functools.partial(backward_kernel, bool(halves)),
        grid_spec=pltpu.PrefetchScalarGridSpec(
            num_scalar_prefetch=1,
            grid=(groups,),
            in_specs=[
                whole(L, depth),
                some(columns, depth),
                some(columns, L),
                some(heads, L, L),
                some(8, L),
                some(width, L),
                whole(L, depth),
            ],
            out_specs=out_specs,
            scratch_shapes=scratch,
        ),
        out_shape=out_shape,
        name="attend_backward",
        compiler_params=limit(26),
        cost_estimate=HINT,
    )(place, x, w, qkv, raised, inverse, grad, start)


def table_kernel(skip, *refs):
    bucket_ref, start_ref, acc_ref, hot_sc = refs[-4:]
    step = pl.program_id(0)
    blocks = [
        (ref, g, h) for ref in refs[:-4] for g in range(ref.shape[0]) for h in range(ref.shape[1])
    ]
    half = 32 * 8

    @pl.when(step == 0)
    def _():
        acc_ref[...] = start_ref[...]

    for u in range(RT // 8):
        part = slice(u * 8, (u + 1) * 8)
        second = bucket_ref[part, :]
        offset = (
            lax.broadcasted_iota(I32, (8, L), 0)
            + ((step + skip) * RT + u * 8)
            - lax.broadcasted_iota(I32, (8, L), 1)
        )
        first = first_bucket_of(offset)
        for t in range(0, 32, 2):
            for base, bucket in ((0, first), (half, second)):
                hot_sc[base + t * 8 : base + (t + 2) * 8, :] = jnp.concatenate(
                    [jnp.where(bucket == t, 1.0, 0.0), jnp.where(bucket == t + 1, 1.0, 0.0)],
                    axis=0,
                ).astype(BF)
        left = jnp.concatenate([ref[g, h, part, :] for ref, g, h in blocks], axis=0)
        acc_ref[...] += lax.dot_general(left, hot_sc[...], NT, preferred_element_type=F32)


def table_products(ds, bucket, start, part):
    heads = sum(item.shape[0] * item.shape[1] for item in ds)
    steps = L // RT // 2
    skip = part * steps
    return pl.pallas_call(
        functools.partial(table_kernel, skip),
        grid=(steps,),
        in_specs=[
            pl.BlockSpec(item.shape[:2] + (RT, L), lambda r: (0, 0, r + skip, 0)) for item in ds
        ]
        + [pl.BlockSpec((RT, L), lambda r: (r + skip, 0)), whole(heads * 8, 512)],
        out_specs=whole(heads * 8, 512),
        out_shape=shaped(F32, heads * 8, 512),
        scratch_shapes=[pltpu.VMEM((512, L), BF)],
        name="table_products",
        compiler_params=limit(14),
        cost_estimate=HINT,
    )(*ds, bucket, start)


def short_kernel(per, count, *refs):
    acc_ref, sums = refs[0], refs[1 : 1 + count]
    down_ref, up_ref, in_ref, out_ref = refs[1 + count :]
    heads = acc_ref.shape[0] // 8
    half = 32 * 8
    shape = (heads * 8, 2 * half)
    same = lax.broadcasted_iota(I32, shape, 0) % 8 == lax.broadcasted_iota(I32, shape, 1) % 8
    kept = jnp.where(same, acc_ref[...], 0.0)
    fold = (2 * half, 64)
    right = (
        lax.broadcasted_iota(I32, fold, 0) // 8 == lax.broadcasted_iota(I32, fold, 1)
    ).astype(F32)
    spread = (16, heads * 8)
    left = (
        lax.broadcasted_iota(I32, spread, 1) // 8 == lax.broadcasted_iota(I32, spread, 0)
    ).astype(F32)
    exact = lax.Precision.HIGHEST
    folded = jnp.dot(kept, right, preferred_element_type=F32, precision=exact)
    tables = jnp.dot(left, folded, preferred_element_type=F32, precision=exact)
    wide = 2 * per * 32
    lanes = None
    for h in range(per):
        shape = (8, 16)
        rows = (
            lax.broadcasted_iota(I32, shape, 1) == lax.broadcasted_iota(I32, shape, 0) * per + h
        ).astype(F32)
        shape = (64, wide)
        source, target = lax.broadcasted_iota(I32, shape, 0), lax.broadcasted_iota(I32, shape, 1)
        moved = jnp.where(source < 32, source + h * 32, source + (per - 1 + h) * 32)
        part = jnp.dot(rows, tables, preferred_element_type=F32, precision=exact)
        part = jnp.dot(
            part, (target == moved).astype(F32), preferred_element_type=F32, precision=exact
        )
        lanes = part if lanes is None else lanes + part
    out_ref[...] = jnp.zeros_like(out_ref)
    out_ref[0:3, :] = down_ref[0:3, :]
    out_ref[3:6, :] = up_ref[0:3, :]
    width = out_ref.shape[1]
    deep = in_ref.shape[1] // width
    for n in range(deep):
        out_ref[6 + n : 7 + n, :] = in_ref[0:1, n * width : (n + 1) * width]
    group = 0
    for ref in sums:
        own = ref.shape[2] // 3
        for g in range(ref.shape[0]):
            row = slice(6 + deep + group, 7 + deep + group)
            out_ref[row, 0:own] = ref[g, :, 0:own]
            out_ref[row, own : 2 * own] = ref[g, :, 2 * own :]
            out_ref[row, 2 * own : 2 * own + wide] = lanes[group : group + 1, :]
            group += 1


def short_rows(acc, sums, down, up, inner, per):
    width = down.shape[1]
    rows = -(-(6 + inner.shape[1] // width + acc.shape[0] // 8 // per) // 8) * 8
    vmem = pl.BlockSpec(memory_space=pltpu.VMEM)
    return pl.pallas_call(
        functools.partial(short_kernel, per, len(sums)),
        in_specs=[vmem] * (4 + len(sums)),
        out_specs=vmem,
        out_shape=shaped(F32, rows, width),
        name="short_rows",
        compiler_params=limit(6),
        cost_estimate=HINT,
    )(acc, *sums, down, up, inner)


def mean_of(rows):
    return jnp.mean(rows, axis=-1, keepdims=True)


def normalize(rows):
    centred = rows - mean_of(rows)
    inverse = lax.rsqrt(mean_of(centred * centred) + EPS)
    return centred * inverse, inverse


def normalize_back(scaled, unit, inverse):
    return inverse * (scaled - mean_of(scaled) - unit * mean_of(scaled * unit))


def gelu_parts(values):
    size = jnp.abs(values)
    t = 1.0 / (1.0 + (0.3275911 * ROOT_HALF) * size)
    bell = jnp.exp(values * values * -0.5)
    series = 1.061405429
    for term in (-1.453152027, 1.421413741, -0.284496736, 0.254829592):
        series = term + t * series
    tail = (0.5 * t) * series * bell
    below = jnp.where(values >= 0, 1.0 - tail, tail)
    return values * below, below + values * (bell * DENSITY_SCALE)


def column_sum(rows):
    return jnp.sum(rows, axis=0, keepdims=True)


def up_kernel(
    place_ref, x_ref, ctx_own_ref, ctx_ref, wo_ref, bo_ref, g1_ref, s1_ref, wi_ref, bi_ref, wb_ref,
    bb_ref, g2_ref, s2_ref, cot_ref,
    out_ref, mid_ref, branch_ref, turned_ref, slope_ref, unit_ref, inverse_ref, low_ref, sums_ref,
    normed_sc, low_sc, acc_sc,
):
    step = pl.program_id(0)
    groups = wo_ref.shape[0]

    @pl.when(step == 0)
    def _():
        @pl.loop(0, L // MB)
        def _(r):
            rows = pl.ds(pl.multiple_of(r * MB, MB), MB)
            total = x_ref[rows, :].astype(F32) + bo_ref[...]
            for s in range(groups):
                ctx = ctx_own_ref[0, rows, :] if s == 0 else ctx_ref[s - 1, rows, :]
                quarter = place_ref[0] ^ s
                total = total + jnp.dot(ctx, wo_ref[quarter], preferred_element_type=F32)
            unit, inverse = normalize(total)
            unit_ref[rows, :] = unit
            inverse_ref[rows, :] = jnp.broadcast_to(inverse, (MB, 128))
            normed = unit * g1_ref[...] + s1_ref[...]
            normed_sc[rows, :] = normed
            low_sc[rows, :] = normed.astype(BF)

        low_ref[...] = jnp.transpose(low_sc[...])
        acc_sc[...] = jnp.zeros_like(acc_sc)

    @pl.loop(0, L // MB)
    def _(r):
        rows = pl.ds(pl.multiple_of(r * MB, MB), MB)
        pre = jnp.dot(low_sc[rows, :], wi_ref[...], preferred_element_type=F32) + bi_ref[...]
        acted, slope = gelu_parts(pre)
        acted = acted.astype(BF)
        slope_ref[rows, :] = slope.astype(BF)
        turned_ref[:, rows] = jnp.transpose(acted)
        acc_sc[rows, :] += jnp.dot(acted, wb_ref[...], preferred_element_type=F32)

    @pl.when(step == pl.num_programs(0) - 1)
    def _():
        sums_ref[...] = jnp.zeros_like(sums_ref)

        @pl.loop(0, L // MB)
        def _(r):
            rows = pl.ds(pl.multiple_of(r * MB, MB), MB)
            unit, inverse = normalize(normed_sc[rows, :] + (acc_sc[rows, :] + bb_ref[...]))
            out_ref[rows, :] = (unit * g2_ref[...] + s2_ref[...]).astype(BF)
            upstream = cot_ref[rows, :].astype(F32)
            middle = normalize_back(upstream * g2_ref[...], unit, inverse)
            mid_ref[rows, :] = middle
            branch = middle.astype(BF)
            branch_ref[rows, :] = branch
            sums_ref[0:1, :] += column_sum(upstream * unit)
            sums_ref[1:2, :] += column_sum(upstream)
            sums_ref[2:3, :] += column_sum(branch.astype(F32))


def feed_up(place, x, ctx_own, ctx, w_out, bo, g1, s1, w_in, bi, w_back, bb, g2, s2, cot):
    width = x.shape[1]
    units = w_in.shape[1]
    groups, own = w_out.shape[0], w_out.shape[1]
    row = whole(1, width)
    return pl.pallas_call(
        up_kernel,
        grid_spec=pltpu.PrefetchScalarGridSpec(
            num_scalar_prefetch=1,
            grid=(units // FC,),
            in_specs=[
                whole(L, width),
                whole(1, L, own),
                whole(groups - 1, L, own),
                whole(groups, own, width),
                row,
                row,
                row,
                pl.BlockSpec((width, FC), lambda n, place: (0, n)),
                pl.BlockSpec((1, FC), lambda n, place: (0, n)),
                pl.BlockSpec((FC, width), lambda n, place: (n, 0)),
                row,
                row,
                row,
                whole(L, width),
            ],
            out_specs=[
                whole(L, width),
                whole(L, width),
                whole(L, width),
                pl.BlockSpec((FC, L), lambda n, place: (n, 0)),
                pl.BlockSpec((L, FC), lambda n, place: (0, n)),
                whole(L, width),
                whole(L, 128),
                whole(width, L),
                whole(8, width),
            ],
            scratch_shapes=[
                pltpu.VMEM((L, width), F32),
                pltpu.VMEM((L, width), BF),
                pltpu.VMEM((L, width), F32),
            ],
        ),
        out_shape=[
            shaped(BF, L, width),
            shaped(F32, L, width),
            shaped(BF, L, width),
            shaped(BF, units, L),
            shaped(BF, L, units),
            shaped(F32, L, width),
            shaped(F32, L, 128),
            shaped(BF, width, L),
            shaped(F32, 8, width),
        ],
        name="feed_up",
        compiler_params=limit(32),
        cost_estimate=HINT,
    )(place, x, ctx_own, ctx, w_out, bo, g1, s1, w_in, bi, w_back, bb, g2, s2, cot)


def down_kernel(
    halved, place_ref, branch_ref, slope_ref, wb_ref, wi_ref, low_ref, mid_ref, unit_ref,
    inverse_ref, g1_ref, wo_ref, turned_own_ref, turned_ref, norm_own_ref, norm_ref, *refs
):
    bias_ref, first_ref, grad_own_ref, grad_ref, sums_ref = refs[:5]
    weight_refs = refs[5 : 7 if halved else 6]
    acc_sc, pre_sc, weight_sc = refs[-3:]
    step = pl.program_id(0)
    last = pl.num_programs(0) - 1
    groups, own = wo_ref.shape[0], wo_ref.shape[1]

    def give():
        if not halved:
            weight_refs[0][...] = weight_sc[...]
            return
        core = place_ref[1]
        chips, size = weight_refs[0].shape[0], weight_refs[0].shape[1]
        for chip in range(chips):
            for side, ref in ((1 - core, weight_refs[0]), (core, weight_refs[1])):
                at = pl.multiple_of((chip * 2 + side) * size, size)
                ref[chip] = weight_sc[pl.ds(at, size), :]

    @pl.when(step == 0)
    def _():
        acc_sc[...] = mid_ref[...]

    @pl.when(step < last)
    def _():
        total = None
        for r in range(L // MB):
            rows = slice(r * MB, (r + 1) * MB)
            pre = lax.dot_general(
                branch_ref[rows, :], wb_ref[...], NT, preferred_element_type=F32
            ) * slope_ref[rows, :].astype(F32)
            pre = pre.astype(BF)
            pre_sc[rows, :] = pre
            part = column_sum(pre.astype(F32))
            total = part if r == 0 else total + part
            acc_sc[rows, :] += lax.dot_general(
                pre, wi_ref[...], NT, preferred_element_type=F32
            )
        bias_ref[0:1, :] = total
        weight_sc[...] = jnp.dot(
            low_ref[...], pre_sc[...], preferred_element_type=F32
        ).astype(BF)
        give()

    @pl.when(step == last)
    def _():
        sums_ref[...] = jnp.zeros_like(sums_ref)

        @pl.loop(0, L // MB)
        def _(r):
            rows = pl.ds(pl.multiple_of(r * MB, MB), MB)
            hidden = acc_sc[rows, :]
            unit = unit_ref[rows, :]
            first = normalize_back(hidden * g1_ref[...], unit, inverse_ref[rows, 0:1])
            first_ref[rows, :] = first
            attended = first.astype(BF)
            pre_sc[rows, :] = attended
            sums_ref[0:1, :] += column_sum(hidden * unit)
            sums_ref[1:2, :] += column_sum(hidden)
            sums_ref[2:3, :] += column_sum(attended.astype(F32))

        def quarter_of(s, turned, norm, out):
            quarter = place_ref[0] ^ s
            at = pl.multiple_of(quarter * own, own)
            weight_sc[pl.ds(at, own), :] = jnp.dot(
                turned, pre_sc[...], preferred_element_type=F32
            ).astype(BF)
            grads = lax.dot_general(
                wo_ref[quarter], pre_sc[...], NT, preferred_element_type=F32
            )
            for h in range(own // HEAD_DIM):
                rows = slice(h * HEAD_DIM, (h + 1) * HEAD_DIM)
                out[rows, :] = (grads[rows, :] * norm[h : h + 1, :]).astype(BF)

        quarter_of(0, turned_own_ref[0], norm_own_ref[0], grad_own_ref.at[0])

        @pl.loop(1, groups)
        def _(s):
            quarter_of(s, turned_ref[s - 1], norm_ref[s - 1], grad_ref.at[s - 1])

        give()


def feed_down(place, halves, branch, slope, w_back, w_in, low, mid, unit, inverse, g1, w_out,
              turned_own, turned, norm_own, norm):
    width = branch.shape[1]
    units = w_in.shape[1]
    groups, own = w_out.shape[0], w_out.shape[1]
    steps = units // FC
    inside = lambda n: jnp.minimum(n, steps - 1)
    out_specs = [
        pl.BlockSpec((8, FC), lambda n, place: (0, inside(n))),
        whole(L, width),
        whole(1, own, L),
        whole(groups - 1, own, L),
        whole(8, width),
    ]
    out_shape = [
        shaped(F32, 8, units),
        shaped(F32, L, width),
        shaped(BF, 1, own, L),
        shaped(BF, groups - 1, own, L),
        shaped(F32, 8, width),
    ]
    if halves:
        size = width // (2 * halves)
        out_specs += [pl.BlockSpec((halves, size, FC), lambda n, place: (0, 0, n))] * 2
        out_shape += [shaped(BF, halves, size, units + width)] * 2
    else:
        out_specs += [pl.BlockSpec((width, FC), lambda n, place: (0, n))]
        out_shape += [shaped(BF, width, units + width)]
    return pl.pallas_call(
        functools.partial(down_kernel, bool(halves)),
        grid_spec=pltpu.PrefetchScalarGridSpec(
            num_scalar_prefetch=1,
            grid=(steps + 1,),
            in_specs=[
                whole(L, width),
                pl.BlockSpec((L, FC), lambda n, place: (0, inside(n))),
                pl.BlockSpec((FC, width), lambda n, place: (inside(n), 0)),
                pl.BlockSpec((width, FC), lambda n, place: (0, inside(n))),
                whole(width, L),
                whole(L, width),
                whole(L, width),
                whole(L, 128),
                whole(1, width),
                whole(groups, own, width),
                whole(1, own, L),
                whole(groups - 1, own, L),
                whole(1, 8, L),
                whole(groups - 1, 8, L),
            ],
            out_specs=out_specs,
            scratch_shapes=[
                pltpu.VMEM((L, width), F32),
                pltpu.VMEM((L, FC), BF),
                pltpu.VMEM((width, FC), BF),
            ],
        ),
        out_shape=out_shape,
        name="feed_down",
        compiler_params=limit(34),
        cost_estimate=HINT,
    )(place, branch, slope, w_back, w_in, low, mid, unit, inverse, g1, w_out,
      turned_own, turned, norm_own, norm)


def product_kernel(place_ref, left_ref, right_ref, out_ref):
    out_ref[...] = jnp.dot(
        left_ref[...], right_ref[...], preferred_element_type=F32
    ).astype(BF)


def product(place, left, right, sizes):
    rows, depth = left.shape
    columns = right.shape[1]
    count, size, halved = sizes
    take = (lambda n, place: (2 * n + 1 - place[1], 0)) if halved else (lambda n, place: (n, 0))
    return pl.pallas_call(
        product_kernel,
        grid_spec=pltpu.PrefetchScalarGridSpec(
            num_scalar_prefetch=1,
            grid=(count,),
            in_specs=[pl.BlockSpec((size, depth), take), whole(depth, columns)],
            out_specs=pl.BlockSpec((size, columns), lambda n, place: (n, 0)),
        ),
        out_shape=shaped(BF, count * size, columns),
        name="back_weights",
        compiler_params=limit(10),
        cost_estimate=HINT,
    )(place, left, right)


def kept_kernel(place_ref, left_ref, right_ref, got_ref, a_sent, a_kept, b_sent, b_kept):
    chip = pl.program_id(0)
    chip_y, chip_x = chip // 2, lax.rem(chip, 2)
    here_x, here_y = place_ref[2], place_ref[3]
    value = jnp.dot(left_ref[...], right_ref[...], preferred_element_type=F32)
    value = (value + got_ref[0].astype(F32)).astype(BF)
    cut = a_sent.shape[1]

    @pl.when(chip_x == here_x)
    def _():
        a_kept[chip_y] = value[:cut, :]

    @pl.when(chip_x != here_x)
    def _():
        a_sent[chip_y] = value[:cut, :]

    @pl.when(chip_y == here_y)
    def _():
        b_kept[chip_x] = value[cut:, :]

    @pl.when(chip_y != here_y)
    def _():
        b_sent[chip_x] = value[cut:, :]


def product_kept(place, left, right, got):
    chips, size, columns = got.shape
    depth = left.shape[1]
    part = whole(2, size // 2, columns)
    return pl.pallas_call(
        kept_kernel,
        grid_spec=pltpu.PrefetchScalarGridSpec(
            num_scalar_prefetch=1,
            grid=(chips,),
            in_specs=[
                pl.BlockSpec((size, depth), lambda n, place: (2 * n + place[1], 0)),
                whole(depth, columns),
                pl.BlockSpec((1, size, columns), lambda n, place: (n, 0, 0)),
            ],
            out_specs=[part] * 4,
        ),
        out_shape=[shaped(BF, 2, size // 2, columns)] * 4,
        name="kept_weights",
        compiler_params=limit(14),
        cost_estimate=HINT,
    )(place, left, right, got)


def total_of(*items):
    total = items[0].astype(F32)
    for item in items[1:]:
        total = total + item.astype(F32)
    return total.astype(BF)


def chips_kernel(count, layout, place_ref, *refs):
    inputs, outs = refs[:count], refs[count:]
    here_x, here_y = place_ref[2], place_ref[3]
    for order, (way, sources) in enumerate(layout):
        sent, kept = outs[2 * order], outs[2 * order + 1]
        start = 0
        for number, low, high in sources:
            kept_ref, got_ref = inputs[2 * number], inputs[2 * number + 1]
            for g in range(kept_ref.shape[0]):
                rows = slice(start, start + high - low)
                start += high - low
                for other in range(2):
                    for out, far in ((sent, 1), (kept, 0)):
                        if way == "x":
                            chip = other * 2 + (here_x ^ far)
                        else:
                            chip = (here_y ^ far) * 2 + other
                        out[other, rows, :] = total_of(
                            kept_ref[g, chip, low:high, :], got_ref[g, chip, low:high, :]
                        )


def sum_chips(place, pairs, parts, block):
    specs, out_specs, out_shape = [], [], []
    columns = pairs[0][0].shape[-1]
    for kept, _ in pairs:
        shape = kept.shape[:3] + (block,)
        specs += [pl.BlockSpec(shape, lambda n, place: (0, 0, 0, n))] * 2
    for _, sources in parts:
        height = sum(pairs[n][0].shape[0] * (high - low) for n, low, high in sources)
        out_specs += [pl.BlockSpec((2, height, block), lambda n, place: (0, 0, n))] * 2
        out_shape += [shaped(BF, 2, height, columns)] * 2
    return pl.pallas_call(
        functools.partial(chips_kernel, 2 * len(pairs), parts),
        grid_spec=pltpu.PrefetchScalarGridSpec(
            num_scalar_prefetch=1, grid=(columns // block,), in_specs=specs, out_specs=out_specs
        ),
        out_shape=out_shape,
        name="sum_chips",
        compiler_params=limit(14),
        cost_estimate=HINT,
    )(place, *[item for pair in pairs for item in pair])


def pairs_kernel(place_ref, a_kept, a_got, b_kept, b_got, a_sent, a_own, b_sent, b_own):
    here_x, here_y = place_ref[2], place_ref[3]
    for here, kept, got, sent, own in (
        (here_y, a_kept, a_got, a_sent, a_own),
        (here_x, b_kept, b_got, b_sent, b_own),
    ):
        sent[...] = total_of(kept[1 - here], got[1 - here])
        own[...] = total_of(kept[here], got[here])


def sum_pairs(place, a_kept, a_got, b_kept, b_got, block):
    columns = a_kept.shape[-1]
    spec = lambda item: pl.BlockSpec((2, item.shape[1], block), lambda n, place: (0, 0, n))
    flat = lambda item: pl.BlockSpec((item.shape[1], block), lambda n, place: (0, n))
    return pl.pallas_call(
        pairs_kernel,
        grid_spec=pltpu.PrefetchScalarGridSpec(
            num_scalar_prefetch=1,
            grid=(columns // block,),
            in_specs=[spec(a_kept), spec(a_got), spec(b_kept), spec(b_got)],
            out_specs=[flat(a_kept)] * 2 + [flat(b_kept)] * 2,
        ),
        out_shape=[shaped(BF, a_kept.shape[1], columns)] * 2
        + [shaped(BF, b_kept.shape[1], columns)] * 2,
        name="sum_pairs",
        compiler_params=limit(12),
        cost_estimate=HINT,
    )(place, a_kept, a_got, b_kept, b_got)


def cut_kernel(place_ref, a_kept, a_got, b_kept, b_got, sent, kept, sum_sc):
    cut = a_kept.shape[0]
    sum_sc[0:cut, :] = a_kept[...].astype(F32) + a_got[...].astype(F32)
    sum_sc[cut:, :] = b_kept[...].astype(F32) + b_got[...].astype(F32)
    size = kept.shape[1]
    for s, out in ((0, kept.at[0]), (1, sent.at[0]), (2, kept.at[1]), (3, sent.at[1])):
        at = pl.multiple_of((place_ref[0] ^ s) * size, 8)
        out[...] = sum_sc[pl.ds(at, size), :].astype(BF)


def cut_quarters(place, a_kept, a_got, b_kept, b_got, block):
    columns = a_kept.shape[-1]
    height = a_kept.shape[0] + b_kept.shape[0]
    spec = lambda item: pl.BlockSpec((item.shape[0], block), lambda n, place: (0, n))
    return pl.pallas_call(
        cut_kernel,
        grid_spec=pltpu.PrefetchScalarGridSpec(
            num_scalar_prefetch=1,
            grid=(columns // block,),
            in_specs=[spec(a_kept), spec(a_got), spec(b_kept), spec(b_got)],
            out_specs=[pl.BlockSpec((2, height // 4, block), lambda n, place: (0, 0, n))] * 2,
            scratch_shapes=[pltpu.VMEM((height, block), F32)],
        ),
        out_shape=[shaped(BF, 2, height // 4, columns)] * 2,
        name="cut_quarters",
        compiler_params=limit(12),
        cost_estimate=HINT,
    )(place, a_kept, a_got, b_kept, b_got)


def halves_kernel(place_ref, a_kept, a_got, b_kept, b_got, *refs):
    outs, sum_sc = refs[:-1], refs[-1]
    cut = a_kept.shape[0]
    sum_sc[0:cut, :] = a_kept[...].astype(F32) + a_got[...].astype(F32)
    sum_sc[cut:, :] = b_kept[...].astype(F32) + b_got[...].astype(F32)
    size, wide = outs[0].shape[1:]
    for out, lanes, first, second in (
        (outs[0], slice(0, wide), 1, 3),
        (outs[1], slice(0, wide), 0, 2),
        (outs[2], slice(wide, 2 * wide), 2, 3),
        (outs[3], slice(wide, 2 * wide), 0, 1),
    ):
        for n, s in ((0, first), (1, second)):
            at = pl.multiple_of((place_ref[0] ^ s) * size, 8)
            out[n] = sum_sc[pl.ds(at, size), lanes].astype(BF)


def cut_halves(place, a_kept, a_got, b_kept, b_got):
    vmem = pl.BlockSpec(memory_space=pltpu.VMEM)
    columns = a_kept.shape[-1]
    height = a_kept.shape[0] + b_kept.shape[0]
    return pl.pallas_call(
        halves_kernel,
        in_specs=[pl.BlockSpec(memory_space=pltpu.SMEM)] + [vmem] * 4,
        out_specs=[vmem] * 4,
        out_shape=[shaped(BF, 2, height // 4, columns // 2)] * 4,
        scratch_shapes=[pltpu.VMEM((height, columns), F32)],
        name="cut_halves",
        compiler_params=limit(8),
        cost_estimate=HINT,
    )(place, a_kept, a_got, b_kept, b_got)


def last_kernel(a_kept, a_got, b_kept, b_got, short_ref, *outs):
    size = outs[0].shape[0] - 16
    many = short_ref.shape[0] // 8 * 8
    first = 10
    for s, out in enumerate(outs):
        rows = slice(s % 2 * size, (s % 2 + 1) * size)
        kept, got = (a_kept, a_got) if s < 2 else (b_kept, b_got)
        out[0:size, :] = total_of(kept[rows, :], got[rows, :])
        row = lax.broadcasted_iota(I32, (many, short_ref.shape[1]), 0)
        short = jnp.where(row < first, short_ref[...], 0.0)
        short = short + jnp.where(row == first, short_ref[first + s : first + s + 1, :], 0.0)
        out[size : size + many, :] = short.astype(BF)


def cut_last(a_kept, a_got, b_kept, b_got, short):
    vmem = pl.BlockSpec(memory_space=pltpu.VMEM)
    size, columns = b_kept.shape[0] // 2, b_kept.shape[1]
    return pl.pallas_call(
        last_kernel,
        in_specs=[vmem] * 5,
        out_specs=[vmem] * 4,
        out_shape=[shaped(BF, size + 16, columns)] * 4,
        name="cut_last",
        compiler_params=limit(8),
        cost_estimate=HINT,
    )(a_kept, a_got, b_kept, b_got, short)


def join_kernel(orders, place_ref, *refs):
    inputs, outs = refs[: 3 * len(orders)], refs[3 * len(orders) :]
    size, wide = inputs[0].shape
    start = 0
    for out in outs:
        done = 0
        while done < out.shape[1]:
            half, low = divmod(start + done, wide)
            many = min(wide - low, out.shape[1] - done)
            own, one, two = inputs[3 * half : 3 * half + 3]
            lanes = slice(low, low + many)
            near, far, farther = orders[half]
            for s, piece in (
                (0, own[:, lanes]), (near, one[:, lanes]), (far, two[0, :, lanes]),
                (farther, two[1, :, lanes]),
            ):
                at = pl.multiple_of((place_ref[0] ^ s) * size, 8)
                out[pl.ds(at, size), done : done + many] = piece.astype(F32)
            done += many
        start += out.shape[1]


def join_quarters(place, parts, orders, widths):
    vmem = pl.BlockSpec(memory_space=pltpu.VMEM)
    return pl.pallas_call(
        functools.partial(join_kernel, orders),
        in_specs=[pl.BlockSpec(memory_space=pltpu.SMEM)] + [vmem] * (3 * len(parts)),
        out_specs=[vmem] * len(widths),
        out_shape=[shaped(F32, 4 * parts[0][0].shape[0], width) for width in widths],
        name="join_quarters",
        compiler_params=limit(8),
        cost_estimate=HINT,
    )(place, *[item for part in parts for item in part])


def chips_join_kernel(place_ref, mine_a, mine_b, got_a, got_b, ends_ref, got_ends, out_ref, *outs):
    core, here_x, here_y = place_ref[1], place_ref[2], place_ref[3]
    cut = mine_a.shape[2]
    size = cut + mine_b.shape[2]
    for far_y in range(2):
        for far_x in range(2):
            chip = (here_y ^ far_y) * 2 + (here_x ^ far_x)
            for side, a_ref, b_ref in ((core, mine_a, mine_b), (1 - core, got_a, got_b)):
                at = (chip * 2 + side) * size
                first = pl.multiple_of(at, 8)
                out_ref[pl.ds(first, cut), :] = a_ref[far_y, far_x].astype(F32)
                second = pl.multiple_of(at + cut, 8)
                out_ref[pl.ds(second, size - cut), :] = b_ref[far_x, far_y].astype(F32)
    total = ends_ref[...].astype(F32) + got_ends[...].astype(F32)
    bias_ref, tables_ref, inner_ref = outs[:3]
    vectors = outs[3:]
    here = (here_y * 2 + here_x) * 2 + core
    width = total.shape[1]
    share = vectors[0].shape[1]
    part = inner_ref.shape[1]
    deep = part * 8 // width
    slices = jnp.zeros((len(vectors), share), F32)
    inner = jnp.zeros((1, part), F32)
    for d in range(8):
        mine = here == d
        slices = slices + jnp.where(
            mine, total[0 : len(vectors), d * share : (d + 1) * share], 0.0
        )
        row, lane = 6 + d * part // width, d * part % width
        inner = inner + jnp.where(mine, total[row : row + 1, lane : lane + part], 0.0)
    inner_ref[...] = inner
    for n, ref in enumerate(vectors):
        ref[...] = slices[n : n + 1, :]
    short = total[6 + deep : 7 + deep, :]
    own = bias_ref.shape[1]
    bias_ref[0:1, :] = short[:, 0:own]
    bias_ref[1:2, :] = short[:, own : 2 * own]
    per, _, buckets = tables_ref.shape
    for n in range(2):
        for h in range(per):
            lane = 2 * own + (n * per + h) * buckets
            tables_ref[h, n : n + 1, :] = short[:, lane : lane + buckets]


def join_chips(place, mine_a, mine_b, got_a, got_b, ends, got_ends, units, own, heads, buckets):
    vmem = pl.BlockSpec(memory_space=pltpu.VMEM)
    rows = 8 * (mine_a.shape[2] + mine_b.shape[2])
    width = mine_a.shape[-1]
    out_shape = [
        shaped(F32, rows, width),
        shaped(F32, 2, own),
        shaped(F32, heads, 2, buckets),
        shaped(F32, 1, units // 8),
    ] + [shaped(F32, 1, width // 8)] * 6
    return pl.pallas_call(
        chips_join_kernel,
        in_specs=[pl.BlockSpec(memory_space=pltpu.SMEM)] + [vmem] * 6,
        out_specs=[vmem] * len(out_shape),
        out_shape=out_shape,
        name="join_chips",
        compiler_params=limit(8),
        cost_estimate=HINT,
    )(place, mine_a, mine_b, got_a, got_b, ends, got_ends)


def tie(values, *others):
    return lax.optimization_barrier((values, others))[0]


def swap(array, bit):
    count = lax.axis_size("docs")
    return lax.ppermute(array, "docs", [(i, i ^ (1 << bit)) for i in range(count)])


def away(array, distance):
    count = lax.axis_size("heads")
    return lax.ppermute(array, "heads", [(i, i ^ distance) for i in range(count)])


def in_order(pieces, z):
    stacked = jnp.stack(pieces)
    picks = [lax.dynamic_index_in_dim(stacked, z ^ s, 0) for s in range(len(pieces))]
    return jnp.concatenate(picks, axis=0)


def tree(items):
    while len(items) > 1:
        items = [items[n] + items[n + 1] for n in range(0, len(items), 2)]
    return items[0]


def sum_everywhere(rows):
    for bit in range(lax.axis_size("docs").bit_length() - 1):
        rows = rows + swap(rows, bit)
    return tree([rows] + [away(rows, s) for s in range(1, lax.axis_size("heads"))])


def spread_plane(first, second):
    got = [swap(first, 1), swap(second, 2)]
    first, second = jnp.stack([first, got[0]]), jnp.stack([second, got[1]])
    got = [swap(first, 2), swap(second, 1)]
    return jnp.stack([first, got[0]]), jnp.stack([second, got[1]])


def reduce_docs(blocks):
    bits = blocks.shape[0].bit_length() - 1
    docs = lax.axis_index("docs")
    current = blocks.reshape((2,) * bits + blocks.shape[1:])
    for bit in range(bits):
        mine = (docs >> bit) & 1
        axis = bits - 1 - bit
        sent = lax.dynamic_index_in_dim(current, 1 - mine, axis, keepdims=False)
        kept = lax.dynamic_index_in_dim(current, mine, axis, keepdims=False)
        current = total_of(kept, swap(sent, bit))
    return current


def spread_docs(block):
    count = lax.axis_size("docs")
    docs = lax.axis_index("docs")
    current = block
    for done, bit in enumerate(range(count.bit_length() - 2, -1, -1)):
        got = swap(current, bit)
        mine = ((docs >> bit) & 1) == 1
        current = jnp.stack(
            [jnp.where(mine, got, current), jnp.where(mine, current, got)], axis=done
        )
    return current.reshape((count,) + block.shape)


def body(
    layer_input, token_boxes, lengths, w_qkv, qv_bias, rel_tables, w_out, out_bias,
    gain_one, shift_one, w_in, in_bias, w_back, back_bias, gain_two, shift_two, cotangent,
):
    width = layer_input.shape[1]
    units = w_in.shape[1]
    groups = lax.axis_size("heads")
    count = lax.axis_size("docs")
    docs = lax.axis_index("docs")
    z = lax.axis_index("heads")
    own = w_qkv.shape[2]
    heads = rel_tables.shape[1]
    buckets = rel_tables.shape[2]
    columns = 3 * own
    share = width // count
    small = columns // count
    chips = 4 if count == 8 and share % 16 == 0 and small % 8 == 0 else 0
    place = jnp.stack([z, docs & 1, (docs >> 1) & 1, (docs >> 2) & 1]).astype(I32)

    matrix = w_qkv.transpose(1, 2, 0).reshape(columns, width)
    room = jnp.zeros((128 - heads * buckets,), BF)
    line = jnp.concatenate(
        [qv_bias[0], qv_bias[1], rel_tables[0].reshape(-1), room, rel_tables[1].reshape(-1), room]
    )
    extra = jnp.pad(line[None], ((0, 7), (0, width - line.shape[0])))
    piece = jnp.concatenate(
        [lax.dynamic_slice_in_dim(matrix, docs * small, small, axis=0), extra], axis=0
    )
    got = [away(piece, s) for s in range(1, groups)]
    bucket, near = buckets_of(place, lengths, token_boxes)

    ctx_own, turned_own, raised_own, qkv_own, norm_own = attend_forward(
        place, layer_input, (matrix[None],), extra[None], bucket, near
    )
    arrived = jnp.stack(tie(got, ctx_own))
    if chips:
        cut = (small // 2 + 7) // 8 * 8
        first, second = spread_plane(arrived[:, :cut], arrived[:, cut:small])
        weights, ctx, turned, raised, qkv, norm = attend_forward(
            place, layer_input, (first, second, swap(first, 0), swap(second, 0)),
            arrived[:, small:], bucket, near,
        )
    else:
        weights = spread_docs(arrived[:, :small]).transpose(1, 0, 2, 3)
        weights = weights.reshape(groups - 1, columns, width)
        ctx, turned, raised, qkv, norm = attend_forward(
            place, layer_input, (weights,), arrived[:, small:], bucket, near
        )

    w_out_heads = w_out.reshape(groups, own, width)
    flat = lambda vector: vector.reshape(1, -1)
    layer_output, grad_mid, grad_branch, acted, slope, unit, inverse, low, up_sums = feed_up(
        place, layer_input, ctx_own, ctx, w_out_heads, flat(out_bias), flat(gain_one),
        flat(shift_one), w_in, flat(in_bias), w_back, flat(back_bias), flat(gain_two),
        flat(shift_two), cotangent,
    )
    down = lambda branch: feed_down(
        place, chips, branch, slope, w_back, w_in, low, grad_mid, unit, inverse, flat(gain_one),
        w_out_heads, turned_own, turned, norm_own, norm,
    )
    own_back = lambda grad, start: attend_backward(
        place, chips, layer_input, matrix[None], qkv_own, raised_own, norm_own, grad, start
    )
    rest_back = lambda span, grad, start: attend_backward(
        place, chips, layer_input, weights, qkv, raised, norm, grad, start, span
    )

    if chips:
        half = share // 2
        back_size = units // count
        sent = product(place, acted, grad_branch, (chips, back_size, True))
        got = swap(sent.reshape(chips, back_size, width), 0)
        back = product_kept(place, acted, grad_branch, got)
        back_got = [swap(back[0], 1), swap(back[2], 2)]

        in_sums, grad_first, grad_own, grad_rest, down_sums, dense_sent, dense_kept = down(
            tie(grad_branch, back[0], back[2])
        )
        back_got = tie(back_got, grad_first)
        back = sum_pairs(place, back[1], back_got[0], back[3], back_got[1], width // 2)
        back_got = [swap(back[0], 2), swap(back[2], 1)]
        dense_sent = tie(dense_sent, back[0])
        dense_got = swap(dense_sent, 0)

        dx, ds_own, sums_own, own_sent, own_kept = own_back(
            tie(grad_own, dense_sent, back[0], back[2]), grad_first
        )
        dense_got, back_got = tie((dense_got, back_got), dx)
        dense = sum_chips(
            place,
            [(dense_kept[None], dense_got[None])],
            (("x", ((0, 0, half),)), ("y", ((0, half, share),))),
            FC,
        )
        back_sent, back = cut_quarters(
            place, back[1], back_got[0], back[3], back_got[1], width // 2
        )
        dense = list(dense)
        dense[0], dense[2], own_sent = tie((dense[0], dense[2], own_sent), back_sent)
        dense_got = [swap(dense[0], 1), swap(dense[2], 2)]
        back_got = away(back_sent, 1)
        own_got = swap(own_sent, 0)

        dx, ds_one, sums_one, one_sent, one_kept = rest_back(
            (0, 1), tie(grad_rest, dense[0], dense[2], own_sent, back_sent), dx
        )
        own_got, back_got = tie((own_got, back_got), dx)
        back = total_of(back, back_got)
        one_sent = tie(one_sent, back)
        one_got = swap(one_sent, 0)
        back_got = away(back[1], 2)

        dx, ds_two, sums_two, two_sent, two_kept = rest_back(
            (1, 3), tie(grad_rest, one_sent, back), dx
        )
        dense_got, back_got, one_got = tie((dense_got, back_got, one_got), dx)
        dense = list(
            sum_pairs(
                place, dense[1], dense_got[0], dense[3], dense_got[1], (units + width) // 3
            )
        )
        back = total_of(back[0], back_got)
        two_sent, dense[0], dense[2], back = tie((two_sent, dense[0], dense[2], back), dense[1])
        two_got = swap(two_sent, 0)
        dense_got = [swap(dense[0], 2), swap(dense[2], 1)]
        back_one = away(back, 2)
        scores = (ds_own, ds_one, ds_two)
        acc = table_products(
            scores, tie(bucket, back, two_sent, dense[0], dense[2]),
            jnp.zeros((groups * heads * 8, 512), F32), 0,
        )

        two_got, dense_got, back_one = tie((two_got, dense_got, back_one), acc)
        dense = cut_halves(place, dense[1], dense_got[0], dense[3], dense_got[1])
        dense_sent, dense = [dense[0], dense[2]], [dense[1], dense[3]]
        own_got, one_got, two_got = tie((own_got, one_got, two_got), dense_sent)
        last_a = sum_chips(
            place, [(own_kept, own_got), (one_kept, one_got)],
            (("x", ((0, 0, small), (1, 0, small))),), width // 2,
        )
        last_b = sum_chips(place, [(two_kept, two_got)], (("y", ((0, 0, small),)),), width // 2)
        back_two = jnp.stack([back, back_one])
        last_a, last_b, dense_sent, back_two = tie((last_a, last_b, dense_sent, back_two))
        last_a_got = swap(last_a[0], 1)
        last_b_got = swap(last_b[0], 2)
        dense_got = [away(dense_sent[0], 1), away(dense_sent[1], 2)]
        back_two = away(back_two, 1)
        acc = table_products(
            scores, tie(bucket, last_b[0], last_a[0], dense_sent), acc, 1
        )
        short = short_rows(acc, (sums_own, sums_one, sums_two), down_sums, up_sums, in_sums, heads)

        last_a_got, last_b_got, dense_got = tie((last_a_got, last_b_got, dense_got), acc)
        last = list(sum_pairs(place, last_a[1], last_a_got, last_b[1], last_b_got, width // 2))
        dense = [total_of(*pair) for pair in zip(dense, dense_got)]
        last[0], last[2], dense = tie((last[0], last[2], dense), last[1])
        last_got = [swap(last[0], 2), swap(last[2], 1)]
        dense_got = [away(dense[0][1], 2), away(dense[1][1], 1)]
        last_got, short = tie((last_got, short), dense, back_two)
        last = cut_last(last[1], last_got[0], last[3], last_got[1], short)
        last_got = [away(last[s], s) for s in range(1, groups)]
        dense_got, back_two = tie((dense_got, back_two), last[0])
        dense = [total_of(item[0], got) for item, got in zip(dense, dense_got)]
        dense_one = [away(dense[0], 2), away(dense[1], 1)]
        (out_back,) = join_quarters(place, [(back, back_one, back_two)], ((2, 1, 3),), (width,))
        last_got = tie(last_got, dense, out_back)
        quarter = total_of(last[0][:small], *[item[:small] for item in last_got])
        ends = tree([item[small:].astype(F32) for item in [last[0]] + last_got]).astype(BF)
        first, second = quarter[:cut], quarter[cut:]
        got = [swap(first, 1), swap(second, 2), swap(ends, 1)]
        dense_one = tie(dense_one, first, second)
        dense_two = [jnp.stack(pair) for pair in zip(dense, dense_one)]
        dense_two = [away(dense_two[0], 1), away(dense_two[1], 2)]
        got = tie(got, dense_one)
        first, second = jnp.stack([first, got[0]]), jnp.stack([second, got[1]])
        ends = total_of(ends, got[2])
        got = [swap(first, 2), swap(second, 1), swap(ends, 2)]
        dense_two = tie(dense_two, first, second)
        first, second = jnp.stack([first, got[0]]), jnp.stack([second, got[1]])
        ends = total_of(ends, got[2])
        got = [swap(first, 0), swap(second, 0), swap(ends, 0)]
        out_in, out_out = join_quarters(
            place, list(zip(dense, dense_one, dense_two)), ((2, 1, 3), (1, 2, 3)), (units, width)
        )
        got = tie(got, out_in)
        full, grad_bias, grad_tables, grad_inner, *vectors = join_chips(
            place, first, second, got[0], got[1], ends, got[2], units, own, heads, buckets
        )
        grad_tables = grad_tables.transpose(1, 0, 2)
        vectors = [vector.reshape(share) for vector in vectors]
        grad_inner = grad_inner.reshape(units // count)
    else:
        back_grads = product(place, acted, grad_branch, (units // FC, FC, False))
        in_sums, grad_first, grad_own, grad_rest, down_sums, dense_grads = down(grad_branch)
        dx, ds_own, sums_own, dw_own = own_back(grad_own, grad_first)
        dx, ds_rest, sums_rest, dw_rest = rest_back(None, grad_rest, dx)
        acc = jnp.zeros((groups * heads * 8, 512), F32)
        for part in range(2):
            acc = table_products((ds_own, ds_rest), bucket, acc, part)
        short = short_rows(acc, (sums_own, sums_rest), down_sums, up_sums, in_sums, heads)
        begin = 6 + units // width
        quarters = in_order([short[begin + s] for s in range(groups)], z)
        total = sum_everywhere(jnp.concatenate([short[:begin], quarters], axis=0))
        ends = lax.dynamic_index_in_dim(total, begin + z, 0, keepdims=False)

        def sum_heads(parts):
            return total_of(parts[0], *[away(parts[s], s) for s in range(1, groups)])

        def dense_rows(grads):
            rows = reduce_docs(grads.reshape(count, -1, grads.shape[1]))
            parts = rows.reshape(-1, groups, width)
            parts = [
                lax.dynamic_index_in_dim(parts, z ^ s, 1, keepdims=False) for s in range(groups)
            ]
            mine = sum_heads(parts)
            pieces = [mine] + [away(mine, s) for s in range(1, groups)]
            return in_order(pieces, z).transpose(1, 0, 2).reshape(rows.shape).astype(F32)

        out_back = dense_rows(back_grads)
        rows = dense_rows(dense_grads)
        out_in, out_out = rows[:, :units], rows[:, units:]
        blocks = jnp.concatenate([dw_own, dw_rest]).reshape(groups, count, small, width)
        blocks = blocks.transpose(1, 0, 2, 3).reshape(count, groups * small, width)
        blocks = reduce_docs(blocks).reshape(groups, small, width)
        full = spread_docs(sum_heads([blocks[s] for s in range(groups)]))
        full = full.reshape(columns, width).astype(F32)

        mine = lambda vector: lax.dynamic_slice_in_dim(
            vector, docs * (vector.shape[0] // count), vector.shape[0] // count
        )
        grad_bias = ends[: 2 * own].reshape(2, own)
        grad_tables = ends[2 * own : 2 * own + 2 * heads * buckets].reshape(2, heads, buckets)
        vectors = [mine(total[n]) for n in range(6)]
        grad_inner = mine(total[6:begin].reshape(-1))
    return (
        layer_output,
        dx.astype(BF),
        full.reshape(3, own, width).transpose(2, 0, 1),
        grad_bias,
        grad_tables,
        out_out,
        vectors[2],
        vectors[0],
        vectors[1],
        out_in,
        grad_inner,
        out_back,
        vectors[5],
        vectors[3],
        vectors[4],
    )


def solution(mesh):
    rows = P(("docs", "heads"), None)
    return jax.shard_map(
        body,
        mesh=mesh,
        in_specs=(
            rows,
            P(None, "docs"),
            P("docs"),
            P(None, None, "heads"),
            P(None, "heads"),
            P(None, "heads", None),
            P(),
            P(),
            P(),
            P(),
            P(),
            P(),
            P(),
            P(),
            P(),
            P(),
            rows,
        ),
        out_specs=(
            rows,
            rows,
            P(None, None, "heads"),
            P(None, "heads"),
            P(None, "heads", None),
            P("docs", None),
            P("docs"),
            P("docs"),
            P("docs"),
            P("docs", None),
            P("docs"),
            P("docs", None),
            P("docs"),
            P("docs"),
            P("docs"),
        ),
        check_vma=False,
    )
```

```python
import functools
import math

import jax
import jax.numpy as jnp
from jax import lax
from jax.experimental import pallas as pl
from jax.experimental.pallas import tpu as pltpu
from jax.sharding import PartitionSpec as P

HEAD_DIM = 64
L = 512
EPS = 1e-05
NEG = -1000000000.0
THRESHOLDS = (1, 2, 3, 4, 6, 8, 12, 16, 24, 32, 48, 64, 96, 128, 192)
ROOT_HALF = 1.0 / math.sqrt(2.0)
DENSITY_SCALE = 1.0 / math.sqrt(2.0 * math.pi)
SCALE = 0.125
KC = 32
QB = 128
RT = 32
FC = 768
MB = 256
BF = jnp.bfloat16
F32 = jnp.float32
I32 = jnp.int32
NT = (((1,), (1,)), ((), ()))


def whole(*shape):
    return pl.BlockSpec(shape, lambda *_: (0,) * len(shape))


def in_hbm(dtype, *shape):
    return pltpu.HBM(shape, dtype)


def limit(mebibytes):
    return pltpu.CompilerParams(vmem_limit_bytes=mebibytes << 20)


HINT = pl.CostEstimate(flops=1, bytes_accessed=1, transcendentals=0)


def shaped(dtype, *shape):
    return jax.ShapeDtypeStruct(shape, dtype)


def first_bucket_of(offset):
    distance = jnp.abs(offset)
    count = jnp.where(offset > 0, 16, 0).astype(I32)
    for threshold in THRESHOLDS:
        count = count + jnp.where(distance >= threshold, 1, 0).astype(I32)
    return count


def second_bucket_of(across, upward):
    horizontal = jnp.zeros(across.shape, I32)
    for threshold in (-128, -32, -8, 0):
        horizontal = horizontal + jnp.where(across >= threshold, 1, 0)
    for threshold in (8, 32, 128):
        horizontal = horizontal + jnp.where(across > threshold, 1, 0)
    vertical = (
        jnp.where(upward >= -24, 8, 0)
        + jnp.where(upward >= 0, 8, 0)
        + jnp.where(upward > 24, 8, 0)
    )
    return vertical + horizontal


PLACE = ("heads", "core", "x", "y")


def bucket_kernel(place_ref, len_ref, box_ref, out_ref, near_ref, turned_sc):
    filled = len_ref[place_ref[0]]
    boxes = box_ref[...].astype(F32)
    turned_sc[...] = jnp.transpose(jnp.concatenate([boxes] * 4, axis=0)).astype(I32)
    size = 64

    @pl.loop(0, L // size)
    def _(step):
        start = pl.multiple_of(step * size, size)
        rows = pl.ds(start, size)
        across = turned_sc[rows, 0:1] - box_ref[0:1, :]
        upward = turned_sc[rows, 1:2] - box_ref[1:2, :]
        key = lax.broadcasted_iota(I32, (size, L), 0) + start
        out_ref[rows, :] = jnp.where(key < filled, second_bucket_of(across, upward), 32)

    @pl.loop(0, near_ref.shape[0])
    def _(tile):
        offset = (
            128 * (tile - 2)
            + lax.broadcasted_iota(I32, (128, 128), 0)
            - lax.broadcasted_iota(I32, (128, 128), 1)
        )
        near_ref[tile] = first_bucket_of(offset)


def buckets_of(place, lengths, boxes):
    return pl.pallas_call(
        bucket_kernel,
        grid_spec=pltpu.PrefetchScalarGridSpec(
            num_scalar_prefetch=2,
            grid=(1,),
            in_specs=[pl.BlockSpec((2, L), lambda i, place, lengths: (0, place[0]))],
            out_specs=[whole(L, L), whole(5, 128, 128)],
            scratch_shapes=[pltpu.VMEM((L, 8), I32)],
        ),
        out_shape=[shaped(I32, L, L), shaped(I32, 5, 128, 128)],
        name="buckets",
        compiler_params=limit(6),
        cost_estimate=HINT,
    )(place, lengths, boxes)


def piece_kernel(place_ref, rows_ref, bias_ref, tables_ref, piece_ref, extra_ref, line_sc):
    line_sc[...] = jnp.zeros_like(line_sc)
    own = bias_ref.shape[1]
    per, _, buckets = tables_ref.shape
    bias = bias_ref[...].astype(F32)
    for n in range(2):
        line_sc[0:1, n * own : (n + 1) * own] = bias[n : n + 1, :]
        for h in range(per):
            at = 2 * own + n * 128 + h * buckets
            line_sc[0:1, at : at + buckets] = tables_ref[h].astype(F32)[n : n + 1, :]
    extra = line_sc[...].astype(BF)
    extra_ref[...] = extra
    size = rows_ref.shape[0]
    piece_ref[0:size, :] = rows_ref[...]
    piece_ref[size:, :] = extra


def first_piece(place, matrix, bias, tables, docs_count):
    columns, depth = matrix.shape
    size = columns // docs_count
    return pl.pallas_call(
        piece_kernel,
        grid_spec=pltpu.PrefetchScalarGridSpec(
            num_scalar_prefetch=1,
            grid=(1,),
            in_specs=[
                pl.BlockSpec(
                    (size, depth),
                    lambda i, place: ((place[3] * 2 + place[2]) * 2 + place[1], 0),
                ),
                whole(*bias.shape),
                whole(*tables.shape),
            ],
            out_specs=[whole(size + 8, depth), whole(8, depth)],
            scratch_shapes=[pltpu.VMEM((8, depth), F32)],
        ),
        out_shape=[shaped(BF, size + 8, depth), shaped(BF, 8, depth)],
        name="first_piece",
        compiler_params=limit(4),
        cost_estimate=HINT,
    )(place, matrix, bias, tables)


def lookup(table_row, index):
    table = jnp.broadcast_to(table_row, (index.shape[0], 128))
    return jnp.concatenate(
        [
            jnp.take_along_axis(
                table, index[:, c : c + 128], axis=1, mode="promise_in_bounds"
            )
            for c in range(0, index.shape[1], 128)
        ],
        axis=1,
    )


def head_window(head, width):
    start = head * HEAD_DIM // 128 * 128
    return start, min(128, width - start), head * HEAD_DIM - start


def eights(rows):
    return rows.reshape(rows.shape[0] // 8, 8, rows.shape[1])


def column(row):
    return jnp.transpose(jnp.broadcast_to(row, (8, row.shape[1])))[:, 0:1]


def forward_kernel(gathered, place_ref, x_ref, *refs):
    sources = refs[: 4 if gathered else 1]
    extra_ref, bucket_ref, index_ref = refs[len(sources) : len(sources) + 3]
    rest = refs[len(sources) + 3 :]
    if gathered:
        w_ref, rest = rest[0], rest[1:]
    else:
        w_ref = sources[0]
    ctx_ref, turned_ref, raised_ref, qkv_ref, inverse_ref = rest[:5]
    near_sc, score_sc, query_sc, key_sc = rest[5:9]
    heads = raised_ref.shape[1]
    width = heads * HEAD_DIM

    @pl.when(pl.program_id(0) == 0)
    def _():
        query_sc[...] = jnp.zeros_like(query_sc)

    if gathered:
        whole_sc = rest[9]
        core, here_x, here_y = place_ref[1], place_ref[2], place_ref[3]
        cut = sources[0].shape[3]
        size = cut + sources[1].shape[3]
        for far_y in range(2):
            for far_x in range(2):
                chip = (here_y ^ far_y) * 2 + (here_x ^ far_x)
                for side, pair in ((core, sources[:2]), (1 - core, sources[2:])):
                    at = (chip * 2 + side) * size
                    first = pl.multiple_of(at, 8)
                    whole_sc[pl.ds(first, cut), :] = pair[0][far_y, far_x, 0].astype(F32)
                    second = pl.multiple_of(at + cut, 8)
                    whole_sc[pl.ds(second, size - cut), :] = pair[1][far_x, far_y, 0].astype(F32)
        w_ref[0] = whole_sc[...].astype(BF)

    extra = extra_ref[0, 0:1, :].astype(F32)
    query_bias, value_bias = extra[:, 0:width], extra[:, width : 2 * width]
    first_tables = extra[:, 2 * width : 2 * width + 128]
    second_tables = extra[:, 2 * width + 128 : 2 * width + 256]
    query = lax.dot_general(w_ref[0, 0:width, :], x_ref[...], NT, preferred_element_type=F32)
    qkv_ref[0, 0:width, :] = (query + column(query_bias)).astype(BF)
    key = lax.dot_general(
        w_ref[0, width : 2 * width, :], x_ref[...], NT, preferred_element_type=F32
    )
    qkv_ref[0, width : 2 * width, :] = key.astype(BF)
    value = lax.dot_general(
        w_ref[0, 2 * width : 3 * width, :], x_ref[...], NT, preferred_element_type=F32
    )
    qkv_ref[0, 2 * width : 3 * width, :] = (value + column(value_bias)).astype(BF)
    key_sc[...] = lax.dot_general(
        x_ref[...], w_ref[0, width : 2 * width, :], NT, preferred_element_type=F32
    ).astype(BF)
    inverse_ref[0] = jnp.zeros_like(inverse_ref[0])
    lane = lax.broadcasted_iota(I32, (1, 128), 1)
    for h in range(heads):
        c0, w, low = head_window(h, width)
        own = slice(h * HEAD_DIM, (h + 1) * HEAD_DIM)
        query_sc[h, low : low + HEAD_DIM, :] = qkv_ref[0, own, :] * jnp.asarray(SCALE, BF)
        row = first_tables if h == 0 else jnp.roll(first_tables, -32 * h, axis=1)
        other = second_tables if h == 0 else jnp.roll(second_tables, -32 * h, axis=1)
        other = jnp.where(lane < 32, other, NEG)
        for d in range(5):
            near_sc[h, d] = lookup(row, index_ref[d])
        far = {
            -3: jnp.broadcast_to(row[:, 15:16], (KC, 128)),
            3: jnp.broadcast_to(row[:, 31:32], (KC, 128)),
        }
        key = key_sc[:, c0 : c0 + w]
        for block in range(L // QB):
            cols = slice(block * QB, (block + 1) * QB)
            score_sc[h] = jnp.dot(key, query_sc[h, 0:w, cols], preferred_element_type=F32)
            peak = None
            for step in range(L // KC):
                rows = slice(step * KC, (step + 1) * KC)
                d, inner = step * KC // 128 - block, step * KC % 128
                near = far[d] if abs(d) == 3 else near_sc[h, d + 2, inner : inner + KC, :]
                scores = score_sc[h, rows, :] + near
                scores = scores + lookup(other, bucket_ref[rows, cols])
                score_sc[h, rows, :] = scores
                part = jnp.max(eights(scores), axis=0)
                peak = part if peak is None else jnp.maximum(peak, part)
            peak = jnp.max(peak, axis=0, keepdims=True)
            sums = None
            for step in range(L // KC):
                rows = slice(step * KC, (step + 1) * KC)
                raised = jnp.exp(score_sc[h, rows, :] - peak)
                raised_ref[0, h, rows, cols] = raised.astype(BF)
                part = jnp.sum(eights(raised), axis=0)
                sums = part if sums is None else sums + part
            inverse_ref[0, h : h + 1, cols] = 1.0 / jnp.sum(sums, axis=0, keepdims=True)
        at = 2 * width + h * HEAD_DIM
        out = jnp.dot(
            qkv_ref[0, at : at + HEAD_DIM, :], raised_ref[0, h], preferred_element_type=F32
        )
        turned_ref[0, own, :] = (out * inverse_ref[0, h : h + 1, :]).astype(BF)
    ctx_ref[0] = jnp.transpose(turned_ref[0])


def each(*shape):
    return pl.BlockSpec((1,) + shape, lambda g, *_: (g,) + (0,) * len(shape))


def attend_forward(place, x, sources, extra, bucket, near):
    gathered = len(sources) == 4
    groups, depth = extra.shape[0], x.shape[1]
    if gathered:
        columns = 8 * (sources[0].shape[3] + sources[1].shape[3])
        inputs = [
            pl.BlockSpec(
                (2, 2, 1) + source.shape[3:], lambda g, place: (0, 0, g, 0, 0)
            )
            for source in sources
        ]
    else:
        columns = sources[0].shape[1]
        inputs = [each(columns, depth)]
    heads = columns // (3 * HEAD_DIM)
    width = columns // 3
    out_specs = [
        each(L, width), each(width, L), each(heads, L, L), each(columns, L), each(8, L)
    ]
    far = in_hbm if gathered else shaped
    out_shape = [
        shaped(BF, groups, L, width),
        far(BF, groups, width, L),
        shaped(BF, groups, heads, L, L),
        far(BF, groups, columns, L),
        shaped(F32, groups, 8, L),
    ]
    scratch = [
        pltpu.VMEM((heads, 5, 128, 128), F32),
        pltpu.VMEM((heads, L, QB), F32),
        pltpu.VMEM((heads, 128, L), BF),
        pltpu.VMEM((L, width), BF),
    ]
    if gathered:
        out_specs = [each(columns, depth)] + out_specs
        out_shape = [in_hbm(BF, groups, columns, depth)] + out_shape
        scratch = scratch + [pltpu.VMEM((columns, depth), F32)]
    return pl.pallas_call(
        functools.partial(forward_kernel, gathered),
        grid_spec=pltpu.PrefetchScalarGridSpec(
            num_scalar_prefetch=1,
            grid=(groups,),
            in_specs=[whole(L, depth)] + inputs + [each(8, depth), whole(L, L), whole(5, 128, 128)],
            out_specs=out_specs,
            scratch_shapes=scratch,
        ),
        out_shape=out_shape,
        name="attend_forward",
        compiler_params=limit(22),
        cost_estimate=HINT,
    )(place, x, *sources, extra, bucket, near)


def backward_kernel(
    halved, place_ref, x_ref, w_ref, qkv_ref, raised_ref, inverse_ref, grad_ref, start_ref, *refs
):
    outs = refs[: 5 if halved else 4]
    dx_ref, ds_ref, sums_ref = outs[:3]
    pad_sc, term_sc, rows_sc, turn_sc, value_sc = refs[len(outs) : len(outs) + 5]
    group = pl.program_id(0)
    heads = raised_ref.shape[1]
    width = heads * HEAD_DIM

    @pl.when(group == 0)
    def _():
        pad_sc[...] = jnp.zeros_like(pad_sc)
        dx_ref[...] = start_ref[...]

    value_sc[...] = jnp.transpose(qkv_ref[0, 2 * width : 3 * width, :])
    for h in range(heads):
        c0, w, low = head_window(h, width)
        own = slice(h * HEAD_DIM, (h + 1) * HEAD_DIM)
        pad_sc[h, low : low + HEAD_DIM, :] = grad_ref[0, own, :]
        value = value_sc[:, c0 : c0 + w]
        for block in range(L // QB):
            cols = slice(block * QB, (block + 1) * QB)
            term_sc[h] = jnp.dot(value, pad_sc[h, 0:w, cols], preferred_element_type=F32)
            sums = None
            for step in range(L // KC):
                rows = slice(step * KC, (step + 1) * KC)
                terms = term_sc[h, rows, :] * raised_ref[0, h, rows, cols].astype(F32)
                term_sc[h, rows, :] = terms
                part = jnp.sum(eights(terms), axis=0)
                sums = part if sums is None else sums + part
            inner = jnp.sum(sums, axis=0, keepdims=True) * inverse_ref[0, h : h + 1, cols]
            for step in range(L // KC):
                rows = slice(step * KC, (step + 1) * KC)
                raised = raised_ref[0, h, rows, cols].astype(F32)
                ds_ref[0, h, rows, cols] = (term_sc[h, rows, :] - raised * inner).astype(BF)
        scale = jnp.asarray(SCALE, BF)
        at = width + h * HEAD_DIM
        turn_sc[own, :] = jnp.dot(
            qkv_ref[0, at : at + HEAD_DIM, :] * scale, ds_ref[0, h], preferred_element_type=F32
        ).astype(BF)
        dk = lax.dot_general(
            ds_ref[0, h], qkv_ref[0, c0 : c0 + w, :] * scale, NT, preferred_element_type=F32
        )
        rows_sc[:, at : at + HEAD_DIM] = dk[:, low : low + HEAD_DIM].astype(BF)
        dv = lax.dot_general(
            raised_ref[0, h], grad_ref[0, c0 : c0 + w, :], NT, preferred_element_type=F32
        )
        at = 2 * width + h * HEAD_DIM
        rows_sc[:, at : at + HEAD_DIM] = dv[:, low : low + HEAD_DIM].astype(BF)
    rows_sc[:, 0:width] = jnp.transpose(turn_sc[0:width, :])
    turn_sc[width:, :] = jnp.transpose(rows_sc[:, width:])
    weights = jnp.dot(turn_sc[...], x_ref[...], preferred_element_type=F32)
    if halved:
        sent_ref, kept_ref = outs[3:]
        all_sc = refs[len(outs) + 5]
        all_sc[...] = weights
        core = place_ref[1]
        chips, size = kept_ref.shape[1], kept_ref.shape[2]
        for chip in range(chips):
            for side, ref in ((1 - core, sent_ref), (core, kept_ref)):
                at = pl.multiple_of((chip * 2 + side) * size, 8)
                ref[0, chip] = all_sc[pl.ds(at, size), :].astype(BF)
    else:
        outs[3][0] = weights.astype(BF)
    dx_ref[...] += jnp.dot(rows_sc[...], w_ref[0], preferred_element_type=F32)
    sums_ref[0] = jnp.sum(rows_sc[...].astype(F32), axis=0, keepdims=True)


def attend_backward(place, halves, x, w, qkv, raised, inverse, grad, start, span=None):
    columns, depth = w.shape[1:]
    skip, stop = span or (0, w.shape[0])
    groups = stop - skip
    some = lambda *shape: pl.BlockSpec(
        (1,) + shape, lambda g, *_: (g + skip,) + (0,) * len(shape)
    )
    heads = columns // (3 * HEAD_DIM)
    width = columns // 3
    out_specs = [whole(L, depth), each(heads, L, L), each(1, columns)]
    out_shape = [
        shaped(F32, L, depth),
        shaped(BF, groups, heads, L, L),
        shaped(F32, groups, 1, columns),
    ]
    scratch = [
        pltpu.VMEM((heads, 128, L), BF),
        pltpu.VMEM((heads, L, QB), F32),
        pltpu.VMEM((L, columns), BF),
        pltpu.VMEM((columns, L), BF),
        pltpu.VMEM((L, width), BF),
    ]
    if halves:
        size = columns // (2 * halves)
        out_specs += [each(halves, size, depth)] * 2
        out_shape += [shaped(BF, groups, halves, size, depth)] * 2
        scratch += [pltpu.VMEM((columns, depth), F32)]
    else:
        out_specs += [each(columns, depth)]
        out_shape += [shaped(BF, groups, columns, depth)]
    return pl.pallas_call(
        functools.partial(backward_kernel, bool(halves)),
        grid_spec=pltpu.PrefetchScalarGridSpec(
            num_scalar_prefetch=1,
            grid=(groups,),
            in_specs=[
                whole(L, depth),
                some(columns, depth),
                some(columns, L),
                some(heads, L, L),
                some(8, L),
                some(width, L),
                whole(L, depth),
            ],
            out_specs=out_specs,
            scratch_shapes=scratch,
        ),
        out_shape=out_shape,
        name="attend_backward",
        compiler_params=limit(26),
        cost_estimate=HINT,
    )(place, x, w, qkv, raised, inverse, grad, start)


def table_kernel(skip, *refs):
    bucket_ref, start_ref, acc_ref, hot_sc = refs[-4:]
    step = pl.program_id(0)
    blocks = [
        (ref, g, h) for ref in refs[:-4] for g in range(ref.shape[0]) for h in range(ref.shape[1])
    ]
    half = 32 * 8

    @pl.when(step == 0)
    def _():
        acc_ref[...] = start_ref[...]

    for u in range(RT // 8):
        part = slice(u * 8, (u + 1) * 8)
        second = bucket_ref[part, :]
        offset = (
            lax.broadcasted_iota(I32, (8, L), 0)
            + ((step + skip) * RT + u * 8)
            - lax.broadcasted_iota(I32, (8, L), 1)
        )
        first = first_bucket_of(offset)
        for t in range(0, 32, 2):
            for base, bucket in ((0, first), (half, second)):
                hot_sc[base + t * 8 : base + (t + 2) * 8, :] = jnp.concatenate(
                    [jnp.where(bucket == t, 1.0, 0.0), jnp.where(bucket == t + 1, 1.0, 0.0)],
                    axis=0,
                ).astype(BF)
        left = jnp.concatenate([ref[g, h, part, :] for ref, g, h in blocks], axis=0)
        acc_ref[...] += lax.dot_general(left, hot_sc[...], NT, preferred_element_type=F32)


def table_products(ds, bucket, start, part):
    heads = sum(item.shape[0] * item.shape[1] for item in ds)
    steps = L // RT // 2
    skip = part * steps
    return pl.pallas_call(
        functools.partial(table_kernel, skip),
        grid=(steps,),
        in_specs=[
            pl.BlockSpec(item.shape[:2] + (RT, L), lambda r: (0, 0, r + skip, 0)) for item in ds
        ]
        + [pl.BlockSpec((RT, L), lambda r: (r + skip, 0)), whole(heads * 8, 512)],
        out_specs=whole(heads * 8, 512),
        out_shape=shaped(F32, heads * 8, 512),
        scratch_shapes=[pltpu.VMEM((512, L), BF)],
        name="table_products",
        compiler_params=limit(14),
        cost_estimate=HINT,
    )(*ds, bucket, start)


def short_kernel(per, count, *refs):
    acc_ref, sums = refs[0], refs[1 : 1 + count]
    down_ref, up_ref, in_ref, out_ref = refs[1 + count :]
    heads = acc_ref.shape[0] // 8
    half = 32 * 8
    shape = (heads * 8, 2 * half)
    same = lax.broadcasted_iota(I32, shape, 0) % 8 == lax.broadcasted_iota(I32, shape, 1) % 8
    kept = jnp.where(same, acc_ref[...], 0.0)
    fold = (2 * half, 64)
    right = (
        lax.broadcasted_iota(I32, fold, 0) // 8 == lax.broadcasted_iota(I32, fold, 1)
    ).astype(F32)
    spread = (16, heads * 8)
    left = (
        lax.broadcasted_iota(I32, spread, 1) // 8 == lax.broadcasted_iota(I32, spread, 0)
    ).astype(F32)
    exact = lax.Precision.HIGHEST
    folded = jnp.dot(kept, right, preferred_element_type=F32, precision=exact)
    tables = jnp.dot(left, folded, preferred_element_type=F32, precision=exact)
    wide = 2 * per * 32
    lanes = None
    for h in range(per):
        shape = (8, 16)
        rows = (
            lax.broadcasted_iota(I32, shape, 1) == lax.broadcasted_iota(I32, shape, 0) * per + h
        ).astype(F32)
        shape = (64, wide)
        source, target = lax.broadcasted_iota(I32, shape, 0), lax.broadcasted_iota(I32, shape, 1)
        moved = jnp.where(source < 32, source + h * 32, source + (per - 1 + h) * 32)
        part = jnp.dot(rows, tables, preferred_element_type=F32, precision=exact)
        part = jnp.dot(
            part, (target == moved).astype(F32), preferred_element_type=F32, precision=exact
        )
        lanes = part if lanes is None else lanes + part
    out_ref[...] = jnp.zeros_like(out_ref)
    out_ref[0:3, :] = down_ref[0:3, :]
    out_ref[3:6, :] = up_ref[0:3, :]
    width = out_ref.shape[1]
    deep = in_ref.shape[1] // width
    for n in range(deep):
        out_ref[6 + n : 7 + n, :] = in_ref[0:1, n * width : (n + 1) * width]
    group = 0
    for ref in sums:
        own = ref.shape[2] // 3
        for g in range(ref.shape[0]):
            row = slice(6 + deep + group, 7 + deep + group)
            out_ref[row, 0:own] = ref[g, :, 0:own]
            out_ref[row, own : 2 * own] = ref[g, :, 2 * own :]
            out_ref[row, 2 * own : 2 * own + wide] = lanes[group : group + 1, :]
            group += 1


def short_rows(acc, sums, down, up, inner, per):
    width = down.shape[1]
    rows = -(-(6 + inner.shape[1] // width + acc.shape[0] // 8 // per) // 8) * 8
    vmem = pl.BlockSpec(memory_space=pltpu.VMEM)
    return pl.pallas_call(
        functools.partial(short_kernel, per, len(sums)),
        in_specs=[vmem] * (4 + len(sums)),
        out_specs=vmem,
        out_shape=shaped(F32, rows, width),
        name="short_rows",
        compiler_params=limit(6),
        cost_estimate=HINT,
    )(acc, *sums, down, up, inner)


def mean_of(rows):
    return jnp.mean(rows, axis=-1, keepdims=True)


def normalize(rows):
    centred = rows - mean_of(rows)
    inverse = lax.rsqrt(mean_of(centred * centred) + EPS)
    return centred * inverse, inverse


def normalize_back(scaled, unit, inverse):
    return inverse * (scaled - mean_of(scaled) - unit * mean_of(scaled * unit))


def gelu_parts(values):
    size = jnp.abs(values)
    t = 1.0 / (1.0 + (0.3275911 * ROOT_HALF) * size)
    bell = jnp.exp(values * values * -0.5)
    series = 1.061405429
    for term in (-1.453152027, 1.421413741, -0.284496736, 0.254829592):
        series = term + t * series
    tail = (0.5 * t) * series * bell
    below = jnp.where(values >= 0, 1.0 - tail, tail)
    return values * below, below + values * (bell * DENSITY_SCALE)


def column_sum(rows):
    return jnp.sum(rows, axis=0, keepdims=True)


def up_kernel(
    place_ref, x_ref, ctx_own_ref, ctx_ref, wo_ref, bo_ref, g1_ref, s1_ref, wi_ref, bi_ref, wb_ref,
    bb_ref, g2_ref, s2_ref, cot_ref,
    out_ref, mid_ref, branch_ref, turned_ref, slope_ref, unit_ref, inverse_ref, low_ref, sums_ref,
    normed_sc, low_sc, acc_sc,
):
    step = pl.program_id(0)
    groups = wo_ref.shape[0]

    @pl.when(step == 0)
    def _():
        @pl.loop(0, L // MB)
        def _(r):
            rows = pl.ds(pl.multiple_of(r * MB, MB), MB)
            total = x_ref[rows, :].astype(F32) + bo_ref[...]
            for s in range(groups):
                ctx = ctx_own_ref[0, rows, :] if s == 0 else ctx_ref[s - 1, rows, :]
                quarter = place_ref[0] ^ s
                total = total + jnp.dot(ctx, wo_ref[quarter], preferred_element_type=F32)
            unit, inverse = normalize(total)
            unit_ref[rows, :] = unit
            inverse_ref[rows, :] = jnp.broadcast_to(inverse, (MB, 128))
            normed = unit * g1_ref[...] + s1_ref[...]
            normed_sc[rows, :] = normed
            low_sc[rows, :] = normed.astype(BF)

        low_ref[...] = jnp.transpose(low_sc[...])
        acc_sc[...] = jnp.zeros_like(acc_sc)

    @pl.loop(0, L // MB)
    def _(r):
        rows = pl.ds(pl.multiple_of(r * MB, MB), MB)
        pre = jnp.dot(low_sc[rows, :], wi_ref[...], preferred_element_type=F32) + bi_ref[...]
        acted, slope = gelu_parts(pre)
        acted = acted.astype(BF)
        slope_ref[rows, :] = slope.astype(BF)
        turned_ref[:, rows] = jnp.transpose(acted)
        acc_sc[rows, :] += jnp.dot(acted, wb_ref[...], preferred_element_type=F32)

    @pl.when(step == pl.num_programs(0) - 1)
    def _():
        sums_ref[...] = jnp.zeros_like(sums_ref)

        @pl.loop(0, L // MB)
        def _(r):
            rows = pl.ds(pl.multiple_of(r * MB, MB), MB)
            unit, inverse = normalize(normed_sc[rows, :] + (acc_sc[rows, :] + bb_ref[...]))
            out_ref[rows, :] = (unit * g2_ref[...] + s2_ref[...]).astype(BF)
            upstream = cot_ref[rows, :].astype(F32)
            middle = normalize_back(upstream * g2_ref[...], unit, inverse)
            mid_ref[rows, :] = middle
            branch = middle.astype(BF)
            branch_ref[rows, :] = branch
            sums_ref[0:1, :] += column_sum(upstream * unit)
            sums_ref[1:2, :] += column_sum(upstream)
            sums_ref[2:3, :] += column_sum(branch.astype(F32))


def feed_up(place, x, ctx_own, ctx, w_out, bo, g1, s1, w_in, bi, w_back, bb, g2, s2, cot):
    width = x.shape[1]
    units = w_in.shape[1]
    groups, own = w_out.shape[0], w_out.shape[1]
    row = whole(1, width)
    return pl.pallas_call(
        up_kernel,
        grid_spec=pltpu.PrefetchScalarGridSpec(
            num_scalar_prefetch=1,
            grid=(units // FC,),
            in_specs=[
                whole(L, width),
                whole(1, L, own),
                whole(groups - 1, L, own),
                whole(groups, own, width),
                row,
                row,
                row,
                pl.BlockSpec((width, FC), lambda n, place: (0, n)),
                pl.BlockSpec((1, FC), lambda n, place: (0, n)),
                pl.BlockSpec((FC, width), lambda n, place: (n, 0)),
                row,
                row,
                row,
                whole(L, width),
            ],
            out_specs=[
                whole(L, width),
                whole(L, width),
                whole(L, width),
                pl.BlockSpec((FC, L), lambda n, place: (n, 0)),
                pl.BlockSpec((L, FC), lambda n, place: (0, n)),
                whole(L, width),
                whole(L, 128),
                whole(width, L),
                whole(8, width),
            ],
            scratch_shapes=[
                pltpu.VMEM((L, width), F32),
                pltpu.VMEM((L, width), BF),
                pltpu.VMEM((L, width), F32),
            ],
        ),
        out_shape=[
            shaped(BF, L, width),
            shaped(F32, L, width),
            shaped(BF, L, width),
            shaped(BF, units, L),
            shaped(BF, L, units),
            shaped(F32, L, width),
            shaped(F32, L, 128),
            shaped(BF, width, L),
            shaped(F32, 8, width),
        ],
        name="feed_up",
        compiler_params=limit(32),
        cost_estimate=HINT,
    )(place, x, ctx_own, ctx, w_out, bo, g1, s1, w_in, bi, w_back, bb, g2, s2, cot)


def down_kernel(
    halved, place_ref, branch_ref, slope_ref, wb_ref, wi_ref, low_ref, mid_ref, unit_ref,
    inverse_ref, g1_ref, wo_ref, turned_own_ref, turned_ref, norm_own_ref, norm_ref, *refs
):
    bias_ref, first_ref, grad_own_ref, grad_ref, sums_ref = refs[:5]
    weight_refs = refs[5 : 7 if halved else 6]
    acc_sc, pre_sc, weight_sc = refs[-3:]
    step = pl.program_id(0)
    last = pl.num_programs(0) - 1
    groups, own = wo_ref.shape[0], wo_ref.shape[1]

    def give():
        if not halved:
            weight_refs[0][...] = weight_sc[...]
            return
        core = place_ref[1]
        chips, size = weight_refs[0].shape[0], weight_refs[0].shape[1]
        for chip in range(chips):
            for side, ref in ((1 - core, weight_refs[0]), (core, weight_refs[1])):
                at = pl.multiple_of((chip * 2 + side) * size, size)
                ref[chip] = weight_sc[pl.ds(at, size), :]

    @pl.when(step == 0)
    def _():
        acc_sc[...] = mid_ref[...]

    @pl.when(step < last)
    def _():
        total = None
        for r in range(L // MB):
            rows = slice(r * MB, (r + 1) * MB)
            pre = lax.dot_general(
                branch_ref[rows, :], wb_ref[...], NT, preferred_element_type=F32
            ) * slope_ref[rows, :].astype(F32)
            pre = pre.astype(BF)
            pre_sc[rows, :] = pre
            part = column_sum(pre.astype(F32))
            total = part if r == 0 else total + part
            acc_sc[rows, :] += lax.dot_general(
                pre, wi_ref[...], NT, preferred_element_type=F32
            )
        bias_ref[0:1, :] = total
        weight_sc[...] = jnp.dot(
            low_ref[...], pre_sc[...], preferred_element_type=F32
        ).astype(BF)
        give()

    @pl.when(step == last)
    def _():
        sums_ref[...] = jnp.zeros_like(sums_ref)

        @pl.loop(0, L // MB)
        def _(r):
            rows = pl.ds(pl.multiple_of(r * MB, MB), MB)
            hidden = acc_sc[rows, :]
            unit = unit_ref[rows, :]
            first = normalize_back(hidden * g1_ref[...], unit, inverse_ref[rows, 0:1])
            first_ref[rows, :] = first
            attended = first.astype(BF)
            pre_sc[rows, :] = attended
            sums_ref[0:1, :] += column_sum(hidden * unit)
            sums_ref[1:2, :] += column_sum(hidden)
            sums_ref[2:3, :] += column_sum(attended.astype(F32))

        def quarter_of(s, turned, norm, out):
            quarter = place_ref[0] ^ s
            at = pl.multiple_of(quarter * own, own)
            weight_sc[pl.ds(at, own), :] = jnp.dot(
                turned, pre_sc[...], preferred_element_type=F32
            ).astype(BF)
            grads = lax.dot_general(
                wo_ref[quarter], pre_sc[...], NT, preferred_element_type=F32
            )
            for h in range(own // HEAD_DIM):
                rows = slice(h * HEAD_DIM, (h + 1) * HEAD_DIM)
                out[rows, :] = (grads[rows, :] * norm[h : h + 1, :]).astype(BF)

        quarter_of(0, turned_own_ref[0], norm_own_ref[0], grad_own_ref.at[0])

        @pl.loop(1, groups)
        def _(s):
            quarter_of(s, turned_ref[s - 1], norm_ref[s - 1], grad_ref.at[s - 1])

        give()


def feed_down(place, halves, branch, slope, w_back, w_in, low, mid, unit, inverse, g1, w_out,
              turned_own, turned, norm_own, norm):
    width = branch.shape[1]
    units = w_in.shape[1]
    groups, own = w_out.shape[0], w_out.shape[1]
    steps = units // FC
    inside = lambda n: jnp.minimum(n, steps - 1)
    out_specs = [
        pl.BlockSpec((8, FC), lambda n, place: (0, inside(n))),
        whole(L, width),
        whole(1, own, L),
        whole(groups - 1, own, L),
        whole(8, width),
    ]
    out_shape = [
        shaped(F32, 8, units),
        shaped(F32, L, width),
        shaped(BF, 1, own, L),
        shaped(BF, groups - 1, own, L),
        shaped(F32, 8, width),
    ]
    if halves:
        size = width // (2 * halves)
        out_specs += [pl.BlockSpec((halves, size, FC), lambda n, place: (0, 0, n))] * 2
        out_shape += [shaped(BF, halves, size, units + width)] * 2
    else:
        out_specs += [pl.BlockSpec((width, FC), lambda n, place: (0, n))]
        out_shape += [shaped(BF, width, units + width)]
    return pl.pallas_call(
        functools.partial(down_kernel, bool(halves)),
        grid_spec=pltpu.PrefetchScalarGridSpec(
            num_scalar_prefetch=1,
            grid=(steps + 1,),
            in_specs=[
                whole(L, width),
                pl.BlockSpec((L, FC), lambda n, place: (0, inside(n))),
                pl.BlockSpec((FC, width), lambda n, place: (inside(n), 0)),
                pl.BlockSpec((width, FC), lambda n, place: (0, inside(n))),
                whole(width, L),
                whole(L, width),
                whole(L, width),
                whole(L, 128),
                whole(1, width),
                whole(groups, own, width),
                whole(1, own, L),
                whole(groups - 1, own, L),
                whole(1, 8, L),
                whole(groups - 1, 8, L),
            ],
            out_specs=out_specs,
            scratch_shapes=[
                pltpu.VMEM((L, width), F32),
                pltpu.VMEM((L, FC), BF),
                pltpu.VMEM((width, FC), BF),
            ],
        ),
        out_shape=out_shape,
        name="feed_down",
        compiler_params=limit(34),
        cost_estimate=HINT,
    )(place, branch, slope, w_back, w_in, low, mid, unit, inverse, g1, w_out,
      turned_own, turned, norm_own, norm)


def product_kernel(place_ref, left_ref, right_ref, out_ref):
    out_ref[...] = jnp.dot(
        left_ref[...], right_ref[...], preferred_element_type=F32
    ).astype(BF)


def product(place, left, right, sizes):
    rows, depth = left.shape
    columns = right.shape[1]
    count, size, halved = sizes
    take = (lambda n, place: (2 * n + 1 - place[1], 0)) if halved else (lambda n, place: (n, 0))
    return pl.pallas_call(
        product_kernel,
        grid_spec=pltpu.PrefetchScalarGridSpec(
            num_scalar_prefetch=1,
            grid=(count,),
            in_specs=[pl.BlockSpec((size, depth), take), whole(depth, columns)],
            out_specs=pl.BlockSpec((size, columns), lambda n, place: (n, 0)),
        ),
        out_shape=shaped(BF, count * size, columns),
        name="back_weights",
        compiler_params=limit(10),
        cost_estimate=HINT,
    )(place, left, right)


def kept_kernel(place_ref, left_ref, right_ref, got_ref, a_sent, a_kept, b_sent, b_kept):
    chip = pl.program_id(0)
    chip_y, chip_x = chip // 2, lax.rem(chip, 2)
    here_x, here_y = place_ref[2], place_ref[3]
    value = jnp.dot(left_ref[...], right_ref[...], preferred_element_type=F32)
    value = (value + got_ref[0].astype(F32)).astype(BF)
    cut = a_sent.shape[1]

    @pl.when(chip_x == here_x)
    def _():
        a_kept[chip_y] = value[:cut, :]

    @pl.when(chip_x != here_x)
    def _():
        a_sent[chip_y] = value[:cut, :]

    @pl.when(chip_y == here_y)
    def _():
        b_kept[chip_x] = value[cut:, :]

    @pl.when(chip_y != here_y)
    def _():
        b_sent[chip_x] = value[cut:, :]


def product_kept(place, left, right, got):
    chips, size, columns = got.shape
    depth = left.shape[1]
    part = whole(2, size // 2, columns)
    return pl.pallas_call(
        kept_kernel,
        grid_spec=pltpu.PrefetchScalarGridSpec(
            num_scalar_prefetch=1,
            grid=(chips,),
            in_specs=[
                pl.BlockSpec((size, depth), lambda n, place: (2 * n + place[1], 0)),
                whole(depth, columns),
                pl.BlockSpec((1, size, columns), lambda n, place: (n, 0, 0)),
            ],
            out_specs=[part] * 4,
        ),
        out_shape=[shaped(BF, 2, size // 2, columns)] * 4,
        name="kept_weights",
        compiler_params=limit(14),
        cost_estimate=HINT,
    )(place, left, right, got)


def total_of(*items):
    total = items[0].astype(F32)
    for item in items[1:]:
        total = total + item.astype(F32)
    return total.astype(BF)


def chips_kernel(count, layout, place_ref, *refs):
    inputs, outs = refs[:count], refs[count:]
    here_x, here_y = place_ref[2], place_ref[3]
    for order, (way, sources) in enumerate(layout):
        sent, kept = outs[2 * order], outs[2 * order + 1]
        start = 0
        for number, low, high in sources:
            kept_ref, got_ref = inputs[2 * number], inputs[2 * number + 1]
            for g in range(kept_ref.shape[0]):
                rows = slice(start, start + high - low)
                start += high - low
                for other in range(2):
                    for out, far in ((sent, 1), (kept, 0)):
                        if way == "x":
                            chip = other * 2 + (here_x ^ far)
                        else:
                            chip = (here_y ^ far) * 2 + other
                        out[other, rows, :] = total_of(
                            kept_ref[g, chip, low:high, :], got_ref[g, chip, low:high, :]
                        )


def sum_chips(place, pairs, parts, block):
    specs, out_specs, out_shape = [], [], []
    columns = pairs[0][0].shape[-1]
    for kept, _ in pairs:
        shape = kept.shape[:3] + (block,)
        specs += [pl.BlockSpec(shape, lambda n, place: (0, 0, 0, n))] * 2
    for _, sources in parts:
        height = sum(pairs[n][0].shape[0] * (high - low) for n, low, high in sources)
        out_specs += [pl.BlockSpec((2, height, block), lambda n, place: (0, 0, n))] * 2
        out_shape += [shaped(BF, 2, height, columns)] * 2
    return pl.pallas_call(
        functools.partial(chips_kernel, 2 * len(pairs), parts),
        grid_spec=pltpu.PrefetchScalarGridSpec(
            num_scalar_prefetch=1, grid=(columns // block,), in_specs=specs, out_specs=out_specs
        ),
        out_shape=out_shape,
        name="sum_chips",
        compiler_params=limit(14),
        cost_estimate=HINT,
    )(place, *[item for pair in pairs for item in pair])


def pairs_kernel(place_ref, a_kept, a_got, b_kept, b_got, a_sent, a_own, b_sent, b_own):
    here_x, here_y = place_ref[2], place_ref[3]
    for here, kept, got, sent, own in (
        (here_y, a_kept, a_got, a_sent, a_own),
        (here_x, b_kept, b_got, b_sent, b_own),
    ):
        sent[...] = total_of(kept[1 - here], got[1 - here])
        own[...] = total_of(kept[here], got[here])


def sum_pairs(place, a_kept, a_got, b_kept, b_got, block):
    columns = a_kept.shape[-1]
    spec = lambda item: pl.BlockSpec((2, item.shape[1], block), lambda n, place: (0, 0, n))
    flat = lambda item: pl.BlockSpec((item.shape[1], block), lambda n, place: (0, n))
    return pl.pallas_call(
        pairs_kernel,
        grid_spec=pltpu.PrefetchScalarGridSpec(
            num_scalar_prefetch=1,
            grid=(columns // block,),
            in_specs=[spec(a_kept), spec(a_got), spec(b_kept), spec(b_got)],
            out_specs=[flat(a_kept)] * 2 + [flat(b_kept)] * 2,
        ),
        out_shape=[shaped(BF, a_kept.shape[1], columns)] * 2
        + [shaped(BF, b_kept.shape[1], columns)] * 2,
        name="sum_pairs",
        compiler_params=limit(12),
        cost_estimate=HINT,
    )(place, a_kept, a_got, b_kept, b_got)


def cut_kernel(place_ref, a_kept, a_got, b_kept, b_got, sent, kept, sum_sc):
    cut = a_kept.shape[0]
    sum_sc[0:cut, :] = a_kept[...].astype(F32) + a_got[...].astype(F32)
    sum_sc[cut:, :] = b_kept[...].astype(F32) + b_got[...].astype(F32)
    size = kept.shape[1]
    for s, out in ((0, kept.at[0]), (1, sent.at[0]), (2, kept.at[1]), (3, sent.at[1])):
        at = pl.multiple_of((place_ref[0] ^ s) * size, 8)
        out[...] = sum_sc[pl.ds(at, size), :].astype(BF)


def cut_quarters(place, a_kept, a_got, b_kept, b_got, block):
    columns = a_kept.shape[-1]
    height = a_kept.shape[0] + b_kept.shape[0]
    spec = lambda item: pl.BlockSpec((item.shape[0], block), lambda n, place: (0, n))
    return pl.pallas_call(
        cut_kernel,
        grid_spec=pltpu.PrefetchScalarGridSpec(
            num_scalar_prefetch=1,
            grid=(columns // block,),
            in_specs=[spec(a_kept), spec(a_got), spec(b_kept), spec(b_got)],
            out_specs=[pl.BlockSpec((2, height // 4, block), lambda n, place: (0, 0, n))] * 2,
            scratch_shapes=[pltpu.VMEM((height, block), F32)],
        ),
        out_shape=[shaped(BF, 2, height // 4, columns)] * 2,
        name="cut_quarters",
        compiler_params=limit(12),
        cost_estimate=HINT,
    )(place, a_kept, a_got, b_kept, b_got)


def halves_kernel(place_ref, a_kept, a_got, b_kept, b_got, *refs):
    outs, sum_sc = refs[:-1], refs[-1]
    cut = a_kept.shape[0]
    sum_sc[0:cut, :] = a_kept[...].astype(F32) + a_got[...].astype(F32)
    sum_sc[cut:, :] = b_kept[...].astype(F32) + b_got[...].astype(F32)
    size, wide = outs[0].shape[1:]
    for out, lanes, first, second in (
        (outs[0], slice(0, wide), 1, 3),
        (outs[1], slice(0, wide), 0, 2),
        (outs[2], slice(wide, 2 * wide), 2, 3),
        (outs[3], slice(wide, 2 * wide), 0, 1),
    ):
        for n, s in ((0, first), (1, second)):
            at = pl.multiple_of((place_ref[0] ^ s) * size, 8)
            out[n] = sum_sc[pl.ds(at, size), lanes].astype(BF)


def cut_halves(place, a_kept, a_got, b_kept, b_got):
    vmem = pl.BlockSpec(memory_space=pltpu.VMEM)
    columns = a_kept.shape[-1]
    height = a_kept.shape[0] + b_kept.shape[0]
    return pl.pallas_call(
        halves_kernel,
        in_specs=[pl.BlockSpec(memory_space=pltpu.SMEM)] + [vmem] * 4,
        out_specs=[vmem] * 4,
        out_shape=[shaped(BF, 2, height // 4, columns // 2)] * 4,
        scratch_shapes=[pltpu.VMEM((height, columns), F32)],
        name="cut_halves",
        compiler_params=limit(8),
        cost_estimate=HINT,
    )(place, a_kept, a_got, b_kept, b_got)


def last_kernel(a_kept, a_got, b_kept, b_got, short_ref, *outs):
    size = outs[0].shape[0] - 16
    many = short_ref.shape[0] // 8 * 8
    first = 10
    for s, out in enumerate(outs):
        rows = slice(s % 2 * size, (s % 2 + 1) * size)
        kept, got = (a_kept, a_got) if s < 2 else (b_kept, b_got)
        out[0:size, :] = total_of(kept[rows, :], got[rows, :])
        row = lax.broadcasted_iota(I32, (many, short_ref.shape[1]), 0)
        short = jnp.where(row < first, short_ref[...], 0.0)
        short = short + jnp.where(row == first, short_ref[first + s : first + s + 1, :], 0.0)
        out[size : size + many, :] = short.astype(BF)


def cut_last(a_kept, a_got, b_kept, b_got, short):
    vmem = pl.BlockSpec(memory_space=pltpu.VMEM)
    size, columns = b_kept.shape[0] // 2, b_kept.shape[1]
    return pl.pallas_call(
        last_kernel,
        in_specs=[vmem] * 5,
        out_specs=[vmem] * 4,
        out_shape=[shaped(BF, size + 16, columns)] * 4,
        name="cut_last",
        compiler_params=limit(8),
        cost_estimate=HINT,
    )(a_kept, a_got, b_kept, b_got, short)


def join_kernel(orders, place_ref, *refs):
    inputs, outs = refs[: 3 * len(orders)], refs[3 * len(orders) :]
    size, wide = inputs[0].shape
    start = 0
    for out in outs:
        done = 0
        while done < out.shape[1]:
            half, low = divmod(start + done, wide)
            many = min(wide - low, out.shape[1] - done)
            own, one, two = inputs[3 * half : 3 * half + 3]
            lanes = slice(low, low + many)
            near, far, farther = orders[half]
            for s, piece in (
                (0, own[:, lanes]), (near, one[:, lanes]), (far, two[0, :, lanes]),
                (farther, two[1, :, lanes]),
            ):
                at = pl.multiple_of((place_ref[0] ^ s) * size, 8)
                out[pl.ds(at, size), done : done + many] = piece.astype(F32)
            done += many
        start += out.shape[1]


def join_quarters(place, parts, orders, widths):
    vmem = pl.BlockSpec(memory_space=pltpu.VMEM)
    return pl.pallas_call(
        functools.partial(join_kernel, orders),
        in_specs=[pl.BlockSpec(memory_space=pltpu.SMEM)] + [vmem] * (3 * len(parts)),
        out_specs=[vmem] * len(widths),
        out_shape=[shaped(F32, 4 * parts[0][0].shape[0], width) for width in widths],
        name="join_quarters",
        compiler_params=limit(8),
        cost_estimate=HINT,
    )(place, *[item for part in parts for item in part])


def chips_join_kernel(place_ref, mine_a, mine_b, got_a, got_b, ends_ref, got_ends, out_ref, *outs):
    core, here_x, here_y = place_ref[1], place_ref[2], place_ref[3]
    cut = mine_a.shape[2]
    size = cut + mine_b.shape[2]
    for far_y in range(2):
        for far_x in range(2):
            chip = (here_y ^ far_y) * 2 + (here_x ^ far_x)
            for side, a_ref, b_ref in ((core, mine_a, mine_b), (1 - core, got_a, got_b)):
                at = (chip * 2 + side) * size
                first = pl.multiple_of(at, 8)
                out_ref[pl.ds(first, cut), :] = a_ref[far_y, far_x].astype(F32)
                second = pl.multiple_of(at + cut, 8)
                out_ref[pl.ds(second, size - cut), :] = b_ref[far_x, far_y].astype(F32)
    total = ends_ref[...].astype(F32) + got_ends[...].astype(F32)
    bias_ref, tables_ref, inner_ref = outs[:3]
    vectors = outs[3:]
    here = (here_y * 2 + here_x) * 2 + core
    width = total.shape[1]
    share = vectors[0].shape[1]
    part = inner_ref.shape[1]
    deep = part * 8 // width
    slices = jnp.zeros((len(vectors), share), F32)
    inner = jnp.zeros((1, part), F32)
    for d in range(8):
        mine = here == d
        slices = slices + jnp.where(
            mine, total[0 : len(vectors), d * share : (d + 1) * share], 0.0
        )
        row, lane = 6 + d * part // width, d * part % width
        inner = inner + jnp.where(mine, total[row : row + 1, lane : lane + part], 0.0)
    inner_ref[...] = inner
    for n, ref in enumerate(vectors):
        ref[...] = slices[n : n + 1, :]
    short = total[6 + deep : 7 + deep, :]
    own = bias_ref.shape[1]
    bias_ref[0:1, :] = short[:, 0:own]
    bias_ref[1:2, :] = short[:, own : 2 * own]
    per, _, buckets = tables_ref.shape
    for n in range(2):
        for h in range(per):
            lane = 2 * own + (n * per + h) * buckets
            tables_ref[h, n : n + 1, :] = short[:, lane : lane + buckets]


def join_chips(place, mine_a, mine_b, got_a, got_b, ends, got_ends, units, own, heads, buckets):
    vmem = pl.BlockSpec(memory_space=pltpu.VMEM)
    rows = 8 * (mine_a.shape[2] + mine_b.shape[2])
    width = mine_a.shape[-1]
    out_shape = [
        shaped(F32, rows, width),
        shaped(F32, 2, own),
        shaped(F32, heads, 2, buckets),
        shaped(F32, 1, units // 8),
    ] + [shaped(F32, 1, width // 8)] * 6
    return pl.pallas_call(
        chips_join_kernel,
        in_specs=[pl.BlockSpec(memory_space=pltpu.SMEM)] + [vmem] * 6,
        out_specs=[vmem] * len(out_shape),
        out_shape=out_shape,
        name="join_chips",
        compiler_params=limit(8),
        cost_estimate=HINT,
    )(place, mine_a, mine_b, got_a, got_b, ends, got_ends)


def tie(values, *others):
    return lax.optimization_barrier((values, others))[0]


def swap(array, bit):
    count = lax.axis_size("docs")
    return lax.ppermute(array, "docs", [(i, i ^ (1 << bit)) for i in range(count)])


def away(array, distance):
    count = lax.axis_size("heads")
    return lax.ppermute(array, "heads", [(i, i ^ distance) for i in range(count)])


def in_order(pieces, z):
    stacked = jnp.stack(pieces)
    picks = [lax.dynamic_index_in_dim(stacked, z ^ s, 0) for s in range(len(pieces))]
    return jnp.concatenate(picks, axis=0)


def tree(items):
    while len(items) > 1:
        items = [items[n] + items[n + 1] for n in range(0, len(items), 2)]
    return items[0]


def sum_everywhere(rows):
    for bit in range(lax.axis_size("docs").bit_length() - 1):
        rows = rows + swap(rows, bit)
    return tree([rows] + [away(rows, s) for s in range(1, lax.axis_size("heads"))])


def spread_plane(first, second):
    got = [swap(first, 1), swap(second, 2)]
    first, second = jnp.stack([first, got[0]]), jnp.stack([second, got[1]])
    got = [swap(first, 2), swap(second, 1)]
    return jnp.stack([first, got[0]]), jnp.stack([second, got[1]])


def reduce_docs(blocks):
    bits = blocks.shape[0].bit_length() - 1
    docs = lax.axis_index("docs")
    current = blocks.reshape((2,) * bits + blocks.shape[1:])
    for bit in range(bits):
        mine = (docs >> bit) & 1
        axis = bits - 1 - bit
        sent = lax.dynamic_index_in_dim(current, 1 - mine, axis, keepdims=False)
        kept = lax.dynamic_index_in_dim(current, mine, axis, keepdims=False)
        current = total_of(kept, swap(sent, bit))
    return current


def spread_docs(block):
    count = lax.axis_size("docs")
    docs = lax.axis_index("docs")
    current = block
    for done, bit in enumerate(range(count.bit_length() - 2, -1, -1)):
        got = swap(current, bit)
        mine = ((docs >> bit) & 1) == 1
        current = jnp.stack(
            [jnp.where(mine, got, current), jnp.where(mine, current, got)], axis=done
        )
    return current.reshape((count,) + block.shape)


def body(
    layer_input, token_boxes, lengths, w_qkv, qv_bias, rel_tables, w_out, out_bias,
    gain_one, shift_one, w_in, in_bias, w_back, back_bias, gain_two, shift_two, cotangent,
):
    width = layer_input.shape[1]
    units = w_in.shape[1]
    groups = lax.axis_size("heads")
    count = lax.axis_size("docs")
    docs = lax.axis_index("docs")
    z = lax.axis_index("heads")
    own = w_qkv.shape[2]
    heads = rel_tables.shape[1]
    buckets = rel_tables.shape[2]
    columns = 3 * own
    share = width // count
    small = columns // count
    chips = 4 if count == 8 and share % 16 == 0 and small % 8 == 0 else 0
    place = jnp.stack([z, docs & 1, (docs >> 1) & 1, (docs >> 2) & 1]).astype(I32)

    still = lambda array: pltpu.with_memory_space_constraint(array, pltpu.HBM)
    matrix = w_qkv.transpose(1, 2, 0).reshape(columns, width)
    if chips:
        piece, extra = first_piece(
            place, still(matrix), still(qv_bias), still(rel_tables.transpose(1, 0, 2)), count
        )
    else:
        room = jnp.zeros((128 - heads * buckets,), BF)
        line = jnp.concatenate(
            [qv_bias[0], qv_bias[1], rel_tables[0].reshape(-1), room, rel_tables[1].reshape(-1), room]
        )
        extra = jnp.pad(line[None], ((0, 7), (0, width - line.shape[0])))
        piece = jnp.concatenate(
            [lax.dynamic_slice_in_dim(matrix, docs * small, small, axis=0), extra], axis=0
        )
    got = [away(piece, s) for s in range(1, groups)]
    bucket, near = buckets_of(place, lengths, still(token_boxes))

    ctx_own, turned_own, raised_own, qkv_own, norm_own = attend_forward(
        place, still(layer_input), (still(matrix[None]),), extra[None], bucket, near
    )
    arrived = jnp.stack(tie(got, ctx_own))
    if chips:
        cut = (small // 2 + 7) // 8 * 8
        first, second = spread_plane(arrived[:, :cut], arrived[:, cut:small])
        weights, ctx, turned, raised, qkv, norm = attend_forward(
            place, layer_input, (first, second, swap(first, 0), swap(second, 0)),
            arrived[:, small:], bucket, near,
        )
    else:
        weights = spread_docs(arrived[:, :small]).transpose(1, 0, 2, 3)
        weights = weights.reshape(groups - 1, columns, width)
        ctx, turned, raised, qkv, norm = attend_forward(
            place, layer_input, (weights,), arrived[:, small:], bucket, near
        )

    w_out_heads = w_out.reshape(groups, own, width)
    flat = lambda vector: vector.reshape(1, -1)
    layer_output, grad_mid, grad_branch, acted, slope, unit, inverse, low, up_sums = feed_up(
        place, layer_input, ctx_own, ctx, w_out_heads, flat(out_bias), flat(gain_one),
        flat(shift_one), w_in, flat(in_bias), w_back, flat(back_bias), flat(gain_two),
        flat(shift_two), cotangent,
    )
    down = lambda branch: feed_down(
        place, chips, branch, slope, w_back, w_in, low, grad_mid, unit, inverse, flat(gain_one),
        w_out_heads, turned_own, turned, norm_own, norm,
    )
    own_back = lambda grad, start: attend_backward(
        place, chips, layer_input, matrix[None], qkv_own, still(raised_own), norm_own, grad, start
    )
    rest_back = lambda span, grad, start: attend_backward(
        place, chips, layer_input, weights, qkv, raised, norm, grad, start, span
    )

    if chips:
        half = share // 2
        back_size = units // count
        sent = product(place, acted, grad_branch, (chips, back_size, True))
        got = swap(sent.reshape(chips, back_size, width), 0)
        back = product_kept(place, acted, grad_branch, got)
        back_got = [swap(back[0], 1), swap(back[2], 2)]

        in_sums, grad_first, grad_own, grad_rest, down_sums, dense_sent, dense_kept = down(
            tie(grad_branch, back[0], back[2])
        )
        back_got = tie(back_got, grad_first)
        back = sum_pairs(place, back[1], back_got[0], back[3], back_got[1], width // 2)
        back_got = [swap(back[0], 2), swap(back[2], 1)]
        dense_sent = tie(dense_sent, back[0])
        dense_got = swap(dense_sent, 0)

        dx, ds_own, sums_own, own_sent, own_kept = own_back(
            tie(grad_own, dense_sent, back[0], back[2]), grad_first
        )
        dense_got, back_got = tie((dense_got, back_got), dx)
        dense = sum_chips(
            place,
            [(dense_kept[None], dense_got[None])],
            (("x", ((0, 0, half),)), ("y", ((0, half, share),))),
            FC,
        )
        back_sent, back = cut_quarters(
            place, back[1], back_got[0], back[3], back_got[1], width // 2
        )
        dense = list(dense)
        dense[0], dense[2], own_sent = tie((dense[0], dense[2], own_sent), back_sent)
        dense_got = [swap(dense[0], 1), swap(dense[2], 2)]
        back_got = away(back_sent, 1)
        own_got = swap(own_sent, 0)

        dx, ds_one, sums_one, one_sent, one_kept = rest_back(
            (0, 1), tie(grad_rest, dense[0], dense[2], own_sent, back_sent), dx
        )
        own_got, back_got = tie((own_got, back_got), dx)
        back = total_of(back, back_got)
        one_sent = tie(one_sent, back)
        one_got = swap(one_sent, 0)
        back_got = away(back[1], 2)

        dx, ds_two, sums_two, two_sent, two_kept = rest_back(
            (1, 3), tie(grad_rest, one_sent, back), dx
        )
        dense_got, back_got, one_got = tie((dense_got, back_got, one_got), dx)
        dense = list(
            sum_pairs(
                place, dense[1], dense_got[0], dense[3], dense_got[1], (units + width) // 3
            )
        )
        back = total_of(back[0], back_got)
        two_sent, dense[0], dense[2], back = tie((two_sent, dense[0], dense[2], back), dense[1])
        two_got = swap(two_sent, 0)
        dense_got = [swap(dense[0], 2), swap(dense[2], 1)]
        back_one = away(back, 2)
        scores = (ds_own, ds_one, ds_two)
        acc = table_products(
            scores, tie(bucket, back, two_sent, dense[0], dense[2]),
            jnp.zeros((groups * heads * 8, 512), F32), 0,
        )

        two_got, dense_got, back_one = tie((two_got, dense_got, back_one), acc)
        dense = cut_halves(place, dense[1], dense_got[0], dense[3], dense_got[1])
        dense_sent, dense = [dense[0], dense[2]], [dense[1], dense[3]]
        own_got, one_got, two_got = tie((own_got, one_got, two_got), dense_sent)
        last_a = sum_chips(
            place, [(own_kept, own_got), (one_kept, one_got)],
            (("x", ((0, 0, small), (1, 0, small))),), width // 2,
        )
        last_b = sum_chips(place, [(two_kept, two_got)], (("y", ((0, 0, small),)),), width // 2)
        back_two = jnp.stack([back, back_one])
        last_a, last_b, dense_sent, back_two = tie((last_a, last_b, dense_sent, back_two))
        last_a_got = swap(last_a[0], 1)
        last_b_got = swap(last_b[0], 2)
        dense_got = [away(dense_sent[0], 1), away(dense_sent[1], 2)]
        back_two = away(back_two, 1)
        acc = table_products(
            scores, tie(bucket, last_b[0], last_a[0], dense_sent), acc, 1
        )
        short = short_rows(acc, (sums_own, sums_one, sums_two), down_sums, up_sums, in_sums, heads)

        last_a_got, last_b_got, dense_got = tie((last_a_got, last_b_got, dense_got), acc)
        last = list(sum_pairs(place, last_a[1], last_a_got, last_b[1], last_b_got, width // 2))
        dense = [total_of(*pair) for pair in zip(dense, dense_got)]
        last[0], last[2], dense = tie((last[0], last[2], dense), last[1])
        last_got = [swap(last[0], 2), swap(last[2], 1)]
        dense_got = [away(dense[0][1], 2), away(dense[1][1], 1)]
        last_got, short = tie((last_got, short), dense, back_two)
        last = cut_last(last[1], last_got[0], last[3], last_got[1], short)
        last_got = [away(last[s], s) for s in range(1, groups)]
        dense_got, back_two = tie((dense_got, back_two), last[0])
        dense = [total_of(item[0], got) for item, got in zip(dense, dense_got)]
        dense_one = [away(dense[0], 2), away(dense[1], 1)]
        (out_back,) = join_quarters(place, [(back, back_one, back_two)], ((2, 1, 3),), (width,))
        last_got = tie(last_got, dense, out_back)
        quarter = total_of(last[0][:small], *[item[:small] for item in last_got])
        ends = tree([item[small:].astype(F32) for item in [last[0]] + last_got]).astype(BF)
        first, second = quarter[:cut], quarter[cut:]
        rest = small - cut
        got = [swap(first, 1), swap(jnp.concatenate([second, ends]), 2)]
        dense_one = tie(dense_one, first, second)
        dense_two = [jnp.stack(pair) for pair in zip(dense, dense_one)]
        dense_two = [away(dense_two[0], 1), away(dense_two[1], 2)]
        got = tie(got, dense_one)
        ends = total_of(ends, got[1][rest:])
        first, second = jnp.stack([first, got[0]]), jnp.stack([second, got[1][:rest]])
        both = jnp.concatenate([second, ends.reshape(2, -1, width)], axis=1)
        got = [swap(first, 2), swap(both, 1)]
        dense_two = tie(dense_two, first, both)
        ends = total_of(ends, got[1][:, rest:].reshape(ends.shape))
        first, second = jnp.stack([first, got[0]]), jnp.stack([second, got[1][:, :rest]])
        got = [swap(first, 0), swap(second, 0), swap(ends, 0)]
        out_in, out_out = join_quarters(
            place, list(zip(dense, dense_one, dense_two)), ((2, 1, 3), (1, 2, 3)), (units, width)
        )
        got = tie(got, out_in)
        full, grad_bias, grad_tables, grad_inner, *vectors = join_chips(
            place, first, second, got[0], got[1], ends, got[2], units, own, heads, buckets
        )
        grad_tables = grad_tables.transpose(1, 0, 2)
        vectors = [vector.reshape(share) for vector in vectors]
        grad_inner = grad_inner.reshape(units // count)
    else:
        back_grads = product(place, acted, grad_branch, (units // FC, FC, False))
        in_sums, grad_first, grad_own, grad_rest, down_sums, dense_grads = down(grad_branch)
        dx, ds_own, sums_own, dw_own = own_back(grad_own, grad_first)
        dx, ds_rest, sums_rest, dw_rest = rest_back(None, grad_rest, dx)
        acc = jnp.zeros((groups * heads * 8, 512), F32)
        for part in range(2):
            acc = table_products((ds_own, ds_rest), bucket, acc, part)
        short = short_rows(acc, (sums_own, sums_rest), down_sums, up_sums, in_sums, heads)
        begin = 6 + units // width
        quarters = in_order([short[begin + s] for s in range(groups)], z)
        total = sum_everywhere(jnp.concatenate([short[:begin], quarters], axis=0))
        ends = lax.dynamic_index_in_dim(total, begin + z, 0, keepdims=False)

        def sum_heads(parts):
            return total_of(parts[0], *[away(parts[s], s) for s in range(1, groups)])

        def dense_rows(grads):
            rows = reduce_docs(grads.reshape(count, -1, grads.shape[1]))
            parts = rows.reshape(-1, groups, width)
            parts = [
                lax.dynamic_index_in_dim(parts, z ^ s, 1, keepdims=False) for s in range(groups)
            ]
            mine = sum_heads(parts)
            pieces = [mine] + [away(mine, s) for s in range(1, groups)]
            return in_order(pieces, z).transpose(1, 0, 2).reshape(rows.shape).astype(F32)

        out_back = dense_rows(back_grads)
        rows = dense_rows(dense_grads)
        out_in, out_out = rows[:, :units], rows[:, units:]
        blocks = jnp.concatenate([dw_own, dw_rest]).reshape(groups, count, small, width)
        blocks = blocks.transpose(1, 0, 2, 3).reshape(count, groups * small, width)
        blocks = reduce_docs(blocks).reshape(groups, small, width)
        full = spread_docs(sum_heads([blocks[s] for s in range(groups)]))
        full = full.reshape(columns, width).astype(F32)

        mine = lambda vector: lax.dynamic_slice_in_dim(
            vector, docs * (vector.shape[0] // count), vector.shape[0] // count
        )
        grad_bias = ends[: 2 * own].reshape(2, own)
        grad_tables = ends[2 * own : 2 * own + 2 * heads * buckets].reshape(2, heads, buckets)
        vectors = [mine(total[n]) for n in range(6)]
        grad_inner = mine(total[6:begin].reshape(-1))
    return (
        layer_output,
        dx.astype(BF),
        full.reshape(3, own, width).transpose(2, 0, 1),
        grad_bias,
        grad_tables,
        out_out,
        vectors[2],
        vectors[0],
        vectors[1],
        out_in,
        grad_inner,
        out_back,
        vectors[5],
        vectors[3],
        vectors[4],
    )


def solution(mesh):
    rows = P(("docs", "heads"), None)
    return jax.shard_map(
        body,
        mesh=mesh,
        in_specs=(
            rows,
            P(None, "docs"),
            P("docs"),
            P(None, None, "heads"),
            P(None, "heads"),
            P(None, "heads", None),
            P(),
            P(),
            P(),
            P(),
            P(),
            P(),
            P(),
            P(),
            P(),
            P(),
            rows,
        ),
        out_specs=(
            rows,
            rows,
            P(None, None, "heads"),
            P(None, "heads"),
            P(None, "heads", None),
            P("docs", None),
            P("docs"),
            P("docs"),
            P("docs"),
            P("docs", None),
            P("docs"),
            P("docs", None),
            P("docs"),
            P("docs"),
            P("docs"),
        ),
        check_vma=False,
    )
```

```python
import functools
import math

import jax
import jax.numpy as jnp
from jax import lax
from jax.experimental import pallas as pl
from jax.experimental.pallas import tpu as pltpu
from jax.sharding import PartitionSpec as P

HEAD_DIM = 64
L = 512
EPS = 1e-05
NEG = -1000000000.0
THRESHOLDS = (1, 2, 3, 4, 6, 8, 12, 16, 24, 32, 48, 64, 96, 128, 192)
ROOT_HALF = 1.0 / math.sqrt(2.0)
DENSITY_SCALE = 1.0 / math.sqrt(2.0 * math.pi)
SCALE = 0.125
KC = 32
QB = 128
RT = 32
FC = 768
MB = 256
BF = jnp.bfloat16
F32 = jnp.float32
I32 = jnp.int32
NT = (((1,), (1,)), ((), ()))


def whole(*shape):
    return pl.BlockSpec(shape, lambda *_: (0,) * len(shape))


def in_hbm(dtype, *shape):
    return pltpu.HBM(shape, dtype)


def limit(mebibytes):
    return pltpu.CompilerParams(vmem_limit_bytes=mebibytes << 20)


HINT = pl.CostEstimate(flops=1, bytes_accessed=1, transcendentals=0)


def shaped(dtype, *shape):
    return jax.ShapeDtypeStruct(shape, dtype)


def first_bucket_of(offset):
    distance = jnp.abs(offset)
    count = jnp.where(offset > 0, 16, 0).astype(I32)
    for threshold in THRESHOLDS:
        count = count + jnp.where(distance >= threshold, 1, 0).astype(I32)
    return count


def second_bucket_of(across, upward):
    horizontal = jnp.zeros(across.shape, I32)
    for threshold in (-128, -32, -8, 0):
        horizontal = horizontal + jnp.where(across >= threshold, 1, 0)
    for threshold in (8, 32, 128):
        horizontal = horizontal + jnp.where(across > threshold, 1, 0)
    vertical = (
        jnp.where(upward >= -24, 8, 0)
        + jnp.where(upward >= 0, 8, 0)
        + jnp.where(upward > 24, 8, 0)
    )
    return vertical + horizontal


PLACE = ("heads", "core", "x", "y")


def bucket_kernel(place_ref, len_ref, box_ref, out_ref, near_ref, turned_sc):
    filled = len_ref[place_ref[0]]
    boxes = box_ref[...].astype(F32)
    turned_sc[...] = jnp.transpose(jnp.concatenate([boxes] * 4, axis=0)).astype(I32)
    size = 64

    @pl.loop(0, L // size)
    def _(step):
        start = pl.multiple_of(step * size, size)
        rows = pl.ds(start, size)
        across = turned_sc[rows, 0:1] - box_ref[0:1, :]
        upward = turned_sc[rows, 1:2] - box_ref[1:2, :]
        key = lax.broadcasted_iota(I32, (size, L), 0) + start
        out_ref[rows, :] = jnp.where(key < filled, second_bucket_of(across, upward), 32)

    @pl.loop(0, near_ref.shape[0])
    def _(tile):
        offset = (
            128 * (tile - 2)
            + lax.broadcasted_iota(I32, (128, 128), 0)
            - lax.broadcasted_iota(I32, (128, 128), 1)
        )
        near_ref[tile] = first_bucket_of(offset)


def buckets_of(place, lengths, boxes):
    return pl.pallas_call(
        bucket_kernel,
        grid_spec=pltpu.PrefetchScalarGridSpec(
            num_scalar_prefetch=2,
            grid=(1,),
            in_specs=[pl.BlockSpec((2, L), lambda i, place, lengths: (0, place[0]))],
            out_specs=[whole(L, L), whole(5, 128, 128)],
            scratch_shapes=[pltpu.VMEM((L, 8), I32)],
        ),
        out_shape=[shaped(I32, L, L), shaped(I32, 5, 128, 128)],
        name="buckets",
        compiler_params=limit(6),
        cost_estimate=HINT,
    )(place, lengths, boxes)


def piece_kernel(place_ref, rows_ref, bias_ref, tables_ref, piece_ref, extra_ref, line_sc):
    line_sc[...] = jnp.zeros_like(line_sc)
    own = bias_ref.shape[1]
    per, _, buckets = tables_ref.shape
    bias = bias_ref[...].astype(F32)
    for n in range(2):
        line_sc[0:1, n * own : (n + 1) * own] = bias[n : n + 1, :]
        for h in range(per):
            at = 2 * own + n * 128 + h * buckets
            line_sc[0:1, at : at + buckets] = tables_ref[h].astype(F32)[n : n + 1, :]
    extra = line_sc[...].astype(BF)
    extra_ref[...] = extra
    size = rows_ref.shape[0]
    piece_ref[0:size, :] = rows_ref[...]
    piece_ref[size:, :] = extra


def first_piece(place, matrix, bias, tables, docs_count):
    columns, depth = matrix.shape
    size = columns // docs_count
    return pl.pallas_call(
        piece_kernel,
        grid_spec=pltpu.PrefetchScalarGridSpec(
            num_scalar_prefetch=1,
            grid=(1,),
            in_specs=[
                pl.BlockSpec(
                    (size, depth),
                    lambda i, place: ((place[3] * 2 + place[2]) * 2 + place[1], 0),
                ),
                whole(*bias.shape),
                whole(*tables.shape),
            ],
            out_specs=[whole(size + 8, depth), whole(8, depth)],
            scratch_shapes=[pltpu.VMEM((8, depth), F32)],
        ),
        out_shape=[shaped(BF, size + 8, depth), shaped(BF, 8, depth)],
        name="first_piece",
        compiler_params=limit(4),
        cost_estimate=HINT,
    )(place, matrix, bias, tables)


def lookup(table_row, index):
    table = jnp.broadcast_to(table_row, (index.shape[0], 128))
    return jnp.concatenate(
        [
            jnp.take_along_axis(
                table, index[:, c : c + 128], axis=1, mode="promise_in_bounds"
            )
            for c in range(0, index.shape[1], 128)
        ],
        axis=1,
    )


def head_window(head, width):
    start = head * HEAD_DIM // 128 * 128
    return start, min(128, width - start), head * HEAD_DIM - start


def eights(rows):
    return rows.reshape(rows.shape[0] // 8, 8, rows.shape[1])


def column(row):
    return jnp.transpose(jnp.broadcast_to(row, (8, row.shape[1])))[:, 0:1]


def forward_kernel(gathered, place_ref, x_ref, *refs):
    sources = refs[: 4 if gathered else 1]
    extra_ref, bucket_ref, index_ref = refs[len(sources) : len(sources) + 3]
    rest = refs[len(sources) + 3 :]
    if gathered:
        w_ref, rest = rest[0], rest[1:]
    else:
        w_ref = sources[0]
    ctx_ref, turned_ref, raised_ref, qkv_ref, inverse_ref = rest[:5]
    near_sc, score_sc, query_sc, key_sc = rest[5:9]
    heads = raised_ref.shape[1]
    width = heads * HEAD_DIM

    @pl.when(pl.program_id(0) == 0)
    def _():
        query_sc[...] = jnp.zeros_like(query_sc)

    if gathered:
        whole_sc = rest[9]
        core, here_x, here_y = place_ref[1], place_ref[2], place_ref[3]
        cut = sources[0].shape[3]
        size = cut + sources[1].shape[3]
        for far_y in range(2):
            for far_x in range(2):
                chip = (here_y ^ far_y) * 2 + (here_x ^ far_x)
                for side, pair in ((core, sources[:2]), (1 - core, sources[2:])):
                    at = (chip * 2 + side) * size
                    first = pl.multiple_of(at, 8)
                    whole_sc[pl.ds(first, cut), :] = pair[0][far_y, far_x, 0].astype(F32)
                    second = pl.multiple_of(at + cut, 8)
                    whole_sc[pl.ds(second, size - cut), :] = pair[1][far_x, far_y, 0].astype(F32)
        w_ref[0] = whole_sc[...].astype(BF)

    extra = extra_ref[0, 0:1, :].astype(F32)
    query_bias, value_bias = extra[:, 0:width], extra[:, width : 2 * width]
    first_tables = extra[:, 2 * width : 2 * width + 128]
    second_tables = extra[:, 2 * width + 128 : 2 * width + 256]
    query = lax.dot_general(w_ref[0, 0:width, :], x_ref[...], NT, preferred_element_type=F32)
    qkv_ref[0, 0:width, :] = (query + column(query_bias)).astype(BF)
    key = lax.dot_general(
        w_ref[0, width : 2 * width, :], x_ref[...], NT, preferred_element_type=F32
    )
    qkv_ref[0, width : 2 * width, :] = key.astype(BF)
    value = lax.dot_general(
        w_ref[0, 2 * width : 3 * width, :], x_ref[...], NT, preferred_element_type=F32
    )
    qkv_ref[0, 2 * width : 3 * width, :] = (value + column(value_bias)).astype(BF)
    key_sc[...] = lax.dot_general(
        x_ref[...], w_ref[0, width : 2 * width, :], NT, preferred_element_type=F32
    ).astype(BF)
    inverse_ref[0] = jnp.zeros_like(inverse_ref[0])
    lane = lax.broadcasted_iota(I32, (1, 128), 1)
    for h in range(heads):
        c0, w, low = head_window(h, width)
        own = slice(h * HEAD_DIM, (h + 1) * HEAD_DIM)
        query_sc[h, low : low + HEAD_DIM, :] = qkv_ref[0, own, :] * jnp.asarray(SCALE, BF)
        row = first_tables if h == 0 else jnp.roll(first_tables, -32 * h, axis=1)
        other = second_tables if h == 0 else jnp.roll(second_tables, -32 * h, axis=1)
        other = jnp.where(lane < 32, other, NEG)
        for d in range(5):
            near_sc[h, d] = lookup(row, index_ref[d])
        far = {
            -3: jnp.broadcast_to(row[:, 15:16], (KC, 128)),
            3: jnp.broadcast_to(row[:, 31:32], (KC, 128)),
        }
        key = key_sc[:, c0 : c0 + w]
        for block in range(L // QB):
            cols = slice(block * QB, (block + 1) * QB)
            score_sc[h] = jnp.dot(key, query_sc[h, 0:w, cols], preferred_element_type=F32)
            peak = None
            for step in range(L // KC):
                rows = slice(step * KC, (step + 1) * KC)
                d, inner = step * KC // 128 - block, step * KC % 128
                near = far[d] if abs(d) == 3 else near_sc[h, d + 2, inner : inner + KC, :]
                scores = score_sc[h, rows, :] + near
                scores = scores + lookup(other, bucket_ref[rows, cols])
                score_sc[h, rows, :] = scores
                part = jnp.max(eights(scores), axis=0)
                peak = part if peak is None else jnp.maximum(peak, part)
            peak = jnp.max(peak, axis=0, keepdims=True)
            sums = None
            for step in range(L // KC):
                rows = slice(step * KC, (step + 1) * KC)
                raised = jnp.exp(score_sc[h, rows, :] - peak)
                raised_ref[0, h, rows, cols] = raised.astype(BF)
                part = jnp.sum(eights(raised), axis=0)
                sums = part if sums is None else sums + part
            inverse_ref[0, h : h + 1, cols] = 1.0 / jnp.sum(sums, axis=0, keepdims=True)
        at = 2 * width + h * HEAD_DIM
        out = jnp.dot(
            qkv_ref[0, at : at + HEAD_DIM, :], raised_ref[0, h], preferred_element_type=F32
        )
        turned_ref[0, own, :] = (out * inverse_ref[0, h : h + 1, :]).astype(BF)
    ctx_ref[0] = jnp.transpose(turned_ref[0])


def each(*shape):
    return pl.BlockSpec((1,) + shape, lambda g, *_: (g,) + (0,) * len(shape))


def attend_forward(place, x, sources, extra, bucket, near):
    gathered = len(sources) == 4
    groups, depth = extra.shape[0], x.shape[1]
    if gathered:
        columns = 8 * (sources[0].shape[3] + sources[1].shape[3])
        inputs = [
            pl.BlockSpec(
                (2, 2, 1) + source.shape[3:], lambda g, place: (0, 0, g, 0, 0)
            )
            for source in sources
        ]
    else:
        columns = sources[0].shape[1]
        inputs = [each(columns, depth)]
    heads = columns // (3 * HEAD_DIM)
    width = columns // 3
    out_specs = [
        each(L, width), each(width, L), each(heads, L, L), each(columns, L), each(8, L)
    ]
    far = in_hbm if gathered else shaped
    out_shape = [
        shaped(BF, groups, L, width),
        far(BF, groups, width, L),
        shaped(BF, groups, heads, L, L),
        far(BF, groups, columns, L),
        shaped(F32, groups, 8, L),
    ]
    scratch = [
        pltpu.VMEM((heads, 5, 128, 128), F32),
        pltpu.VMEM((heads, L, QB), F32),
        pltpu.VMEM((heads, 128, L), BF),
        pltpu.VMEM((L, width), BF),
    ]
    if gathered:
        out_specs = [each(columns, depth)] + out_specs
        out_shape = [in_hbm(BF, groups, columns, depth)] + out_shape
        scratch = scratch + [pltpu.VMEM((columns, depth), F32)]
    return pl.pallas_call(
        functools.partial(forward_kernel, gathered),
        grid_spec=pltpu.PrefetchScalarGridSpec(
            num_scalar_prefetch=1,
            grid=(groups,),
            in_specs=[whole(L, depth)] + inputs + [each(8, depth), whole(L, L), whole(5, 128, 128)],
            out_specs=out_specs,
            scratch_shapes=scratch,
        ),
        out_shape=out_shape,
        name="attend_forward",
        compiler_params=limit(22),
        cost_estimate=HINT,
    )(place, x, *sources, extra, bucket, near)


def backward_kernel(
    halved, place_ref, x_ref, w_ref, qkv_ref, raised_ref, inverse_ref, grad_ref, start_ref, *refs
):
    outs = refs[: 5 if halved else 4]
    dx_ref, ds_ref, sums_ref = outs[:3]
    pad_sc, term_sc, rows_sc, turn_sc, value_sc = refs[len(outs) : len(outs) + 5]
    group = pl.program_id(0)
    heads = raised_ref.shape[1]
    width = heads * HEAD_DIM

    @pl.when(group == 0)
    def _():
        pad_sc[...] = jnp.zeros_like(pad_sc)
        dx_ref[...] = start_ref[...]

    value_sc[...] = jnp.transpose(qkv_ref[0, 2 * width : 3 * width, :])
    for h in range(heads):
        c0, w, low = head_window(h, width)
        own = slice(h * HEAD_DIM, (h + 1) * HEAD_DIM)
        pad_sc[h, low : low + HEAD_DIM, :] = grad_ref[0, own, :]
        value = value_sc[:, c0 : c0 + w]
        for block in range(L // QB):
            cols = slice(block * QB, (block + 1) * QB)
            term_sc[h] = jnp.dot(value, pad_sc[h, 0:w, cols], preferred_element_type=F32)
            sums = None
            for step in range(L // KC):
                rows = slice(step * KC, (step + 1) * KC)
                terms = term_sc[h, rows, :] * raised_ref[0, h, rows, cols].astype(F32)
                term_sc[h, rows, :] = terms
                part = jnp.sum(eights(terms), axis=0)
                sums = part if sums is None else sums + part
            inner = jnp.sum(sums, axis=0, keepdims=True) * inverse_ref[0, h : h + 1, cols]
            for step in range(L // KC):
                rows = slice(step * KC, (step + 1) * KC)
                raised = raised_ref[0, h, rows, cols].astype(F32)
                ds_ref[0, h, rows, cols] = (term_sc[h, rows, :] - raised * inner).astype(BF)
        scale = jnp.asarray(SCALE, BF)
        at = width + h * HEAD_DIM
        turn_sc[own, :] = jnp.dot(
            qkv_ref[0, at : at + HEAD_DIM, :] * scale, ds_ref[0, h], preferred_element_type=F32
        ).astype(BF)
        dk = lax.dot_general(
            ds_ref[0, h], qkv_ref[0, c0 : c0 + w, :] * scale, NT, preferred_element_type=F32
        )
        rows_sc[:, at : at + HEAD_DIM] = dk[:, low : low + HEAD_DIM].astype(BF)
        dv = lax.dot_general(
            raised_ref[0, h], grad_ref[0, c0 : c0 + w, :], NT, preferred_element_type=F32
        )
        at = 2 * width + h * HEAD_DIM
        rows_sc[:, at : at + HEAD_DIM] = dv[:, low : low + HEAD_DIM].astype(BF)
    rows_sc[:, 0:width] = jnp.transpose(turn_sc[0:width, :])
    turn_sc[width:, :] = jnp.transpose(rows_sc[:, width:])
    weights = jnp.dot(turn_sc[...], x_ref[...], preferred_element_type=F32)
    if halved:
        sent_ref, kept_ref = outs[3:]
        all_sc = refs[len(outs) + 5]
        all_sc[...] = weights
        core = place_ref[1]
        chips, size = kept_ref.shape[1], kept_ref.shape[2]
        for chip in range(chips):
            for side, ref in ((1 - core, sent_ref), (core, kept_ref)):
                at = pl.multiple_of((chip * 2 + side) * size, 8)
                ref[0, chip] = all_sc[pl.ds(at, size), :].astype(BF)
    else:
        outs[3][0] = weights.astype(BF)
    dx_ref[...] += jnp.dot(rows_sc[...], w_ref[0], preferred_element_type=F32)
    sums_ref[0] = jnp.sum(rows_sc[...].astype(F32), axis=0, keepdims=True)


def attend_backward(place, halves, x, w, qkv, raised, inverse, grad, start, span=None):
    columns, depth = w.shape[1:]
    skip, stop = span or (0, w.shape[0])
    groups = stop - skip
    some = lambda *shape: pl.BlockSpec(
        (1,) + shape, lambda g, *_: (g + skip,) + (0,) * len(shape)
    )
    heads = columns // (3 * HEAD_DIM)
    width = columns // 3
    out_specs = [whole(L, depth), each(heads, L, L), each(1, columns)]
    out_shape = [
        shaped(F32, L, depth),
        shaped(BF, groups, heads, L, L),
        shaped(F32, groups, 1, columns),
    ]
    scratch = [
        pltpu.VMEM((heads, 128, L), BF),
        pltpu.VMEM((heads, L, QB), F32),
        pltpu.VMEM((L, columns), BF),
        pltpu.VMEM((columns, L), BF),
        pltpu.VMEM((L, width), BF),
    ]
    if halves:
        size = columns // (2 * halves)
        out_specs += [each(halves, size, depth)] * 2
        out_shape += [shaped(BF, groups, halves, size, depth)] * 2
        scratch += [pltpu.VMEM((columns, depth), F32)]
    else:
        out_specs += [each(columns, depth)]
        out_shape += [shaped(BF, groups, columns, depth)]
    return pl.pallas_call(
        functools.partial(backward_kernel, bool(halves)),
        grid_spec=pltpu.PrefetchScalarGridSpec(
            num_scalar_prefetch=1,
            grid=(groups,),
            in_specs=[
                whole(L, depth),
                some(columns, depth),
                some(columns, L),
                some(heads, L, L),
                some(8, L),
                some(width, L),
                whole(L, depth),
            ],
            out_specs=out_specs,
            scratch_shapes=scratch,
        ),
        out_shape=out_shape,
        name="attend_backward",
        compiler_params=limit(30),
        cost_estimate=HINT,
    )(place, x, w, qkv, raised, inverse, grad, start)


def table_kernel(skip, *refs):
    bucket_ref, start_ref, acc_ref, hot_sc = refs[-4:]
    step = pl.program_id(0)
    blocks = [
        (ref, g, h) for ref in refs[:-4] for g in range(ref.shape[0]) for h in range(ref.shape[1])
    ]
    half = 32 * 8

    @pl.when(step == 0)
    def _():
        acc_ref[...] = start_ref[...]

    for u in range(RT // 8):
        part = slice(u * 8, (u + 1) * 8)
        second = bucket_ref[part, :]
        offset = (
            lax.broadcasted_iota(I32, (8, L), 0)
            + ((step + skip) * RT + u * 8)
            - lax.broadcasted_iota(I32, (8, L), 1)
        )
        first = first_bucket_of(offset)
        for t in range(0, 32, 2):
            for base, bucket in ((0, first), (half, second)):
                hot_sc[base + t * 8 : base + (t + 2) * 8, :] = jnp.concatenate(
                    [jnp.where(bucket == t, 1.0, 0.0), jnp.where(bucket == t + 1, 1.0, 0.0)],
                    axis=0,
                ).astype(BF)
        left = jnp.concatenate([ref[g, h, part, :] for ref, g, h in blocks], axis=0)
        acc_ref[...] += lax.dot_general(left, hot_sc[...], NT, preferred_element_type=F32)


def table_products(ds, bucket, start, part):
    heads = sum(item.shape[0] * item.shape[1] for item in ds)
    steps = L // RT // 2
    skip = part * steps
    return pl.pallas_call(
        functools.partial(table_kernel, skip),
        grid=(steps,),
        in_specs=[
            pl.BlockSpec(item.shape[:2] + (RT, L), lambda r: (0, 0, r + skip, 0)) for item in ds
        ]
        + [pl.BlockSpec((RT, L), lambda r: (r + skip, 0)), whole(heads * 8, 512)],
        out_specs=whole(heads * 8, 512),
        out_shape=shaped(F32, heads * 8, 512),
        scratch_shapes=[pltpu.VMEM((512, L), BF)],
        name="table_products",
        compiler_params=limit(14),
        cost_estimate=HINT,
    )(*ds, bucket, start)


def short_kernel(per, count, *refs):
    acc_ref, sums = refs[0], refs[1 : 1 + count]
    down_ref, up_ref, in_ref, out_ref = refs[1 + count :]
    heads = acc_ref.shape[0] // 8
    half = 32 * 8
    shape = (heads * 8, 2 * half)
    same = lax.broadcasted_iota(I32, shape, 0) % 8 == lax.broadcasted_iota(I32, shape, 1) % 8
    kept = jnp.where(same, acc_ref[...], 0.0)
    fold = (2 * half, 64)
    right = (
        lax.broadcasted_iota(I32, fold, 0) // 8 == lax.broadcasted_iota(I32, fold, 1)
    ).astype(F32)
    spread = (16, heads * 8)
    left = (
        lax.broadcasted_iota(I32, spread, 1) // 8 == lax.broadcasted_iota(I32, spread, 0)
    ).astype(F32)
    exact = lax.Precision.HIGHEST
    folded = jnp.dot(kept, right, preferred_element_type=F32, precision=exact)
    tables = jnp.dot(left, folded, preferred_element_type=F32, precision=exact)
    wide = 2 * per * 32
    lanes = None
    for h in range(per):
        shape = (8, 16)
        rows = (
            lax.broadcasted_iota(I32, shape, 1) == lax.broadcasted_iota(I32, shape, 0) * per + h
        ).astype(F32)
        shape = (64, wide)
        source, target = lax.broadcasted_iota(I32, shape, 0), lax.broadcasted_iota(I32, shape, 1)
        moved = jnp.where(source < 32, source + h * 32, source + (per - 1 + h) * 32)
        part = jnp.dot(rows, tables, preferred_element_type=F32, precision=exact)
        part = jnp.dot(
            part, (target == moved).astype(F32), preferred_element_type=F32, precision=exact
        )
        lanes = part if lanes is None else lanes + part
    out_ref[...] = jnp.zeros_like(out_ref)
    out_ref[0:3, :] = down_ref[0:3, :]
    out_ref[3:6, :] = up_ref[0:3, :]
    width = out_ref.shape[1]
    deep = in_ref.shape[1] // width
    for n in range(deep):
        out_ref[6 + n : 7 + n, :] = in_ref[0:1, n * width : (n + 1) * width]
    group = 0
    for ref in sums:
        own = ref.shape[2] // 3
        for g in range(ref.shape[0]):
            row = slice(6 + deep + group, 7 + deep + group)
            out_ref[row, 0:own] = ref[g, :, 0:own]
            out_ref[row, own : 2 * own] = ref[g, :, 2 * own :]
            out_ref[row, 2 * own : 2 * own + wide] = lanes[group : group + 1, :]
            group += 1


def short_rows(acc, sums, down, up, inner, per):
    width = down.shape[1]
    rows = -(-(6 + inner.shape[1] // width + acc.shape[0] // 8 // per) // 8) * 8
    vmem = pl.BlockSpec(memory_space=pltpu.VMEM)
    return pl.pallas_call(
        functools.partial(short_kernel, per, len(sums)),
        in_specs=[vmem] * (4 + len(sums)),
        out_specs=vmem,
        out_shape=shaped(F32, rows, width),
        name="short_rows",
        compiler_params=limit(6),
        cost_estimate=HINT,
    )(acc, *sums, down, up, inner)


def mean_of(rows):
    return jnp.mean(rows, axis=-1, keepdims=True)


def normalize(rows):
    centred = rows - mean_of(rows)
    inverse = lax.rsqrt(mean_of(centred * centred) + EPS)
    return centred * inverse, inverse


def normalize_back(scaled, unit, inverse):
    return inverse * (scaled - mean_of(scaled) - unit * mean_of(scaled * unit))


def gelu_parts(values):
    size = jnp.abs(values)
    t = 1.0 / (1.0 + (0.3275911 * ROOT_HALF) * size)
    bell = jnp.exp(values * values * -0.5)
    series = 1.061405429
    for term in (-1.453152027, 1.421413741, -0.284496736, 0.254829592):
        series = term + t * series
    tail = (0.5 * t) * series * bell
    below = jnp.where(values >= 0, 1.0 - tail, tail)
    return values * below, below + values * (bell * DENSITY_SCALE)


def column_sum(rows):
    return jnp.sum(rows, axis=0, keepdims=True)


def up_kernel(
    place_ref, x_ref, ctx_own_ref, ctx_ref, wo_ref, bo_ref, g1_ref, s1_ref, wi_ref, bi_ref, wb_ref,
    bb_ref, g2_ref, s2_ref, cot_ref,
    out_ref, mid_ref, branch_ref, turned_ref, slope_ref, unit_ref, inverse_ref, low_ref, sums_ref,
    normed_sc, low_sc, acc_sc,
):
    step = pl.program_id(0)
    groups = wo_ref.shape[0]

    @pl.when(step == 0)
    def _():
        @pl.loop(0, L // MB)
        def _(r):
            rows = pl.ds(pl.multiple_of(r * MB, MB), MB)
            total = x_ref[rows, :].astype(F32) + bo_ref[...]
            for s in range(groups):
                ctx = ctx_own_ref[0, rows, :] if s == 0 else ctx_ref[s - 1, rows, :]
                quarter = place_ref[0] ^ s
                total = total + jnp.dot(ctx, wo_ref[quarter], preferred_element_type=F32)
            unit, inverse = normalize(total)
            unit_ref[rows, :] = unit
            inverse_ref[rows, :] = jnp.broadcast_to(inverse, (MB, 128))
            normed = unit * g1_ref[...] + s1_ref[...]
            normed_sc[rows, :] = normed
            low_sc[rows, :] = normed.astype(BF)

        low_ref[...] = jnp.transpose(low_sc[...])
        acc_sc[...] = jnp.zeros_like(acc_sc)

    @pl.loop(0, L // MB)
    def _(r):
        rows = pl.ds(pl.multiple_of(r * MB, MB), MB)
        pre = jnp.dot(low_sc[rows, :], wi_ref[...], preferred_element_type=F32) + bi_ref[...]
        acted, slope = gelu_parts(pre)
        acted = acted.astype(BF)
        slope_ref[rows, :] = slope.astype(BF)
        turned_ref[:, rows] = jnp.transpose(acted)
        acc_sc[rows, :] += jnp.dot(acted, wb_ref[...], preferred_element_type=F32)

    @pl.when(step == pl.num_programs(0) - 1)
    def _():
        sums_ref[...] = jnp.zeros_like(sums_ref)

        @pl.loop(0, L // MB)
        def _(r):
            rows = pl.ds(pl.multiple_of(r * MB, MB), MB)
            unit, inverse = normalize(normed_sc[rows, :] + (acc_sc[rows, :] + bb_ref[...]))
            out_ref[rows, :] = (unit * g2_ref[...] + s2_ref[...]).astype(BF)
            upstream = cot_ref[rows, :].astype(F32)
            middle = normalize_back(upstream * g2_ref[...], unit, inverse)
            mid_ref[rows, :] = middle
            branch = middle.astype(BF)
            branch_ref[rows, :] = branch
            sums_ref[0:1, :] += column_sum(upstream * unit)
            sums_ref[1:2, :] += column_sum(upstream)
            sums_ref[2:3, :] += column_sum(branch.astype(F32))


def feed_up(place, x, ctx_own, ctx, w_out, bo, g1, s1, w_in, bi, w_back, bb, g2, s2, cot):
    width = x.shape[1]
    units = w_in.shape[1]
    groups, own = w_out.shape[0], w_out.shape[1]
    row = whole(1, width)
    return pl.pallas_call(
        up_kernel,
        grid_spec=pltpu.PrefetchScalarGridSpec(
            num_scalar_prefetch=1,
            grid=(units // FC,),
            in_specs=[
                whole(L, width),
                whole(1, L, own),
                whole(groups - 1, L, own),
                whole(groups, own, width),
                row,
                row,
                row,
                pl.BlockSpec((width, FC), lambda n, place: (0, n)),
                pl.BlockSpec((1, FC), lambda n, place: (0, n)),
                pl.BlockSpec((FC, width), lambda n, place: (n, 0)),
                row,
                row,
                row,
                whole(L, width),
            ],
            out_specs=[
                whole(L, width),
                whole(L, width),
                whole(L, width),
                pl.BlockSpec((FC, L), lambda n, place: (n, 0)),
                pl.BlockSpec((L, FC), lambda n, place: (0, n)),
                whole(L, width),
                whole(L, 128),
                whole(width, L),
                whole(8, width),
            ],
            scratch_shapes=[
                pltpu.VMEM((L, width), F32),
                pltpu.VMEM((L, width), BF),
                pltpu.VMEM((L, width), F32),
            ],
        ),
        out_shape=[
            shaped(BF, L, width),
            shaped(F32, L, width),
            shaped(BF, L, width),
            shaped(BF, units, L),
            shaped(BF, L, units),
            shaped(F32, L, width),
            shaped(F32, L, 128),
            shaped(BF, width, L),
            shaped(F32, 8, width),
        ],
        name="feed_up",
        compiler_params=limit(32),
        cost_estimate=HINT,
    )(place, x, ctx_own, ctx, w_out, bo, g1, s1, w_in, bi, w_back, bb, g2, s2, cot)


def down_kernel(
    halved, place_ref, branch_ref, slope_ref, wb_ref, wi_ref, low_ref, mid_ref, unit_ref,
    inverse_ref, g1_ref, wo_ref, turned_own_ref, turned_ref, norm_own_ref, norm_ref, *refs
):
    bias_ref, first_ref, grad_own_ref, grad_ref, sums_ref = refs[:5]
    weight_refs = refs[5 : 7 if halved else 6]
    acc_sc, pre_sc, weight_sc = refs[-3:]
    step = pl.program_id(0)
    last = pl.num_programs(0) - 1
    groups, own = wo_ref.shape[0], wo_ref.shape[1]

    def give():
        if not halved:
            weight_refs[0][...] = weight_sc[...]
            return
        core = place_ref[1]
        chips, size = weight_refs[0].shape[0], weight_refs[0].shape[1]
        for chip in range(chips):
            for side, ref in ((1 - core, weight_refs[0]), (core, weight_refs[1])):
                at = pl.multiple_of((chip * 2 + side) * size, size)
                ref[chip] = weight_sc[pl.ds(at, size), :]

    @pl.when(step == 0)
    def _():
        acc_sc[...] = mid_ref[...]

    @pl.when(step < last)
    def _():
        total = None
        for r in range(L // MB):
            rows = slice(r * MB, (r + 1) * MB)
            pre = lax.dot_general(
                branch_ref[rows, :], wb_ref[...], NT, preferred_element_type=F32
            ) * slope_ref[rows, :].astype(F32)
            pre = pre.astype(BF)
            pre_sc[rows, :] = pre
            part = column_sum(pre.astype(F32))
            total = part if r == 0 else total + part
            acc_sc[rows, :] += lax.dot_general(
                pre, wi_ref[...], NT, preferred_element_type=F32
            )
        bias_ref[0:1, :] = total
        weight_sc[...] = jnp.dot(
            low_ref[...], pre_sc[...], preferred_element_type=F32
        ).astype(BF)
        give()

    @pl.when(step == last)
    def _():
        sums_ref[...] = jnp.zeros_like(sums_ref)

        @pl.loop(0, L // MB)
        def _(r):
            rows = pl.ds(pl.multiple_of(r * MB, MB), MB)
            hidden = acc_sc[rows, :]
            unit = unit_ref[rows, :]
            first = normalize_back(hidden * g1_ref[...], unit, inverse_ref[rows, 0:1])
            first_ref[rows, :] = first
            attended = first.astype(BF)
            pre_sc[rows, :] = attended
            sums_ref[0:1, :] += column_sum(hidden * unit)
            sums_ref[1:2, :] += column_sum(hidden)
            sums_ref[2:3, :] += column_sum(attended.astype(F32))

        def quarter_of(s, turned, norm, out):
            quarter = place_ref[0] ^ s
            at = pl.multiple_of(quarter * own, own)
            weight_sc[pl.ds(at, own), :] = jnp.dot(
                turned, pre_sc[...], preferred_element_type=F32
            ).astype(BF)
            grads = lax.dot_general(
                wo_ref[quarter], pre_sc[...], NT, preferred_element_type=F32
            )
            for h in range(own // HEAD_DIM):
                rows = slice(h * HEAD_DIM, (h + 1) * HEAD_DIM)
                out[rows, :] = (grads[rows, :] * norm[h : h + 1, :]).astype(BF)

        quarter_of(0, turned_own_ref[0], norm_own_ref[0], grad_own_ref.at[0])

        @pl.loop(1, groups)
        def _(s):
            quarter_of(s, turned_ref[s - 1], norm_ref[s - 1], grad_ref.at[s - 1])

        give()


def feed_down(place, halves, branch, slope, w_back, w_in, low, mid, unit, inverse, g1, w_out,
              turned_own, turned, norm_own, norm):
    width = branch.shape[1]
    units = w_in.shape[1]
    groups, own = w_out.shape[0], w_out.shape[1]
    steps = units // FC
    inside = lambda n: jnp.minimum(n, steps - 1)
    out_specs = [
        pl.BlockSpec((8, FC), lambda n, place: (0, inside(n))),
        whole(L, width),
        whole(1, own, L),
        whole(groups - 1, own, L),
        whole(8, width),
    ]
    out_shape = [
        shaped(F32, 8, units),
        shaped(F32, L, width),
        shaped(BF, 1, own, L),
        shaped(BF, groups - 1, own, L),
        shaped(F32, 8, width),
    ]
    if halves:
        size = width // (2 * halves)
        out_specs += [pl.BlockSpec((halves, size, FC), lambda n, place: (0, 0, n))] * 2
        out_shape += [shaped(BF, halves, size, units + width)] * 2
    else:
        out_specs += [pl.BlockSpec((width, FC), lambda n, place: (0, n))]
        out_shape += [shaped(BF, width, units + width)]
    return pl.pallas_call(
        functools.partial(down_kernel, bool(halves)),
        grid_spec=pltpu.PrefetchScalarGridSpec(
            num_scalar_prefetch=1,
            grid=(steps + 1,),
            in_specs=[
                whole(L, width),
                pl.BlockSpec((L, FC), lambda n, place: (0, inside(n))),
                pl.BlockSpec((FC, width), lambda n, place: (inside(n), 0)),
                pl.BlockSpec((width, FC), lambda n, place: (0, inside(n))),
                whole(width, L),
                whole(L, width),
                whole(L, width),
                whole(L, 128),
                whole(1, width),
                whole(groups, own, width),
                whole(1, own, L),
                whole(groups - 1, own, L),
                whole(1, 8, L),
                whole(groups - 1, 8, L),
            ],
            out_specs=out_specs,
            scratch_shapes=[
                pltpu.VMEM((L, width), F32),
                pltpu.VMEM((L, FC), BF),
                pltpu.VMEM((width, FC), BF),
            ],
        ),
        out_shape=out_shape,
        name="feed_down",
        compiler_params=limit(34),
        cost_estimate=HINT,
    )(place, branch, slope, w_back, w_in, low, mid, unit, inverse, g1, w_out,
      turned_own, turned, norm_own, norm)


def product_kernel(place_ref, left_ref, right_ref, out_ref):
    out_ref[...] = jnp.dot(
        left_ref[...], right_ref[...], preferred_element_type=F32
    ).astype(BF)


def product(place, left, right, sizes):
    rows, depth = left.shape
    columns = right.shape[1]
    count, size, halved = sizes
    take = (lambda n, place: (2 * n + 1 - place[1], 0)) if halved else (lambda n, place: (n, 0))
    return pl.pallas_call(
        product_kernel,
        grid_spec=pltpu.PrefetchScalarGridSpec(
            num_scalar_prefetch=1,
            grid=(count,),
            in_specs=[pl.BlockSpec((size, depth), take), whole(depth, columns)],
            out_specs=pl.BlockSpec((size, columns), lambda n, place: (n, 0)),
        ),
        out_shape=shaped(BF, count * size, columns),
        name="back_weights",
        compiler_params=limit(10),
        cost_estimate=HINT,
    )(place, left, right)


def kept_kernel(place_ref, left_ref, right_ref, got_ref, a_sent, a_kept, b_sent, b_kept):
    chip = pl.program_id(0)
    chip_y, chip_x = chip // 2, lax.rem(chip, 2)
    here_x, here_y = place_ref[2], place_ref[3]
    value = jnp.dot(left_ref[...], right_ref[...], preferred_element_type=F32)
    value = (value + got_ref[0].astype(F32)).astype(BF)
    cut = a_sent.shape[1]

    @pl.when(chip_x == here_x)
    def _():
        a_kept[chip_y] = value[:cut, :]

    @pl.when(chip_x != here_x)
    def _():
        a_sent[chip_y] = value[:cut, :]

    @pl.when(chip_y == here_y)
    def _():
        b_kept[chip_x] = value[cut:, :]

    @pl.when(chip_y != here_y)
    def _():
        b_sent[chip_x] = value[cut:, :]


def product_kept(place, left, right, got):
    chips, size, columns = got.shape
    depth = left.shape[1]
    part = whole(2, size // 2, columns)
    return pl.pallas_call(
        kept_kernel,
        grid_spec=pltpu.PrefetchScalarGridSpec(
            num_scalar_prefetch=1,
            grid=(chips,),
            in_specs=[
                pl.BlockSpec((size, depth), lambda n, place: (2 * n + place[1], 0)),
                whole(depth, columns),
                pl.BlockSpec((1, size, columns), lambda n, place: (n, 0, 0)),
            ],
            out_specs=[part] * 4,
        ),
        out_shape=[shaped(BF, 2, size // 2, columns)] * 4,
        name="kept_weights",
        compiler_params=limit(14),
        cost_estimate=HINT,
    )(place, left, right, got)


def total_of(*items):
    total = items[0].astype(F32)
    for item in items[1:]:
        total = total + item.astype(F32)
    return total.astype(BF)


def chips_kernel(count, layout, place_ref, *refs):
    inputs, outs = refs[:count], refs[count:]
    here_x, here_y = place_ref[2], place_ref[3]
    for order, (way, sources) in enumerate(layout):
        sent, kept = outs[2 * order], outs[2 * order + 1]
        start = 0
        for number, low, high in sources:
            kept_ref, got_ref = inputs[2 * number], inputs[2 * number + 1]
            for g in range(kept_ref.shape[0]):
                rows = slice(start, start + high - low)
                start += high - low
                for other in range(2):
                    for out, far in ((sent, 1), (kept, 0)):
                        if way == "x":
                            chip = other * 2 + (here_x ^ far)
                        else:
                            chip = (here_y ^ far) * 2 + other
                        out[other, rows, :] = total_of(
                            kept_ref[g, chip, low:high, :], got_ref[g, chip, low:high, :]
                        )


def sum_chips(place, pairs, parts, block):
    specs, out_specs, out_shape = [], [], []
    columns = pairs[0][0].shape[-1]
    for kept, _ in pairs:
        shape = kept.shape[:3] + (block,)
        specs += [pl.BlockSpec(shape, lambda n, place: (0, 0, 0, n))] * 2
    for _, sources in parts:
        height = sum(pairs[n][0].shape[0] * (high - low) for n, low, high in sources)
        out_specs += [pl.BlockSpec((2, height, block), lambda n, place: (0, 0, n))] * 2
        out_shape += [shaped(BF, 2, height, columns)] * 2
    return pl.pallas_call(
        functools.partial(chips_kernel, 2 * len(pairs), parts),
        grid_spec=pltpu.PrefetchScalarGridSpec(
            num_scalar_prefetch=1, grid=(columns // block,), in_specs=specs, out_specs=out_specs
        ),
        out_shape=out_shape,
        name="sum_chips",
        compiler_params=limit(14),
        cost_estimate=HINT,
    )(place, *[item for pair in pairs for item in pair])


def pairs_kernel(place_ref, a_kept, a_got, b_kept, b_got, a_sent, a_own, b_sent, b_own):
    here_x, here_y = place_ref[2], place_ref[3]
    for here, kept, got, sent, own in (
        (here_y, a_kept, a_got, a_sent, a_own),
        (here_x, b_kept, b_got, b_sent, b_own),
    ):
        sent[...] = total_of(kept[1 - here], got[1 - here])
        own[...] = total_of(kept[here], got[here])


def sum_pairs(place, a_kept, a_got, b_kept, b_got, block):
    columns = a_kept.shape[-1]
    spec = lambda item: pl.BlockSpec((2, item.shape[1], block), lambda n, place: (0, 0, n))
    flat = lambda item: pl.BlockSpec((item.shape[1], block), lambda n, place: (0, n))
    return pl.pallas_call(
        pairs_kernel,
        grid_spec=pltpu.PrefetchScalarGridSpec(
            num_scalar_prefetch=1,
            grid=(columns // block,),
            in_specs=[spec(a_kept), spec(a_got), spec(b_kept), spec(b_got)],
            out_specs=[flat(a_kept)] * 2 + [flat(b_kept)] * 2,
        ),
        out_shape=[shaped(BF, a_kept.shape[1], columns)] * 2
        + [shaped(BF, b_kept.shape[1], columns)] * 2,
        name="sum_pairs",
        compiler_params=limit(12),
        cost_estimate=HINT,
    )(place, a_kept, a_got, b_kept, b_got)


def cut_kernel(place_ref, a_kept, a_got, b_kept, b_got, sent, kept, sum_sc):
    cut = a_kept.shape[0]
    sum_sc[0:cut, :] = a_kept[...].astype(F32) + a_got[...].astype(F32)
    sum_sc[cut:, :] = b_kept[...].astype(F32) + b_got[...].astype(F32)
    size = kept.shape[1]
    for s, out in ((0, kept.at[0]), (1, sent.at[0]), (2, kept.at[1]), (3, sent.at[1])):
        at = pl.multiple_of((place_ref[0] ^ s) * size, 8)
        out[...] = sum_sc[pl.ds(at, size), :].astype(BF)


def cut_quarters(place, a_kept, a_got, b_kept, b_got, block):
    columns = a_kept.shape[-1]
    height = a_kept.shape[0] + b_kept.shape[0]
    spec = lambda item: pl.BlockSpec((item.shape[0], block), lambda n, place: (0, n))
    return pl.pallas_call(
        cut_kernel,
        grid_spec=pltpu.PrefetchScalarGridSpec(
            num_scalar_prefetch=1,
            grid=(columns // block,),
            in_specs=[spec(a_kept), spec(a_got), spec(b_kept), spec(b_got)],
            out_specs=[pl.BlockSpec((2, height // 4, block), lambda n, place: (0, 0, n))] * 2,
            scratch_shapes=[pltpu.VMEM((height, block), F32)],
        ),
        out_shape=[shaped(BF, 2, height // 4, columns)] * 2,
        name="cut_quarters",
        compiler_params=limit(12),
        cost_estimate=HINT,
    )(place, a_kept, a_got, b_kept, b_got)


def halves_kernel(place_ref, a_kept, a_got, b_kept, b_got, *refs):
    outs, sum_sc = refs[:-1], refs[-1]
    cut = a_kept.shape[0]
    sum_sc[0:cut, :] = a_kept[...].astype(F32) + a_got[...].astype(F32)
    sum_sc[cut:, :] = b_kept[...].astype(F32) + b_got[...].astype(F32)
    size, wide = outs[0].shape[1:]
    for out, lanes, first, second in (
        (outs[0], slice(0, wide), 1, 3),
        (outs[1], slice(0, wide), 0, 2),
        (outs[2], slice(wide, 2 * wide), 2, 3),
        (outs[3], slice(wide, 2 * wide), 0, 1),
    ):
        for n, s in ((0, first), (1, second)):
            at = pl.multiple_of((place_ref[0] ^ s) * size, 8)
            out[n] = sum_sc[pl.ds(at, size), lanes].astype(BF)


def cut_halves(place, a_kept, a_got, b_kept, b_got):
    vmem = pl.BlockSpec(memory_space=pltpu.VMEM)
    columns = a_kept.shape[-1]
    height = a_kept.shape[0] + b_kept.shape[0]
    return pl.pallas_call(
        halves_kernel,
        in_specs=[pl.BlockSpec(memory_space=pltpu.SMEM)] + [vmem] * 4,
        out_specs=[vmem] * 4,
        out_shape=[shaped(BF, 2, height // 4, columns // 2)] * 4,
        scratch_shapes=[pltpu.VMEM((height, columns), F32)],
        name="cut_halves",
        compiler_params=limit(8),
        cost_estimate=HINT,
    )(place, a_kept, a_got, b_kept, b_got)


def last_kernel(a_kept, a_got, b_kept, b_got, short_ref, *outs):
    size = outs[0].shape[0] - 16
    many = short_ref.shape[0] // 8 * 8
    first = 10
    for s, out in enumerate(outs):
        rows = slice(s % 2 * size, (s % 2 + 1) * size)
        kept, got = (a_kept, a_got) if s < 2 else (b_kept, b_got)
        out[0:size, :] = total_of(kept[rows, :], got[rows, :])
        row = lax.broadcasted_iota(I32, (many, short_ref.shape[1]), 0)
        short = jnp.where(row < first, short_ref[...], 0.0)
        short = short + jnp.where(row == first, short_ref[first + s : first + s + 1, :], 0.0)
        out[size : size + many, :] = short.astype(BF)


def cut_last(a_kept, a_got, b_kept, b_got, short):
    vmem = pl.BlockSpec(memory_space=pltpu.VMEM)
    size, columns = b_kept.shape[0] // 2, b_kept.shape[1]
    return pl.pallas_call(
        last_kernel,
        in_specs=[vmem] * 5,
        out_specs=[vmem] * 4,
        out_shape=[shaped(BF, size + 16, columns)] * 4,
        name="cut_last",
        compiler_params=limit(8),
        cost_estimate=HINT,
    )(a_kept, a_got, b_kept, b_got, short)


def join_kernel(orders, place_ref, *refs):
    inputs, outs = refs[: 3 * len(orders)], refs[3 * len(orders) :]
    size, wide = inputs[0].shape
    start = 0
    for out in outs:
        done = 0
        while done < out.shape[1]:
            half, low = divmod(start + done, wide)
            many = min(wide - low, out.shape[1] - done)
            own, one, two = inputs[3 * half : 3 * half + 3]
            lanes = slice(low, low + many)
            near, far, farther = orders[half]
            for s, piece in (
                (0, own[:, lanes]), (near, one[:, lanes]), (far, two[0, :, lanes]),
                (farther, two[1, :, lanes]),
            ):
                at = pl.multiple_of((place_ref[0] ^ s) * size, 8)
                out[pl.ds(at, size), done : done + many] = piece.astype(F32)
            done += many
        start += out.shape[1]


def join_quarters(place, parts, orders, widths):
    vmem = pl.BlockSpec(memory_space=pltpu.VMEM)
    return pl.pallas_call(
        functools.partial(join_kernel, orders),
        in_specs=[pl.BlockSpec(memory_space=pltpu.SMEM)] + [vmem] * (3 * len(parts)),
        out_specs=[vmem] * len(widths),
        out_shape=[shaped(F32, 4 * parts[0][0].shape[0], width) for width in widths],
        name="join_quarters",
        compiler_params=limit(8),
        cost_estimate=HINT,
    )(place, *[item for part in parts for item in part])


def chips_join_kernel(place_ref, mine_a, mine_b, got_a, got_b, ends_ref, got_ends, out_ref, *outs):
    core, here_x, here_y = place_ref[1], place_ref[2], place_ref[3]
    cut = mine_a.shape[2]
    size = cut + mine_b.shape[2]
    for far_y in range(2):
        for far_x in range(2):
            chip = (here_y ^ far_y) * 2 + (here_x ^ far_x)
            for side, a_ref, b_ref in ((core, mine_a, mine_b), (1 - core, got_a, got_b)):
                at = (chip * 2 + side) * size
                first = pl.multiple_of(at, 8)
                out_ref[pl.ds(first, cut), :] = a_ref[far_y, far_x].astype(F32)
                second = pl.multiple_of(at + cut, 8)
                out_ref[pl.ds(second, size - cut), :] = b_ref[far_x, far_y].astype(F32)
    total = ends_ref[...].astype(F32) + got_ends[...].astype(F32)
    bias_ref, tables_ref, inner_ref = outs[:3]
    vectors = outs[3:]
    here = (here_y * 2 + here_x) * 2 + core
    width = total.shape[1]
    share = vectors[0].shape[1]
    part = inner_ref.shape[1]
    deep = part * 8 // width
    slices = jnp.zeros((len(vectors), share), F32)
    inner = jnp.zeros((1, part), F32)
    for d in range(8):
        mine = here == d
        slices = slices + jnp.where(
            mine, total[0 : len(vectors), d * share : (d + 1) * share], 0.0
        )
        row, lane = 6 + d * part // width, d * part % width
        inner = inner + jnp.where(mine, total[row : row + 1, lane : lane + part], 0.0)
    inner_ref[...] = inner
    for n, ref in enumerate(vectors):
        ref[...] = slices[n : n + 1, :]
    short = total[6 + deep : 7 + deep, :]
    own = bias_ref.shape[1]
    bias_ref[0:1, :] = short[:, 0:own]
    bias_ref[1:2, :] = short[:, own : 2 * own]
    per, _, buckets = tables_ref.shape
    for n in range(2):
        for h in range(per):
            lane = 2 * own + (n * per + h) * buckets
            tables_ref[h, n : n + 1, :] = short[:, lane : lane + buckets]


def join_chips(place, mine_a, mine_b, got_a, got_b, ends, got_ends, units, own, heads, buckets):
    vmem = pl.BlockSpec(memory_space=pltpu.VMEM)
    rows = 8 * (mine_a.shape[2] + mine_b.shape[2])
    width = mine_a.shape[-1]
    out_shape = [
        shaped(F32, rows, width),
        shaped(F32, 2, own),
        shaped(F32, heads, 2, buckets),
        shaped(F32, 1, units // 8),
    ] + [shaped(F32, 1, width // 8)] * 6
    return pl.pallas_call(
        chips_join_kernel,
        in_specs=[pl.BlockSpec(memory_space=pltpu.SMEM)] + [vmem] * 6,
        out_specs=[vmem] * len(out_shape),
        out_shape=out_shape,
        name="join_chips",
        compiler_params=limit(8),
        cost_estimate=HINT,
    )(place, mine_a, mine_b, got_a, got_b, ends, got_ends)


def tie(values, *others):
    return lax.optimization_barrier((values, others))[0]


def swap(array, bit):
    count = lax.axis_size("docs")
    return lax.ppermute(array, "docs", [(i, i ^ (1 << bit)) for i in range(count)])


def away(array, distance):
    count = lax.axis_size("heads")
    return lax.ppermute(array, "heads", [(i, i ^ distance) for i in range(count)])


def in_order(pieces, z):
    stacked = jnp.stack(pieces)
    picks = [lax.dynamic_index_in_dim(stacked, z ^ s, 0) for s in range(len(pieces))]
    return jnp.concatenate(picks, axis=0)


def tree(items):
    while len(items) > 1:
        items = [items[n] + items[n + 1] for n in range(0, len(items), 2)]
    return items[0]


def sum_everywhere(rows):
    for bit in range(lax.axis_size("docs").bit_length() - 1):
        rows = rows + swap(rows, bit)
    return tree([rows] + [away(rows, s) for s in range(1, lax.axis_size("heads"))])


def spread_plane(first, second):
    got = [swap(first, 1), swap(second, 2)]
    first, second = jnp.stack([first, got[0]]), jnp.stack([second, got[1]])
    got = [swap(first, 2), swap(second, 1)]
    return jnp.stack([first, got[0]]), jnp.stack([second, got[1]])


def reduce_docs(blocks):
    bits = blocks.shape[0].bit_length() - 1
    docs = lax.axis_index("docs")
    current = blocks.reshape((2,) * bits + blocks.shape[1:])
    for bit in range(bits):
        mine = (docs >> bit) & 1
        axis = bits - 1 - bit
        sent = lax.dynamic_index_in_dim(current, 1 - mine, axis, keepdims=False)
        kept = lax.dynamic_index_in_dim(current, mine, axis, keepdims=False)
        current = total_of(kept, swap(sent, bit))
    return current


def spread_docs(block):
    count = lax.axis_size("docs")
    docs = lax.axis_index("docs")
    current = block
    for done, bit in enumerate(range(count.bit_length() - 2, -1, -1)):
        got = swap(current, bit)
        mine = ((docs >> bit) & 1) == 1
        current = jnp.stack(
            [jnp.where(mine, got, current), jnp.where(mine, current, got)], axis=done
        )
    return current.reshape((count,) + block.shape)


def body(
    layer_input, token_boxes, lengths, w_qkv, qv_bias, rel_tables, w_out, out_bias,
    gain_one, shift_one, w_in, in_bias, w_back, back_bias, gain_two, shift_two, cotangent,
):
    width = layer_input.shape[1]
    units = w_in.shape[1]
    groups = lax.axis_size("heads")
    count = lax.axis_size("docs")
    docs = lax.axis_index("docs")
    z = lax.axis_index("heads")
    own = w_qkv.shape[2]
    heads = rel_tables.shape[1]
    buckets = rel_tables.shape[2]
    columns = 3 * own
    share = width // count
    small = columns // count
    chips = 4 if count == 8 and share % 16 == 0 and small % 8 == 0 else 0
    place = jnp.stack([z, docs & 1, (docs >> 1) & 1, (docs >> 2) & 1]).astype(I32)

    still = lambda array: pltpu.with_memory_space_constraint(array, pltpu.HBM)
    matrix = w_qkv.transpose(1, 2, 0).reshape(columns, width)
    if chips:
        piece, extra = first_piece(
            place, still(matrix), still(qv_bias), still(rel_tables.transpose(1, 0, 2)), count
        )
    else:
        room = jnp.zeros((128 - heads * buckets,), BF)
        line = jnp.concatenate(
            [qv_bias[0], qv_bias[1], rel_tables[0].reshape(-1), room, rel_tables[1].reshape(-1), room]
        )
        extra = jnp.pad(line[None], ((0, 7), (0, width - line.shape[0])))
        piece = jnp.concatenate(
            [lax.dynamic_slice_in_dim(matrix, docs * small, small, axis=0), extra], axis=0
        )
    got = [away(piece, s) for s in range(1, groups)]
    bucket, near = buckets_of(place, lengths, still(token_boxes))

    ctx_own, turned_own, raised_own, qkv_own, norm_own = attend_forward(
        place, still(layer_input), (still(matrix[None]),), extra[None], bucket, near
    )
    arrived = jnp.stack(tie(got, ctx_own))
    if chips:
        cut = (small // 2 + 7) // 8 * 8
        first, second = spread_plane(arrived[:, :cut], arrived[:, cut:small])
        weights, ctx, turned, raised, qkv, norm = attend_forward(
            place, layer_input, (first, second, swap(first, 0), swap(second, 0)),
            arrived[:, small:], bucket, near,
        )
    else:
        weights = spread_docs(arrived[:, :small]).transpose(1, 0, 2, 3)
        weights = weights.reshape(groups - 1, columns, width)
        ctx, turned, raised, qkv, norm = attend_forward(
            place, layer_input, (weights,), arrived[:, small:], bucket, near
        )

    w_out_heads = w_out.reshape(groups, own, width)
    flat = lambda vector: vector.reshape(1, -1)
    layer_output, grad_mid, grad_branch, acted, slope, unit, inverse, low, up_sums = feed_up(
        place, layer_input, ctx_own, ctx, w_out_heads, flat(out_bias), flat(gain_one),
        flat(shift_one), w_in, flat(in_bias), w_back, flat(back_bias), flat(gain_two),
        flat(shift_two), cotangent,
    )
    down = lambda branch: feed_down(
        place, chips, branch, slope, w_back, w_in, low, grad_mid, unit, inverse, flat(gain_one),
        w_out_heads, turned_own, turned, norm_own, norm,
    )
    own_back = lambda grad, start: attend_backward(
        place, chips, layer_input, matrix[None], qkv_own, still(raised_own), norm_own, grad, start
    )
    rest_back = lambda span, grad, start: attend_backward(
        place, chips, layer_input, weights, qkv, raised, norm, grad, start, span
    )

    if chips:
        half = share // 2
        back_size = units // count
        sent = product(place, acted, grad_branch, (chips, back_size, True))
        got = swap(sent.reshape(chips, back_size, width), 0)
        back = product_kept(place, acted, grad_branch, got)
        back_got = [swap(back[0], 1), swap(back[2], 2)]

        in_sums, grad_first, grad_own, grad_rest, down_sums, dense_sent, dense_kept = down(
            tie(grad_branch, back[0], back[2])
        )
        back_got = tie(back_got, grad_first)
        back = sum_pairs(place, back[1], back_got[0], back[3], back_got[1], width // 2)
        back_got = [swap(back[0], 2), swap(back[2], 1)]
        dense_sent = tie(dense_sent, back[0])
        dense_got = swap(dense_sent, 0)

        dx, ds_own, sums_own, own_sent, own_kept = own_back(
            tie(grad_own, dense_sent, back[0], back[2]), grad_first
        )
        dense_got, back_got = tie((dense_got, back_got), dx)
        dense = sum_chips(
            place,
            [(dense_kept[None], dense_got[None])],
            (("x", ((0, 0, half),)), ("y", ((0, half, share),))),
            FC,
        )
        back_sent, back = cut_quarters(
            place, back[1], back_got[0], back[3], back_got[1], width // 2
        )
        dense = list(dense)
        dense[0], dense[2], own_sent = tie((dense[0], dense[2], own_sent), back_sent)
        dense_got = [swap(dense[0], 1), swap(dense[2], 2)]
        back_got = away(back_sent, 1)
        own_got = swap(own_sent, 0)

        dx, ds_one, sums_one, one_sent, one_kept = rest_back(
            (0, 1), tie(grad_rest, dense[0], dense[2], own_sent, back_sent), dx
        )
        own_got, back_got = tie((own_got, back_got), dx)
        back = total_of(back, back_got)
        one_sent = tie(one_sent, back)
        one_got = swap(one_sent, 0)
        back_got = away(back[1], 2)

        dx, ds_two, sums_two, two_sent, two_kept = rest_back(
            (1, 3), tie(grad_rest, one_sent, back), dx
        )
        dense_got, back_got, one_got = tie((dense_got, back_got, one_got), dx)
        dense = list(
            sum_pairs(
                place, dense[1], dense_got[0], dense[3], dense_got[1], (units + width) // 3
            )
        )
        back = total_of(back[0], back_got)
        two_sent, dense[0], dense[2], back = tie((two_sent, dense[0], dense[2], back), dense[1])
        two_got = swap(two_sent, 0)
        dense_got = [swap(dense[0], 2), swap(dense[2], 1)]
        back_one = away(back, 2)
        scores = (ds_own, ds_one, ds_two)
        acc = table_products(
            scores, tie(bucket, back, two_sent, dense[0], dense[2]),
            jnp.zeros((groups * heads * 8, 512), F32), 0,
        )

        two_got, dense_got, back_one = tie((two_got, dense_got, back_one), acc)
        dense = cut_halves(place, dense[1], dense_got[0], dense[3], dense_got[1])
        dense_sent, dense = [dense[0], dense[2]], [dense[1], dense[3]]
        own_got, one_got, two_got = tie((own_got, one_got, two_got), dense_sent)
        last_a = sum_chips(
            place, [(own_kept, own_got), (one_kept, one_got)],
            (("x", ((0, 0, small), (1, 0, small))),), width // 2,
        )
        last_b = sum_chips(place, [(two_kept, two_got)], (("y", ((0, 0, small),)),), width // 2)
        back_two = jnp.stack([back, back_one])
        last_a, last_b, dense_sent, back_two = tie((last_a, last_b, dense_sent, back_two))
        last_a_got = swap(last_a[0], 1)
        last_b_got = swap(last_b[0], 2)
        dense_got = [away(dense_sent[0], 1), away(dense_sent[1], 2)]
        back_two = away(back_two, 1)
        acc = table_products(
            scores, tie(bucket, last_b[0], last_a[0], dense_sent), acc, 1
        )
        short = short_rows(acc, (sums_own, sums_one, sums_two), down_sums, up_sums, in_sums, heads)

        last_a_got, last_b_got, dense_got = tie((last_a_got, last_b_got, dense_got), acc)
        last = list(sum_pairs(place, last_a[1], last_a_got, last_b[1], last_b_got, width // 2))
        dense = [total_of(*pair) for pair in zip(dense, dense_got)]
        last[0], last[2], dense = tie((last[0], last[2], dense), last[1])
        last_got = [swap(last[0], 2), swap(last[2], 1)]
        dense_got = [away(dense[0][1], 2), away(dense[1][1], 1)]
        last_got, short = tie((last_got, short), dense, back_two)
        last = cut_last(last[1], last_got[0], last[3], last_got[1], short)
        last_got = [away(last[s], s) for s in range(1, groups)]
        dense_got, back_two = tie((dense_got, back_two), last[0])
        dense = [total_of(item[0], got) for item, got in zip(dense, dense_got)]
        dense_one = [away(dense[0], 2), away(dense[1], 1)]
        (out_back,) = join_quarters(place, [(back, back_one, back_two)], ((2, 1, 3),), (width,))
        grad_input = dx.astype(BF)
        last_got = tie(last_got, dense, out_back, grad_input)
        quarter = total_of(last[0][:small], *[item[:small] for item in last_got])
        ends = tree([item[small:].astype(F32) for item in [last[0]] + last_got]).astype(BF)
        first, second = quarter[:cut], quarter[cut:]
        rest = small - cut
        got = [swap(first, 1), swap(jnp.concatenate([second, ends]), 2)]
        dense_one = tie(dense_one, first, second)
        dense_two = [jnp.stack(pair) for pair in zip(dense, dense_one)]
        dense_two = [away(dense_two[0], 1), away(dense_two[1], 2)]
        got = tie(got, dense_one)
        ends = total_of(ends, got[1][rest:])
        first, second = jnp.stack([first, got[0]]), jnp.stack([second, got[1][:rest]])
        both = jnp.concatenate([second, ends.reshape(2, -1, width)], axis=1)
        got = [swap(first, 2), swap(both, 1)]
        dense_two = tie(dense_two, first, both)
        ends = total_of(ends, got[1][:, rest:].reshape(ends.shape))
        first, second = jnp.stack([first, got[0]]), jnp.stack([second, got[1][:, :rest]])
        got = [swap(first, 0), swap(second, 0), swap(ends, 0)]
        out_in, out_out = join_quarters(
            place, list(zip(dense, dense_one, dense_two)), ((2, 1, 3), (1, 2, 3)), (units, width)
        )
        got = tie(got, out_in)
        full, grad_bias, grad_tables, grad_inner, *vectors = join_chips(
            place, first, second, got[0], got[1], ends, got[2], units, own, heads, buckets
        )
        grad_tables = grad_tables.transpose(1, 0, 2)
        vectors = [vector.reshape(share) for vector in vectors]
        grad_inner = grad_inner.reshape(units // count)
    else:
        back_grads = product(place, acted, grad_branch, (units // FC, FC, False))
        in_sums, grad_first, grad_own, grad_rest, down_sums, dense_grads = down(grad_branch)
        dx, ds_own, sums_own, dw_own = own_back(grad_own, grad_first)
        dx, ds_rest, sums_rest, dw_rest = rest_back(None, grad_rest, dx)
        acc = jnp.zeros((groups * heads * 8, 512), F32)
        for part in range(2):
            acc = table_products((ds_own, ds_rest), bucket, acc, part)
        short = short_rows(acc, (sums_own, sums_rest), down_sums, up_sums, in_sums, heads)
        begin = 6 + units // width
        quarters = in_order([short[begin + s] for s in range(groups)], z)
        total = sum_everywhere(jnp.concatenate([short[:begin], quarters], axis=0))
        ends = lax.dynamic_index_in_dim(total, begin + z, 0, keepdims=False)

        def sum_heads(parts):
            return total_of(parts[0], *[away(parts[s], s) for s in range(1, groups)])

        def dense_rows(grads):
            rows = reduce_docs(grads.reshape(count, -1, grads.shape[1]))
            parts = rows.reshape(-1, groups, width)
            parts = [
                lax.dynamic_index_in_dim(parts, z ^ s, 1, keepdims=False) for s in range(groups)
            ]
            mine = sum_heads(parts)
            pieces = [mine] + [away(mine, s) for s in range(1, groups)]
            return in_order(pieces, z).transpose(1, 0, 2).reshape(rows.shape).astype(F32)

        out_back = dense_rows(back_grads)
        rows = dense_rows(dense_grads)
        out_in, out_out = rows[:, :units], rows[:, units:]
        blocks = jnp.concatenate([dw_own, dw_rest]).reshape(groups, count, small, width)
        blocks = blocks.transpose(1, 0, 2, 3).reshape(count, groups * small, width)
        blocks = reduce_docs(blocks).reshape(groups, small, width)
        full = spread_docs(sum_heads([blocks[s] for s in range(groups)]))
        full = full.reshape(columns, width).astype(F32)

        grad_input = dx.astype(BF)
        mine = lambda vector: lax.dynamic_slice_in_dim(
            vector, docs * (vector.shape[0] // count), vector.shape[0] // count
        )
        grad_bias = ends[: 2 * own].reshape(2, own)
        grad_tables = ends[2 * own : 2 * own + 2 * heads * buckets].reshape(2, heads, buckets)
        vectors = [mine(total[n]) for n in range(6)]
        grad_inner = mine(total[6:begin].reshape(-1))
    return (
        layer_output,
        grad_input,
        full.reshape(3, own, width).transpose(2, 0, 1),
        grad_bias,
        grad_tables,
        out_out,
        vectors[2],
        vectors[0],
        vectors[1],
        out_in,
        grad_inner,
        out_back,
        vectors[5],
        vectors[3],
        vectors[4],
    )


def solution(mesh):
    rows = P(("docs", "heads"), None)
    return jax.shard_map(
        body,
        mesh=mesh,
        in_specs=(
            rows,
            P(None, "docs"),
            P("docs"),
            P(None, None, "heads"),
            P(None, "heads"),
            P(None, "heads", None),
            P(),
            P(),
            P(),
            P(),
            P(),
            P(),
            P(),
            P(),
            P(),
            P(),
            rows,
        ),
        out_specs=(
            rows,
            rows,
            P(None, None, "heads"),
            P(None, "heads"),
            P(None, "heads", None),
            P("docs", None),
            P("docs"),
            P("docs"),
            P("docs"),
            P("docs", None),
            P("docs"),
            P("docs", None),
            P("docs"),
            P("docs"),
            P("docs"),
        ),
        check_vma=False,
    )
```
